32 devices in a mesh: seq: 2 (over x), fsdp: 16 (over z, y, core).
Axes of the slice: x: 2, y: 2, z: 4, core: 2. Of those that a mesh axis runs over, the one named last changes fastest.
Arguments:
- residual_in: bfloat16 [16, 1024, 767], P('fsdp', 'seq'), may hold values from -6 to 6
- cotangent: bfloat16 [16, 1024, 767], P('fsdp', 'seq'), may hold values from -6 to 6
- w_qkv: bfloat16 [768, 2304], P('fsdp'), may hold values from -0.3125 to 0.3125
- w_out: bfloat16 [768, 768], P('fsdp'), may hold values from -1.25 to 1.25
- w_fc: bfloat16 [768, 3072], P('fsdp'), may hold values from -0.21875 to 0.21875
- w_proj: bfloat16 [3072, 768], P('fsdp'), may hold values from -0.109375 to 0.109375
- attn_bias: bfloat16 [3, 768], P(None, 'fsdp'), may hold values from -1.5 to 1.5
- fc_bias: bfloat16 [3072], P('fsdp'), may hold values from -1.5 to 1.5
- proj_bias: bfloat16 [768], P('fsdp'), may hold values from -1.5 to 1.5
- gains: bfloat16 [2, 768], P(None, 'fsdp'), may hold values from 0.099609375 to 1.8984375
Outputs:
- residual_out: bfloat16 [16, 1024, 767], P('fsdp', 'seq')
- input_grad: bfloat16 [16, 1024, 767], P('fsdp', 'seq')
- grad_qkv: float32 [768, 2304], P('fsdp')
- grad_out: float32 [768, 768], P('fsdp')
- grad_fc: float32 [768, 3072], P('fsdp')
- grad_proj: float32 [3072, 768], P('fsdp')
- grad_attn_bias: float32 [3, 768], P(None, 'fsdp')
- grad_fc_bias: float32 [3072], P('fsdp')
- grad_proj_bias: float32 [768], P('fsdp')
- grad_gains: float32 [2, 768], P(None, 'fsdp')
The draws below stay inside these ranges and needn't reach their ends.
All inputs are finite; a program needn't handle non-finite values.
Results may differ from the reference program's by a relative error of at most 0.014.
The reference program's roundings to bfloat16 on the way count: a program that leaves them out, or rounds other values in their place, can miss the bound.
Values may be sent and summed in bfloat16 or wider, within the bound.
A program may use at most 192 MiB of HBM per device.

```python
import math
import jax
import jax.numpy as jnp
from jax import lax

D = 768
H = 12
HD = 64
FF = 3072
LENGTH = 1024
RES = 767
SEQS = 16


def draw_residual_in(key, part):
    base = jax.random.truncated_normal(key, -4.0, 4.0, (SEQS, LENGTH, D), jnp.float32)
    return ((base[..., :-1] - base[..., 1:]) * 0.75).astype(jnp.bfloat16)


def level_of(stream_key, dims, cuts, low, high):
    loudness = 1.0
    for axis_at, shards_of in cuts:
        draws = jax.random.uniform(jax.random.fold_in(jax.random.fold_in(stream_key, 6), axis_at), (shards_of,), jnp.float32, low / len(cuts), high / len(cuts))
        loudness = loudness * jnp.repeat(jnp.exp(draws), dims[axis_at] // shards_of).reshape((-1,) + (1,) * (len(dims) - 1 - axis_at))
    return loudness


def noise(stream_key, dims, scale, most, shards=(), kind=jnp.bfloat16):
    values = jax.random.normal(stream_key, dims, jnp.float32) * scale
    if len(shards) > 0:
        values = level_of(stream_key, dims, shards, -0.22, 0.18) * values
    return jnp.clip(values, min=-most, max=most).astype(kind)


def setup_inputs(seed: int = 0) -> dict:
    keys = jax.random.split(jax.random.key(seed), 11)
    return {
        "residual_in": draw_residual_in(jax.random.fold_in(keys[10], 71), 0),
        "cotangent": noise(keys[1], (SEQS, LENGTH, RES), 1.0, 6.0, ((0, 16), (1, 2))),
        "w_qkv": noise(keys[2], (D, 3 * D), (D // 2) ** -0.5, 0.3125, ((0, 16),)),
        "w_out": noise(keys[3], (D, D), (D // 32) ** -0.5, 1.25, ((0, 16),)),
        "w_fc": noise(keys[4], (D, FF), D ** -0.5, 0.21875, ((0, 16),)),
        "w_proj": noise(keys[5], (FF, D), FF ** -0.5, 0.109375, ((0, 16),)),
        "attn_bias": noise(keys[6], (3, D), 0.3, 1.5, ((1, 16),)),
        "fc_bias": noise(keys[7], (FF,), 0.3, 1.5, ((0, 16),)),
        "proj_bias": noise(keys[8], (D,), 0.3, 1.5, ((0, 16),)),
        "gains": jnp.clip(1.0 + 0.18 * jax.random.normal(keys[9], (2, D), jnp.float32), 0.099609375, 1.8984375).astype(jnp.bfloat16),
    }


EPSILON = 1e-05
HIGHEST = lax.Precision.HIGHEST

@jax.custom_vjp
def low(v):
    return lax.optimization_barrier(v.astype(jnp.bfloat16)).astype(jnp.float32)

@jax.custom_vjp
def low_back(v):
    return v

def low_keep(v):
    return (low(v), None)

def low_pass(kept, grad):
    return (grad,)

def back_keep(v):
    return (v, None)

def back_low(kept, grad):
    return (low(grad),)
low.defvjp(low_keep, low_pass)
low_back.defvjp(back_keep, back_low)

def rms_norm(values, gain):
    return values * lax.rsqrt(lax.optimization_barrier(jnp.mean(values * values, axis=-1, keepdims=True)) + EPSILON) * gain

def center(values):
    return values - lax.optimization_barrier(jnp.mean(values, axis=-1, keepdims=True))

def project(left, weight):
    return jnp.einsum('gtd,de->gte', left, weight, precision=HIGHEST)

def attention(queries, keys_all, values_all):
    length = queries.shape[1]
    block = min(512, length)
    count = length // block
    scale = HD ** (-0.5)
    key_pos = jnp.arange(length, dtype=jnp.int32)

    @jax.checkpoint
    def one_block(block_index):
        start = (block_index * block).astype(jnp.int32)
        query_block = lax.dynamic_slice_in_dim(queries, start, block, 1)
        scores = jnp.einsum('gqhd,gkhd->ghqk', query_block, keys_all, precision=HIGHEST) * scale
        scores = low_back(scores)
        query_pos = start + jnp.arange(block, dtype=jnp.int32)
        allowed = query_pos[:, None] >= key_pos[None, :]
        scores = jnp.where(allowed, scores, -1e+30)
        peak = lax.optimization_barrier(jnp.max(scores, axis=-1, keepdims=True))
        weights = jnp.exp(scores - peak)
        weights = weights / lax.optimization_barrier(jnp.sum(weights, axis=-1, keepdims=True))
        return jnp.einsum('ghqk,gkhd->gqhd', low(weights), values_all, precision=HIGHEST)
    blocks = lax.map(one_block, jnp.arange(count, dtype=jnp.int32))
    return jnp.moveaxis(blocks, 0, 1).reshape(queries.shape)

def forward(residual, w_qkv, w_out, w_fc, w_proj, attn_bias, fc_bias, proj_bias, gains):
    groups = residual.shape[0]
    length = residual.shape[1]
    full = jnp.concatenate([residual, -lax.optimization_barrier(jnp.sum(residual, axis=-1, keepdims=True))], axis=-1)
    normed = low(rms_norm(full, gains[0]))
    bias_qkv = jnp.concatenate([attn_bias[0], jnp.zeros_like(attn_bias[0]), attn_bias[1]])
    projected = low(low_back(project(normed, w_qkv) + bias_qkv))
    split = projected.reshape(groups, length, 3, H, HD)
    mixed = attention(split[:, :, 0], split[:, :, 1], split[:, :, 2]).reshape(groups, length, D)
    mixed = low(low_back(mixed))
    branch = low_back(project(mixed, w_out) + attn_bias[2])
    middle = full + center(branch)
    normed_two = low(rms_norm(middle, gains[1]))
    hidden = low_back(project(normed_two, w_fc) + fc_bias)
    activated = low(jax.nn.gelu(hidden, approximate=True))
    branch_two = low_back(project(activated, w_proj) + proj_bias)
    final = middle + center(branch_two)
    return final[..., :-1]

def reference(residual_in, cotangent, w_qkv, w_out, w_fc, w_proj, attn_bias, fc_bias, proj_bias, gains):
    params = (w_qkv.astype(jnp.float32), w_out.astype(jnp.float32), w_fc.astype(jnp.float32), w_proj.astype(jnp.float32), attn_bias.astype(jnp.float32), fc_bias.astype(jnp.float32), proj_bias.astype(jnp.float32), gains.astype(jnp.float32))
    group = math.gcd(SEQS, max(1, 4096 // LENGTH))
    inputs = residual_in.astype(jnp.float32).reshape(SEQS // group, group, LENGTH, RES)
    upstream = cotangent.astype(jnp.float32).reshape(SEQS // group, group, LENGTH, RES)

    def step(totals, item):
        residual, grad_in = item
        result, pull = jax.vjp(forward, residual, *params)
        grads = pull(grad_in)
        totals = tuple((total + grad for total, grad in zip(totals, grads[1:])))
        return (totals, (result.astype(jnp.bfloat16), grads[0].astype(jnp.bfloat16)))
    start = tuple((jnp.zeros_like(param) for param in params))
    totals, (results, input_grads) = lax.scan(step, start, (inputs, upstream))
    residual_out = results.reshape(SEQS, LENGTH, RES)
    input_grad = input_grads.reshape(SEQS, LENGTH, RES)
    return (residual_out, input_grad, totals[0], totals[1], totals[2], totals[3], totals[4], totals[5], totals[6], totals[7])
```

```python
import functools

import jax
import jax.numpy as jnp
from jax import lax
from jax.experimental import pallas as pl
from jax.experimental.pallas import tpu as pltpu
from jax.sharding import PartitionSpec as P

HD = 64
EPSILON = 1e-05
MASKED = -1e30
MESH = pl.DeviceIdType.MESH
ANY = pl.BlockSpec(memory_space=pl.ANY)


class Place:
    def __init__(self, shards):
        self.length = shards // 4
        self.x = lax.axis_index("seq")
        index = lax.axis_index("fsdp")
        self.index = index
        self.core = lax.rem(index, 2)
        self.y = lax.rem(index // 2, 2)
        self.line = index // 4

    def at(self, **moved):
        x = moved.get("x", self.x)
        line = moved.get("line", self.line)
        y = moved.get("y", self.y)
        core = moved.get("core", self.core)
        return (x, (line * 2 + y) * 2 + core)

    def beside_x(self):
        return self.at(x=1 - self.x)

    def beside_y(self):
        return self.at(y=1 - self.y)

    def sibling(self):
        return self.at(core=1 - self.core)

    def above(self):
        return self.at(line=self.line + 1)

    def below(self):
        return self.at(line=self.line - 1)

    def greet(self):
        barrier = pltpu.get_barrier_semaphore()

        def signal(device):
            pl.semaphore_signal(barrier, inc=1, device_id=device, device_id_type=MESH)

        signal(self.beside_x())
        signal(self.beside_y())
        signal(self.sibling())
        has_below = self.line > 0
        has_above = self.line < self.length - 1
        pl.when(has_below)(lambda: signal(self.below()))
        pl.when(has_above)(lambda: signal(self.above()))
        pl.semaphore_wait(
            barrier, 3 + has_below.astype(jnp.int32) + has_above.astype(jnp.int32)
        )


def remote(src, dst, send, recv, device):
    return pltpu.make_async_remote_copy(
        src_ref=src, dst_ref=dst, send_sem=send, recv_sem=recv, device_id=device, device_id_type=MESH
    )


class Gather:
    def __init__(self, place, shard, out, sems):
        self.p = place
        self.shard = shard
        self.out = out
        self.rows, self.cols = shard.shape
        (self.up, self.down, self.line_in, self.ys, self.yr, self.xs, self.xr, self.ds, self.dr, self.own) = sems

    @staticmethod
    def sem_shapes(length):
        dma = pltpu.SemaphoreType.DMA
        return [dma((length,))] * 7 + [dma((3, length))] * 2 + [dma]

    def half(self, ref, which):
        width = self.cols // 2
        return ref.at[:, pl.ds(pl.multiple_of(which * width, width), width)]

    def slot(self, line, y, core):
        return self.out.at[line, y, core]

    def up_copy(self, line, src=None):
        p = self.p
        dst = self.slot(line, p.y, p.core)
        return remote(dst if src is None else src, dst, self.up.at[line], self.line_in.at[line], p.above())

    def down_copy(self, line, src=None):
        p = self.p
        dst = self.slot(line, p.y, p.core)
        return remote(dst if src is None else src, dst, self.down.at[line], self.line_in.at[line], p.below())

    def y_copy(self, line, src=None):
        p = self.p
        dst = self.half(self.slot(line, p.y, p.core), p.x)
        src = dst if src is None else self.half(src, p.x)
        return remote(src, dst, self.ys.at[line], self.yr.at[line], p.beside_y())

    def y_landing(self, line):
        p = self.p
        dst = self.half(self.slot(line, 1 - p.y, p.core), p.x)
        return remote(dst, dst, self.ys.at[line], self.yr.at[line], p.beside_y())

    def x_copy(self, line):
        p = self.p
        dst = self.half(self.slot(line, 1 - p.y, p.core), p.x)
        return remote(dst, dst, self.xs.at[line], self.xr.at[line], p.beside_x())

    def x_landing(self, line):
        p = self.p
        dst = self.half(self.slot(line, 1 - p.y, p.core), 1 - p.x)
        return remote(dst, dst, self.xs.at[line], self.xr.at[line], p.beside_x())

    def d_copy(self, kind, line, src=None, core=None):
        p = self.p
        core = p.core if core is None else core
        if kind == 0:
            dst = self.slot(line, p.y, core)
        else:
            dst = self.half(self.slot(line, 1 - p.y, core), p.x if kind == 1 else 1 - p.x)
        return remote(dst if src is None else src, dst, self.ds.at[kind, line], self.dr.at[kind, line], p.sibling())

    def own_copy(self):
        p = self.p
        return pltpu.make_async_copy(self.shard, self.slot(p.line, p.y, p.core), self.own)

    def each_at(self, distance, act):
        p = self.p
        if distance == 0:
            act(p.line, 0)
            return
        pl.when(p.line - distance >= 0)(lambda: act(p.line - distance, 1))
        pl.when(p.line + distance < p.length)(lambda: act(p.line + distance, -1))

    def arrive(self, distance):
        p = self.p

        def act(line, way):
            src = None
            if way == 0:
                src = self.shard
                self.own_copy().start()
            else:
                self.up_copy(line).wait_recv()
            if way >= 0:
                pl.when(p.line < p.length - 1)(lambda: self.up_copy(line, src).start())
            if way <= 0:
                pl.when(p.line > 0)(lambda: self.down_copy(line, src).start())
            self.y_copy(line, src).start()
            self.d_copy(0, line, src).start()

        self.each_at(distance, act)

    def arrive_y(self, distance):
        def act(line, way):
            self.y_landing(line).wait_recv()
            self.x_copy(line).start()
            self.d_copy(1, line).start()

        self.each_at(distance, act)

    def arrive_x(self, distance):
        def act(line, way):
            self.x_landing(line).wait_recv()
            self.d_copy(2, line).start()

        self.each_at(distance, act)

    def stage(self, time):
        length = self.p.length
        if 0 <= time < length:
            self.arrive(time)
        if 0 <= time - 1 < length:
            self.arrive_y(time - 1)
        if 0 <= time - 2 < length:
            self.arrive_x(time - 2)

    def stages(self):
        return self.p.length + 2

    def finish(self):
        p = self.p

        def one(line):
            for kind in range(3):
                self.d_copy(kind, line, core=1 - p.core).wait_recv()
            for kind in range(3):
                self.d_copy(kind, line).wait_send()
            self.y_copy(line).wait_send()
            self.x_copy(line).wait_send()
            pl.when((p.line >= line) & (p.line < p.length - 1))(lambda: self.up_copy(line).wait_send())
            pl.when((p.line <= line) & (p.line > 0))(lambda: self.down_copy(line).wait_send())

        for line in range(p.length):
            one(line)
        self.own_copy().wait()


def gather_kernel(shards, lag, count, *refs):
    ins, outs, rest = refs[:count], refs[count : 2 * count], refs[2 * count :]
    place = Place(shards)
    place.greet()
    per = len(Gather.sem_shapes(1))
    gathers = [Gather(place, ins[k], outs[k], rest[k * per : (k + 1) * per]) for k in range(count)]
    total = max(lag[k] + g.stages() for k, g in enumerate(gathers))
    for time in range(total):
        for k, g in enumerate(gathers):
            g.stage(time - lag[k])
    for g in gathers:
        g.finish()


def gather_all(arrays, shards, lag, collective_id):
    length = shards // 4
    out = pl.pallas_call(
        functools.partial(gather_kernel, shards, lag, len(arrays)),
        out_shape=[jax.ShapeDtypeStruct((length, 2, 2) + a.shape, a.dtype) for a in arrays],
        in_specs=[ANY] * len(arrays),
        out_specs=[ANY] * len(arrays),
        scratch_shapes=Gather.sem_shapes(length) * len(arrays),
        compiler_params=pltpu.CompilerParams(collective_id=collective_id, has_side_effects=True),
        name="gather_weights",
    )(*arrays)
    return [o.reshape((shards,) + a.shape) for o, a in zip(out, arrays)]


class Scatter:
    def __init__(self, place, partial, out, refs):
        self.p = place
        self.g = partial
        self.out = out
        self.rows, self.cols = out.shape
        (self.s, self.d, self.xb, self.yb, self.lo, self.hi, self.fb, self.tb,
         self.load, self.ds, self.dr, self.xs, self.xr, self.ys, self.yr,
         self.us, self.ur, self.ns, self.nr, self.fs, self.fr) = refs

    @staticmethod
    def scratch(length, rows, cols, dtype):
        dma = pltpu.SemaphoreType.DMA
        full = pltpu.VMEM((length, 2, rows, cols), dtype)
        half = pltpu.VMEM((length, rows, cols // 2), dtype)
        line = pltpu.VMEM((length, rows, cols), dtype)
        one = pltpu.VMEM((rows, cols), dtype)
        return [full, full, half, half, line, line, one, one] + [dma] * 7 + [dma((length,))] * 4 + [dma] * 2

    def half(self, which):
        width = self.cols // 2
        return pl.ds(pl.multiple_of(which * width, width), width)

    def load_copy(self):
        return pltpu.make_async_copy(self.g.at[:, :, self.p.core], self.s, self.load)

    def d_copy(self):
        p = self.p
        return remote(self.g.at[:, :, 1 - p.core], self.d, self.ds, self.dr, p.sibling())

    def x_copy(self):
        p = self.p
        src = self.s.at[:, 1 - p.y, :, self.half(1 - p.x)]
        return remote(src, self.xb, self.xs, self.xr, p.beside_x())

    def y_copy(self):
        p = self.p
        src = self.s.at[:, 1 - p.y, :, self.half(p.x)]
        return remote(src, self.yb, self.ys, self.yr, p.beside_y())

    def up_copy(self, line):
        p = self.p
        return remote(self.s.at[line, p.y], self.lo.at[line], self.us.at[line], self.ur.at[line], p.above())

    def down_copy(self, line):
        p = self.p
        return remote(self.s.at[line, p.y], self.hi.at[line], self.ns.at[line], self.nr.at[line], p.below())

    def f_copy(self):
        return remote(self.tb, self.fb, self.fs, self.fr, self.p.beside_x())

    def each(self, act):
        def body(line, carry):
            act(line)
            return carry

        lax.fori_loop(0, self.p.length, body, 0)

    def start(self):
        self.load_copy().start()
        self.d_copy().start()

    def pair(self):
        p = self.p
        self.load_copy().wait()
        self.d_copy().wait()

        def other(line):
            self.s[line, 1 - p.y] = self.s[line, 1 - p.y] + self.d[line, 1 - p.y]

        self.each(other)
        self.x_copy().start()

        def own(line):
            self.s[line, p.y] = self.s[line, p.y] + self.d[line, p.y]

        self.each(own)

    def over_x(self):
        p = self.p
        self.x_copy().wait()

        def act(line):
            cols = self.half(p.x)
            self.s[line, 1 - p.y, :, cols] = self.s[line, 1 - p.y, :, cols] + self.xb[line]

        self.each(act)
        self.y_copy().start()

    def over_y(self):
        p = self.p
        self.y_copy().wait()

        def act(line):
            cols = self.half(p.x)
            self.s[line, p.y, :, cols] = self.s[line, p.y, :, cols] + self.yb[line]

        self.each(act)

    def hop(self, step):
        p = self.p
        last = p.length - 1
        up = last - step + p.line

        def upward():
            @pl.when(p.line > 0)
            def _():
                self.up_copy(up).wait_recv()
                self.s[up, p.y] = self.s[up, p.y] + self.lo[up]

            self.up_copy(up).start()

        pl.when(p.line <= step)(upward)
        down = step - last + p.line

        def downward():
            @pl.when(p.line < last)
            def _():
                self.down_copy(down).wait_recv()
                self.s[down, p.y] = self.s[down, p.y] + self.hi[down]

            self.down_copy(down).start()

        pl.when(down >= 0)(downward)

    def total(self):
        p = self.p
        mine = p.line

        @pl.when(p.line > 0)
        def _():
            self.up_copy(mine).wait_recv()
            self.s[mine, p.y] = self.s[mine, p.y] + self.lo[mine]

        @pl.when(p.line < p.length - 1)
        def _():
            self.down_copy(mine).wait_recv()
            self.s[mine, p.y] = self.s[mine, p.y] + self.hi[mine]

        self.tb[...] = self.s[mine, p.y]
        self.f_copy().start()

    def finish(self):
        p = self.p
        self.f_copy().wait()
        self.out[...] = self.tb[...].astype(jnp.float32) + self.fb[...].astype(jnp.float32)
        for line in range(p.length):
            pl.when(line > p.line)(lambda line=line: self.up_copy(line).wait_send())
            pl.when(line < p.line)(lambda line=line: self.down_copy(line).wait_send())

    def stages(self):
        acts = [self.start, self.pair, self.over_x, self.over_y]
        acts += [functools.partial(self.hop, step) for step in range(self.p.length - 1)]
        return acts + [self.total, self.finish]


def scatter_kernel(shards, lag, count, *refs):
    ins, outs, rest = refs[:count], refs[count : 2 * count], refs[2 * count :]
    place = Place(shards)
    place.greet()
    per = len(rest) // count
    lists = [
        Scatter(place, ins[k], outs[k], rest[k * per : (k + 1) * per]).stages() for k in range(count)
    ]
    total = max(lag[k] + len(s) for k, s in enumerate(lists))
    for time in range(total):
        for k, acts in enumerate(lists):
            if 0 <= time - lag[k] < len(acts):
                acts[time - lag[k]]()


def scatter_all(arrays, shards, lag, collective_id):
    length = shards // 4
    parts = [a.reshape((length, 2, 2) + a.shape[1:]) for a in arrays]
    scratch = []
    for a in arrays:
        scratch += Scatter.scratch(length, a.shape[1], a.shape[2], a.dtype)
    return pl.pallas_call(
        functools.partial(scatter_kernel, shards, lag, len(arrays)),
        out_shape=[jax.ShapeDtypeStruct(a.shape[1:], jnp.float32) for a in arrays],
        in_specs=[ANY] * len(arrays),
        out_specs=[pl.BlockSpec(memory_space=pltpu.VMEM)] * len(arrays),
        scratch_shapes=scratch,
        compiler_params=pltpu.CompilerParams(
            collective_id=collective_id, has_side_effects=True, vmem_limit_bytes=60 << 20
        ),
        name="scatter_grads",
    )(*parts)


def rms_norm(values, gain):
    return values * lax.rsqrt(jnp.mean(values * values, axis=-1, keepdims=True) + EPSILON) * gain


def center(values):
    return values - jnp.mean(values, axis=-1, keepdims=True)


def gelu_tanh(values):
    return jax.nn.gelu(values, approximate=True)


def matmul(left, right):
    return jnp.dot(left, right, preferred_element_type=jnp.float32)


def weight_grad(inputs, grads):
    return lax.dot_general(
        inputs, grads, (((0,), (0,)), ((), ())), preferred_element_type=jnp.float32
    )


def input_grad_of(grads, weight):
    return lax.dot_general(
        grads, weight, (((1,), (1,)), ((), ())), preferred_element_type=jnp.float32
    )


def block_rows(length):
    return min(length, max(512, length // 8))


def score_block(query_block, keys_part, start, scale):
    scores = (
        jnp.einsum("qhd,khd->hqk", query_block, keys_part, preferred_element_type=jnp.float32)
        * scale
    )
    query_pos = start + jnp.arange(query_block.shape[0], dtype=jnp.int32)
    key_pos = jnp.arange(keys_part.shape[0], dtype=jnp.int32)
    allowed = query_pos[:, None] >= key_pos[None, :]
    return jnp.where(allowed[None], scores, MASKED)


def attend(queries, keys_all, values_all, scale):
    length, head_count, width = queries.shape
    block = block_rows(length)
    count = length // block
    results = []
    log_totals = []
    for index in range(count):
        start = index * block
        finish = start + block
        scores = score_block(queries[start:finish], keys_all[:finish], start, scale)
        peak = jnp.max(scores, axis=-1, keepdims=True)
        weights = jnp.exp(scores - peak)
        total = jnp.sum(weights, axis=-1, keepdims=True)
        weights = weights / total
        result = jnp.einsum(
            "hqk,khd->qhd",
            weights.astype(jnp.bfloat16),
            values_all[:finish],
            preferred_element_type=jnp.float32,
        )
        results.append(result.astype(jnp.bfloat16))
        log_totals.append((peak + jnp.log(total))[..., 0])
    joined = jnp.concatenate(results, axis=0)
    return (joined.reshape(length, head_count * width), log_totals)


def attend_back(queries, keys_all, values_all, log_totals, grad_heads, scale):
    length, head_count, width = queries.shape
    block = block_rows(length)
    count = length // block
    key_sum = jnp.zeros((length, head_count, width), jnp.float32)
    value_sum = jnp.zeros((length, head_count, width), jnp.float32)
    query_grads = []
    for index in range(count):
        start = index * block
        finish = start + block
        query_block = queries[start:finish]
        grad_block = grad_heads[start:finish]
        keys_part = keys_all[:finish]
        scores = score_block(query_block, keys_part, start, scale)
        weights = jnp.exp(scores - log_totals[index][..., None])
        grad_weights = jnp.einsum(
            "qhd,khd->hqk", grad_block, values_all[:finish], preferred_element_type=jnp.float32
        )
        inner = jnp.sum(weights * grad_weights, axis=-1, keepdims=True)
        grad_scores = (weights * (grad_weights - inner)).astype(jnp.bfloat16)
        query_grad = (
            jnp.einsum("hqk,khd->qhd", grad_scores, keys_part, preferred_element_type=jnp.float32)
            * scale
        )
        key_part = (
            jnp.einsum("hqk,qhd->khd", grad_scores, query_block, preferred_element_type=jnp.float32)
            * scale
        )
        value_part = jnp.einsum(
            "hqk,qhd->khd",
            weights.astype(jnp.bfloat16),
            grad_block,
            preferred_element_type=jnp.float32,
        )
        key_sum = key_sum.at[:finish].add(key_part)
        value_sum = value_sum.at[:finish].add(value_part)
        query_grads.append(query_grad.astype(jnp.bfloat16))
    return (
        jnp.concatenate(query_grads, axis=0),
        key_sum.astype(jnp.bfloat16),
        value_sum.astype(jnp.bfloat16),
    )


def swap_halves(value):
    shards = lax.axis_size("fsdp")
    pairs = []
    for x in range(2):
        for index in range(shards):
            core = index % 2
            goal = (x, index) if core == x else (1 - x, index ^ 1)
            pairs.append((x * shards + index, goal[0] * shards + goal[1]))
    return lax.ppermute(value, ("seq", "fsdp"), pairs)


def pair_all_to_all(value, split_axis, concat_axis):
    shards = lax.axis_size("fsdp")
    groups = [[k, k + 1] for k in range(0, shards, 2)]
    return lax.all_to_all(
        value, "fsdp", split_axis=split_axis, concat_axis=concat_axis, axis_index_groups=groups, tiled=True
    )


def column_parts(cols):
    return 3 if cols % 768 == 0 and cols >= 2304 else 1


def pack_rows(parts, width):
    rows = [jnp.pad(p, ((0, 0), (0, width - p.shape[1]))) for p in parts]
    packed = jnp.concatenate(rows, axis=0)
    return jnp.pad(packed, ((0, 16 - packed.shape[0]), (0, 0)))


def local(residual_in, cotangent, w_qkv, w_out, w_fc, w_proj, attn_bias, fc_bias, proj_bias, gains):
    shards = lax.axis_size("fsdp")
    tok_rows = residual_in.shape[1]
    model_width = w_qkv.shape[1] // 3
    hidden_width = w_fc.shape[1]
    unit = gains.shape[1]
    share = model_width // 2
    head_count = share // HD
    scale = HD ** (-0.5)
    small = pack_rows([attn_bias, gains, proj_bias[None], fc_bias[None]], 256)
    compact = swap_halves(residual_in[0]).astype(jnp.float32)
    upstream = swap_halves(cotangent[0]).astype(jnp.float32)
    qkv_w, small_all, out_w, fc_w, proj_w = gather_all(
        [w_qkv, small, w_out, w_fc, w_proj], shards, [0, 0, 2, 3, 5], 0
    )
    qkv_w = qkv_w.reshape(model_width, 3 * model_width)
    out_w = out_w.reshape(model_width, model_width)
    fc_w = fc_w.reshape(model_width, hidden_width)
    proj_w = proj_w.reshape(hidden_width, model_width)
    vectors = small_all[:, :6, :unit].transpose(1, 0, 2).reshape(6, model_width).astype(jnp.float32)
    bias_all, gain_all, proj_b = vectors[:3], vectors[3:5], vectors[5]
    fc_b = small_all[:, 6, : fc_bias.shape[0]].reshape(hidden_width).astype(jnp.float32)
    full = jnp.concatenate([compact, -jnp.sum(compact, axis=-1, keepdims=True)], axis=-1)
    normed = rms_norm(full, gain_all[0]).astype(jnp.bfloat16)
    bias_qkv = jnp.concatenate([bias_all[0], jnp.zeros_like(bias_all[0]), bias_all[1]])
    projected = (matmul(normed, qkv_w) + bias_qkv).astype(jnp.bfloat16)
    by_heads = pair_all_to_all(projected.reshape(tok_rows, 3, 2, share), 2, 0)
    length = by_heads.shape[0]
    queries = by_heads[:, 0, 0].reshape(length, head_count, HD)
    keys_all = by_heads[:, 1, 0].reshape(length, head_count, HD)
    values_all = by_heads[:, 2, 0].reshape(length, head_count, HD)
    attended, log_totals = attend(queries, keys_all, values_all, scale)
    mixed = pair_all_to_all(attended.reshape(length, 1, share), 0, 1)
    mixed = mixed.reshape(tok_rows, model_width)
    branch = matmul(mixed, out_w) + bias_all[2]
    middle = full + center(branch)
    normed_two = rms_norm(middle, gain_all[1]).astype(jnp.bfloat16)
    hidden = matmul(normed_two, fc_w) + fc_b
    activated = gelu_tanh(hidden).astype(jnp.bfloat16)
    branch_two = matmul(activated, proj_w) + proj_b
    final = middle + center(branch_two)
    residual_out = swap_halves(final[:, :-1].astype(jnp.bfloat16))[None]
    grad_final = jnp.concatenate([upstream, jnp.zeros((tok_rows, 1), jnp.float32)], axis=-1)
    grad_branch_two = center(grad_final).astype(jnp.bfloat16)
    grad_proj = weight_grad(activated, grad_branch_two)
    grad_proj_bias = jnp.sum(grad_branch_two.astype(jnp.float32), axis=0)
    grad_activated = input_grad_of(grad_branch_two, proj_w)
    gelu_pull = jax.vjp(gelu_tanh, hidden)[1]
    grad_hidden = gelu_pull(grad_activated)[0].astype(jnp.bfloat16)
    grad_fc = weight_grad(normed_two, grad_hidden)
    grad_fc_bias = jnp.sum(grad_hidden.astype(jnp.float32), axis=0)
    grad_normed_two = input_grad_of(grad_hidden, fc_w)
    second_pull = jax.vjp(rms_norm, middle, gain_all[1])[1]
    grad_middle_norm, grad_gain_two = second_pull(grad_normed_two)
    grad_middle = grad_final + grad_middle_norm
    grad_branch = center(grad_middle).astype(jnp.bfloat16)
    grad_out = weight_grad(mixed, grad_branch)
    grad_out_bias = jnp.sum(grad_branch.astype(jnp.float32), axis=0)
    grad_mixed = input_grad_of(grad_branch, out_w).astype(jnp.bfloat16)
    grad_heads = pair_all_to_all(grad_mixed.reshape(tok_rows, 2, share), 1, 0)
    grad_heads = grad_heads.reshape(length, head_count, HD)
    grad_queries, grad_keys, grad_values = attend_back(
        queries, keys_all, values_all, log_totals, grad_heads, scale
    )
    stacked = jnp.stack([grad_queries, grad_keys, grad_values], axis=1).reshape(length, 3, 1, share)
    grad_projected = pair_all_to_all(stacked, 0, 2)
    grad_projected = grad_projected.reshape(tok_rows, 3 * model_width)
    grad_qkv = weight_grad(normed, grad_projected)
    column_sums = jnp.sum(grad_projected.astype(jnp.float32), axis=0)
    grad_normed = input_grad_of(grad_projected, qkv_w)
    first_pull = jax.vjp(rms_norm, full, gain_all[0])[1]
    grad_full_norm, grad_gain_one = first_pull(grad_normed)
    grad_full = grad_middle + grad_full_norm
    input_grad = swap_halves((grad_full[:, :-1] - grad_full[:, -1:]).astype(jnp.bfloat16))[None]
    rows = jnp.stack(
        [
            column_sums[:model_width],
            column_sums[2 * model_width :],
            grad_out_bias,
            grad_gain_one,
            grad_gain_two,
            grad_proj_bias,
        ]
    )
    rows = rows.reshape(6, shards, unit).transpose(1, 0, 2)
    last = grad_fc_bias.reshape(shards, 1, fc_bias.shape[0])
    grad_small = jnp.concatenate(
        [
            jnp.pad(rows, ((0, 0), (0, 0), (0, 256 - unit))),
            jnp.pad(last, ((0, 0), (0, 9), (0, 256 - fc_bias.shape[0]))),
        ],
        axis=1,
    )

    def split(grad):
        return grad.astype(jnp.bfloat16).reshape(shards, grad.shape[0] // shards, grad.shape[1])

    total_proj, total_fc, total_out, total_qkv, total_small = scatter_all(
        [split(grad_proj), split(grad_fc), split(grad_out), split(grad_qkv), grad_small.astype(jnp.bfloat16)],
        shards,
        [0, 1, 2, 3, 3],
        1,
    )
    return (
        residual_out,
        input_grad,
        total_qkv,
        total_out,
        total_fc,
        total_proj,
        total_small[:3, :unit],
        total_small[6, : fc_bias.shape[0]],
        total_small[5, :unit],
        total_small[3:5, :unit],
    )


def solution(mesh):
    in_specs = (
        P("fsdp", "seq", None),
        P("fsdp", "seq", None),
        P("fsdp", None),
        P("fsdp", None),
        P("fsdp", None),
        P("fsdp", None),
        P(None, "fsdp"),
        P("fsdp"),
        P("fsdp"),
        P(None, "fsdp"),
    )
    out_specs = (
        P("fsdp", "seq", None),
        P("fsdp", "seq", None),
        P("fsdp", None),
        P("fsdp", None),
        P("fsdp", None),
        P("fsdp", None),
        P(None, "fsdp"),
        P("fsdp"),
        P("fsdp"),
        P(None, "fsdp"),
    )
    return jax.shard_map(local, mesh=mesh, in_specs=in_specs, out_specs=out_specs, check_vma=False)
```

```python
import functools

import jax
import jax.numpy as jnp
from jax import lax
from jax.experimental import pallas as pl
from jax.experimental.pallas import tpu as pltpu
from jax.sharding import PartitionSpec as P

HD = 64
EPSILON = 1e-05
MASKED = -1e30
MESH = pl.DeviceIdType.MESH
ANY = pl.BlockSpec(memory_space=pl.ANY)


class Place:
    def __init__(self, shards):
        self.length = shards // 4
        self.x = lax.axis_index("seq")
        index = lax.axis_index("fsdp")
        self.index = index
        self.core = lax.rem(index, 2)
        self.y = lax.rem(index // 2, 2)
        self.line = index // 4

    def at(self, **moved):
        x = moved.get("x", self.x)
        line = moved.get("line", self.line)
        y = moved.get("y", self.y)
        core = moved.get("core", self.core)
        return (x, (line * 2 + y) * 2 + core)

    def beside_x(self):
        return self.at(x=1 - self.x)

    def beside_y(self):
        return self.at(y=1 - self.y)

    def sibling(self):
        return self.at(core=1 - self.core)

    def above(self):
        return self.at(line=self.line + 1)

    def below(self):
        return self.at(line=self.line - 1)

    def greet(self, diagonal=False):
        barrier = pltpu.get_barrier_semaphore()

        def signal(device):
            pl.semaphore_signal(barrier, inc=1, device_id=device, device_id_type=MESH)

        signal(self.beside_x())
        signal(self.beside_y())
        signal(self.sibling())
        has_below = self.line > 0
        has_above = self.line < self.length - 1
        pl.when(has_below)(lambda: signal(self.below()))
        pl.when(has_above)(lambda: signal(self.above()))
        count = 3 + has_below.astype(jnp.int32) + has_above.astype(jnp.int32)
        if diagonal:
            across = self.x != self.core
            pl.when(across)(lambda: signal(self.at(x=1 - self.x, core=1 - self.core)))
            count = count + across.astype(jnp.int32)
        pl.semaphore_wait(barrier, count)


def remote(src, dst, send, recv, device):
    return pltpu.make_async_remote_copy(
        src_ref=src, dst_ref=dst, send_sem=send, recv_sem=recv, device_id=device, device_id_type=MESH
    )


class Gather:
    def __init__(self, place, shard, out, sems):
        self.p = place
        self.shard = shard
        self.out = out
        self.rows, self.cols = shard.shape
        (self.up, self.down, self.line_in, self.ys, self.yr, self.xs, self.xr, self.ds, self.dr, self.own) = sems

    @staticmethod
    def sem_shapes(length):
        dma = pltpu.SemaphoreType.DMA
        return [dma((length,))] * 7 + [dma((3, length))] * 2 + [dma]

    def half(self, ref, which):
        width = self.cols // 2
        return ref.at[:, pl.ds(pl.multiple_of(which * width, width), width)]

    def slot(self, line, y, core):
        return self.out.at[line, y, core]

    def up_copy(self, line, src=None):
        p = self.p
        dst = self.slot(line, p.y, p.core)
        return remote(dst if src is None else src, dst, self.up.at[line], self.line_in.at[line], p.above())

    def down_copy(self, line, src=None):
        p = self.p
        dst = self.slot(line, p.y, p.core)
        return remote(dst if src is None else src, dst, self.down.at[line], self.line_in.at[line], p.below())

    def y_copy(self, line, src=None):
        p = self.p
        dst = self.half(self.slot(line, p.y, p.core), p.x)
        src = dst if src is None else self.half(src, p.x)
        return remote(src, dst, self.ys.at[line], self.yr.at[line], p.beside_y())

    def y_landing(self, line):
        p = self.p
        dst = self.half(self.slot(line, 1 - p.y, p.core), p.x)
        return remote(dst, dst, self.ys.at[line], self.yr.at[line], p.beside_y())

    def x_copy(self, line):
        p = self.p
        dst = self.half(self.slot(line, 1 - p.y, p.core), p.x)
        return remote(dst, dst, self.xs.at[line], self.xr.at[line], p.beside_x())

    def x_landing(self, line):
        p = self.p
        dst = self.half(self.slot(line, 1 - p.y, p.core), 1 - p.x)
        return remote(dst, dst, self.xs.at[line], self.xr.at[line], p.beside_x())

    def d_copy(self, kind, line, src=None, core=None):
        p = self.p
        core = p.core if core is None else core
        if kind == 0:
            dst = self.slot(line, p.y, core)
        else:
            dst = self.half(self.slot(line, 1 - p.y, core), p.x if kind == 1 else 1 - p.x)
        return remote(dst if src is None else src, dst, self.ds.at[kind, line], self.dr.at[kind, line], p.sibling())

    def own_copy(self):
        p = self.p
        return pltpu.make_async_copy(self.shard, self.slot(p.line, p.y, p.core), self.own)

    def each_at(self, distance, act):
        p = self.p
        if distance == 0:
            act(p.line, 0)
            return
        pl.when(p.line - distance >= 0)(lambda: act(p.line - distance, 1))
        pl.when(p.line + distance < p.length)(lambda: act(p.line + distance, -1))

    def arrive(self, distance):
        p = self.p

        def act(line, way):
            src = None
            if way == 0:
                src = self.shard
                self.own_copy().start()
            else:
                self.up_copy(line).wait_recv()
            if way >= 0:
                pl.when(p.line < p.length - 1)(lambda: self.up_copy(line, src).start())
            if way <= 0:
                pl.when(p.line > 0)(lambda: self.down_copy(line, src).start())
            self.y_copy(line, src).start()
            self.d_copy(0, line, src).start()

        self.each_at(distance, act)

    def arrive_y(self, distance):
        def act(line, way):
            self.y_landing(line).wait_recv()
            self.x_copy(line).start()
            self.d_copy(1, line).start()

        self.each_at(distance, act)

    def arrive_x(self, distance):
        def act(line, way):
            self.x_landing(line).wait_recv()
            self.d_copy(2, line).start()

        self.each_at(distance, act)

    def stage(self, time):
        length = self.p.length
        if 0 <= time < length:
            self.arrive(time)
        if 0 <= time - 1 < length:
            self.arrive_y(time - 1)
        if 0 <= time - 2 < length:
            self.arrive_x(time - 2)

    def stages(self):
        return self.p.length + 2

    def finish(self):
        p = self.p

        def one(line):
            for kind in range(3):
                self.d_copy(kind, line, core=1 - p.core).wait_recv()
            for kind in range(3):
                self.d_copy(kind, line).wait_send()
            self.y_copy(line).wait_send()
            self.x_copy(line).wait_send()
            pl.when((p.line >= line) & (p.line < p.length - 1))(lambda: self.up_copy(line).wait_send())
            pl.when((p.line <= line) & (p.line > 0))(lambda: self.down_copy(line).wait_send())

        for line in range(p.length):
            one(line)
        self.own_copy().wait()


def gather_kernel(shards, lag, count, *refs):
    ins, outs, rest = refs[:count], refs[count : 2 * count], refs[2 * count :]
    place = Place(shards)
    place.greet()
    per = len(Gather.sem_shapes(1))
    gathers = [Gather(place, ins[k], outs[k], rest[k * per : (k + 1) * per]) for k in range(count)]
    total = max(lag[k] + g.stages() for k, g in enumerate(gathers))
    for time in range(total):
        for k, g in enumerate(gathers):
            g.stage(time - lag[k])
    for g in gathers:
        g.finish()


def gather_all(arrays, shards, lag, collective_id):
    length = shards // 4
    out = pl.pallas_call(
        functools.partial(gather_kernel, shards, lag, len(arrays)),
        out_shape=[jax.ShapeDtypeStruct((length, 2, 2) + a.shape, a.dtype) for a in arrays],
        in_specs=[ANY] * len(arrays),
        out_specs=[ANY] * len(arrays),
        scratch_shapes=Gather.sem_shapes(length) * len(arrays),
        compiler_params=pltpu.CompilerParams(collective_id=collective_id, has_side_effects=True),
        name="gather_weights",
    )(*arrays)
    return [o.reshape((shards,) + a.shape) for o, a in zip(out, arrays)]


class Scatter:
    def __init__(self, place, partial, out, refs):
        self.p = place
        self.g = partial
        self.out = out
        self.rows, self.cols = out.shape
        (self.s, self.d, self.xb, self.yb, self.lo, self.hi, self.fb, self.tb,
         self.load, self.ds, self.dr, self.xs, self.xr, self.ys, self.yr,
         self.us, self.ur, self.ns, self.nr, self.fs, self.fr) = refs

    @staticmethod
    def scratch(length, rows, cols, dtype):
        dma = pltpu.SemaphoreType.DMA
        full = pltpu.VMEM((length, 2, rows, cols), dtype)
        half = pltpu.VMEM((length, rows, cols // 2), dtype)
        line = pltpu.VMEM((length, rows, cols), dtype)
        one = pltpu.VMEM((rows, cols), dtype)
        return [full, full, half, half, line, line, one, one] + [dma] * 7 + [dma((length,))] * 4 + [dma] * 2

    def half(self, which):
        width = self.cols // 2
        return pl.ds(pl.multiple_of(which * width, width), width)

    def load_copy(self):
        return pltpu.make_async_copy(self.g.at[:, :, self.p.core], self.s, self.load)

    def d_copy(self):
        p = self.p
        return remote(self.g.at[:, :, 1 - p.core], self.d, self.ds, self.dr, p.sibling())

    def x_copy(self):
        p = self.p
        src = self.s.at[:, 1 - p.y, :, self.half(1 - p.x)]
        return remote(src, self.xb, self.xs, self.xr, p.beside_x())

    def y_copy(self):
        p = self.p
        src = self.s.at[:, 1 - p.y, :, self.half(p.x)]
        return remote(src, self.yb, self.ys, self.yr, p.beside_y())

    def up_copy(self, line):
        p = self.p
        return remote(self.s.at[line, p.y], self.lo.at[line], self.us.at[line], self.ur.at[line], p.above())

    def down_copy(self, line):
        p = self.p
        return remote(self.s.at[line, p.y], self.hi.at[line], self.ns.at[line], self.nr.at[line], p.below())

    def f_copy(self):
        return remote(self.tb, self.fb, self.fs, self.fr, self.p.beside_x())

    def each(self, act):
        def body(line, carry):
            act(line)
            return carry

        lax.fori_loop(0, self.p.length, body, 0)

    def start(self):
        self.load_copy().start()
        self.d_copy().start()

    def pair(self):
        p = self.p
        self.load_copy().wait()
        self.d_copy().wait()

        def other(line):
            self.s[line, 1 - p.y] = self.s[line, 1 - p.y] + self.d[line, 1 - p.y]

        self.each(other)
        self.x_copy().start()

        def own(line):
            self.s[line, p.y] = self.s[line, p.y] + self.d[line, p.y]

        self.each(own)

    def over_x(self):
        p = self.p
        self.x_copy().wait()

        def act(line):
            cols = self.half(p.x)
            self.s[line, 1 - p.y, :, cols] = self.s[line, 1 - p.y, :, cols] + self.xb[line]

        self.each(act)
        self.y_copy().start()

    def over_y(self):
        p = self.p
        self.y_copy().wait()

        def act(line):
            cols = self.half(p.x)
            self.s[line, p.y, :, cols] = self.s[line, p.y, :, cols] + self.yb[line]

        self.each(act)

    def hop(self, step):
        p = self.p
        last = p.length - 1
        up = last - step + p.line

        def upward():
            @pl.when(p.line > 0)
            def _():
                self.up_copy(up).wait_recv()
                self.s[up, p.y] = self.s[up, p.y] + self.lo[up]

            self.up_copy(up).start()

        pl.when(p.line <= step)(upward)
        down = step - last + p.line

        def downward():
            @pl.when(p.line < last)
            def _():
                self.down_copy(down).wait_recv()
                self.s[down, p.y] = self.s[down, p.y] + self.hi[down]

            self.down_copy(down).start()

        pl.when(down >= 0)(downward)

    def total(self):
        p = self.p
        mine = p.line

        @pl.when(p.line > 0)
        def _():
            self.up_copy(mine).wait_recv()
            self.s[mine, p.y] = self.s[mine, p.y] + self.lo[mine]

        @pl.when(p.line < p.length - 1)
        def _():
            self.down_copy(mine).wait_recv()
            self.s[mine, p.y] = self.s[mine, p.y] + self.hi[mine]

        self.tb[...] = self.s[mine, p.y]
        self.f_copy().start()

    def finish(self):
        p = self.p
        self.f_copy().wait()
        self.out[...] = self.tb[...].astype(jnp.float32) + self.fb[...].astype(jnp.float32)
        for line in range(p.length):
            pl.when(line > p.line)(lambda line=line: self.up_copy(line).wait_send())
            pl.when(line < p.line)(lambda line=line: self.down_copy(line).wait_send())

    def stages(self):
        acts = [self.start, self.pair, self.over_x, self.over_y]
        acts += [functools.partial(self.hop, step) for step in range(self.p.length - 1)]
        return acts + [self.total, self.finish]


def scatter_kernel(shards, lag, count, *refs):
    ins, outs, rest = refs[:count], refs[count : 2 * count], refs[2 * count :]
    place = Place(shards)
    place.greet()
    per = len(rest) // count
    lists = [
        Scatter(place, ins[k], outs[k], rest[k * per : (k + 1) * per]).stages() for k in range(count)
    ]
    total = max(lag[k] + len(s) for k, s in enumerate(lists))
    for time in range(total):
        for k, acts in enumerate(lists):
            if 0 <= time - lag[k] < len(acts):
                acts[time - lag[k]]()


def scatter_all(arrays, shards, lag, collective_id):
    length = shards // 4
    parts = [a.reshape((length, 2, 2) + a.shape[1:]) for a in arrays]
    scratch = []
    for a in arrays:
        scratch += Scatter.scratch(length, a.shape[1], a.shape[2], a.dtype)
    return pl.pallas_call(
        functools.partial(scatter_kernel, shards, lag, len(arrays)),
        out_shape=[jax.ShapeDtypeStruct(a.shape[1:], jnp.float32) for a in arrays],
        in_specs=[ANY] * len(arrays),
        out_specs=[pl.BlockSpec(memory_space=pltpu.VMEM)] * len(arrays),
        scratch_shapes=scratch,
        compiler_params=pltpu.CompilerParams(
            collective_id=collective_id, has_side_effects=True, vmem_limit_bytes=60 << 20
        ),
        name="scatter_grads",
    )(*parts)


def rms_norm(values, gain):
    return values * lax.rsqrt(jnp.mean(values * values, axis=-1, keepdims=True) + EPSILON) * gain


def center(values):
    return values - jnp.mean(values, axis=-1, keepdims=True)


def gelu_tanh(values):
    return jax.nn.gelu(values, approximate=True)


def matmul(left, right):
    return jnp.dot(left, right, preferred_element_type=jnp.float32)


def weight_grad(inputs, grads):
    return lax.dot_general(
        inputs, grads, (((0,), (0,)), ((), ())), preferred_element_type=jnp.float32
    )


def input_grad_of(grads, weight):
    return lax.dot_general(
        grads, weight, (((1,), (1,)), ((), ())), preferred_element_type=jnp.float32
    )


def block_rows(length):
    return min(length, max(512, length // 8))


def score_block(query_block, keys_part, start, scale):
    scores = (
        jnp.einsum("qhd,khd->hqk", query_block, keys_part, preferred_element_type=jnp.float32)
        * scale
    )
    query_pos = start + jnp.arange(query_block.shape[0], dtype=jnp.int32)
    key_pos = jnp.arange(keys_part.shape[0], dtype=jnp.int32)
    allowed = query_pos[:, None] >= key_pos[None, :]
    return jnp.where(allowed[None], scores, MASKED)


def attend(queries, keys_all, values_all, scale):
    length, head_count, width = queries.shape
    block = block_rows(length)
    count = length // block
    results = []
    log_totals = []
    for index in range(count):
        start = index * block
        finish = start + block
        scores = score_block(queries[start:finish], keys_all[:finish], start, scale)
        peak = jnp.max(scores, axis=-1, keepdims=True)
        weights = jnp.exp(scores - peak)
        total = jnp.sum(weights, axis=-1, keepdims=True)
        weights = weights / total
        result = jnp.einsum(
            "hqk,khd->qhd",
            weights.astype(jnp.bfloat16),
            values_all[:finish],
            preferred_element_type=jnp.float32,
        )
        results.append(result.astype(jnp.bfloat16))
        log_totals.append((peak + jnp.log(total))[..., 0])
    joined = jnp.concatenate(results, axis=0)
    return (joined.reshape(length, head_count * width), log_totals)


def attend_back(queries, keys_all, values_all, log_totals, grad_heads, scale):
    length, head_count, width = queries.shape
    block = block_rows(length)
    count = length // block
    key_sum = jnp.zeros((length, head_count, width), jnp.float32)
    value_sum = jnp.zeros((length, head_count, width), jnp.float32)
    query_grads = []
    for index in range(count):
        start = index * block
        finish = start + block
        query_block = queries[start:finish]
        grad_block = grad_heads[start:finish]
        keys_part = keys_all[:finish]
        scores = score_block(query_block, keys_part, start, scale)
        weights = jnp.exp(scores - log_totals[index][..., None])
        grad_weights = jnp.einsum(
            "qhd,khd->hqk", grad_block, values_all[:finish], preferred_element_type=jnp.float32
        )
        inner = jnp.sum(weights * grad_weights, axis=-1, keepdims=True)
        grad_scores = (weights * (grad_weights - inner)).astype(jnp.bfloat16)
        query_grad = (
            jnp.einsum("hqk,khd->qhd", grad_scores, keys_part, preferred_element_type=jnp.float32)
            * scale
        )
        key_part = (
            jnp.einsum("hqk,qhd->khd", grad_scores, query_block, preferred_element_type=jnp.float32)
            * scale
        )
        value_part = jnp.einsum(
            "hqk,qhd->khd",
            weights.astype(jnp.bfloat16),
            grad_block,
            preferred_element_type=jnp.float32,
        )
        key_sum = key_sum.at[:finish].add(key_part)
        value_sum = value_sum.at[:finish].add(value_part)
        query_grads.append(query_grad.astype(jnp.bfloat16))
    return (
        jnp.concatenate(query_grads, axis=0),
        key_sum.astype(jnp.bfloat16),
        value_sum.astype(jnp.bfloat16),
    )


def dot_nn(left, right):
    return jnp.dot(left, right, preferred_element_type=jnp.float32)


def dot_nt(left, right):
    return lax.dot_general(
        left, right, (((1,), (1,)), ((), ())), preferred_element_type=jnp.float32
    )


def dot_tn(left, right):
    return lax.dot_general(
        left, right, (((0,), (0,)), ((), ())), preferred_element_type=jnp.float32
    )


def lane_block(index, width):
    return pl.ds(pl.multiple_of(index * width, width), width)


def widen(value):
    value = value.astype(jnp.float32)
    lanes = lax.broadcasted_iota(jnp.int32, value.shape, 1)
    missing = -jnp.sum(value, axis=-1, keepdims=True)
    return jnp.where(lanes == value.shape[1] - 1, missing, value)


def unit_scale(value):
    return lax.rsqrt(jnp.mean(value * value, axis=-1, keepdims=True) + EPSILON)


def over_rows(total, block, act):
    def body(step, carry):
        act(pl.ds(pl.multiple_of(step * block, block), block))
        return carry

    lax.fori_loop(0, total // block, body, 0)


def head_mask(shape, head):
    lanes = lax.broadcasted_iota(jnp.int32, shape, 1)
    return (lanes // HD) == head


class Swap:
    def __init__(self, place, src, dst, sems):
        self.p = place
        self.src, self.dst = src, dst
        self.send, self.recv = sems

    def moved(self):
        p = self.p
        return remote(self.src, self.dst, self.send, self.recv, p.at(x=1 - p.x, core=1 - p.core))

    def kept(self):
        return pltpu.make_async_copy(self.src, self.dst, self.send)

    def start(self):
        p = self.p
        pl.when(p.x != p.core)(lambda: self.moved().start())
        pl.when(p.x == p.core)(lambda: self.kept().start())

    def wait(self):
        p = self.p
        pl.when(p.x != p.core)(lambda: self.moved().wait())
        pl.when(p.x == p.core)(lambda: self.kept().wait())


def attend_pair(qkv, pair, put):
    total = qkv.shape[1]
    block = min(256, total)
    lanes = pl.ds(pair * 2 * HD, 2 * HD)
    scale = jnp.asarray(HD ** (-0.5), jnp.bfloat16)
    zero = jnp.zeros((), jnp.bfloat16)
    rows = lax.broadcasted_iota(jnp.int32, (block, block), 0)
    cols = lax.broadcasted_iota(jnp.int32, (block, block), 1)
    allowed = rows >= cols
    for index in range(total // block):
        start = index * block
        here = pl.ds(start, block)
        query = qkv[0, here, lanes] * scale
        results = []
        for head in range(2):
            masked = jnp.where(head_mask(query.shape, head), query, zero)
            near = dot_nt(masked, qkv[1, here, lanes])
            near = jnp.where(allowed, near, MASKED)
            peak = jnp.max(near, axis=-1, keepdims=True)
            if start:
                far = dot_nt(masked, qkv[1, pl.ds(0, start), lanes])
                peak = jnp.maximum(peak, jnp.max(far, axis=-1, keepdims=True))
            near = jnp.exp(near - peak)
            total_weight = jnp.sum(near, axis=-1, keepdims=True)
            if start:
                far = jnp.exp(far - peak)
                total_weight = total_weight + jnp.sum(far, axis=-1, keepdims=True)
            share = 1.0 / total_weight
            result = dot_nn((near * share).astype(jnp.bfloat16), qkv[2, here, lanes])
            if start:
                result += dot_nn(
                    (far * share).astype(jnp.bfloat16), qkv[2, pl.ds(0, start), lanes]
                )
            results.append(result)
        merged = jnp.where(head_mask(results[0].shape, 0), results[0], results[1])
        put(start, block, merged.astype(jnp.bfloat16))


def front_kernel(shards, lag, *refs):
    (resid, cot, w_qkv, small, w_out, w_fc, w_proj,
     qkv_o, out_o, fc_o, proj_o, resid_o, cot_o, normed_o, heads_o, mixed_o, vec_o,
     qkv_w, small_w, rs, cs, heads, send_heads, att, mixed, *sems) = refs
    place = Place(shards)
    place.greet(diagonal=True)
    width = rs.shape[1]
    rows = rs.shape[0]
    share = width // 2
    per = len(Gather.sem_shapes(1))
    pairs = [(w_qkv, qkv_w), (small, small_w), (w_out, out_o), (w_fc, fc_o), (w_proj, proj_o)]
    gathers = []
    for src, dst in pairs:
        gathers.append(Gather(place, src, dst, sems[:per]))
        sems = sems[per:]
    swap_in = Swap(place, resid, rs, sems[:2])
    swap_cot = Swap(place, cot, cs, sems[2:4])
    heads_s, heads_r, att_s, att_r, done = sems[4:]
    clock = [0]
    final = max(lag[k] + g.stages() for k, g in enumerate(gathers))

    def tick(count=1):
        for _ in range(count):
            for k, g in enumerate(gathers):
                g.stage(clock[0] - lag[k])
            clock[0] += 1

    tick()
    swap_in.start()
    tick()
    swap_in.wait()
    gathers_first = gathers[:2]
    while clock[0] < max(g.stages() for g in gathers_first):
        tick()
    swap_cot.start()
    gathers[1].finish()
    vec_o[...] = jnp.sum(small_w[...].astype(jnp.float32), axis=(0, 1, 2))

    def normalize(here):
        full = widen(rs[here, :])
        normed_o[here, :] = (full * unit_scale(full) * vec_o[3:4, :]).astype(jnp.bfloat16)

    over_rows(rows, 64, normalize)
    gathers[0].finish()

    weight = qkv_w.reshape(width, 3 * width)

    def exchange(block):
        src = send_heads.at[block]
        dst = heads.at[block, pl.ds(pl.multiple_of(place.core * rows, rows), rows)]
        return remote(src, dst, heads_s.at[block], heads_r.at[block], place.sibling())

    def project(block, group):
        at = block * 2 + group
        result = dot_nn(normed_o[...], weight[:, lane_block(at, share)])
        if block == 0:
            result = result + vec_o[0:1, lane_block(group, share)]
        if block == 2:
            result = result + vec_o[1:2, lane_block(group, share)]
        return result.astype(jnp.bfloat16)

    for block in range(3):
        send_heads[block] = project(block, 1 - place.core)
        exchange(block).start()
    for block in range(3):
        heads[block, pl.ds(pl.multiple_of(place.core * rows, rows), rows), :] = project(block, place.core)
    for block in range(3):
        exchange(block).wait()

    def back(pair):
        lanes = pl.ds(pair * 2 * HD, 2 * HD)
        src = att.at[1 - place.core, :, lanes]
        dst = mixed.at[:, pl.ds(pl.multiple_of(place.core * share + pair * 2 * HD, 2 * HD), 2 * HD)]
        return remote(src, dst, att_s.at[pair], att_r.at[pair], place.sibling())

    count = share // (2 * HD)
    for pair in range(count):
        lanes = pl.ds(pair * 2 * HD, 2 * HD)

        def put(start, block, value):
            att[start // rows, pl.ds(start % rows, block), lanes] = value

        attend_pair(heads, pair, put)
        back(pair).start()
        mine = pl.ds(pl.multiple_of(place.core * share + pair * 2 * HD, 2 * HD), 2 * HD)
        mixed[:, mine] = att[place.core, :, lanes]
        tick(2)
    while clock[0] < final:
        tick()
    outs = [(qkv_w, qkv_o), (rs, resid_o), (heads, heads_o)]
    copies = [pltpu.make_async_copy(s, d, done.at[k]) for k, (s, d) in enumerate(outs)]
    for copy in copies:
        copy.start()
    for pair in range(count):
        back(pair).wait()
    mixed_o[...] = mixed[...]
    swap_cot.wait()
    cot_o[...] = cs[...]
    for g in gathers[2:]:
        g.finish()
    for copy in copies:
        copy.wait()


def front(resid, cot, w_qkv, small, w_out, w_fc, w_proj, shards, collective_id):
    length = shards // 4
    rows, width = resid.shape
    share = width // 2
    low = jnp.bfloat16
    sums = [w_qkv, w_out, w_fc, w_proj]
    gathered = [jax.ShapeDtypeStruct((length, 2, 2) + a.shape, low) for a in sums]
    shapes = gathered + [
        jax.ShapeDtypeStruct((rows, width), low),
        jax.ShapeDtypeStruct((rows, width), low),
        jax.ShapeDtypeStruct((rows, width), low),
        jax.ShapeDtypeStruct((3, 2 * rows, share), low),
        jax.ShapeDtypeStruct((rows, width), low),
        jax.ShapeDtypeStruct(small.shape, jnp.float32),
    ]
    vmem = pl.BlockSpec(memory_space=pltpu.VMEM)
    dma = pltpu.SemaphoreType.DMA
    pairs = share // (2 * HD)
    return pl.pallas_call(
        functools.partial(front_kernel, shards, [0, 0, 3, 3, 4]),
        out_shape=shapes,
        in_specs=[ANY] * 7,
        out_specs=[ANY] * 5 + [vmem, vmem, ANY, vmem, vmem],
        scratch_shapes=[
            pltpu.VMEM((length, 2, 2) + w_qkv.shape, low),
            pltpu.VMEM((length, 2, 2) + small.shape, low),
            pltpu.VMEM((rows, width), low),
            pltpu.VMEM((rows, width), low),
            pltpu.VMEM((3, 2 * rows, share), low),
            pltpu.VMEM((3, rows, share), low),
            pltpu.VMEM((2, rows, share), low),
            pltpu.VMEM((rows, width), low),
        ]
        + Gather.sem_shapes(length) * 5
        + [dma, dma, dma, dma, dma((3,)), dma((3,)), dma((pairs,)), dma((pairs,)), dma((3,))],
        compiler_params=pltpu.CompilerParams(
            collective_id=collective_id, has_side_effects=True, vmem_limit_bytes=60 << 20
        ),
        name="front",
    )(resid, cot, w_qkv, small, w_out, w_fc, w_proj)


def place_small(vectors, shards, width):
    index = lax.axis_index("fsdp")
    rows = []
    for value in vectors:
        piece = value.shape[1]
        length = piece * shards
        spread = jnp.tile(value, (1, shards))
        here = jnp.arange(length, dtype=jnp.int32)[None] // piece == index
        spread = jnp.where(here, spread, jnp.zeros((), value.dtype))
        rows.append(spread.reshape(-1, width))
    packed = jnp.concatenate(rows, axis=0)
    return jnp.pad(packed, ((0, 16 - packed.shape[0]), (0, 0)))


def attend_back_pair(qkv, grads, pair, key_sum, value_sum, put):
    total = qkv.shape[1]
    block = min(256, total)
    lanes = pl.ds(pair * 2 * HD, 2 * HD)
    scale = jnp.asarray(HD ** (-0.5), jnp.bfloat16)
    zero = jnp.zeros((), jnp.bfloat16)
    rows = lax.broadcasted_iota(jnp.int32, (block, block), 0)
    cols = lax.broadcasted_iota(jnp.int32, (block, block), 1)
    allowed = rows <= cols
    key_sum[...] = jnp.zeros_like(key_sum)
    value_sum[...] = jnp.zeros_like(value_sum)
    for index in range(total // block):
        start = index * block
        here = pl.ds(start, block)
        spans = [here] + ([pl.ds(0, start)] if start else [])
        query = qkv[0, here, lanes] * scale
        grad = grads[start // grads.shape[1], pl.ds(start % grads.shape[1], block), lanes]
        query_grads = []
        for head in range(2):
            mask = head_mask(query.shape, head)
            masked = jnp.where(mask, query, zero)
            grad_masked = jnp.where(mask, grad, zero)
            scores = [dot_nt(qkv[1, span, lanes], masked) for span in spans]
            scores[0] = jnp.where(allowed, scores[0], MASKED)
            peak = functools.reduce(
                jnp.maximum, [jnp.max(s, axis=0, keepdims=True) for s in scores]
            )
            weights = [jnp.exp(s - peak) for s in scores]
            sums = sum(jnp.sum(w, axis=0, keepdims=True) for w in weights)
            share = 1.0 / sums
            weights = [w * share for w in weights]
            pulled = [dot_nt(qkv[2, span, lanes], grad_masked) for span in spans]
            inner = sum(jnp.sum(w * g, axis=0, keepdims=True) for w, g in zip(weights, pulled))
            query_grad = None
            for span, w, g in zip(spans, weights, pulled):
                value_sum[span, :] += dot_nn(w.astype(jnp.bfloat16), grad_masked)
                slope = (w * (g - inner)).astype(jnp.bfloat16)
                key_sum[span, :] += dot_nn(slope, masked)
                part = dot_tn(slope, qkv[1, span, lanes])
                query_grad = part if query_grad is None else query_grad + part
            query_grads.append(query_grad)
        merged = jnp.where(head_mask(query_grads[0].shape, 0), query_grads[0], query_grads[1])
        put(0, start, block, (merged * HD ** (-0.5)).astype(jnp.bfloat16))
    half = grads.shape[1]
    for start in range(0, total, half):
        put(1, start, half, key_sum[pl.ds(start, half), :].astype(jnp.bfloat16))
        put(2, start, half, value_sum[pl.ds(start, half), :].astype(jnp.bfloat16))


def back_kernel(shards, *refs):
    (grad_mixed, heads, grads_o, got, parts, projected, key_sum, value_sum, gs, gr, ps, pr) = refs
    place = Place(shards)
    place.greet()
    rows = grad_mixed.shape[0]
    share = grad_mixed.shape[1] // 2
    width = 2 * HD

    def group_lanes(group):
        return pl.ds(pl.multiple_of(group * share, 2 * HD), share)

    give = remote(
        grad_mixed.at[:, group_lanes(1 - place.core)], got.at[place.core], gs, gr, place.sibling()
    )
    give.start()
    got[place.core] = grad_mixed[:, group_lanes(place.core)]
    give.wait()

    def send(block, pair):
        lanes = pl.ds(pair * width, width)
        src = parts.at[block, 1 - place.core, :, lanes]
        at = pl.multiple_of((block * 2 + place.core) * share + pair * width, width)
        return remote(src, projected.at[:, pl.ds(at, width)], ps.at[block, pair], pr.at[block, pair], place.sibling())

    for pair in range(share // width):
        lanes = pl.ds(pair * width, width)

        def put(block, start, size, value):
            parts[block, start // rows, pl.ds(start % rows, size), lanes] = value

        attend_back_pair(heads, got, pair, key_sum, value_sum, put)
        for block in range(3):
            send(block, pair).start()
            at = pl.multiple_of((block * 2 + place.core) * share + pair * width, width)
            projected[:, pl.ds(at, width)] = parts[block, place.core, :, lanes]
    for pair in range(share // width):
        for block in range(3):
            send(block, pair).wait()
    grads_o[...] = projected[...]


def back(grad_mixed, heads, shards, collective_id):
    rows, width = grad_mixed.shape
    share = width // 2
    pairs = share // (2 * HD)
    vmem = pl.BlockSpec(memory_space=pltpu.VMEM)
    dma = pltpu.SemaphoreType.DMA
    low = jnp.bfloat16
    return pl.pallas_call(
        functools.partial(back_kernel, shards),
        out_shape=jax.ShapeDtypeStruct((rows, 3 * width), low),
        in_specs=[vmem, vmem],
        out_specs=vmem,
        scratch_shapes=[
            pltpu.VMEM((2, rows, share), low),
            pltpu.VMEM((3, 2, rows, share), low),
            pltpu.VMEM((rows, 3 * width), low),
            pltpu.VMEM((2 * rows, 2 * HD), jnp.float32),
            pltpu.VMEM((2 * rows, 2 * HD), jnp.float32),
            dma, dma, dma((3, pairs)), dma((3, pairs)),
        ],
        compiler_params=pltpu.CompilerParams(
            collective_id=collective_id, has_side_effects=True, vmem_limit_bytes=60 << 20
        ),
        name="attention_back",
    )(grad_mixed, heads)


def swap_halves(value):
    shards = lax.axis_size("fsdp")
    pairs = []
    for x in range(2):
        for index in range(shards):
            core = index % 2
            goal = (x, index) if core == x else (1 - x, index ^ 1)
            pairs.append((x * shards + index, goal[0] * shards + goal[1]))
    return lax.ppermute(value, ("seq", "fsdp"), pairs)


def pair_all_to_all(value, split_axis, concat_axis):
    shards = lax.axis_size("fsdp")
    groups = [[k, k + 1] for k in range(0, shards, 2)]
    return lax.all_to_all(
        value, "fsdp", split_axis=split_axis, concat_axis=concat_axis, axis_index_groups=groups, tiled=True
    )


def pack_rows(parts, width):
    rows = [jnp.pad(p, ((0, 0), (0, width - p.shape[1]))) for p in parts]
    packed = jnp.concatenate(rows, axis=0)
    return jnp.pad(packed, ((0, 16 - packed.shape[0]), (0, 0)))


def local_general(residual_in, cotangent, w_qkv, w_out, w_fc, w_proj, attn_bias, fc_bias, proj_bias, gains):
    shards = lax.axis_size("fsdp")
    tok_rows = residual_in.shape[1]
    model_width = w_qkv.shape[1] // 3
    hidden_width = w_fc.shape[1]
    unit = gains.shape[1]
    share = model_width // 2
    head_count = share // HD
    scale = HD ** (-0.5)
    small = pack_rows([attn_bias, gains, proj_bias[None], fc_bias[None]], 256)
    compact = swap_halves(residual_in[0]).astype(jnp.float32)
    upstream = swap_halves(cotangent[0]).astype(jnp.float32)
    qkv_w, small_all, out_w, fc_w, proj_w = gather_all(
        [w_qkv, small, w_out, w_fc, w_proj], shards, [0, 0, 2, 3, 5], 0
    )
    qkv_w = qkv_w.reshape(model_width, 3 * model_width)
    out_w = out_w.reshape(model_width, model_width)
    fc_w = fc_w.reshape(model_width, hidden_width)
    proj_w = proj_w.reshape(hidden_width, model_width)
    vectors = small_all[:, :6, :unit].transpose(1, 0, 2).reshape(6, model_width).astype(jnp.float32)
    bias_all, gain_all, proj_b = vectors[:3], vectors[3:5], vectors[5]
    fc_b = small_all[:, 6, : fc_bias.shape[0]].reshape(hidden_width).astype(jnp.float32)
    full = jnp.concatenate([compact, -jnp.sum(compact, axis=-1, keepdims=True)], axis=-1)
    normed = rms_norm(full, gain_all[0]).astype(jnp.bfloat16)
    bias_qkv = jnp.concatenate([bias_all[0], jnp.zeros_like(bias_all[0]), bias_all[1]])
    projected = (matmul(normed, qkv_w) + bias_qkv).astype(jnp.bfloat16)
    by_heads = pair_all_to_all(projected.reshape(tok_rows, 3, 2, share), 2, 0)
    length = by_heads.shape[0]
    queries = by_heads[:, 0, 0].reshape(length, head_count, HD)
    keys_all = by_heads[:, 1, 0].reshape(length, head_count, HD)
    values_all = by_heads[:, 2, 0].reshape(length, head_count, HD)
    attended, log_totals = attend(queries, keys_all, values_all, scale)
    mixed = pair_all_to_all(attended.reshape(length, 1, share), 0, 1)
    mixed = mixed.reshape(tok_rows, model_width)
    branch = matmul(mixed, out_w) + bias_all[2]
    middle = full + center(branch)
    normed_two = rms_norm(middle, gain_all[1]).astype(jnp.bfloat16)
    hidden = matmul(normed_two, fc_w) + fc_b
    activated = gelu_tanh(hidden).astype(jnp.bfloat16)
    branch_two = matmul(activated, proj_w) + proj_b
    final = middle + center(branch_two)
    residual_out = swap_halves(final[:, :-1].astype(jnp.bfloat16))[None]
    grad_final = jnp.concatenate([upstream, jnp.zeros((tok_rows, 1), jnp.float32)], axis=-1)
    grad_branch_two = center(grad_final).astype(jnp.bfloat16)
    grad_proj = weight_grad(activated, grad_branch_two)
    grad_proj_bias = jnp.sum(grad_branch_two.astype(jnp.float32), axis=0)
    grad_activated = input_grad_of(grad_branch_two, proj_w)
    gelu_pull = jax.vjp(gelu_tanh, hidden)[1]
    grad_hidden = gelu_pull(grad_activated)[0].astype(jnp.bfloat16)
    grad_fc = weight_grad(normed_two, grad_hidden)
    grad_fc_bias = jnp.sum(grad_hidden.astype(jnp.float32), axis=0)
    grad_normed_two = input_grad_of(grad_hidden, fc_w)
    second_pull = jax.vjp(rms_norm, middle, gain_all[1])[1]
    grad_middle_norm, grad_gain_two = second_pull(grad_normed_two)
    grad_middle = grad_final + grad_middle_norm
    grad_branch = center(grad_middle).astype(jnp.bfloat16)
    grad_out = weight_grad(mixed, grad_branch)
    grad_out_bias = jnp.sum(grad_branch.astype(jnp.float32), axis=0)
    grad_mixed = input_grad_of(grad_branch, out_w).astype(jnp.bfloat16)
    grad_heads = pair_all_to_all(grad_mixed.reshape(tok_rows, 2, share), 1, 0)
    grad_heads = grad_heads.reshape(length, head_count, HD)
    grad_queries, grad_keys, grad_values = attend_back(
        queries, keys_all, values_all, log_totals, grad_heads, scale
    )
    stacked = jnp.stack([grad_queries, grad_keys, grad_values], axis=1).reshape(length, 3, 1, share)
    grad_projected = pair_all_to_all(stacked, 0, 2)
    grad_projected = grad_projected.reshape(tok_rows, 3 * model_width)
    grad_qkv = weight_grad(normed, grad_projected)
    column_sums = jnp.sum(grad_projected.astype(jnp.float32), axis=0)
    grad_normed = input_grad_of(grad_projected, qkv_w)
    first_pull = jax.vjp(rms_norm, full, gain_all[0])[1]
    grad_full_norm, grad_gain_one = first_pull(grad_normed)
    grad_full = grad_middle + grad_full_norm
    input_grad = swap_halves((grad_full[:, :-1] - grad_full[:, -1:]).astype(jnp.bfloat16))[None]
    rows = jnp.stack(
        [
            column_sums[:model_width],
            column_sums[2 * model_width :],
            grad_out_bias,
            grad_gain_one,
            grad_gain_two,
            grad_proj_bias,
        ]
    )
    rows = rows.reshape(6, shards, unit).transpose(1, 0, 2)
    last = grad_fc_bias.reshape(shards, 1, fc_bias.shape[0])
    grad_small = jnp.concatenate(
        [
            jnp.pad(rows, ((0, 0), (0, 0), (0, 256 - unit))),
            jnp.pad(last, ((0, 0), (0, 9), (0, 256 - fc_bias.shape[0]))),
        ],
        axis=1,
    )

    def split(grad):
        return grad.astype(jnp.bfloat16).reshape(shards, grad.shape[0] // shards, grad.shape[1])

    total_proj, total_fc, total_out, total_qkv, total_small = scatter_all(
        [split(grad_proj), split(grad_fc), split(grad_out), split(grad_qkv), grad_small.astype(jnp.bfloat16)],
        shards,
        [0, 1, 2, 3, 3],
        1,
    )
    return (
        residual_out,
        input_grad,
        total_qkv,
        total_out,
        total_fc,
        total_proj,
        total_small[:3, :unit],
        total_small[6, : fc_bias.shape[0]],
        total_small[5, :unit],
        total_small[3:5, :unit],
    )


def local(residual_in, cotangent, w_qkv, w_out, w_fc, w_proj, attn_bias, fc_bias, proj_bias, gains):
    arguments = (residual_in, cotangent, w_qkv, w_out, w_fc, w_proj, attn_bias, fc_bias, proj_bias, gains)
    if w_qkv.shape[0] % 16:
        return local_general(*arguments)
    return local_tiled(*arguments)


def local_tiled(residual_in, cotangent, w_qkv, w_out, w_fc, w_proj, attn_bias, fc_bias, proj_bias, gains):
    shards = lax.axis_size("fsdp")
    tok_rows = residual_in.shape[1]
    model_width = w_qkv.shape[1] // 3
    hidden_width = w_fc.shape[1]
    unit = gains.shape[1]
    small = place_small([attn_bias, gains, proj_bias[None], fc_bias[None]], shards, model_width)
    padding = ((0, 0), (0, 1))
    (qkv_w, out_w, fc_w, proj_w, compact, upstream, normed, heads, mixed, vectors) = front(
        jnp.pad(residual_in[0], padding), jnp.pad(cotangent[0], padding),
        w_qkv, small, w_out, w_fc, w_proj, shards, 0,
    )
    qkv_w = qkv_w.reshape(model_width, 3 * model_width)
    out_w = out_w.reshape(model_width, model_width)
    fc_w = fc_w.reshape(model_width, hidden_width)
    proj_w = proj_w.reshape(hidden_width, model_width)
    bias_all, gain_all, proj_b = vectors[:3], vectors[3:5], vectors[5]
    fc_b = vectors[6 : 6 + hidden_width // model_width].reshape(hidden_width)
    compact = compact.astype(jnp.float32)[:, :-1]
    full = jnp.concatenate([compact, -jnp.sum(compact, axis=-1, keepdims=True)], axis=-1)
    grad_final = upstream.astype(jnp.float32)
    branch = matmul(mixed, out_w) + bias_all[2]
    middle = full + center(branch)
    normed_two = rms_norm(middle, gain_all[1]).astype(jnp.bfloat16)
    hidden = matmul(normed_two, fc_w) + fc_b
    activated = gelu_tanh(hidden).astype(jnp.bfloat16)
    branch_two = matmul(activated, proj_w) + proj_b
    final = middle + center(branch_two)
    residual_out = swap_halves(final[:, :-1].astype(jnp.bfloat16))[None]
    grad_branch_two = center(grad_final).astype(jnp.bfloat16)
    grad_proj = weight_grad(activated, grad_branch_two)
    grad_proj_bias = jnp.sum(grad_branch_two.astype(jnp.float32), axis=0)
    grad_activated = input_grad_of(grad_branch_two, proj_w)
    gelu_pull = jax.vjp(gelu_tanh, hidden)[1]
    grad_hidden = gelu_pull(grad_activated)[0].astype(jnp.bfloat16)
    grad_fc = weight_grad(normed_two, grad_hidden)
    grad_fc_bias = jnp.sum(grad_hidden.astype(jnp.float32), axis=0)
    grad_normed_two = input_grad_of(grad_hidden, fc_w)
    second_pull = jax.vjp(rms_norm, middle, gain_all[1])[1]
    grad_middle_norm, grad_gain_two = second_pull(grad_normed_two)
    grad_middle = grad_final + grad_middle_norm
    grad_branch = center(grad_middle).astype(jnp.bfloat16)
    grad_out = weight_grad(mixed, grad_branch)
    grad_out_bias = jnp.sum(grad_branch.astype(jnp.float32), axis=0)
    grad_mixed = input_grad_of(grad_branch, out_w).astype(jnp.bfloat16)
    grad_projected = back(grad_mixed, heads, shards, 2)
    grad_qkv = weight_grad(normed, grad_projected)
    column_sums = jnp.sum(grad_projected.astype(jnp.float32), axis=0)
    grad_normed = input_grad_of(grad_projected, qkv_w)
    first_pull = jax.vjp(rms_norm, full, gain_all[0])[1]
    grad_full_norm, grad_gain_one = first_pull(grad_normed)
    grad_full = grad_middle + grad_full_norm
    input_grad = swap_halves((grad_full[:, :-1] - grad_full[:, -1:]).astype(jnp.bfloat16))[None]
    rows = jnp.stack(
        [
            column_sums[:model_width],
            column_sums[2 * model_width :],
            grad_out_bias,
            grad_gain_one,
            grad_gain_two,
            grad_proj_bias,
        ]
    )
    rows = rows.reshape(6, shards, unit).transpose(1, 0, 2)
    last = grad_fc_bias.reshape(shards, 1, fc_bias.shape[0])
    grad_small = jnp.concatenate(
        [
            jnp.pad(rows, ((0, 0), (0, 0), (0, 256 - unit))),
            jnp.pad(last, ((0, 0), (0, 9), (0, 256 - fc_bias.shape[0]))),
        ],
        axis=1,
    )

    def split(grad):
        return grad.astype(jnp.bfloat16).reshape(shards, grad.shape[0] // shards, grad.shape[1])

    total_proj, total_fc, total_out, total_qkv, total_small = scatter_all(
        [split(grad_proj), split(grad_fc), split(grad_out), split(grad_qkv), grad_small.astype(jnp.bfloat16)],
        shards,
        [0, 1, 2, 3, 3],
        1,
    )
    return (
        residual_out,
        input_grad,
        total_qkv,
        total_out,
        total_fc,
        total_proj,
        total_small[:3, :unit],
        total_small[6, : fc_bias.shape[0]],
        total_small[5, :unit],
        total_small[3:5, :unit],
    )


def solution(mesh):
    in_specs = (
        P("fsdp", "seq", None),
        P("fsdp", "seq", None),
        P("fsdp", None),
        P("fsdp", None),
        P("fsdp", None),
        P("fsdp", None),
        P(None, "fsdp"),
        P("fsdp"),
        P("fsdp"),
        P(None, "fsdp"),
    )
    out_specs = (
        P("fsdp", "seq", None),
        P("fsdp", "seq", None),
        P("fsdp", None),
        P("fsdp", None),
        P("fsdp", None),
        P("fsdp", None),
        P(None, "fsdp"),
        P("fsdp"),
        P("fsdp"),
        P(None, "fsdp"),
    )
    return jax.shard_map(local, mesh=mesh, in_specs=in_specs, out_specs=out_specs, check_vma=False)
```

```python
import functools

import jax
import jax.numpy as jnp
from jax import lax
from jax.experimental import pallas as pl
from jax.experimental.pallas import tpu as pltpu
from jax.sharding import PartitionSpec as P

HD = 64
EPSILON = 1e-05
MASKED = -1e30
MESH = pl.DeviceIdType.MESH
ANY = pl.BlockSpec(memory_space=pl.ANY)


class Place:
    def __init__(self, shards):
        self.length = shards // 4
        self.x = lax.axis_index("seq")
        index = lax.axis_index("fsdp")
        self.index = index
        self.core = lax.rem(index, 2)
        self.y = lax.rem(index // 2, 2)
        self.line = index // 4

    def at(self, **moved):
        x = moved.get("x", self.x)
        line = moved.get("line", self.line)
        y = moved.get("y", self.y)
        core = moved.get("core", self.core)
        return (x, (line * 2 + y) * 2 + core)

    def beside_x(self):
        return self.at(x=1 - self.x)

    def beside_y(self):
        return self.at(y=1 - self.y)

    def sibling(self):
        return self.at(core=1 - self.core)

    def above(self):
        return self.at(line=self.line + 1)

    def below(self):
        return self.at(line=self.line - 1)

    def greet(self, diagonal=False, whole_line=False):
        barrier = pltpu.get_barrier_semaphore()

        def signal(device):
            pl.semaphore_signal(barrier, inc=1, device_id=device, device_id_type=MESH)

        signal(self.beside_x())
        signal(self.beside_y())
        signal(self.sibling())
        has_below = self.line > 0
        has_above = self.line < self.length - 1
        if whole_line:
            for line in range(self.length):
                pl.when(self.line != line)(lambda line=line: signal(self.at(line=line)))
            count = 3 + self.length - 1
        else:
            pl.when(has_below)(lambda: signal(self.below()))
            pl.when(has_above)(lambda: signal(self.above()))
            count = 3 + has_below.astype(jnp.int32) + has_above.astype(jnp.int32)
        if diagonal:
            across = self.x != self.core
            pl.when(across)(lambda: signal(self.at(x=1 - self.x, core=1 - self.core)))
            count = count + across.astype(jnp.int32)
        pl.semaphore_wait(barrier, count)


def remote(src, dst, send, recv, device):
    return pltpu.make_async_remote_copy(
        src_ref=src, dst_ref=dst, send_sem=send, recv_sem=recv, device_id=device, device_id_type=MESH
    )


class Gather:
    def __init__(self, place, shard, out, sems):
        self.p = place
        self.shard = shard
        self.out = out
        self.rows, self.cols = shard.shape
        (self.up, self.down, self.line_in, self.ys, self.yr, self.xs, self.xr, self.ds, self.dr, self.own) = sems

    @staticmethod
    def sem_shapes(length):
        dma = pltpu.SemaphoreType.DMA
        return [dma((length,))] * 7 + [dma((3, length))] * 2 + [dma]

    def half(self, ref, which):
        width = self.cols // 2
        return ref.at[:, pl.ds(pl.multiple_of(which * width, width), width)]

    def slot(self, line, y, core):
        return self.out.at[line, y, core]

    def up_copy(self, line, src=None):
        p = self.p
        dst = self.slot(line, p.y, p.core)
        return remote(dst if src is None else src, dst, self.up.at[line], self.line_in.at[line], p.above())

    def down_copy(self, line, src=None):
        p = self.p
        dst = self.slot(line, p.y, p.core)
        return remote(dst if src is None else src, dst, self.down.at[line], self.line_in.at[line], p.below())

    def y_copy(self, line, src=None):
        p = self.p
        dst = self.half(self.slot(line, p.y, p.core), p.x)
        src = dst if src is None else self.half(src, p.x)
        return remote(src, dst, self.ys.at[line], self.yr.at[line], p.beside_y())

    def y_landing(self, line):
        p = self.p
        dst = self.half(self.slot(line, 1 - p.y, p.core), p.x)
        return remote(dst, dst, self.ys.at[line], self.yr.at[line], p.beside_y())

    def x_copy(self, line):
        p = self.p
        dst = self.half(self.slot(line, 1 - p.y, p.core), p.x)
        return remote(dst, dst, self.xs.at[line], self.xr.at[line], p.beside_x())

    def x_landing(self, line):
        p = self.p
        dst = self.half(self.slot(line, 1 - p.y, p.core), 1 - p.x)
        return remote(dst, dst, self.xs.at[line], self.xr.at[line], p.beside_x())

    def d_copy(self, kind, line, src=None, core=None):
        p = self.p
        core = p.core if core is None else core
        if kind == 0:
            dst = self.slot(line, p.y, core)
        else:
            dst = self.half(self.slot(line, 1 - p.y, core), p.x if kind == 1 else 1 - p.x)
        return remote(dst if src is None else src, dst, self.ds.at[kind, line], self.dr.at[kind, line], p.sibling())

    def own_copy(self):
        p = self.p
        return pltpu.make_async_copy(self.shard, self.slot(p.line, p.y, p.core), self.own)

    def each_at(self, distance, act):
        p = self.p
        if distance == 0:
            act(p.line, 0)
            return
        pl.when(p.line - distance >= 0)(lambda: act(p.line - distance, 1))
        pl.when(p.line + distance < p.length)(lambda: act(p.line + distance, -1))

    def arrive(self, distance):
        p = self.p

        def act(line, way):
            src = None
            if way == 0:
                src = self.shard
                self.own_copy().start()
            else:
                self.up_copy(line).wait_recv()
            if way >= 0:
                pl.when(p.line < p.length - 1)(lambda: self.up_copy(line, src).start())
            if way <= 0:
                pl.when(p.line > 0)(lambda: self.down_copy(line, src).start())
            self.y_copy(line, src).start()
            self.d_copy(0, line, src).start()

        self.each_at(distance, act)

    def arrive_y(self, distance):
        def act(line, way):
            self.y_landing(line).wait_recv()
            self.x_copy(line).start()
            self.d_copy(1, line).start()

        self.each_at(distance, act)

    def arrive_x(self, distance):
        def act(line, way):
            self.x_landing(line).wait_recv()
            self.d_copy(2, line).start()

        self.each_at(distance, act)

    def stage(self, time):
        length = self.p.length
        if 0 <= time < length:
            self.arrive(time)
        if 0 <= time - 1 < length:
            self.arrive_y(time - 1)
        if 0 <= time - 2 < length:
            self.arrive_x(time - 2)

    def stages(self):
        return self.p.length + 2

    def finish(self):
        p = self.p

        def one(line):
            for kind in range(3):
                self.d_copy(kind, line, core=1 - p.core).wait_recv()
            for kind in range(3):
                self.d_copy(kind, line).wait_send()
            self.y_copy(line).wait_send()
            self.x_copy(line).wait_send()
            pl.when((p.line >= line) & (p.line < p.length - 1))(lambda: self.up_copy(line).wait_send())
            pl.when((p.line <= line) & (p.line > 0))(lambda: self.down_copy(line).wait_send())

        for line in range(p.length):
            one(line)
        self.own_copy().wait()


def gather_kernel(shards, lag, count, *refs):
    ins, outs, rest = refs[:count], refs[count : 2 * count], refs[2 * count :]
    place = Place(shards)
    place.greet()
    per = len(Gather.sem_shapes(1))
    gathers = [Gather(place, ins[k], outs[k], rest[k * per : (k + 1) * per]) for k in range(count)]
    total = max(lag[k] + g.stages() for k, g in enumerate(gathers))
    for time in range(total):
        for k, g in enumerate(gathers):
            g.stage(time - lag[k])
    for g in gathers:
        g.finish()


def gather_all(arrays, shards, lag, collective_id):
    length = shards // 4
    out = pl.pallas_call(
        functools.partial(gather_kernel, shards, lag, len(arrays)),
        out_shape=[jax.ShapeDtypeStruct((length, 2, 2) + a.shape, a.dtype) for a in arrays],
        in_specs=[ANY] * len(arrays),
        out_specs=[ANY] * len(arrays),
        scratch_shapes=Gather.sem_shapes(length) * len(arrays),
        compiler_params=pltpu.CompilerParams(collective_id=collective_id, has_side_effects=True),
        name="gather_weights",
    )(*arrays)
    return [o.reshape((shards,) + a.shape) for o, a in zip(out, arrays)]


class Scatter:
    def __init__(self, place, partial, out, refs):
        self.p = place
        self.g = partial
        self.out = out
        self.rows, self.cols = out.shape
        (self.s, self.d, self.xb, self.yb, self.lo, self.hi, self.fb, self.tb,
         self.load, self.ds, self.dr, self.xs, self.xr, self.ys, self.yr,
         self.us, self.ur, self.ns, self.nr, self.fs, self.fr) = refs

    @staticmethod
    def scratch(length, rows, cols, dtype):
        dma = pltpu.SemaphoreType.DMA
        full = pltpu.VMEM((length, 2, rows, cols), dtype)
        half = pltpu.VMEM((length, rows, cols // 2), dtype)
        line = pltpu.VMEM((length, rows, cols), dtype)
        one = pltpu.VMEM((rows, cols), dtype)
        return [full, full, half, half, line, line, one, one] + [dma] * 7 + [dma((length,))] * 4 + [dma] * 2

    def half(self, which):
        width = self.cols // 2
        return pl.ds(pl.multiple_of(which * width, width), width)

    def load_copy(self):
        return pltpu.make_async_copy(self.g.at[:, :, self.p.core], self.s, self.load)

    def d_copy(self):
        p = self.p
        return remote(self.g.at[:, :, 1 - p.core], self.d, self.ds, self.dr, p.sibling())

    def x_copy(self):
        p = self.p
        src = self.s.at[:, 1 - p.y, :, self.half(1 - p.x)]
        return remote(src, self.xb, self.xs, self.xr, p.beside_x())

    def y_copy(self):
        p = self.p
        src = self.s.at[:, 1 - p.y, :, self.half(p.x)]
        return remote(src, self.yb, self.ys, self.yr, p.beside_y())

    def up_copy(self, line):
        p = self.p
        return remote(self.s.at[line, p.y], self.lo.at[line], self.us.at[line], self.ur.at[line], p.above())

    def down_copy(self, line):
        p = self.p
        return remote(self.s.at[line, p.y], self.hi.at[line], self.ns.at[line], self.nr.at[line], p.below())

    def f_copy(self):
        return remote(self.tb, self.fb, self.fs, self.fr, self.p.beside_x())

    def each(self, act):
        def body(line, carry):
            act(line)
            return carry

        lax.fori_loop(0, self.p.length, body, 0)

    def start(self):
        self.load_copy().start()
        self.d_copy().start()

    def pair(self):
        p = self.p
        self.load_copy().wait()
        self.d_copy().wait()

        def other(line):
            self.s[line, 1 - p.y] = self.s[line, 1 - p.y] + self.d[line, 1 - p.y]

        self.each(other)
        self.x_copy().start()

        def own(line):
            self.s[line, p.y] = self.s[line, p.y] + self.d[line, p.y]

        self.each(own)

    def over_x(self):
        p = self.p
        self.x_copy().wait()

        def act(line):
            cols = self.half(p.x)
            self.s[line, 1 - p.y, :, cols] = self.s[line, 1 - p.y, :, cols] + self.xb[line]

        self.each(act)
        self.y_copy().start()

    def over_y(self):
        p = self.p
        self.y_copy().wait()

        def act(line):
            cols = self.half(p.x)
            self.s[line, p.y, :, cols] = self.s[line, p.y, :, cols] + self.yb[line]

        self.each(act)

    def hop(self, step):
        p = self.p
        last = p.length - 1
        up = last - step + p.line

        def upward():
            @pl.when(p.line > 0)
            def _():
                self.up_copy(up).wait_recv()
                self.s[up, p.y] = self.s[up, p.y] + self.lo[up]

            self.up_copy(up).start()

        pl.when(p.line <= step)(upward)
        down = step - last + p.line

        def downward():
            @pl.when(p.line < last)
            def _():
                self.down_copy(down).wait_recv()
                self.s[down, p.y] = self.s[down, p.y] + self.hi[down]

            self.down_copy(down).start()

        pl.when(down >= 0)(downward)

    def total(self):
        p = self.p
        mine = p.line

        @pl.when(p.line > 0)
        def _():
            self.up_copy(mine).wait_recv()
            self.s[mine, p.y] = self.s[mine, p.y] + self.lo[mine]

        @pl.when(p.line < p.length - 1)
        def _():
            self.down_copy(mine).wait_recv()
            self.s[mine, p.y] = self.s[mine, p.y] + self.hi[mine]

        self.tb[...] = self.s[mine, p.y]
        self.f_copy().start()

    def finish(self):
        p = self.p
        self.f_copy().wait()
        self.out[...] = self.tb[...].astype(jnp.float32) + self.fb[...].astype(jnp.float32)
        for line in range(p.length):
            pl.when(line > p.line)(lambda line=line: self.up_copy(line).wait_send())
            pl.when(line < p.line)(lambda line=line: self.down_copy(line).wait_send())

    def stages(self):
        acts = [self.start, self.pair, self.over_x, self.over_y]
        acts += [functools.partial(self.hop, step) for step in range(self.p.length - 1)]
        return acts + [self.total, self.finish]


def scatter_kernel(shards, lag, count, *refs):
    ins, outs, rest = refs[:count], refs[count : 2 * count], refs[2 * count :]
    place = Place(shards)
    place.greet()
    per = len(rest) // count
    lists = [
        Scatter(place, ins[k], outs[k], rest[k * per : (k + 1) * per]).stages() for k in range(count)
    ]
    total = max(lag[k] + len(s) for k, s in enumerate(lists))
    for time in range(total):
        for k, acts in enumerate(lists):
            if 0 <= time - lag[k] < len(acts):
                acts[time - lag[k]]()


def scatter_all(arrays, shards, lag, collective_id):
    length = shards // 4
    parts = [a.reshape((length, 2, 2) + a.shape[1:]) for a in arrays]
    scratch = []
    for a in arrays:
        scratch += Scatter.scratch(length, a.shape[1], a.shape[2], a.dtype)
    return pl.pallas_call(
        functools.partial(scatter_kernel, shards, lag, len(arrays)),
        out_shape=[jax.ShapeDtypeStruct(a.shape[1:], jnp.float32) for a in arrays],
        in_specs=[ANY] * len(arrays),
        out_specs=[pl.BlockSpec(memory_space=pltpu.VMEM)] * len(arrays),
        scratch_shapes=scratch,
        compiler_params=pltpu.CompilerParams(
            collective_id=collective_id, has_side_effects=True, vmem_limit_bytes=60 << 20
        ),
        name="scatter_grads",
    )(*parts)


def rms_norm(values, gain):
    return values * lax.rsqrt(jnp.mean(values * values, axis=-1, keepdims=True) + EPSILON) * gain


def center(values):
    return values - jnp.mean(values, axis=-1, keepdims=True)


def gelu_tanh(values):
    return jax.nn.gelu(values, approximate=True)


def matmul(left, right):
    return jnp.dot(left, right, preferred_element_type=jnp.float32)


def weight_grad(inputs, grads):
    return lax.dot_general(
        inputs, grads, (((0,), (0,)), ((), ())), preferred_element_type=jnp.float32
    )


def input_grad_of(grads, weight):
    return lax.dot_general(
        grads, weight, (((1,), (1,)), ((), ())), preferred_element_type=jnp.float32
    )


def block_rows(length):
    return min(length, max(512, length // 8))


def score_block(query_block, keys_part, start, scale):
    scores = (
        jnp.einsum("qhd,khd->hqk", query_block, keys_part, preferred_element_type=jnp.float32)
        * scale
    )
    query_pos = start + jnp.arange(query_block.shape[0], dtype=jnp.int32)
    key_pos = jnp.arange(keys_part.shape[0], dtype=jnp.int32)
    allowed = query_pos[:, None] >= key_pos[None, :]
    return jnp.where(allowed[None], scores, MASKED)


def attend(queries, keys_all, values_all, scale):
    length, head_count, width = queries.shape
    block = block_rows(length)
    count = length // block
    results = []
    log_totals = []
    for index in range(count):
        start = index * block
        finish = start + block
        scores = score_block(queries[start:finish], keys_all[:finish], start, scale)
        peak = jnp.max(scores, axis=-1, keepdims=True)
        weights = jnp.exp(scores - peak)
        total = jnp.sum(weights, axis=-1, keepdims=True)
        weights = weights / total
        result = jnp.einsum(
            "hqk,khd->qhd",
            weights.astype(jnp.bfloat16),
            values_all[:finish],
            preferred_element_type=jnp.float32,
        )
        results.append(result.astype(jnp.bfloat16))
        log_totals.append((peak + jnp.log(total))[..., 0])
    joined = jnp.concatenate(results, axis=0)
    return (joined.reshape(length, head_count * width), log_totals)


def attend_back(queries, keys_all, values_all, log_totals, grad_heads, scale):
    length, head_count, width = queries.shape
    block = block_rows(length)
    count = length // block
    key_sum = jnp.zeros((length, head_count, width), jnp.float32)
    value_sum = jnp.zeros((length, head_count, width), jnp.float32)
    query_grads = []
    for index in range(count):
        start = index * block
        finish = start + block
        query_block = queries[start:finish]
        grad_block = grad_heads[start:finish]
        keys_part = keys_all[:finish]
        scores = score_block(query_block, keys_part, start, scale)
        weights = jnp.exp(scores - log_totals[index][..., None])
        grad_weights = jnp.einsum(
            "qhd,khd->hqk", grad_block, values_all[:finish], preferred_element_type=jnp.float32
        )
        inner = jnp.sum(weights * grad_weights, axis=-1, keepdims=True)
        grad_scores = (weights * (grad_weights - inner)).astype(jnp.bfloat16)
        query_grad = (
            jnp.einsum("hqk,khd->qhd", grad_scores, keys_part, preferred_element_type=jnp.float32)
            * scale
        )
        key_part = (
            jnp.einsum("hqk,qhd->khd", grad_scores, query_block, preferred_element_type=jnp.float32)
            * scale
        )
        value_part = jnp.einsum(
            "hqk,qhd->khd",
            weights.astype(jnp.bfloat16),
            grad_block,
            preferred_element_type=jnp.float32,
        )
        key_sum = key_sum.at[:finish].add(key_part)
        value_sum = value_sum.at[:finish].add(value_part)
        query_grads.append(query_grad.astype(jnp.bfloat16))
    return (
        jnp.concatenate(query_grads, axis=0),
        key_sum.astype(jnp.bfloat16),
        value_sum.astype(jnp.bfloat16),
    )


def dot_nn(left, right):
    return jnp.dot(left, right, preferred_element_type=jnp.float32)


def dot_nt(left, right):
    return lax.dot_general(
        left, right, (((1,), (1,)), ((), ())), preferred_element_type=jnp.float32
    )


def dot_tn(left, right):
    return lax.dot_general(
        left, right, (((0,), (0,)), ((), ())), preferred_element_type=jnp.float32
    )


def lane_block(index, width):
    return pl.ds(pl.multiple_of(index * width, width), width)


def widen(value):
    value = value.astype(jnp.float32)
    lanes = lax.broadcasted_iota(jnp.int32, value.shape, 1)
    missing = -jnp.sum(value, axis=-1, keepdims=True)
    return jnp.where(lanes == value.shape[1] - 1, missing, value)


def unit_scale(value):
    return lax.rsqrt(jnp.mean(value * value, axis=-1, keepdims=True) + EPSILON)


def over_rows(total, block, act):
    def body(step, carry):
        act(pl.ds(pl.multiple_of(step * block, block), block))
        return carry

    lax.fori_loop(0, total // block, body, 0)


def head_mask(shape, head):
    lanes = lax.broadcasted_iota(jnp.int32, shape, 1)
    return (lanes // HD) == head


class Swap:
    def __init__(self, place, src, dst, sems):
        self.p = place
        self.src, self.dst = src, dst
        self.send, self.recv = sems

    def moved(self):
        p = self.p
        return remote(self.src, self.dst, self.send, self.recv, p.at(x=1 - p.x, core=1 - p.core))

    def kept(self):
        return pltpu.make_async_copy(self.src, self.dst, self.send)

    def start(self):
        p = self.p
        pl.when(p.x != p.core)(lambda: self.moved().start())
        pl.when(p.x == p.core)(lambda: self.kept().start())

    def wait(self):
        p = self.p
        pl.when(p.x != p.core)(lambda: self.moved().wait())
        pl.when(p.x == p.core)(lambda: self.kept().wait())


def attend_pair(qkv, pair, put):
    total = qkv.shape[1]
    block = min(256, total)
    lanes = pl.ds(pair * 2 * HD, 2 * HD)
    scale = jnp.asarray(HD ** (-0.5), jnp.bfloat16)
    zero = jnp.zeros((), jnp.bfloat16)
    rows = lax.broadcasted_iota(jnp.int32, (block, block), 0)
    cols = lax.broadcasted_iota(jnp.int32, (block, block), 1)
    allowed = rows >= cols
    for index in range(total // block):
        start = index * block
        here = pl.ds(start, block)
        query = qkv[0, here, lanes] * scale
        results = []
        for head in range(2):
            masked = jnp.where(head_mask(query.shape, head), query, zero)
            near = dot_nt(masked, qkv[1, here, lanes])
            near = jnp.where(allowed, near, MASKED)
            peak = jnp.max(near, axis=-1, keepdims=True)
            if start:
                far = dot_nt(masked, qkv[1, pl.ds(0, start), lanes])
                peak = jnp.maximum(peak, jnp.max(far, axis=-1, keepdims=True))
            near = jnp.exp(near - peak)
            total_weight = jnp.sum(near, axis=-1, keepdims=True)
            if start:
                far = jnp.exp(far - peak)
                total_weight = total_weight + jnp.sum(far, axis=-1, keepdims=True)
            share = 1.0 / total_weight
            result = dot_nn((near * share).astype(jnp.bfloat16), qkv[2, here, lanes])
            if start:
                result += dot_nn(
                    (far * share).astype(jnp.bfloat16), qkv[2, pl.ds(0, start), lanes]
                )
            results.append(result)
        merged = jnp.where(head_mask(results[0].shape, 0), results[0], results[1])
        put(start, block, merged.astype(jnp.bfloat16))


def front_kernel(shards, lag, *refs):
    (resid, cot, w_qkv, small, w_out, w_fc, w_proj,
     qkv_o, out_o, fc_o, proj_o, resid_o, cot_o, normed_o, heads_o, mixed_o, vec_o,
     qkv_w, small_w, rs, cs, heads, send_heads, att, mixed, *sems) = refs
    place = Place(shards)
    place.greet(diagonal=True)
    width = rs.shape[1]
    rows = rs.shape[0]
    share = width // 2
    per = len(Gather.sem_shapes(1))
    pairs = [(w_qkv, qkv_w), (small, small_w), (w_out, out_o), (w_fc, fc_o), (w_proj, proj_o)]
    gathers = []
    for src, dst in pairs:
        gathers.append(Gather(place, src, dst, sems[:per]))
        sems = sems[per:]
    swap_in = Swap(place, resid, rs, sems[:2])
    swap_cot = Swap(place, cot, cs, sems[2:4])
    heads_s, heads_r, att_s, att_r, done = sems[4:]
    clock = [0]
    final = max(lag[k] + g.stages() for k, g in enumerate(gathers))

    def tick(count=1):
        for _ in range(count):
            for k, g in enumerate(gathers):
                g.stage(clock[0] - lag[k])
            clock[0] += 1

    tick()
    swap_in.start()
    tick()
    swap_in.wait()
    gathers_first = gathers[:2]
    while clock[0] < max(g.stages() for g in gathers_first):
        tick()
    swap_cot.start()
    gathers[1].finish()
    vec_o[...] = jnp.sum(small_w[...].astype(jnp.float32), axis=(0, 1, 2))

    def normalize(here):
        full = widen(rs[here, :])
        normed_o[here, :] = (full * unit_scale(full) * vec_o[3:4, :]).astype(jnp.bfloat16)

    over_rows(rows, 64, normalize)
    gathers[0].finish()

    weight = qkv_w.reshape(width, 3 * width)

    def exchange(block):
        src = send_heads.at[block]
        dst = heads.at[block, pl.ds(pl.multiple_of(place.core * rows, rows), rows)]
        return remote(src, dst, heads_s.at[block], heads_r.at[block], place.sibling())

    def project(block, group):
        at = block * 2 + group
        result = dot_nn(normed_o[...], weight[:, lane_block(at, share)])
        if block == 0:
            result = result + vec_o[0:1, lane_block(group, share)]
        if block == 2:
            result = result + vec_o[1:2, lane_block(group, share)]
        return result.astype(jnp.bfloat16)

    for block in range(3):
        send_heads[block] = project(block, 1 - place.core)
        exchange(block).start()
    for block in range(3):
        heads[block, pl.ds(pl.multiple_of(place.core * rows, rows), rows), :] = project(block, place.core)
    for block in range(3):
        exchange(block).wait()

    def back(pair):
        lanes = pl.ds(pair * 2 * HD, 2 * HD)
        src = att.at[1 - place.core, :, lanes]
        dst = mixed.at[:, pl.ds(pl.multiple_of(place.core * share + pair * 2 * HD, 2 * HD), 2 * HD)]
        return remote(src, dst, att_s.at[pair], att_r.at[pair], place.sibling())

    count = share // (2 * HD)
    for pair in range(count):
        lanes = pl.ds(pair * 2 * HD, 2 * HD)

        def put(start, block, value):
            att[start // rows, pl.ds(start % rows, block), lanes] = value

        attend_pair(heads, pair, put)
        back(pair).start()
        mine = pl.ds(pl.multiple_of(place.core * share + pair * 2 * HD, 2 * HD), 2 * HD)
        mixed[:, mine] = att[place.core, :, lanes]
        tick(2)
    while clock[0] < final:
        tick()
    outs = [(qkv_w, qkv_o), (rs, resid_o), (heads, heads_o)]
    copies = [pltpu.make_async_copy(s, d, done.at[k]) for k, (s, d) in enumerate(outs)]
    for copy in copies:
        copy.start()
    for pair in range(count):
        back(pair).wait()
    mixed_o[...] = mixed[...]
    swap_cot.wait()
    cot_o[...] = cs[...]
    for g in gathers[2:]:
        g.finish()
    for copy in copies:
        copy.wait()


def front(resid, cot, w_qkv, small, w_out, w_fc, w_proj, shards, collective_id):
    length = shards // 4
    rows, width = resid.shape
    share = width // 2
    low = jnp.bfloat16
    sums = [w_qkv, w_out, w_fc, w_proj]
    gathered = [jax.ShapeDtypeStruct((length, 2, 2) + a.shape, low) for a in sums]
    shapes = gathered + [
        jax.ShapeDtypeStruct((rows, width), low),
        jax.ShapeDtypeStruct((rows, width), low),
        jax.ShapeDtypeStruct((rows, width), low),
        jax.ShapeDtypeStruct((3, 2 * rows, share), low),
        jax.ShapeDtypeStruct((rows, width), low),
        jax.ShapeDtypeStruct(small.shape, jnp.float32),
    ]
    vmem = pl.BlockSpec(memory_space=pltpu.VMEM)
    dma = pltpu.SemaphoreType.DMA
    pairs = share // (2 * HD)
    return pl.pallas_call(
        functools.partial(front_kernel, shards, [0, 0, 3, 3, 4]),
        out_shape=shapes,
        in_specs=[ANY] * 7,
        out_specs=[ANY] * 5 + [vmem, vmem, ANY, vmem, vmem],
        scratch_shapes=[
            pltpu.VMEM((length, 2, 2) + w_qkv.shape, low),
            pltpu.VMEM((length, 2, 2) + small.shape, low),
            pltpu.VMEM((rows, width), low),
            pltpu.VMEM((rows, width), low),
            pltpu.VMEM((3, 2 * rows, share), low),
            pltpu.VMEM((3, rows, share), low),
            pltpu.VMEM((2, rows, share), low),
            pltpu.VMEM((rows, width), low),
        ]
        + Gather.sem_shapes(length) * 5
        + [dma, dma, dma, dma, dma((3,)), dma((3,)), dma((pairs,)), dma((pairs,)), dma((3,))],
        compiler_params=pltpu.CompilerParams(
            collective_id=collective_id, has_side_effects=True, vmem_limit_bytes=60 << 20
        ),
        name="front",
    )(resid, cot, w_qkv, small, w_out, w_fc, w_proj)


def place_small(vectors, shards, width):
    index = lax.axis_index("fsdp")
    rows = []
    for value in vectors:
        piece = value.shape[1]
        length = piece * shards
        spread = jnp.tile(value, (1, shards))
        here = jnp.arange(length, dtype=jnp.int32)[None] // piece == index
        spread = jnp.where(here, spread, jnp.zeros((), value.dtype))
        rows.append(spread.reshape(-1, width))
    packed = jnp.concatenate(rows, axis=0)
    return jnp.pad(packed, ((0, 16 - packed.shape[0]), (0, 0)))


def attend_back_pair(qkv, grads, pair, key_sum, value_sum, put):
    total = qkv.shape[1]
    block = min(256, total)
    lanes = pl.ds(pair * 2 * HD, 2 * HD)
    scale = jnp.asarray(HD ** (-0.5), jnp.bfloat16)
    zero = jnp.zeros((), jnp.bfloat16)
    rows = lax.broadcasted_iota(jnp.int32, (block, block), 0)
    cols = lax.broadcasted_iota(jnp.int32, (block, block), 1)
    allowed = rows <= cols
    key_sum[...] = jnp.zeros_like(key_sum)
    value_sum[...] = jnp.zeros_like(value_sum)
    for index in range(total // block):
        start = index * block
        here = pl.ds(start, block)
        spans = [here] + ([pl.ds(0, start)] if start else [])
        query = qkv[0, here, lanes] * scale
        grad = grads[start // grads.shape[1], pl.ds(start % grads.shape[1], block), lanes]
        query_grads = []
        for head in range(2):
            mask = head_mask(query.shape, head)
            masked = jnp.where(mask, query, zero)
            grad_masked = jnp.where(mask, grad, zero)
            scores = [dot_nt(qkv[1, span, lanes], masked) for span in spans]
            scores[0] = jnp.where(allowed, scores[0], MASKED)
            peak = functools.reduce(
                jnp.maximum, [jnp.max(s, axis=0, keepdims=True) for s in scores]
            )
            weights = [jnp.exp(s - peak) for s in scores]
            sums = sum(jnp.sum(w, axis=0, keepdims=True) for w in weights)
            share = 1.0 / sums
            weights = [w * share for w in weights]
            pulled = [dot_nt(qkv[2, span, lanes], grad_masked) for span in spans]
            inner = sum(jnp.sum(w * g, axis=0, keepdims=True) for w, g in zip(weights, pulled))
            query_grad = None
            for span, w, g in zip(spans, weights, pulled):
                value_sum[span, :] += dot_nn(w.astype(jnp.bfloat16), grad_masked)
                slope = (w * (g - inner)).astype(jnp.bfloat16)
                key_sum[span, :] += dot_nn(slope, masked)
                part = dot_tn(slope, qkv[1, span, lanes])
                query_grad = part if query_grad is None else query_grad + part
            query_grads.append(query_grad)
        merged = jnp.where(head_mask(query_grads[0].shape, 0), query_grads[0], query_grads[1])
        put(0, start, block, (merged * HD ** (-0.5)).astype(jnp.bfloat16))
    half = grads.shape[1]
    for start in range(0, total, half):
        put(1, start, half, key_sum[pl.ds(start, half), :].astype(jnp.bfloat16))
        put(2, start, half, value_sum[pl.ds(start, half), :].astype(jnp.bfloat16))


class Chunk:
    def __init__(self, place, index, refs, store):
        self.p = place
        self.store = store
        (grads, self_d, xb, yb, lo, hi, tb, fb, ds, dr, xs, xr, ys, yr, us, ur, ns, nr, fs, fr) = refs
        self.mine, self.other = grads.at[index, 0], grads.at[index, 1]
        self.d, self.xb, self.yb = self_d.at[index], xb.at[index], yb.at[index]
        self.lo, self.hi = lo.at[index], hi.at[index]
        self.tb, self.fb = tb.at[index], fb.at[index]
        self.sems = [s.at[index] for s in (ds, dr, xs, xr, ys, yr)]
        self.us, self.ur, self.ns, self.nr = us.at[index], ur.at[index], ns.at[index], nr.at[index]
        self.fs, self.fr = fs.at[index], fr.at[index]

    @staticmethod
    def scratch(count, length, rows, cols):
        low = jnp.bfloat16
        dma = pltpu.SemaphoreType.DMA
        return [
            pltpu.VMEM((count, 2, length, 2, rows, cols), low),
            pltpu.VMEM((count, length, 2, rows, cols), low),
            pltpu.VMEM((count, length, rows, cols // 2), low),
            pltpu.VMEM((count, length, rows, cols // 2), low),
            pltpu.VMEM((count, length - 1, rows, cols), low),
            pltpu.VMEM((count, length - 1, rows, cols), low),
            pltpu.VMEM((count, rows, cols), low),
            pltpu.VMEM((count, rows, cols), low),
        ] + [dma((count,))] * 6 + [dma((count, length))] * 4 + [dma((count,))] * 2

    def half(self, which):
        width = self.tb.shape[1] // 2
        return pl.ds(pl.multiple_of(which * width, width), width)

    def d_copy(self):
        return remote(self.other, self.d, self.sems[0], self.sems[1], self.p.sibling())

    def x_copy(self):
        p = self.p
        src = self.mine.at[:, 1 - p.y, :, self.half(1 - p.x)]
        return remote(src, self.xb, self.sems[2], self.sems[3], p.beside_x())

    def y_copy(self):
        p = self.p
        src = self.mine.at[:, 1 - p.y, :, self.half(p.x)]
        return remote(src, self.yb, self.sems[4], self.sems[5], p.beside_y())

    def up_copy(self, line):
        p = self.p
        return remote(self.mine.at[line, p.y], self.lo.at[line - 1], self.us.at[line], self.ur.at[line], p.above())

    def down_copy(self, line):
        p = self.p
        return remote(self.mine.at[line, p.y], self.hi.at[line], self.ns.at[line], self.nr.at[line], p.below())

    def f_copy(self):
        return remote(self.tb, self.fb, self.fs, self.fr, self.p.beside_x())

    def each(self, act):
        def body(line, carry):
            act(line)
            return carry

        lax.fori_loop(0, self.p.length, body, 0)

    def start(self):
        self.d_copy().start()

    def pair(self):
        p = self.p
        self.d_copy().wait()

        def other(line):
            self.mine[line, 1 - p.y] = self.mine[line, 1 - p.y] + self.d[line, 1 - p.y]

        self.each(other)
        self.x_copy().start()

        def own(line):
            self.mine[line, p.y] = self.mine[line, p.y] + self.d[line, p.y]

        self.each(own)

    def over_x(self):
        p = self.p
        self.x_copy().wait()

        def act(line):
            cols = self.half(p.x)
            self.mine[line, 1 - p.y, :, cols] = self.mine[line, 1 - p.y, :, cols] + self.xb[line]

        self.each(act)
        self.y_copy().start()

    def over_y(self):
        p = self.p
        self.y_copy().wait()

        def act(line):
            cols = self.half(p.x)
            self.mine[line, p.y, :, cols] = self.mine[line, p.y, :, cols] + self.yb[line]

        self.each(act)
        self.hop(0)

    def take_low(self, line):
        self.up_copy(line).wait_recv()
        self.mine[line, self.p.y] = self.mine[line, self.p.y] + self.lo[line - 1]

    def take_high(self, line):
        self.down_copy(line).wait_recv()
        self.mine[line, self.p.y] = self.mine[line, self.p.y] + self.hi[line]

    def hop(self, step):
        p = self.p
        last = p.length - 1
        up = last - step + p.line

        def upward():
            pl.when(p.line > 0)(lambda: self.take_low(up))
            self.up_copy(up).start()

        pl.when(p.line <= step)(upward)
        down = step - last + p.line

        def downward():
            pl.when(p.line < last)(lambda: self.take_high(down))
            self.down_copy(down).start()

        pl.when(down >= 0)(downward)

    def total(self):
        p = self.p
        mine = p.line
        pl.when(mine > 0)(lambda: self.take_low(mine))
        pl.when(mine < p.length - 1)(lambda: self.take_high(mine))
        self.tb[...] = self.mine[mine, p.y]
        self.f_copy().start()

    def finish(self):
        p = self.p
        self.f_copy().wait()
        self.store(self.tb[...].astype(jnp.float32) + self.fb[...].astype(jnp.float32))
        for line in range(p.length - 1):
            pl.when(line + 1 > p.line)(lambda line=line: self.up_copy(line + 1).wait_send())
            pl.when(line < p.line)(lambda line=line: self.down_copy(line).wait_send())

    def acts(self):
        hops = [functools.partial(self.hop, step) for step in range(1, self.p.length - 1)]
        return [self.pair, self.over_x, self.over_y] + hops + [self.total, self.finish]


class Train:
    def __init__(self):
        self.running = []

    def add(self, acts):
        self.running.append(list(acts))

    def tick(self):
        for acts in self.running:
            acts.pop(0)()
        self.running = [acts for acts in self.running if acts]

    def drain(self):
        while self.running:
            self.tick()


class SmallSum:
    def __init__(self, place, refs):
        self.p = place
        self.stages, self.got, self.lines, self.ss, self.sr, self.ls, self.lr = refs

    def copy(self, step):
        p = self.p
        goal = [p.sibling, p.beside_x, p.beside_y][step]()
        return remote(self.stages.at[step], self.got.at[step], self.ss.at[step], self.sr.at[step], goal)

    def line_copy(self, line):
        p = self.p
        return remote(
            self.stages.at[3], self.lines.at[p.line], self.ls.at[line], self.lr.at[p.line], p.at(line=line)
        )

    def line_landing(self, line):
        p = self.p
        return remote(self.stages.at[3], self.lines.at[line], self.ls.at[line], self.lr.at[line], p.at(line=line))

    def begin(self):
        self.copy(0).start()

    def step(self, index):
        p = self.p
        self.copy(index).wait()
        self.stages[index + 1] = self.stages[index] + self.got[index]
        if index < 2:
            self.copy(index + 1).start()
            return
        for line in range(p.length):
            pl.when(p.line != line)(lambda line=line: self.line_copy(line).start())
        self.lines[p.line] = self.stages[3]

    def end(self, store):
        p = self.p
        for line in range(p.length):
            pl.when(p.line != line)(lambda line=line: self.line_copy(line).wait_send())
            pl.when(p.line != line)(lambda line=line: self.line_landing(line).wait_recv())
        total = self.lines[0]
        for line in range(1, p.length):
            total = total + self.lines[line]
        store(total)

    def acts(self, store):
        return [functools.partial(self.step, k) for k in range(3)] + [lambda: self.end(store)]


def gelu_pair(hidden):
    ratio = (2.0 / 3.141592653589793) ** 0.5
    square = hidden * hidden
    curve = jnp.tanh(ratio * (hidden + 0.044715 * (square * hidden)))
    cdf = 0.5 * (1.0 + curve)
    slope = cdf + hidden * (0.5 * (1.0 - curve * curve)) * (ratio * (1.0 + (3.0 * 0.044715) * square))
    return hidden * cdf, slope


def norm_back(value, gain, grad):
    scale = unit_scale(value)
    unit = value * scale
    lifted = grad * gain
    pull = jnp.mean(lifted * unit, axis=-1, keepdims=True)
    return scale * (lifted - unit * pull), grad * unit


def column_sum(value):
    return jnp.sum(value.astype(jnp.float32), axis=0, keepdims=True)


def rear_kernel(shards, *refs):
    (rs, cs, normed, heads, mixed, vec, qkv_w, out_w, fc_w, proj_w,
     total_qkv, total_out, total_fc, total_proj, total_small, resid_o, input_o,
     wo, tiles, work, middle, acc, gn, got, gproj, key_sum, value_sum, ro, sg, *rest) = refs
    chunk_refs, rest = rest[:20], rest[20:]
    small_refs, rest = rest[:7], rest[7:]
    wsem, osem, ro_s, ro_r, ig_s, ig_r, gm_s, gm_r, gp_s, gp_r = rest
    place = Place(shards)
    low = jnp.bfloat16
    rows, width = mixed.shape
    share = width // 2
    unit = width // shards
    parts = fc_w.shape[-1] // width
    block = min(256, rows)
    train = Train()

    def fc_load(tile):
        src = fc_w.at[:, :, :, :, pl.ds(tile * width, width)]
        return pltpu.make_async_copy(src, tiles.at[tile % 2], wsem.at[tile % 2])

    def proj_load(tile):
        return pltpu.make_async_copy(proj_w.at[tile], tiles.at[2 + tile % 2], wsem.at[2 + tile % 2])

    def qkv_load(part):
        src = qkv_w.at[:, :, :, :, pl.ds(part * width, width)]
        return pltpu.make_async_copy(src, tiles.at[part], wsem.at[part])

    out_load = pltpu.make_async_copy(out_w, wo, osem)
    out_load.start()
    fc_load(0).start()
    proj_load(0).start()
    fc_load(1).start()
    proj_load(1).start()
    flat = tiles.reshape(4, width, width)
    out_flat = wo.reshape(width, width)
    place.greet(diagonal=True, whole_line=True)
    sg[...] = jnp.zeros_like(sg)

    def chunk(index, store):
        return Chunk(place, index, chunk_refs, store)

    def put_qkv(part):
        def store(value):
            total_qkv[:, pl.ds(part * width, width)] = value
        return store

    def put_fc(tile):
        def store(value):
            total_fc[:, pl.ds(tile * width, width)] = value
        return store

    def put_proj(part):
        def store(value):
            total_proj[pl.ds(part * unit, unit), :] = value
        return store

    def put_out(value):
        total_out[...] = value

    fc_chunks = [chunk(k, put_fc(k)) for k in range(parts)]
    proj_chunks = [chunk(parts + k, put_proj(k)) for k in range(parts)]
    out_chunk = chunk(2 * parts, put_out)
    qkv_chunks = [chunk(2 * parts + 1 + k, put_qkv(k)) for k in range(3)]
    grads = chunk_refs[0]

    def keep_rows(index, first, value):
        value = value.astype(low)
        for k in range(value.shape[0] // unit):
            shard = first + k
            side = lax.rem(place.core + shard % 2, 2)
            grads[index, side, shard // 4, (shard // 2) % 2] = value[k * unit : (k + 1) * unit]

    def weight_grad_chunk(item, index, left, right):
        for part in range(2):
            lanes = pl.ds(part * share, share)
            keep_rows(index, part * (shards // 2), dot_tn(left[:, lanes], right))
        item.start()
        train.add(item.acts())

    act_ref, slope_ref, n2, g2 = work.at[0], work.at[1], work.at[2], work.at[3]
    out_load.wait()

    def enter(here):
        branch = dot_nn(mixed[here, :], out_flat[...]) + vec[2:3, :]
        value = widen(rs[here, :]) + branch - jnp.mean(branch, axis=-1, keepdims=True)
        middle[here, :] = value
        n2[here, :] = (value * unit_scale(value) * vec[4:5, :]).astype(low)
        upstream = cs[here, :].astype(jnp.float32)
        grad = (upstream - jnp.mean(upstream, axis=-1, keepdims=True)).astype(low)
        g2[here, :] = grad
        sg[5:6, :] += column_sum(grad)

    over_rows(rows, block, enter)

    for tile in range(parts):
        fc_load(tile).wait()
        proj_load(tile).wait()
        fc_tile, proj_tile = flat.at[tile % 2], flat.at[2 + tile % 2]

        def feed(here):
            hidden = dot_nn(n2[here, :], fc_tile[...]) + vec[6 + tile : 7 + tile, :]
            value, slope = gelu_pair(hidden)
            value = value.astype(low)
            act_ref[here, :] = value
            grad = (dot_nt(g2[here, :], proj_tile[...]) * slope).astype(low)
            slope_ref[here, :] = grad
            sg[6 + tile : 7 + tile, :] += column_sum(grad)
            forward = dot_nn(value, proj_tile[...])
            backward = dot_nt(grad, fc_tile[...])
            if tile == 0:
                acc[here, :] = forward
                gn[here, :] = backward
            else:
                acc[here, :] += forward
                gn[here, :] += backward

        over_rows(rows, block, feed)
        if tile + 2 < parts:
            fc_load(tile + 2).start()
            proj_load(tile + 2).start()
        train.tick()
        weight_grad_chunk(fc_chunks[tile], tile, n2, slope_ref[...])
        deep = total_proj.shape[0]
        for part in range(2):
            lanes = pl.ds(part * share, share)
            value = dot_tn(act_ref[:, lanes], g2[...])
            first = (tile * width + part * share) // deep
            for k in range(share // deep):
                for q in range(parts):
                    at = k * deep + q * unit
                    keep_rows(parts + q, first + k, value[at : at + unit])
        train.tick()

    for item in proj_chunks[:2]:
        item.start()
        train.add(item.acts())

    def leave(here):
        branch = acc[here, :] + vec[5:6, :]
        value = middle[here, :]
        ro[here, :] = (value + branch - jnp.mean(branch, axis=-1, keepdims=True)).astype(low)
        pull, terms = norm_back(value, vec[4:5, :], gn[here, :])
        sg[4:5, :] += jnp.sum(terms, axis=0, keepdims=True)
        grad = cs[here, :].astype(jnp.float32) + pull
        acc[here, :] = grad
        grad = (grad - jnp.mean(grad, axis=-1, keepdims=True)).astype(low)
        g2[here, :] = grad
        sg[2:3, :] += column_sum(grad)

    over_rows(rows, block // 2, leave)
    swap_out = Swap(place, ro, resid_o, (ro_s, ro_r))
    swap_out.start()
    train.tick()

    def group_lanes(group):
        return pl.ds(pl.multiple_of(group * share, 2 * HD), share)

    def mixed_grad(group):
        lanes = pl.ds(pl.multiple_of(group * share, 128), share)
        return dot_nt(g2[...], out_flat[lanes, :]).astype(low)

    n2[:, pl.ds(0, share)] = mixed_grad(1 - place.core)
    give = remote(n2.at[:, pl.ds(0, share)], got.at[place.core], gm_s, gm_r, place.sibling())
    give.start()
    got[place.core] = mixed_grad(place.core)
    weight_grad_chunk(out_chunk, 2 * parts, mixed, g2[...])
    for item in proj_chunks[2:]:
        item.start()
        train.add(item.acts())
    for part in range(3):
        qkv_load(part).start()
    train.tick()
    give.wait()
    span = 2 * HD

    def send(part, pair):
        lanes = pl.multiple_of((1 - place.core) * share + pair * span, span)
        src = work.at[part, :, pl.ds(lanes, span)]
        at = pl.multiple_of((part * 2 + place.core) * share + pair * span, span)
        return remote(src, gproj.at[:, pl.ds(at, span)], gp_s.at[part, pair], gp_r.at[part, pair], place.sibling())

    for pair in range(share // span):

        def put(part, start, size, value):
            lanes = pl.ds(start // rows * share + pair * span, span)
            work[part, pl.ds(start % rows, size), lanes] = value
            if part == 0:
                train.tick()

        attend_back_pair(heads, got, pair, key_sum, value_sum, put)
        for part in range(3):
            send(part, pair).start()
            at = pl.multiple_of((part * 2 + place.core) * share + pair * span, span)
            lanes = pl.multiple_of(place.core * share + pair * span, span)
            gproj[:, pl.ds(at, span)] = work[part, :, pl.ds(lanes, span)]
    for pair in range(share // span):
        for part in range(3):
            send(part, pair).wait()

    for part in range(3):
        lanes = pl.ds(part * width, width)
        weight_grad_chunk(qkv_chunks[part], 2 * parts + 1 + part, normed, gproj[:, lanes])
        train.tick()

    for part in range(3):
        qkv_load(part).wait()

    def last(here):
        grad = dot_nt(gproj[here, pl.ds(0, width)], flat[0])
        grad += dot_nt(gproj[here, pl.ds(width, width)], flat[1])
        grad += dot_nt(gproj[here, pl.ds(2 * width, width)], flat[2])
        sg[0:1, :] += column_sum(gproj[here, pl.ds(0, width)])
        sg[1:2, :] += column_sum(gproj[here, pl.ds(2 * width, width)])
        value = widen(rs[here, :])
        pull, terms = norm_back(value, vec[3:4, :], grad)
        sg[3:4, :] += jnp.sum(terms, axis=0, keepdims=True)
        grad = acc[here, :] + pull
        lanes = lax.broadcasted_iota(jnp.int32, grad.shape, 1)
        edge = jnp.sum(jnp.where(lanes == width - 1, grad, 0.0), axis=-1, keepdims=True)
        work[3, here, :] = (grad - edge).astype(low)

    over_rows(rows, block, last)
    swap_in = Swap(place, work.at[3], input_o, (ig_s, ig_r))
    swap_in.start()
    small = SmallSum(place, small_refs)
    small_refs[0][0] = sg[...]
    small.begin()

    def put_small(value):
        total_small[...] = value

    train.add(small.acts(put_small))
    train.drain()
    swap_out.wait()
    swap_in.wait()


def rear(rs, cs, normed, heads, mixed, vec, qkv_w, out_w, fc_w, proj_w, shards, collective_id):
    length = shards // 4
    rows, width = rs.shape
    share = width // 2
    unit = width // shards
    parts = fc_w.shape[-1] // width
    deep = proj_w.shape[-2]
    proj_tiles = proj_w.reshape((parts, length, 2, 2, unit, width))
    low = jnp.bfloat16
    vmem = pl.BlockSpec(memory_space=pltpu.VMEM)
    dma = pltpu.SemaphoreType.DMA
    pairs = share // (2 * HD)
    f32 = jnp.float32
    return pl.pallas_call(
        functools.partial(rear_kernel, shards),
        out_shape=[
            jax.ShapeDtypeStruct((unit, 3 * width), f32),
            jax.ShapeDtypeStruct((unit, width), f32),
            jax.ShapeDtypeStruct((unit, parts * width), f32),
            jax.ShapeDtypeStruct((deep, width), f32),
            jax.ShapeDtypeStruct(vec.shape, f32),
            jax.ShapeDtypeStruct((rows, width), low),
            jax.ShapeDtypeStruct((rows, width), low),
        ],
        in_specs=[vmem] * 6 + [ANY] * 4,
        out_specs=[vmem] * 5 + [ANY] * 2,
        scratch_shapes=[
            pltpu.VMEM((length, 2, 2, unit, width), low),
            pltpu.VMEM((4, length, 2, 2, unit, width), low),
            pltpu.VMEM((4, rows, width), low),
            pltpu.VMEM((rows, width), f32),
            pltpu.VMEM((rows, width), f32),
            pltpu.VMEM((rows, width), f32),
            pltpu.VMEM((2, rows, share), low),
            pltpu.VMEM((rows, 3 * width), low),
            pltpu.VMEM((2 * rows, 2 * HD), f32),
            pltpu.VMEM((2 * rows, 2 * HD), f32),
            pltpu.VMEM((rows, width), low),
            pltpu.VMEM(vec.shape, f32),
        ]
        + Chunk.scratch(2 * parts + 4, length, unit, width)
        + [
            pltpu.VMEM((4,) + vec.shape, f32),
            pltpu.VMEM((3,) + vec.shape, f32),
            pltpu.VMEM((length,) + vec.shape, f32),
            dma((3,)), dma((3,)), dma((length,)), dma((length,)),
            dma((4,)), dma, dma, dma, dma, dma, dma, dma, dma((3, pairs)), dma((3, pairs)),
        ],
        compiler_params=pltpu.CompilerParams(
            collective_id=collective_id, has_side_effects=True, vmem_limit_bytes=62 << 20
        ),
        name="rear",
    )(rs, cs, normed, heads, mixed, vec, qkv_w, out_w, fc_w, proj_tiles)


def swap_halves(value):
    shards = lax.axis_size("fsdp")
    pairs = []
    for x in range(2):
        for index in range(shards):
            core = index % 2
            goal = (x, index) if core == x else (1 - x, index ^ 1)
            pairs.append((x * shards + index, goal[0] * shards + goal[1]))
    return lax.ppermute(value, ("seq", "fsdp"), pairs)


def pair_all_to_all(value, split_axis, concat_axis):
    shards = lax.axis_size("fsdp")
    groups = [[k, k + 1] for k in range(0, shards, 2)]
    return lax.all_to_all(
        value, "fsdp", split_axis=split_axis, concat_axis=concat_axis, axis_index_groups=groups, tiled=True
    )


def pack_rows(parts, width):
    rows = [jnp.pad(p, ((0, 0), (0, width - p.shape[1]))) for p in parts]
    packed = jnp.concatenate(rows, axis=0)
    return jnp.pad(packed, ((0, 16 - packed.shape[0]), (0, 0)))


def local_general(residual_in, cotangent, w_qkv, w_out, w_fc, w_proj, attn_bias, fc_bias, proj_bias, gains):
    shards = lax.axis_size("fsdp")
    tok_rows = residual_in.shape[1]
    model_width = w_qkv.shape[1] // 3
    hidden_width = w_fc.shape[1]
    unit = gains.shape[1]
    share = model_width // 2
    head_count = share // HD
    scale = HD ** (-0.5)
    small = pack_rows([attn_bias, gains, proj_bias[None], fc_bias[None]], 256)
    compact = swap_halves(residual_in[0]).astype(jnp.float32)
    upstream = swap_halves(cotangent[0]).astype(jnp.float32)
    qkv_w, small_all, out_w, fc_w, proj_w = gather_all(
        [w_qkv, small, w_out, w_fc, w_proj], shards, [0, 0, 2, 3, 5], 0
    )
    qkv_w = qkv_w.reshape(model_width, 3 * model_width)
    out_w = out_w.reshape(model_width, model_width)
    fc_w = fc_w.reshape(model_width, hidden_width)
    proj_w = proj_w.reshape(hidden_width, model_width)
    vectors = small_all[:, :6, :unit].transpose(1, 0, 2).reshape(6, model_width).astype(jnp.float32)
    bias_all, gain_all, proj_b = vectors[:3], vectors[3:5], vectors[5]
    fc_b = small_all[:, 6, : fc_bias.shape[0]].reshape(hidden_width).astype(jnp.float32)
    full = jnp.concatenate([compact, -jnp.sum(compact, axis=-1, keepdims=True)], axis=-1)
    normed = rms_norm(full, gain_all[0]).astype(jnp.bfloat16)
    bias_qkv = jnp.concatenate([bias_all[0], jnp.zeros_like(bias_all[0]), bias_all[1]])
    projected = (matmul(normed, qkv_w) + bias_qkv).astype(jnp.bfloat16)
    by_heads = pair_all_to_all(projected.reshape(tok_rows, 3, 2, share), 2, 0)
    length = by_heads.shape[0]
    queries = by_heads[:, 0, 0].reshape(length, head_count, HD)
    keys_all = by_heads[:, 1, 0].reshape(length, head_count, HD)
    values_all = by_heads[:, 2, 0].reshape(length, head_count, HD)
    attended, log_totals = attend(queries, keys_all, values_all, scale)
    mixed = pair_all_to_all(attended.reshape(length, 1, share), 0, 1)
    mixed = mixed.reshape(tok_rows, model_width)
    branch = matmul(mixed, out_w) + bias_all[2]
    middle = full + center(branch)
    normed_two = rms_norm(middle, gain_all[1]).astype(jnp.bfloat16)
    hidden = matmul(normed_two, fc_w) + fc_b
    activated = gelu_tanh(hidden).astype(jnp.bfloat16)
    branch_two = matmul(activated, proj_w) + proj_b
    final = middle + center(branch_two)
    residual_out = swap_halves(final[:, :-1].astype(jnp.bfloat16))[None]
    grad_final = jnp.concatenate([upstream, jnp.zeros((tok_rows, 1), jnp.float32)], axis=-1)
    grad_branch_two = center(grad_final).astype(jnp.bfloat16)
    grad_proj = weight_grad(activated, grad_branch_two)
    grad_proj_bias = jnp.sum(grad_branch_two.astype(jnp.float32), axis=0)
    grad_activated = input_grad_of(grad_branch_two, proj_w)
    gelu_pull = jax.vjp(gelu_tanh, hidden)[1]
    grad_hidden = gelu_pull(grad_activated)[0].astype(jnp.bfloat16)
    grad_fc = weight_grad(normed_two, grad_hidden)
    grad_fc_bias = jnp.sum(grad_hidden.astype(jnp.float32), axis=0)
    grad_normed_two = input_grad_of(grad_hidden, fc_w)
    second_pull = jax.vjp(rms_norm, middle, gain_all[1])[1]
    grad_middle_norm, grad_gain_two = second_pull(grad_normed_two)
    grad_middle = grad_final + grad_middle_norm
    grad_branch = center(grad_middle).astype(jnp.bfloat16)
    grad_out = weight_grad(mixed, grad_branch)
    grad_out_bias = jnp.sum(grad_branch.astype(jnp.float32), axis=0)
    grad_mixed = input_grad_of(grad_branch, out_w).astype(jnp.bfloat16)
    grad_heads = pair_all_to_all(grad_mixed.reshape(tok_rows, 2, share), 1, 0)
    grad_heads = grad_heads.reshape(length, head_count, HD)
    grad_queries, grad_keys, grad_values = attend_back(
        queries, keys_all, values_all, log_totals, grad_heads, scale
    )
    stacked = jnp.stack([grad_queries, grad_keys, grad_values], axis=1).reshape(length, 3, 1, share)
    grad_projected = pair_all_to_all(stacked, 0, 2)
    grad_projected = grad_projected.reshape(tok_rows, 3 * model_width)
    grad_qkv = weight_grad(normed, grad_projected)
    column_sums = jnp.sum(grad_projected.astype(jnp.float32), axis=0)
    grad_normed = input_grad_of(grad_projected, qkv_w)
    first_pull = jax.vjp(rms_norm, full, gain_all[0])[1]
    grad_full_norm, grad_gain_one = first_pull(grad_normed)
    grad_full = grad_middle + grad_full_norm
    input_grad = swap_halves((grad_full[:, :-1] - grad_full[:, -1:]).astype(jnp.bfloat16))[None]
    rows = jnp.stack(
        [
            column_sums[:model_width],
            column_sums[2 * model_width :],
            grad_out_bias,
            grad_gain_one,
            grad_gain_two,
            grad_proj_bias,
        ]
    )
    rows = rows.reshape(6, shards, unit).transpose(1, 0, 2)
    last = grad_fc_bias.reshape(shards, 1, fc_bias.shape[0])
    grad_small = jnp.concatenate(
        [
            jnp.pad(rows, ((0, 0), (0, 0), (0, 256 - unit))),
            jnp.pad(last, ((0, 0), (0, 9), (0, 256 - fc_bias.shape[0]))),
        ],
        axis=1,
    )

    def split(grad):
        return grad.astype(jnp.bfloat16).reshape(shards, grad.shape[0] // shards, grad.shape[1])

    total_proj, total_fc, total_out, total_qkv, total_small = scatter_all(
        [split(grad_proj), split(grad_fc), split(grad_out), split(grad_qkv), grad_small.astype(jnp.bfloat16)],
        shards,
        [0, 1, 2, 3, 3],
        1,
    )
    return (
        residual_out,
        input_grad,
        total_qkv,
        total_out,
        total_fc,
        total_proj,
        total_small[:3, :unit],
        total_small[6, : fc_bias.shape[0]],
        total_small[5, :unit],
        total_small[3:5, :unit],
    )


def local(residual_in, cotangent, w_qkv, w_out, w_fc, w_proj, attn_bias, fc_bias, proj_bias, gains):
    arguments = (residual_in, cotangent, w_qkv, w_out, w_fc, w_proj, attn_bias, fc_bias, proj_bias, gains)
    if w_qkv.shape[0] % 16:
        return local_general(*arguments)
    return local_tiled(*arguments)


def local_tiled(residual_in, cotangent, w_qkv, w_out, w_fc, w_proj, attn_bias, fc_bias, proj_bias, gains):
    shards = lax.axis_size("fsdp")
    model_width = w_qkv.shape[1] // 3
    unit = gains.shape[1]
    hidden_unit = fc_bias.shape[0]
    small = place_small([attn_bias, gains, proj_bias[None], fc_bias[None]], shards, model_width)
    padding = ((0, 0), (0, 1))
    (qkv_w, out_w, fc_w, proj_w, compact, upstream, normed, heads, mixed, vectors) = front(
        jnp.pad(residual_in[0], padding), jnp.pad(cotangent[0], padding),
        w_qkv, small, w_out, w_fc, w_proj, shards, 0,
    )
    total_qkv, total_out, total_fc, total_proj, total_small, residual_out, input_grad = rear(
        compact, upstream, normed, heads, mixed, vectors, qkv_w, out_w, fc_w, proj_w, shards, 1
    )
    index = lax.axis_index("fsdp")
    mine = lax.dynamic_slice_in_dim(total_small[:6], index * unit, unit, 1)
    hidden = total_small[6 : 6 + hidden_unit * shards // model_width].reshape(hidden_unit * shards)
    return (
        residual_out[None, :, :-1],
        input_grad[None, :, :-1],
        total_qkv,
        total_out,
        total_fc,
        total_proj,
        mine[:3],
        lax.dynamic_slice_in_dim(hidden, index * hidden_unit, hidden_unit, 0),
        mine[5],
        mine[3:5],
    )


def solution(mesh):
    in_specs = (
        P("fsdp", "seq", None),
        P("fsdp", "seq", None),
        P("fsdp", None),
        P("fsdp", None),
        P("fsdp", None),
        P("fsdp", None),
        P(None, "fsdp"),
        P("fsdp"),
        P("fsdp"),
        P(None, "fsdp"),
    )
    out_specs = (
        P("fsdp", "seq", None),
        P("fsdp", "seq", None),
        P("fsdp", None),
        P("fsdp", None),
        P("fsdp", None),
        P("fsdp", None),
        P(None, "fsdp"),
        P("fsdp"),
        P("fsdp"),
        P(None, "fsdp"),
    )
    return jax.shard_map(local, mesh=mesh, in_specs=in_specs, out_specs=out_specs, check_vma=False)
```

```python
import functools

import jax
import jax.numpy as jnp
from jax import lax
from jax.experimental import pallas as pl
from jax.experimental.pallas import tpu as pltpu
from jax.sharding import PartitionSpec as P

HD = 64
EPSILON = 1e-05
MASKED = -1e30
MESH = pl.DeviceIdType.MESH
ANY = pl.BlockSpec(memory_space=pl.ANY)


class Place:
    def __init__(self, shards):
        self.length = shards // 4
        self.x = lax.axis_index("seq")
        index = lax.axis_index("fsdp")
        self.index = index
        self.core = lax.rem(index, 2)
        self.y = lax.rem(index // 2, 2)
        self.line = index // 4

    def at(self, **moved):
        x = moved.get("x", self.x)
        line = moved.get("line", self.line)
        y = moved.get("y", self.y)
        core = moved.get("core", self.core)
        return (x, (line * 2 + y) * 2 + core)

    def beside_x(self):
        return self.at(x=1 - self.x)

    def beside_y(self):
        return self.at(y=1 - self.y)

    def sibling(self):
        return self.at(core=1 - self.core)

    def above(self):
        return self.at(line=self.line + 1)

    def below(self):
        return self.at(line=self.line - 1)

    def greet(self, diagonal=False, whole_line=False):
        barrier = pltpu.get_barrier_semaphore()

        def signal(device):
            pl.semaphore_signal(barrier, inc=1, device_id=device, device_id_type=MESH)

        signal(self.beside_x())
        signal(self.beside_y())
        signal(self.sibling())
        has_below = self.line > 0
        has_above = self.line < self.length - 1
        if whole_line:
            for line in range(self.length):
                pl.when(self.line != line)(lambda line=line: signal(self.at(line=line)))
            count = 3 + self.length - 1
        else:
            pl.when(has_below)(lambda: signal(self.below()))
            pl.when(has_above)(lambda: signal(self.above()))
            count = 3 + has_below.astype(jnp.int32) + has_above.astype(jnp.int32)
        if diagonal:
            across = self.x != self.core
            pl.when(across)(lambda: signal(self.at(x=1 - self.x, core=1 - self.core)))
            count = count + across.astype(jnp.int32)
        pl.semaphore_wait(barrier, count)


def remote(src, dst, send, recv, device):
    return pltpu.make_async_remote_copy(
        src_ref=src, dst_ref=dst, send_sem=send, recv_sem=recv, device_id=device, device_id_type=MESH
    )


class PlainGather:
    def __init__(self, place, shard, out, sems):
        self.p = place
        self.shard = shard
        self.out = out
        self.rows, self.cols = shard.shape
        (self.up, self.down, self.line_in, self.ys, self.yr, self.xs, self.xr, self.ds, self.dr, self.own) = sems

    @staticmethod
    def sem_shapes(length):
        dma = pltpu.SemaphoreType.DMA
        return [dma((length,))] * 7 + [dma((3, length))] * 2 + [dma]

    def half(self, ref, which):
        width = self.cols // 2
        return ref.at[:, pl.ds(pl.multiple_of(which * width, width), width)]

    def slot(self, line, y, core):
        return self.out.at[line, y, core]

    def up_copy(self, line, src=None):
        p = self.p
        dst = self.slot(line, p.y, p.core)
        return remote(dst if src is None else src, dst, self.up.at[line], self.line_in.at[line], p.above())

    def down_copy(self, line, src=None):
        p = self.p
        dst = self.slot(line, p.y, p.core)
        return remote(dst if src is None else src, dst, self.down.at[line], self.line_in.at[line], p.below())

    def y_copy(self, line, src=None):
        p = self.p
        dst = self.half(self.slot(line, p.y, p.core), p.x)
        src = dst if src is None else self.half(src, p.x)
        return remote(src, dst, self.ys.at[line], self.yr.at[line], p.beside_y())

    def y_landing(self, line):
        p = self.p
        dst = self.half(self.slot(line, 1 - p.y, p.core), p.x)
        return remote(dst, dst, self.ys.at[line], self.yr.at[line], p.beside_y())

    def x_copy(self, line):
        p = self.p
        dst = self.half(self.slot(line, 1 - p.y, p.core), p.x)
        return remote(dst, dst, self.xs.at[line], self.xr.at[line], p.beside_x())

    def x_landing(self, line):
        p = self.p
        dst = self.half(self.slot(line, 1 - p.y, p.core), 1 - p.x)
        return remote(dst, dst, self.xs.at[line], self.xr.at[line], p.beside_x())

    def d_copy(self, kind, line, src=None, core=None):
        p = self.p
        core = p.core if core is None else core
        if kind == 0:
            dst = self.slot(line, p.y, core)
        else:
            dst = self.half(self.slot(line, 1 - p.y, core), p.x if kind == 1 else 1 - p.x)
        return remote(dst if src is None else src, dst, self.ds.at[kind, line], self.dr.at[kind, line], p.sibling())

    def own_copy(self):
        p = self.p
        return pltpu.make_async_copy(self.shard, self.slot(p.line, p.y, p.core), self.own)

    def each_at(self, distance, act):
        p = self.p
        if distance == 0:
            act(p.line, 0)
            return
        pl.when(p.line - distance >= 0)(lambda: act(p.line - distance, 1))
        pl.when(p.line + distance < p.length)(lambda: act(p.line + distance, -1))

    def arrive(self, distance):
        p = self.p

        def act(line, way):
            src = None
            if way == 0:
                src = self.shard
                self.own_copy().start()
            else:
                self.up_copy(line).wait_recv()
            if way >= 0:
                pl.when(p.line < p.length - 1)(lambda: self.up_copy(line, src).start())
            if way <= 0:
                pl.when(p.line > 0)(lambda: self.down_copy(line, src).start())
            self.y_copy(line, src).start()
            self.d_copy(0, line, src).start()

        self.each_at(distance, act)

    def arrive_y(self, distance):
        def act(line, way):
            self.y_landing(line).wait_recv()
            self.x_copy(line).start()
            self.d_copy(1, line).start()

        self.each_at(distance, act)

    def arrive_x(self, distance):
        def act(line, way):
            self.x_landing(line).wait_recv()
            self.d_copy(2, line).start()

        self.each_at(distance, act)

    def stage(self, time):
        length = self.p.length
        if 0 <= time < length:
            self.arrive(time)
        if 0 <= time - 1 < length:
            self.arrive_y(time - 1)
        if 0 <= time - 2 < length:
            self.arrive_x(time - 2)

    def stages(self):
        return self.p.length + 2

    def finish(self):
        p = self.p

        def one(line):
            for kind in range(3):
                self.d_copy(kind, line, core=1 - p.core).wait_recv()
            for kind in range(3):
                self.d_copy(kind, line).wait_send()
            self.y_copy(line).wait_send()
            self.x_copy(line).wait_send()
            pl.when((p.line >= line) & (p.line < p.length - 1))(lambda: self.up_copy(line).wait_send())
            pl.when((p.line <= line) & (p.line > 0))(lambda: self.down_copy(line).wait_send())

        for line in range(p.length):
            one(line)
        self.own_copy().wait()


def gather_kernel(shards, lag, count, *refs):
    ins, outs, rest = refs[:count], refs[count : 2 * count], refs[2 * count :]
    place = Place(shards)
    place.greet()
    per = len(PlainGather.sem_shapes(1))
    gathers = [PlainGather(place, ins[k], outs[k], rest[k * per : (k + 1) * per]) for k in range(count)]
    total = max(lag[k] + g.stages() for k, g in enumerate(gathers))
    for time in range(total):
        for k, g in enumerate(gathers):
            g.stage(time - lag[k])
    for g in gathers:
        g.finish()


def gather_all(arrays, shards, lag, collective_id):
    length = shards // 4
    out = pl.pallas_call(
        functools.partial(gather_kernel, shards, lag, len(arrays)),
        out_shape=[jax.ShapeDtypeStruct((length, 2, 2) + a.shape, a.dtype) for a in arrays],
        in_specs=[ANY] * len(arrays),
        out_specs=[ANY] * len(arrays),
        scratch_shapes=PlainGather.sem_shapes(length) * len(arrays),
        compiler_params=pltpu.CompilerParams(collective_id=collective_id, has_side_effects=True),
        name="gather_weights",
    )(*arrays)
    return [o.reshape((shards,) + a.shape) for o, a in zip(out, arrays)]


class Scatter:
    def __init__(self, place, partial, out, refs):
        self.p = place
        self.g = partial
        self.out = out
        self.rows, self.cols = out.shape
        (self.s, self.d, self.xb, self.yb, self.lo, self.hi, self.fb, self.tb,
         self.load, self.ds, self.dr, self.xs, self.xr, self.ys, self.yr,
         self.us, self.ur, self.ns, self.nr, self.fs, self.fr) = refs

    @staticmethod
    def scratch(length, rows, cols, dtype):
        dma = pltpu.SemaphoreType.DMA
        full = pltpu.VMEM((length, 2, rows, cols), dtype)
        half = pltpu.VMEM((length, rows, cols // 2), dtype)
        line = pltpu.VMEM((length, rows, cols), dtype)
        one = pltpu.VMEM((rows, cols), dtype)
        return [full, full, half, half, line, line, one, one] + [dma] * 7 + [dma((length,))] * 4 + [dma] * 2

    def half(self, which):
        width = self.cols // 2
        return pl.ds(pl.multiple_of(which * width, width), width)

    def load_copy(self):
        return pltpu.make_async_copy(self.g.at[:, :, self.p.core], self.s, self.load)

    def d_copy(self):
        p = self.p
        return remote(self.g.at[:, :, 1 - p.core], self.d, self.ds, self.dr, p.sibling())

    def x_copy(self):
        p = self.p
        src = self.s.at[:, 1 - p.y, :, self.half(1 - p.x)]
        return remote(src, self.xb, self.xs, self.xr, p.beside_x())

    def y_copy(self):
        p = self.p
        src = self.s.at[:, 1 - p.y, :, self.half(p.x)]
        return remote(src, self.yb, self.ys, self.yr, p.beside_y())

    def up_copy(self, line):
        p = self.p
        return remote(self.s.at[line, p.y], self.lo.at[line], self.us.at[line], self.ur.at[line], p.above())

    def down_copy(self, line):
        p = self.p
        return remote(self.s.at[line, p.y], self.hi.at[line], self.ns.at[line], self.nr.at[line], p.below())

    def f_copy(self):
        return remote(self.tb, self.fb, self.fs, self.fr, self.p.beside_x())

    def each(self, act):
        def body(line, carry):
            act(line)
            return carry

        lax.fori_loop(0, self.p.length, body, 0)

    def start(self):
        self.load_copy().start()
        self.d_copy().start()

    def pair(self):
        p = self.p
        self.load_copy().wait()
        self.d_copy().wait()

        def other(line):
            self.s[line, 1 - p.y] = self.s[line, 1 - p.y] + self.d[line, 1 - p.y]

        self.each(other)
        self.x_copy().start()

        def own(line):
            self.s[line, p.y] = self.s[line, p.y] + self.d[line, p.y]

        self.each(own)

    def over_x(self):
        p = self.p
        self.x_copy().wait()

        def act(line):
            cols = self.half(p.x)
            self.s[line, 1 - p.y, :, cols] = self.s[line, 1 - p.y, :, cols] + self.xb[line]

        self.each(act)
        self.y_copy().start()

    def over_y(self):
        p = self.p
        self.y_copy().wait()

        def act(line):
            cols = self.half(p.x)
            self.s[line, p.y, :, cols] = self.s[line, p.y, :, cols] + self.yb[line]

        self.each(act)

    def hop(self, step):
        p = self.p
        last = p.length - 1
        up = last - step + p.line

        def upward():
            @pl.when(p.line > 0)
            def _():
                self.up_copy(up).wait_recv()
                self.s[up, p.y] = self.s[up, p.y] + self.lo[up]

            self.up_copy(up).start()

        pl.when(p.line <= step)(upward)
        down = step - last + p.line

        def downward():
            @pl.when(p.line < last)
            def _():
                self.down_copy(down).wait_recv()
                self.s[down, p.y] = self.s[down, p.y] + self.hi[down]

            self.down_copy(down).start()

        pl.when(down >= 0)(downward)

    def total(self):
        p = self.p
        mine = p.line

        @pl.when(p.line > 0)
        def _():
            self.up_copy(mine).wait_recv()
            self.s[mine, p.y] = self.s[mine, p.y] + self.lo[mine]

        @pl.when(p.line < p.length - 1)
        def _():
            self.down_copy(mine).wait_recv()
            self.s[mine, p.y] = self.s[mine, p.y] + self.hi[mine]

        self.tb[...] = self.s[mine, p.y]
        self.f_copy().start()

    def finish(self):
        p = self.p
        self.f_copy().wait()
        self.out[...] = self.tb[...].astype(jnp.float32) + self.fb[...].astype(jnp.float32)
        for line in range(p.length):
            pl.when(line > p.line)(lambda line=line: self.up_copy(line).wait_send())
            pl.when(line < p.line)(lambda line=line: self.down_copy(line).wait_send())

    def stages(self):
        acts = [self.start, self.pair, self.over_x, self.over_y]
        acts += [functools.partial(self.hop, step) for step in range(self.p.length - 1)]
        return acts + [self.total, self.finish]


def scatter_kernel(shards, lag, count, *refs):
    ins, outs, rest = refs[:count], refs[count : 2 * count], refs[2 * count :]
    place = Place(shards)
    place.greet()
    per = len(rest) // count
    lists = [
        Scatter(place, ins[k], outs[k], rest[k * per : (k + 1) * per]).stages() for k in range(count)
    ]
    total = max(lag[k] + len(s) for k, s in enumerate(lists))
    for time in range(total):
        for k, acts in enumerate(lists):
            if 0 <= time - lag[k] < len(acts):
                acts[time - lag[k]]()


def scatter_all(arrays, shards, lag, collective_id):
    length = shards // 4
    parts = [a.reshape((length, 2, 2) + a.shape[1:]) for a in arrays]
    scratch = []
    for a in arrays:
        scratch += Scatter.scratch(length, a.shape[1], a.shape[2], a.dtype)
    return pl.pallas_call(
        functools.partial(scatter_kernel, shards, lag, len(arrays)),
        out_shape=[jax.ShapeDtypeStruct(a.shape[1:], jnp.float32) for a in arrays],
        in_specs=[ANY] * len(arrays),
        out_specs=[pl.BlockSpec(memory_space=pltpu.VMEM)] * len(arrays),
        scratch_shapes=scratch,
        compiler_params=pltpu.CompilerParams(
            collective_id=collective_id, has_side_effects=True, vmem_limit_bytes=60 << 20
        ),
        name="scatter_grads",
    )(*parts)


def rms_norm(values, gain):
    return values * lax.rsqrt(jnp.mean(values * values, axis=-1, keepdims=True) + EPSILON) * gain


def center(values):
    return values - jnp.mean(values, axis=-1, keepdims=True)


def gelu_tanh(values):
    return jax.nn.gelu(values, approximate=True)


def matmul(left, right):
    return jnp.dot(left, right, preferred_element_type=jnp.float32)


def weight_grad(inputs, grads):
    return lax.dot_general(
        inputs, grads, (((0,), (0,)), ((), ())), preferred_element_type=jnp.float32
    )


def input_grad_of(grads, weight):
    return lax.dot_general(
        grads, weight, (((1,), (1,)), ((), ())), preferred_element_type=jnp.float32
    )


def block_rows(length):
    return min(length, max(512, length // 8))


def score_block(query_block, keys_part, start, scale):
    scores = (
        jnp.einsum("qhd,khd->hqk", query_block, keys_part, preferred_element_type=jnp.float32)
        * scale
    )
    query_pos = start + jnp.arange(query_block.shape[0], dtype=jnp.int32)
    key_pos = jnp.arange(keys_part.shape[0], dtype=jnp.int32)
    allowed = query_pos[:, None] >= key_pos[None, :]
    return jnp.where(allowed[None], scores, MASKED)


def attend(queries, keys_all, values_all, scale):
    length, head_count, width = queries.shape
    block = block_rows(length)
    count = length // block
    results = []
    log_totals = []
    for index in range(count):
        start = index * block
        finish = start + block
        scores = score_block(queries[start:finish], keys_all[:finish], start, scale)
        peak = jnp.max(scores, axis=-1, keepdims=True)
        weights = jnp.exp(scores - peak)
        total = jnp.sum(weights, axis=-1, keepdims=True)
        weights = weights / total
        result = jnp.einsum(
            "hqk,khd->qhd",
            weights.astype(jnp.bfloat16),
            values_all[:finish],
            preferred_element_type=jnp.float32,
        )
        results.append(result.astype(jnp.bfloat16))
        log_totals.append((peak + jnp.log(total))[..., 0])
    joined = jnp.concatenate(results, axis=0)
    return (joined.reshape(length, head_count * width), log_totals)


def attend_back(queries, keys_all, values_all, log_totals, grad_heads, scale):
    length, head_count, width = queries.shape
    block = block_rows(length)
    count = length // block
    key_sum = jnp.zeros((length, head_count, width), jnp.float32)
    value_sum = jnp.zeros((length, head_count, width), jnp.float32)
    query_grads = []
    for index in range(count):
        start = index * block
        finish = start + block
        query_block = queries[start:finish]
        grad_block = grad_heads[start:finish]
        keys_part = keys_all[:finish]
        scores = score_block(query_block, keys_part, start, scale)
        weights = jnp.exp(scores - log_totals[index][..., None])
        grad_weights = jnp.einsum(
            "qhd,khd->hqk", grad_block, values_all[:finish], preferred_element_type=jnp.float32
        )
        inner = jnp.sum(weights * grad_weights, axis=-1, keepdims=True)
        grad_scores = (weights * (grad_weights - inner)).astype(jnp.bfloat16)
        query_grad = (
            jnp.einsum("hqk,khd->qhd", grad_scores, keys_part, preferred_element_type=jnp.float32)
            * scale
        )
        key_part = (
            jnp.einsum("hqk,qhd->khd", grad_scores, query_block, preferred_element_type=jnp.float32)
            * scale
        )
        value_part = jnp.einsum(
            "hqk,qhd->khd",
            weights.astype(jnp.bfloat16),
            grad_block,
            preferred_element_type=jnp.float32,
        )
        key_sum = key_sum.at[:finish].add(key_part)
        value_sum = value_sum.at[:finish].add(value_part)
        query_grads.append(query_grad.astype(jnp.bfloat16))
    return (
        jnp.concatenate(query_grads, axis=0),
        key_sum.astype(jnp.bfloat16),
        value_sum.astype(jnp.bfloat16),
    )


def dot_nn(left, right):
    return jnp.dot(left, right, preferred_element_type=jnp.float32)


def dot_nt(left, right):
    return lax.dot_general(
        left, right, (((1,), (1,)), ((), ())), preferred_element_type=jnp.float32
    )


def dot_tn(left, right):
    return lax.dot_general(
        left, right, (((0,), (0,)), ((), ())), preferred_element_type=jnp.float32
    )


def lane_block(index, width):
    return pl.ds(pl.multiple_of(index * width, width), width)


def unit_scale(value):
    return lax.rsqrt(jnp.mean(value * value, axis=-1, keepdims=True) + EPSILON)


def over_rows(total, block, act):
    def body(step, carry):
        act(pl.ds(pl.multiple_of(step * block, block), block))
        return carry

    lax.fori_loop(0, total // block, body, 0)


def head_mask(shape, head):
    lanes = lax.broadcasted_iota(jnp.int32, shape, 1)
    return (lanes // HD) == head


class Swap:
    def __init__(self, place, src, dst, sems):
        self.p = place
        self.src, self.dst = src, dst
        self.send, self.recv = sems

    def moved(self):
        p = self.p
        return remote(self.src, self.dst, self.send, self.recv, p.at(x=1 - p.x, core=1 - p.core))

    def kept(self):
        return pltpu.make_async_copy(self.src, self.dst, self.send)

    def start(self):
        p = self.p
        pl.when(p.x != p.core)(lambda: self.moved().start())
        pl.when(p.x == p.core)(lambda: self.kept().start())

    def wait(self):
        p = self.p
        pl.when(p.x != p.core)(lambda: self.moved().wait())
        pl.when(p.x == p.core)(lambda: self.kept().wait())


def attend_pair(qkv, pair, put):
    total = qkv.shape[1]
    block = min(256, total)
    lanes = pl.ds(pair * 2 * HD, 2 * HD)
    scale = jnp.asarray(HD ** (-0.5), jnp.bfloat16)
    zero = jnp.zeros((), jnp.bfloat16)
    rows = lax.broadcasted_iota(jnp.int32, (block, block), 0)
    cols = lax.broadcasted_iota(jnp.int32, (block, block), 1)
    allowed = rows >= cols
    for index in range(total // block):
        start = index * block
        here = pl.ds(start, block)
        query = qkv[0, here, lanes] * scale
        results = []
        for head in range(2):
            masked = jnp.where(head_mask(query.shape, head), query, zero)
            near = dot_nt(masked, qkv[1, here, lanes])
            near = jnp.where(allowed, near, MASKED)
            peak = jnp.max(near, axis=-1, keepdims=True)
            if start:
                far = dot_nt(masked, qkv[1, pl.ds(0, start), lanes])
                peak = jnp.maximum(peak, jnp.max(far, axis=-1, keepdims=True))
            near = jnp.exp(near - peak)
            total_weight = jnp.sum(near, axis=-1, keepdims=True)
            if start:
                far = jnp.exp(far - peak)
                total_weight = total_weight + jnp.sum(far, axis=-1, keepdims=True)
            share = 1.0 / total_weight
            result = dot_nn((near * share).astype(jnp.bfloat16), qkv[2, here, lanes])
            if start:
                result += dot_nn(
                    (far * share).astype(jnp.bfloat16), qkv[2, pl.ds(0, start), lanes]
                )
            results.append(result)
        merged = jnp.where(head_mask(results[0].shape, 0), results[0], results[1])
        put(start, block, merged.astype(jnp.bfloat16))


def attend_back_pair(qkv, grads, pair, key_sum, value_sum, put):
    total = qkv.shape[1]
    block = min(256, total)
    lanes = pl.ds(pair * 2 * HD, 2 * HD)
    scale = jnp.asarray(HD ** (-0.5), jnp.bfloat16)
    zero = jnp.zeros((), jnp.bfloat16)
    rows = lax.broadcasted_iota(jnp.int32, (block, block), 0)
    cols = lax.broadcasted_iota(jnp.int32, (block, block), 1)
    allowed = rows <= cols
    key_sum[...] = jnp.zeros_like(key_sum)
    value_sum[...] = jnp.zeros_like(value_sum)
    for index in range(total // block):
        start = index * block
        here = pl.ds(start, block)
        spans = [here] + ([pl.ds(0, start)] if start else [])
        query = qkv[0, here, lanes] * scale
        grad = grads[start // grads.shape[1], pl.ds(start % grads.shape[1], block), lanes]
        query_grads = []
        for head in range(2):
            mask = head_mask(query.shape, head)
            masked = jnp.where(mask, query, zero)
            grad_masked = jnp.where(mask, grad, zero)
            scores = [dot_nt(qkv[1, span, lanes], masked) for span in spans]
            scores[0] = jnp.where(allowed, scores[0], MASKED)
            peak = functools.reduce(
                jnp.maximum, [jnp.max(s, axis=0, keepdims=True) for s in scores]
            )
            weights = [jnp.exp(s - peak) for s in scores]
            sums = sum(jnp.sum(w, axis=0, keepdims=True) for w in weights)
            share = 1.0 / sums
            weights = [w * share for w in weights]
            pulled = [dot_nt(qkv[2, span, lanes], grad_masked) for span in spans]
            inner = sum(jnp.sum(w * g, axis=0, keepdims=True) for w, g in zip(weights, pulled))
            query_grad = None
            for span, w, g in zip(spans, weights, pulled):
                value_sum[span, :] += dot_nn(w.astype(jnp.bfloat16), grad_masked)
                slope = (w * (g - inner)).astype(jnp.bfloat16)
                key_sum[span, :] += dot_nn(slope, masked)
                part = dot_tn(slope, qkv[1, span, lanes])
                query_grad = part if query_grad is None else query_grad + part
            query_grads.append(query_grad)
        merged = jnp.where(head_mask(query_grads[0].shape, 0), query_grads[0], query_grads[1])
        put(0, start, block, (merged * HD ** (-0.5)).astype(jnp.bfloat16))
    half = grads.shape[1]
    for start in range(0, total, half):
        put(1, start, half, key_sum[pl.ds(start, half), :].astype(jnp.bfloat16))
        put(2, start, half, value_sum[pl.ds(start, half), :].astype(jnp.bfloat16))


class Gather:
    def __init__(self, place, shard, out, sems, split=False):
        self.p = place
        self.shard = shard
        self.out = out
        self.split = split
        self.width = shard.shape[1] // 3
        (self.up, self.down, self.line_in, self.ys, self.yr, self.xs, self.xr, self.ds, self.dr, self.own) = sems
        self.time = 0

    @staticmethod
    def sem_shapes(length):
        dma = pltpu.SemaphoreType.DMA
        return [dma((length,))] * 5 + [dma((2, length))] * 2 + [dma((4, length))] * 2 + [dma]

    def thirds(self, ref, which, count=1):
        return ref.at[:, pl.ds(pl.multiple_of(which * self.width, self.width), count * self.width)]

    def slot(self, line, y, core=None):
        return self.out.at[line, y, self.p.core if core is None else core]

    def on_line(self, ref):
        return self.thirds(ref, self.p.x, 2) if self.split else ref

    def up_copy(self, line, src=None):
        p = self.p
        dst = self.slot(line, p.y)
        src = self.on_line(dst if src is None else src)
        return remote(src, self.on_line(dst), self.up.at[line], self.line_in.at[line], p.above())

    def down_copy(self, line, src=None):
        p = self.p
        dst = self.slot(line, p.y)
        src = self.on_line(dst if src is None else src)
        return remote(src, self.on_line(dst), self.down.at[line], self.line_in.at[line], p.below())

    def y_copy(self, line, src=None):
        p = self.p
        dst = self.slot(line, p.y)
        src = self.thirds(dst if src is None else src, p.x, 2)
        return remote(src, self.thirds(dst, p.x, 2), self.ys.at[line], self.yr.at[line], p.beside_y())

    def y_landing(self, line):
        p = self.p
        dst = self.thirds(self.slot(line, 1 - p.y), p.x, 2)
        return remote(dst, dst, self.ys.at[line], self.yr.at[line], p.beside_y())

    def x_copy(self, line, own):
        p = self.p
        dst = self.thirds(self.slot(line, p.y if own else 1 - p.y), 2 * p.x)
        return remote(dst, dst, self.xs.at[int(own), line], self.xr.at[int(own), line], p.beside_x())

    def x_landing(self, line, own):
        p = self.p
        dst = self.thirds(self.slot(line, p.y if own else 1 - p.y), 2 * (1 - p.x))
        return remote(dst, dst, self.xs.at[int(own), line], self.xr.at[int(own), line], p.beside_x())

    def d_copy(self, kind, line, whole=False, src=None, core=None):
        p = self.p
        dst = self.slot(line, p.y if kind in (0, 3) else 1 - p.y, core)
        src = dst if src is None else src
        if kind == 0 and not whole:
            src, dst = self.on_line(src), self.on_line(dst)
        if kind == 1:
            src, dst = self.thirds(src, p.x, 2), self.thirds(dst, p.x, 2)
        if kind >= 2:
            src, dst = self.thirds(src, 2 * (1 - p.x)), self.thirds(dst, 2 * (1 - p.x))
        return remote(src, dst, self.ds.at[kind, line], self.dr.at[kind, line], p.sibling())

    def own_copy(self):
        p = self.p
        return pltpu.make_async_copy(self.shard, self.slot(p.line, p.y), self.own)

    def each_at(self, distance, act):
        p = self.p
        if distance == 0:
            act(p.line, 0)
            return
        pl.when(p.line - distance >= 0)(lambda: act(p.line - distance, 1))
        pl.when(p.line + distance < p.length)(lambda: act(p.line + distance, -1))

    def arrive(self, distance):
        p = self.p

        def act(line, way):
            src = None
            if way == 0:
                src = self.shard
                self.own_copy().start()
            else:
                self.up_copy(line).wait_recv()
            if way >= 0:
                pl.when(p.line < p.length - 1)(lambda: self.up_copy(line, src).start())
            if way <= 0:
                pl.when(p.line > 0)(lambda: self.down_copy(line, src).start())
            self.y_copy(line, src).start()
            if way and self.split:
                self.x_copy(line, True).start()
            self.d_copy(0, line, way == 0, src).start()

        self.each_at(distance, act)

    def arrive_y(self, distance):
        def act(line, way):
            self.y_landing(line).wait_recv()
            self.x_copy(line, False).start()
            self.d_copy(1, line).start()
            if way and self.split:
                self.x_landing(line, True).wait_recv()
                self.d_copy(3, line).start()

        self.each_at(distance, act)

    def arrive_x(self, distance):
        def act(line, way):
            self.x_landing(line, False).wait_recv()
            self.d_copy(2, line).start()

        self.each_at(distance, act)

    def stage(self):
        time, length = self.time, self.p.length
        self.time += 1
        if time < length:
            self.arrive(time)
        if 0 <= time - 1 < length:
            self.arrive_y(time - 1)
        if 0 <= time - 2 < length:
            self.arrive_x(time - 2)

    def under_way(self):
        return self.time < self.p.length + 2

    def take(self):
        p = self.p
        self.own_copy().wait()
        for line in range(p.length):
            for kind in range(3):
                if kind or not self.split:
                    self.d_copy(kind, line, core=1 - p.core).wait_recv()
            if self.split:
                pl.when(p.line == line)(lambda line=line: self.d_copy(0, line, True, core=1 - p.core).wait_recv())

                @pl.when(p.line != line)
                def _(line=line):
                    self.d_copy(0, line, core=1 - p.core).wait_recv()
                    self.d_copy(3, line, core=1 - p.core).wait_recv()

    def close(self):
        p = self.p
        for line in range(p.length):
            for kind in range(3):
                if kind or not self.split:
                    self.d_copy(kind, line).wait_send()
            if self.split:
                pl.when(p.line == line)(lambda line=line: self.d_copy(0, line, True).wait_send())

                @pl.when(p.line != line)
                def _(line=line):
                    self.d_copy(0, line).wait_send()
                    self.d_copy(3, line).wait_send()
                    self.x_copy(line, True).wait_send()

            self.y_copy(line).wait_send()
            self.x_copy(line, False).wait_send()
            pl.when((p.line >= line) & (p.line < p.length - 1))(lambda line=line: self.up_copy(line).wait_send())
            pl.when((p.line <= line) & (p.line > 0))(lambda line=line: self.down_copy(line).wait_send())


class Supply:
    def __init__(self, gathers, starts):
        self.entries = list(zip(starts, gathers))
        self.time = 0

    def tick(self):
        for start, gather in self.entries:
            if start <= self.time and gather.under_way():
                gather.stage()
        self.time += 1

    def need(self, gather):
        while gather.under_way():
            self.tick()
        gather.take()


class Chunk:
    def __init__(self, place, index, refs, store):
        self.p = place
        self.store = store
        (grads, self_d, xy, lo, hi, tb, fb, ds, dr, xs, xr, ys, yr, us, ur, ns, nr, fs, fr) = refs
        self.mine, self.other = grads.at[index, 0], grads.at[index, 1]
        self.d, self.xy = self_d.at[index], xy.at[index]
        third = xy.shape[-1] // 3
        self.xb, self.yb = self.xy.at[:, :, pl.ds(0, third)], self.xy.at[:, :, pl.ds(third, 2 * third)]
        self.lo, self.hi = lo.at[index], hi.at[index]
        self.tb, self.fb = tb.at[index], fb.at[index]
        self.sems = [s.at[index] for s in (ds, dr, xs, xr, ys, yr)]
        self.us, self.ur, self.ns, self.nr = us.at[index], ur.at[index], ns.at[index], nr.at[index]
        self.fs, self.fr = fs.at[index], fr.at[index]

    @staticmethod
    def scratch(count, length, rows, cols):
        low = jnp.bfloat16
        dma = pltpu.SemaphoreType.DMA
        return [
            pltpu.VMEM((count, 2, length, 2, rows, cols), low),
            pltpu.VMEM((count, length, 2, rows, cols), low),
            pltpu.VMEM((count, length, rows, cols), low),
            pltpu.VMEM((count, length - 1, rows, cols), low),
            pltpu.VMEM((count, length - 1, rows, cols), low),
            pltpu.VMEM((count, rows, cols), low),
            pltpu.VMEM((count, rows, cols), low),
        ] + [dma((count,))] * 6 + [dma((count, length))] * 4 + [dma((count,))] * 2

    def third(self, which, count=1):
        width = self.tb.shape[1] // 3
        return pl.ds(pl.multiple_of(which * width, width), count * width)

    def d_copy(self):
        return remote(self.other, self.d, self.sems[0], self.sems[1], self.p.sibling())

    def x_copy(self):
        p = self.p
        src = self.mine.at[:, 1 - p.y, :, self.third(2 * (1 - p.x))]
        return remote(src, self.xb, self.sems[2], self.sems[3], p.beside_x())

    def y_copy(self):
        p = self.p
        src = self.mine.at[:, 1 - p.y, :, self.third(p.x, 2)]
        return remote(src, self.yb, self.sems[4], self.sems[5], p.beside_y())

    def up_copy(self, line):
        p = self.p
        return remote(self.mine.at[line, p.y], self.lo.at[line - 1], self.us.at[line], self.ur.at[line], p.above())

    def down_copy(self, line):
        p = self.p
        return remote(self.mine.at[line, p.y], self.hi.at[line], self.ns.at[line], self.nr.at[line], p.below())

    def f_copy(self):
        return remote(self.tb, self.fb, self.fs, self.fr, self.p.beside_x())

    def each(self, act):
        def body(line, carry):
            act(line)
            return carry

        lax.fori_loop(0, self.p.length, body, 0)

    def start(self):
        self.d_copy().start()

    def pair(self):
        p = self.p
        self.d_copy().wait()

        def other(line):
            self.mine[line, 1 - p.y] = self.mine[line, 1 - p.y] + self.d[line, 1 - p.y]

        self.each(other)
        self.x_copy().start()

        def own(line):
            self.mine[line, p.y] = self.mine[line, p.y] + self.d[line, p.y]

        self.each(own)

    def over_x(self):
        p = self.p
        self.x_copy().wait()

        def act(line):
            cols = self.third(2 * p.x)
            self.mine[line, 1 - p.y, :, cols] = self.mine[line, 1 - p.y, :, cols] + self.xb[line]

        self.each(act)
        self.y_copy().start()

    def over_y(self):
        p = self.p
        self.y_copy().wait()

        def act(line):
            cols = self.third(p.x, 2)
            self.mine[line, p.y, :, cols] = self.mine[line, p.y, :, cols] + self.yb[line]

        self.each(act)
        self.hop(0)

    def take_low(self, line):
        self.up_copy(line).wait_recv()
        self.mine[line, self.p.y] = self.mine[line, self.p.y] + self.lo[line - 1]

    def take_high(self, line):
        self.down_copy(line).wait_recv()
        self.mine[line, self.p.y] = self.mine[line, self.p.y] + self.hi[line]

    def hop(self, step):
        p = self.p
        last = p.length - 1
        up = last - step + p.line

        def upward():
            pl.when(p.line > 0)(lambda: self.take_low(up))
            self.up_copy(up).start()

        pl.when(p.line <= step)(upward)
        down = step - last + p.line

        def downward():
            pl.when(p.line < last)(lambda: self.take_high(down))
            self.down_copy(down).start()

        pl.when(down >= 0)(downward)

    def total(self):
        p = self.p
        mine = p.line
        pl.when(mine > 0)(lambda: self.take_low(mine))
        pl.when(mine < p.length - 1)(lambda: self.take_high(mine))
        self.tb[...] = self.mine[mine, p.y]
        self.f_copy().start()

    def finish(self):
        p = self.p
        self.f_copy().wait()
        self.store(self.tb[...].astype(jnp.float32) + self.fb[...].astype(jnp.float32))
        for line in range(p.length - 1):
            pl.when(line + 1 > p.line)(lambda line=line: self.up_copy(line + 1).wait_send())
            pl.when(line < p.line)(lambda line=line: self.down_copy(line).wait_send())

    def acts(self):
        hops = [functools.partial(self.hop, step) for step in range(1, self.p.length - 1)]
        return [self.pair, self.over_x, self.over_y] + hops + [self.total, self.finish]


class Train:
    def __init__(self):
        self.running = []

    def add(self, acts):
        self.running.append(list(acts))

    def tick(self):
        for acts in self.running:
            acts.pop(0)()
        self.running = [acts for acts in self.running if acts]

    def drain(self):
        while self.running:
            self.tick()


class SmallSum:
    def __init__(self, place, refs):
        self.p = place
        self.stages, self.got, self.lines, self.ss, self.sr, self.ls, self.lr = refs

    def copy(self, step):
        p = self.p
        goal = [p.sibling, p.beside_x, p.beside_y][step]()
        return remote(self.stages.at[step], self.got.at[step], self.ss.at[step], self.sr.at[step], goal)

    def line_copy(self, line):
        p = self.p
        return remote(
            self.stages.at[3], self.lines.at[p.line], self.ls.at[line], self.lr.at[p.line], p.at(line=line)
        )

    def line_landing(self, line):
        p = self.p
        return remote(self.stages.at[3], self.lines.at[line], self.ls.at[line], self.lr.at[line], p.at(line=line))

    def begin(self):
        self.copy(0).start()

    def step(self, index):
        p = self.p
        self.copy(index).wait()
        self.stages[index + 1] = self.stages[index] + self.got[index]
        if index < 2:
            self.copy(index + 1).start()
            return
        for line in range(p.length):
            pl.when(p.line != line)(lambda line=line: self.line_copy(line).start())
        self.lines[p.line] = self.stages[3]

    def end(self, store):
        p = self.p
        for line in range(p.length):
            pl.when(p.line != line)(lambda line=line: self.line_copy(line).wait_send())
            pl.when(p.line != line)(lambda line=line: self.line_landing(line).wait_recv())
        total = self.lines[0]
        for line in range(1, p.length):
            total = total + self.lines[line]
        store(total)

    def acts(self, store):
        return [functools.partial(self.step, k) for k in range(3)] + [lambda: self.end(store)]


def gelu_pair(hidden):
    ratio = (2.0 / 3.141592653589793) ** 0.5
    square = hidden * hidden
    curve = jnp.tanh(ratio * (hidden + 0.044715 * (square * hidden)))
    cdf = 0.5 * (1.0 + curve)
    slope = cdf + hidden * (0.5 * (1.0 - curve * curve)) * (ratio * (1.0 + (3.0 * 0.044715) * square))
    return hidden * cdf, slope


def norm_back(value, gain, grad):
    scale = unit_scale(value)
    unit = value * scale
    lifted = grad * gain
    pull = jnp.mean(lifted * unit, axis=-1, keepdims=True)
    return scale * (lifted - unit * pull), grad * unit


def column_sum(value):
    return jnp.sum(value.astype(jnp.float32), axis=0, keepdims=True)


def swap_halves(value):
    shards = lax.axis_size("fsdp")
    pairs = []
    for x in range(2):
        for index in range(shards):
            core = index % 2
            goal = (x, index) if core == x else (1 - x, index ^ 1)
            pairs.append((x * shards + index, goal[0] * shards + goal[1]))
    return lax.ppermute(value, ("seq", "fsdp"), pairs)


def pair_all_to_all(value, split_axis, concat_axis):
    shards = lax.axis_size("fsdp")
    groups = [[k, k + 1] for k in range(0, shards, 2)]
    return lax.all_to_all(
        value, "fsdp", split_axis=split_axis, concat_axis=concat_axis, axis_index_groups=groups, tiled=True
    )


def pack_rows(parts, width):
    rows = [jnp.pad(p, ((0, 0), (0, width - p.shape[1]))) for p in parts]
    packed = jnp.concatenate(rows, axis=0)
    return jnp.pad(packed, ((0, 16 - packed.shape[0]), (0, 0)))


def local_general(residual_in, cotangent, w_qkv, w_out, w_fc, w_proj, attn_bias, fc_bias, proj_bias, gains):
    shards = lax.axis_size("fsdp")
    tok_rows = residual_in.shape[1]
    model_width = w_qkv.shape[1] // 3
    hidden_width = w_fc.shape[1]
    unit = gains.shape[1]
    share = model_width // 2
    head_count = share // HD
    scale = HD ** (-0.5)
    small = pack_rows([attn_bias, gains, proj_bias[None], fc_bias[None]], 256)
    compact = swap_halves(residual_in[0]).astype(jnp.float32)
    upstream = swap_halves(cotangent[0]).astype(jnp.float32)
    qkv_w, small_all, out_w, fc_w, proj_w = gather_all(
        [w_qkv, small, w_out, w_fc, w_proj], shards, [0, 0, 2, 3, 5], 0
    )
    qkv_w = qkv_w.reshape(model_width, 3 * model_width)
    out_w = out_w.reshape(model_width, model_width)
    fc_w = fc_w.reshape(model_width, hidden_width)
    proj_w = proj_w.reshape(hidden_width, model_width)
    vectors = small_all[:, :6, :unit].transpose(1, 0, 2).reshape(6, model_width).astype(jnp.float32)
    bias_all, gain_all, proj_b = vectors[:3], vectors[3:5], vectors[5]
    fc_b = small_all[:, 6, : fc_bias.shape[0]].reshape(hidden_width).astype(jnp.float32)
    full = jnp.concatenate([compact, -jnp.sum(compact, axis=-1, keepdims=True)], axis=-1)
    normed = rms_norm(full, gain_all[0]).astype(jnp.bfloat16)
    bias_qkv = jnp.concatenate([bias_all[0], jnp.zeros_like(bias_all[0]), bias_all[1]])
    projected = (matmul(normed, qkv_w) + bias_qkv).astype(jnp.bfloat16)
    by_heads = pair_all_to_all(projected.reshape(tok_rows, 3, 2, share), 2, 0)
    length = by_heads.shape[0]
    queries = by_heads[:, 0, 0].reshape(length, head_count, HD)
    keys_all = by_heads[:, 1, 0].reshape(length, head_count, HD)
    values_all = by_heads[:, 2, 0].reshape(length, head_count, HD)
    attended, log_totals = attend(queries, keys_all, values_all, scale)
    mixed = pair_all_to_all(attended.reshape(length, 1, share), 0, 1)
    mixed = mixed.reshape(tok_rows, model_width)
    branch = matmul(mixed, out_w) + bias_all[2]
    middle = full + center(branch)
    normed_two = rms_norm(middle, gain_all[1]).astype(jnp.bfloat16)
    hidden = matmul(normed_two, fc_w) + fc_b
    activated = gelu_tanh(hidden).astype(jnp.bfloat16)
    branch_two = matmul(activated, proj_w) + proj_b
    final = middle + center(branch_two)
    residual_out = swap_halves(final[:, :-1].astype(jnp.bfloat16))[None]
    grad_final = jnp.concatenate([upstream, jnp.zeros((tok_rows, 1), jnp.float32)], axis=-1)
    grad_branch_two = center(grad_final).astype(jnp.bfloat16)
    grad_proj = weight_grad(activated, grad_branch_two)
    grad_proj_bias = jnp.sum(grad_branch_two.astype(jnp.float32), axis=0)
    grad_activated = input_grad_of(grad_branch_two, proj_w)
    gelu_pull = jax.vjp(gelu_tanh, hidden)[1]
    grad_hidden = gelu_pull(grad_activated)[0].astype(jnp.bfloat16)
    grad_fc = weight_grad(normed_two, grad_hidden)
    grad_fc_bias = jnp.sum(grad_hidden.astype(jnp.float32), axis=0)
    grad_normed_two = input_grad_of(grad_hidden, fc_w)
    second_pull = jax.vjp(rms_norm, middle, gain_all[1])[1]
    grad_middle_norm, grad_gain_two = second_pull(grad_normed_two)
    grad_middle = grad_final + grad_middle_norm
    grad_branch = center(grad_middle).astype(jnp.bfloat16)
    grad_out = weight_grad(mixed, grad_branch)
    grad_out_bias = jnp.sum(grad_branch.astype(jnp.float32), axis=0)
    grad_mixed = input_grad_of(grad_branch, out_w).astype(jnp.bfloat16)
    grad_heads = pair_all_to_all(grad_mixed.reshape(tok_rows, 2, share), 1, 0)
    grad_heads = grad_heads.reshape(length, head_count, HD)
    grad_queries, grad_keys, grad_values = attend_back(
        queries, keys_all, values_all, log_totals, grad_heads, scale
    )
    stacked = jnp.stack([grad_queries, grad_keys, grad_values], axis=1).reshape(length, 3, 1, share)
    grad_projected = pair_all_to_all(stacked, 0, 2)
    grad_projected = grad_projected.reshape(tok_rows, 3 * model_width)
    grad_qkv = weight_grad(normed, grad_projected)
    column_sums = jnp.sum(grad_projected.astype(jnp.float32), axis=0)
    grad_normed = input_grad_of(grad_projected, qkv_w)
    first_pull = jax.vjp(rms_norm, full, gain_all[0])[1]
    grad_full_norm, grad_gain_one = first_pull(grad_normed)
    grad_full = grad_middle + grad_full_norm
    input_grad = swap_halves((grad_full[:, :-1] - grad_full[:, -1:]).astype(jnp.bfloat16))[None]
    rows = jnp.stack(
        [
            column_sums[:model_width],
            column_sums[2 * model_width :],
            grad_out_bias,
            grad_gain_one,
            grad_gain_two,
            grad_proj_bias,
        ]
    )
    rows = rows.reshape(6, shards, unit).transpose(1, 0, 2)
    last = grad_fc_bias.reshape(shards, 1, fc_bias.shape[0])
    grad_small = jnp.concatenate(
        [
            jnp.pad(rows, ((0, 0), (0, 0), (0, 256 - unit))),
            jnp.pad(last, ((0, 0), (0, 9), (0, 256 - fc_bias.shape[0]))),
        ],
        axis=1,
    )

    def split(grad):
        return grad.astype(jnp.bfloat16).reshape(shards, grad.shape[0] // shards, grad.shape[1])

    total_proj, total_fc, total_out, total_qkv, total_small = scatter_all(
        [split(grad_proj), split(grad_fc), split(grad_out), split(grad_qkv), grad_small.astype(jnp.bfloat16)],
        shards,
        [0, 1, 2, 3, 3],
        1,
    )
    return (
        residual_out,
        input_grad,
        total_qkv,
        total_out,
        total_fc,
        total_proj,
        total_small[:3, :unit],
        total_small[6, : fc_bias.shape[0]],
        total_small[5, :unit],
        total_small[3:5, :unit],
    )


def layer_kernel(shards, starts, *refs):
    (resid, cot, w_qkv, w_out, w_fc, w_proj, attn_bias, fc_bias, proj_bias, gains,
     total_qkv, total_out, total_fc, total_proj, total_attn_bias, total_fc_bias, total_proj_bias, total_gains,
     resid_o, input_o, qkv_o, fc_o, proj_o,
     fc_own, proj_own, fetch, own_small, small_w, spread, vec, rs, cs, normed, heads, mixed,
     wo, tiles, work, middle, acc, gn, got, gproj, key_sum, value_sum, ro, ig, sg, *rest) = refs
    chunk_refs, rest = rest[:19], rest[19:]
    small_refs, rest = rest[:7], rest[7:]
    place = Place(shards)
    low = jnp.bfloat16
    rows, width = mixed.shape
    share = width // 2
    unit = width // shards
    parts = fc_o.shape[0]
    deep = total_proj.shape[0]
    span = 2 * HD
    pairs = share // span
    block = min(256, rows)
    per = len(Gather.sem_shapes(1))

    def columns(ref, part):
        return ref.at[:, pl.ds(part * width, width)]

    gathers = []

    def gather(src, dst, split=False):
        nonlocal rest
        item = Gather(place, src, dst, rest[:per], split)
        rest = rest[per:]
        gathers.append(item)
        return item

    qkv_in = [gather(columns(w_qkv, part), tiles.at[part]) for part in range(3)]
    small_in = gather(own_small, small_w)
    out_in = gather(w_out, wo)
    fc_in = [gather(columns(fc_own, part), fc_o.at[part]) for part in range(parts)]
    proj_in = gather(proj_own, proj_o, True)
    own_loads = [
        pltpu.make_async_copy(w_fc, fc_own, fetch.at[0]),
        pltpu.make_async_copy(w_proj, proj_own, fetch.at[1]),
    ]
    for load in own_loads:
        load.start()
    supply = Supply(gathers, starts)
    (si_s, si_r, sc_s, sc_r, ex_s, ex_r, at_s, at_r, ks, wsem, ro_s, ro_r, ig_s, ig_r,
     gm_s, gm_r, gp_s, gp_r) = rest
    swap_in = Swap(place, resid.at[0], rs, (si_s, si_r))
    swap_cot = Swap(place, cot.at[0], cs, (sc_s, sc_r))

    spread[...] = jnp.zeros_like(spread)
    spread[0, 0:3, 0:unit] = attn_bias[...].astype(jnp.float32)
    spread[0, 3:5, 0:unit] = gains[...].astype(jnp.float32)
    spread[0, 5:6, 0:unit] = proj_bias[...].reshape(1, unit).astype(jnp.float32)
    wide = fc_bias.shape[0]
    in_row = width // wide
    for part in range(parts):
        spread[1, 6 + part : 7 + part, 0:wide] = fc_bias[...].reshape(1, wide).astype(jnp.float32)
    moved = pltpu.roll(spread[0], place.index * unit, 1)
    hidden_rows = pltpu.roll(spread[1], lax.rem(place.index, in_row) * wide, 1)
    row_ids = lax.broadcasted_iota(jnp.int32, moved.shape, 0)
    moved = jnp.where(row_ids < 6, moved, jnp.where(row_ids == 6 + place.index // in_row, hidden_rows, 0.0))
    own_small[...] = moved.astype(low)

    for load in own_loads:
        load.wait()
    place.greet(diagonal=True, whole_line=True)
    supply.tick()
    swap_in.start()
    supply.need(small_in)
    swap_cot.start()
    vec[...] = jnp.sum(small_w[...].astype(jnp.float32), axis=(0, 1, 2))
    swap_in.wait()

    def whole(here):
        value = rs[here, :].astype(jnp.float32)
        return jnp.concatenate([value, -jnp.sum(value, axis=-1, keepdims=True)], axis=1)

    def normalize(here):
        full = whole(here)
        normed[here, :] = (full * unit_scale(full) * vec[3:4, :]).astype(low)

    over_rows(rows, 128, normalize)
    for item in qkv_in:
        supply.need(item)

    flat = tiles.reshape(4, width, width)
    out_flat = wo.reshape(width, width)
    keep = [pltpu.make_async_copy(tiles.at[part], qkv_o.at[part], ks.at[part]) for part in range(3)]
    for copy in keep:
        copy.start()
    my_rows = pl.ds(pl.multiple_of(place.core * rows, rows), rows)

    def exchange(part):
        src = work.at[part, :, pl.ds(0, share)]
        return remote(src, heads.at[part, my_rows], ex_s.at[part], ex_r.at[part], place.sibling())

    def project(part, group):
        result = dot_nn(normed[...], flat[part, :, lane_block(group, share)])
        if part != 1:
            bias = part // 2
            result = result + vec[bias : bias + 1, lane_block(group, share)]
        return result.astype(low)

    for part in range(3):
        work[part, :, pl.ds(0, share)] = project(part, 1 - place.core)
        exchange(part).start()
    supply.tick()
    for part in range(3):
        heads[part, my_rows, :] = project(part, place.core)
    supply.tick()
    for part in range(3):
        exchange(part).wait()

    def my_pair(pair):
        return pl.ds(pl.multiple_of(place.core * share + pair * span, span), span)

    def back(pair):
        src = got.at[1 - place.core, :, pl.ds(pair * span, span)]
        return remote(src, mixed.at[:, my_pair(pair)], at_s.at[pair], at_r.at[pair], place.sibling())

    for pair in range(pairs):
        lanes = pl.ds(pair * span, span)

        def put_result(start, size, value):
            got[start // rows, pl.ds(start % rows, size), lanes] = value

        attend_pair(heads, pair, put_result)
        back(pair).start()
        mixed[:, my_pair(pair)] = got[place.core, :, lanes]
        supply.tick()
    for copy in keep:
        copy.wait()
    for item in qkv_in:
        item.close()

    train = Train()

    def fc_load(tile):
        return pltpu.make_async_copy(fc_o.at[tile], tiles.at[tile % 2], wsem.at[tile % 2])

    def proj_load(tile):
        src = proj_o.reshape(parts, width, width).at[tile]
        return pltpu.make_async_copy(src, flat.at[2 + tile % 2], wsem.at[2 + tile % 2])

    def qkv_load(part):
        return pltpu.make_async_copy(qkv_o.at[part], tiles.at[part], wsem.at[part])

    sg[...] = jnp.zeros_like(sg)

    def put_qkv(part):
        def store(value):
            total_qkv[:, pl.ds(part * width, width)] = value
        return store

    def put_fc(tile):
        def store(value):
            total_fc[:, pl.ds(tile * width, width)] = value
        return store

    def put_proj(part):
        def store(value):
            total_proj[pl.ds(part * unit, unit), :] = value
        return store

    def put_out(value):
        total_out[...] = value

    stores = [put_fc(k) for k in range(parts)] + [put_proj(k) for k in range(parts)]
    stores += [put_out] + [put_qkv(k) for k in range(3)]
    chunks = [Chunk(place, k, chunk_refs, store) for k, store in enumerate(stores)]
    fc_chunks, proj_chunks = chunks[:parts], chunks[parts : 2 * parts]
    out_chunk, qkv_chunks = chunks[2 * parts], chunks[2 * parts + 1 :]
    grads = chunk_refs[0]

    def keep_rows(index, first, value):
        value = value.astype(low)
        for k in range(value.shape[0] // unit):
            shard = first + k
            side = lax.rem(place.core + shard % 2, 2)
            grads[index, side, shard // 4, (shard // 2) % 2] = value[k * unit : (k + 1) * unit]

    def weight_grad_chunk(index, left, right):
        for part in range(2):
            lanes = pl.ds(part * share, share)
            keep_rows(index, part * (shards // 2), dot_tn(left[:, lanes], right))
        chunks[index].start()

    act_ref, slope_ref, n2, g2 = work.at[0], work.at[1], work.at[2], work.at[3]
    supply.need(out_in)
    for pair in range(pairs):
        back(pair).wait()
    swap_cot.wait()

    def upstream(here):
        value = cs[here, :].astype(jnp.float32)
        return jnp.concatenate([value, jnp.zeros((value.shape[0], 1), jnp.float32)], axis=1)

    def enter(here):
        branch = dot_nn(mixed[here, :], out_flat[...]) + vec[2:3, :]
        value = whole(here) + branch - jnp.mean(branch, axis=-1, keepdims=True)
        middle[here, :] = value
        n2[here, :] = (value * unit_scale(value) * vec[4:5, :]).astype(low)
        grad = upstream(here)
        grad = (grad - jnp.mean(grad, axis=-1, keepdims=True)).astype(low)
        g2[here, :] = grad
        sg[5:6, :] += column_sum(grad)

    over_rows(rows, block, enter)
    supply.need(fc_in[0])
    fc_load(0).start()
    supply.need(proj_in)
    proj_load(0).start()
    proj_load(1).start()

    for tile in range(parts):
        if tile:
            supply.need(fc_in[tile])
            fc_load(tile).start()
        fc_load(tile).wait()
        proj_load(tile).wait()
        fc_tile, proj_tile = flat.at[tile % 2], flat.at[2 + tile % 2]

        def feed(here):
            hidden = dot_nn(n2[here, :], fc_tile[...]) + vec[6 + tile : 7 + tile, :]
            value, slope = gelu_pair(hidden)
            value = value.astype(low)
            act_ref[here, :] = value
            grad = (dot_nt(g2[here, :], proj_tile[...]) * slope).astype(low)
            slope_ref[here, :] = grad
            sg[6 + tile : 7 + tile, :] += column_sum(grad)
            forward = dot_nn(value, proj_tile[...])
            backward = dot_nt(grad, fc_tile[...])
            if tile == 0:
                acc[here, :] = forward
                gn[here, :] = backward
            else:
                acc[here, :] += forward
                gn[here, :] += backward

        over_rows(rows, block, feed)
        if tile + 2 < parts:
            proj_load(tile + 2).start()
        weight_grad_chunk(tile, n2, slope_ref[...])
        train.add(fc_chunks[tile].acts())
        for part in range(2):
            lanes = pl.ds(part * share, share)
            value = dot_tn(act_ref[:, lanes], g2[...])
            first = (tile * width + part * share) // deep
            for k in range(share // deep):
                for q in range(parts):
                    at = k * deep + q * unit
                    keep_rows(parts + q, first + k, value[at : at + unit])
        train.tick()

    for item in proj_chunks:
        item.start()

    def leave(here):
        branch = acc[here, :] + vec[5:6, :]
        value = middle[here, :]
        final = value + branch - jnp.mean(branch, axis=-1, keepdims=True)
        ro[here, :] = final[:, : width - 1].astype(low)
        pull, terms = norm_back(value, vec[4:5, :], gn[here, :])
        sg[4:5, :] += jnp.sum(terms, axis=0, keepdims=True)
        grad = upstream(here) + pull
        acc[here, :] = grad
        grad = (grad - jnp.mean(grad, axis=-1, keepdims=True)).astype(low)
        g2[here, :] = grad
        sg[2:3, :] += column_sum(grad)

    over_rows(rows, block // 2, leave)
    swap_out = Swap(place, ro, resid_o.at[0], (ro_s, ro_r))
    swap_out.start()
    train.add(proj_chunks[0].acts())
    train.tick()

    def mixed_grad(group):
        lanes = pl.ds(pl.multiple_of(group * share, 128), share)
        return dot_nt(g2[...], out_flat[lanes, :]).astype(low)

    n2[:, pl.ds(0, share)] = mixed_grad(1 - place.core)
    give = remote(n2.at[:, pl.ds(0, share)], got.at[place.core], gm_s, gm_r, place.sibling())
    give.start()
    got[place.core] = mixed_grad(place.core)
    weight_grad_chunk(2 * parts, mixed, g2[...])
    train.add(proj_chunks[1].acts())
    for part in range(3):
        qkv_load(part).start()
    train.tick()
    give.wait()

    def send(part, pair):
        lanes = pl.multiple_of((1 - place.core) * share + pair * span, span)
        src = work.at[part, :, pl.ds(lanes, span)]
        at = pl.multiple_of((part * 2 + place.core) * share + pair * span, span)
        return remote(src, gproj.at[:, pl.ds(at, span)], gp_s.at[part, pair], gp_r.at[part, pair], place.sibling())

    waiting = proj_chunks[2:] + [out_chunk]
    for pair in range(pairs):
        for item in waiting[: -(-len(waiting) // (pairs - pair))]:
            train.add(item.acts())
            waiting.remove(item)

        def put(part, start, size, value):
            lanes = pl.ds(start // rows * share + pair * span, span)
            work[part, pl.ds(start % rows, size), lanes] = value

        attend_back_pair(heads, got, pair, key_sum, value_sum, put)
        train.tick()
        for part in range(3):
            send(part, pair).start()
            at = pl.multiple_of((part * 2 + place.core) * share + pair * span, span)
            gproj[:, pl.ds(at, span)] = work[part, :, my_pair(pair)]
    for pair in range(pairs):
        for part in range(3):
            send(part, pair).wait()

    for part in range(3):
        lanes = pl.ds(part * width, width)
        weight_grad_chunk(2 * parts + 1 + part, normed, gproj[:, lanes])
        train.add(qkv_chunks[part].acts())
        train.tick()

    for part in range(3):
        qkv_load(part).wait()

    def last(here):
        grad = dot_nt(gproj[here, pl.ds(0, width)], flat[0])
        grad += dot_nt(gproj[here, pl.ds(width, width)], flat[1])
        grad += dot_nt(gproj[here, pl.ds(2 * width, width)], flat[2])
        sg[0:1, :] += column_sum(gproj[here, pl.ds(0, width)])
        sg[1:2, :] += column_sum(gproj[here, pl.ds(2 * width, width)])
        pull, terms = norm_back(whole(here), vec[3:4, :], grad)
        sg[3:4, :] += jnp.sum(terms, axis=0, keepdims=True)
        grad = acc[here, :] + pull
        ig[here, :] = (grad[:, : width - 1] - grad[:, width - 1 :]).astype(low)

    for start in range(0, rows, block):
        last(pl.ds(start, block))
        train.tick()
    swap_back = Swap(place, ig, input_o.at[0], (ig_s, ig_r))
    swap_back.start()
    small = SmallSum(place, small_refs)
    small_refs[0][0] = sg[...]
    small.begin()

    def put_small(value):
        mine = pltpu.roll(value, width - place.index * unit, 1)
        total_attn_bias[...] = mine[0:3, :unit]
        total_gains[...] = mine[3:5, :unit]
        total_proj_bias[...] = mine[5:6, :unit].reshape(unit)
        hidden = pltpu.roll(value, width - lax.rem(place.index, in_row) * wide, 1)[:, :wide]
        hidden_ids = lax.broadcasted_iota(jnp.int32, hidden.shape, 0)
        hidden = jnp.where(hidden_ids == 6 + place.index // in_row, hidden, 0.0)
        total_fc_bias[...] = jnp.sum(hidden, axis=0, keepdims=True).reshape(wide)

    train.add(small.acts(put_small))
    train.drain()
    for item in gathers[3:]:
        item.close()
    swap_out.wait()
    swap_back.wait()


def finish_kernel(count, *refs):
    for k in range(count):
        refs[count + k][...] = refs[k][...]


def finish(arrays):
    count = len(arrays)
    vmem = pl.BlockSpec(memory_space=pltpu.VMEM)
    return pl.pallas_call(
        functools.partial(finish_kernel, count),
        out_shape=[jax.ShapeDtypeStruct(a.shape, a.dtype) for a in arrays],
        in_specs=[vmem] * count,
        out_specs=[vmem] * count,
        compiler_params=pltpu.CompilerParams(vmem_limit_bytes=32 << 20),
        name="finish",
    )(*arrays)


def local_tiled(residual_in, cotangent, w_qkv, w_out, w_fc, w_proj, attn_bias, fc_bias, proj_bias, gains):
    shards = lax.axis_size("fsdp")
    length = shards // 4
    rows = residual_in.shape[1]
    width = w_qkv.shape[1] // 3
    share = width // 2
    unit = width // shards
    parts = w_fc.shape[1] // width
    deep = w_proj.shape[0]
    pairs = share // (2 * HD)
    low, f32 = jnp.bfloat16, jnp.float32
    vmem = pl.BlockSpec(memory_space=pltpu.VMEM)
    dma = pltpu.SemaphoreType.DMA
    small = (16, width)
    starts = [0, 0, 0, 0, 3] + [4 + 2 * part for part in range(parts)] + [5]
    outs = [
        jax.ShapeDtypeStruct((unit, 3 * width), f32),
        jax.ShapeDtypeStruct((unit, width), f32),
        jax.ShapeDtypeStruct((unit, parts * width), f32),
        jax.ShapeDtypeStruct((deep, width), f32),
        jax.ShapeDtypeStruct(attn_bias.shape, f32),
        jax.ShapeDtypeStruct(fc_bias.shape, f32),
        jax.ShapeDtypeStruct(proj_bias.shape, f32),
        jax.ShapeDtypeStruct(gains.shape, f32),
        jax.ShapeDtypeStruct(residual_in.shape, low),
        jax.ShapeDtypeStruct(residual_in.shape, low),
        jax.ShapeDtypeStruct((3, length, 2, 2, unit, width), low),
        jax.ShapeDtypeStruct((parts, length, 2, 2, unit, width), low),
        jax.ShapeDtypeStruct((length, 2, 2, deep, width), low),
    ]
    scratch = [
        pltpu.VMEM(w_fc.shape, low),
        pltpu.VMEM(w_proj.shape, low),
        dma((2,)),
        pltpu.VMEM(small, low),
        pltpu.VMEM((length, 2, 2) + small, low),
        pltpu.VMEM((2,) + small, f32),
        pltpu.VMEM(small, f32),
        pltpu.VMEM((rows, width - 1), low),
        pltpu.VMEM((rows, width - 1), low),
        pltpu.VMEM((rows, width), low),
        pltpu.VMEM((3, 2 * rows, share), low),
        pltpu.VMEM((rows, width), low),
        pltpu.VMEM((length, 2, 2, unit, width), low),
        pltpu.VMEM((4, length, 2, 2, unit, width), low),
        pltpu.VMEM((4, rows, width), low),
        pltpu.VMEM((rows, width), f32),
        pltpu.VMEM((rows, width), f32),
        pltpu.VMEM((rows, width), f32),
        pltpu.VMEM((2, rows, share), low),
        pltpu.VMEM((rows, 3 * width), low),
        pltpu.VMEM((2 * rows, 2 * HD), f32),
        pltpu.VMEM((2 * rows, 2 * HD), f32),
        pltpu.VMEM((rows, width - 1), low),
        pltpu.VMEM((rows, width - 1), low),
        pltpu.VMEM(small, f32),
    ]
    scratch += Chunk.scratch(2 * parts + 4, length, unit, width)
    scratch += [
        pltpu.VMEM((4,) + small, f32),
        pltpu.VMEM((3,) + small, f32),
        pltpu.VMEM((length,) + small, f32),
        dma((3,)), dma((3,)), dma((length,)), dma((length,)),
    ]
    scratch += Gather.sem_shapes(length) * len(starts)
    scratch += [dma, dma, dma, dma, dma((3,)), dma((3,)), dma((pairs,)), dma((pairs,)), dma((3,)), dma((4,))]
    scratch += [dma, dma, dma, dma, dma, dma, dma((3, pairs)), dma((3, pairs))]
    results = pl.pallas_call(
        functools.partial(layer_kernel, shards, starts),
        out_shape=outs,
        in_specs=[ANY] * 6 + [vmem] * 4,
        out_specs=[vmem] * 8 + [ANY] * 5,
        scratch_shapes=scratch,
        compiler_params=pltpu.CompilerParams(
            collective_id=0, has_side_effects=True, vmem_limit_bytes=62 << 20
        ),
        name="layer",
    )(residual_in, cotangent, w_qkv, w_out, w_fc, w_proj, attn_bias, fc_bias, proj_bias, gains)
    (total_qkv, total_out, total_fc, total_proj, total_attn_bias, total_fc_bias, total_proj_bias, total_gains,
     residual_out, input_grad) = finish(results[:10])
    return (
        residual_out, input_grad, total_qkv, total_out, total_fc, total_proj,
        total_attn_bias, total_fc_bias, total_proj_bias, total_gains,
    )


def local(residual_in, cotangent, w_qkv, w_out, w_fc, w_proj, attn_bias, fc_bias, proj_bias, gains):
    arguments = (residual_in, cotangent, w_qkv, w_out, w_fc, w_proj, attn_bias, fc_bias, proj_bias, gains)
    if w_qkv.shape[0] % 16:
        return local_general(*arguments)
    return local_tiled(*arguments)


def solution(mesh):
    in_specs = (
        P("fsdp", "seq", None),
        P("fsdp", "seq", None),
        P("fsdp", None),
        P("fsdp", None),
        P("fsdp", None),
        P("fsdp", None),
        P(None, "fsdp"),
        P("fsdp"),
        P("fsdp"),
        P(None, "fsdp"),
    )
    out_specs = (
        P("fsdp", "seq", None),
        P("fsdp", "seq", None),
        P("fsdp", None),
        P("fsdp", None),
        P("fsdp", None),
        P("fsdp", None),
        P(None, "fsdp"),
        P("fsdp"),
        P("fsdp"),
        P(None, "fsdp"),
    )
    return jax.shard_map(local, mesh=mesh, in_specs=in_specs, out_specs=out_specs, check_vma=False)
```

```python
import functools

import jax
import jax.numpy as jnp
from jax import lax
from jax.experimental import pallas as pl
from jax.experimental.pallas import tpu as pltpu
from jax.sharding import PartitionSpec as P

HD = 64
EPSILON = 1e-05
MASKED = -1e30
MESH = pl.DeviceIdType.MESH
ANY = pl.BlockSpec(memory_space=pl.ANY)


class Place:
    def __init__(self, shards):
        self.length = shards // 4
        self.x = lax.axis_index("seq")
        index = lax.axis_index("fsdp")
        self.index = index
        self.core = lax.rem(index, 2)
        self.y = lax.rem(index // 2, 2)
        self.line = index // 4

    def at(self, **moved):
        x = moved.get("x", self.x)
        line = moved.get("line", self.line)
        y = moved.get("y", self.y)
        core = moved.get("core", self.core)
        return (x, (line * 2 + y) * 2 + core)

    def beside_x(self):
        return self.at(x=1 - self.x)

    def beside_y(self):
        return self.at(y=1 - self.y)

    def sibling(self):
        return self.at(core=1 - self.core)

    def above(self):
        return self.at(line=self.line + 1)

    def below(self):
        return self.at(line=self.line - 1)

    def greet(self, diagonal=False, whole_line=False):
        barrier = pltpu.get_barrier_semaphore()

        def signal(device):
            pl.semaphore_signal(barrier, inc=1, device_id=device, device_id_type=MESH)

        signal(self.beside_x())
        signal(self.beside_y())
        signal(self.sibling())
        has_below = self.line > 0
        has_above = self.line < self.length - 1
        if whole_line:
            for line in range(self.length):
                pl.when(self.line != line)(lambda line=line: signal(self.at(line=line)))
            count = 3 + self.length - 1
        else:
            pl.when(has_below)(lambda: signal(self.below()))
            pl.when(has_above)(lambda: signal(self.above()))
            count = 3 + has_below.astype(jnp.int32) + has_above.astype(jnp.int32)
        if diagonal:
            across = self.x != self.core
            pl.when(across)(lambda: signal(self.at(x=1 - self.x, core=1 - self.core)))
            count = count + across.astype(jnp.int32)
        pl.semaphore_wait(barrier, count)


def remote(src, dst, send, recv, device):
    return pltpu.make_async_remote_copy(
        src_ref=src, dst_ref=dst, send_sem=send, recv_sem=recv, device_id=device, device_id_type=MESH
    )


class PlainGather:
    def __init__(self, place, shard, out, sems):
        self.p = place
        self.shard = shard
        self.out = out
        self.rows, self.cols = shard.shape
        (self.up, self.down, self.line_in, self.ys, self.yr, self.xs, self.xr, self.ds, self.dr, self.own) = sems

    @staticmethod
    def sem_shapes(length):
        dma = pltpu.SemaphoreType.DMA
        return [dma((length,))] * 7 + [dma((3, length))] * 2 + [dma]

    def half(self, ref, which):
        width = self.cols // 2
        return ref.at[:, pl.ds(pl.multiple_of(which * width, width), width)]

    def slot(self, line, y, core):
        return self.out.at[line, y, core]

    def up_copy(self, line, src=None):
        p = self.p
        dst = self.slot(line, p.y, p.core)
        return remote(dst if src is None else src, dst, self.up.at[line], self.line_in.at[line], p.above())

    def down_copy(self, line, src=None):
        p = self.p
        dst = self.slot(line, p.y, p.core)
        return remote(dst if src is None else src, dst, self.down.at[line], self.line_in.at[line], p.below())

    def y_copy(self, line, src=None):
        p = self.p
        dst = self.half(self.slot(line, p.y, p.core), p.x)
        src = dst if src is None else self.half(src, p.x)
        return remote(src, dst, self.ys.at[line], self.yr.at[line], p.beside_y())

    def y_landing(self, line):
        p = self.p
        dst = self.half(self.slot(line, 1 - p.y, p.core), p.x)
        return remote(dst, dst, self.ys.at[line], self.yr.at[line], p.beside_y())

    def x_copy(self, line):
        p = self.p
        dst = self.half(self.slot(line, 1 - p.y, p.core), p.x)
        return remote(dst, dst, self.xs.at[line], self.xr.at[line], p.beside_x())

    def x_landing(self, line):
        p = self.p
        dst = self.half(self.slot(line, 1 - p.y, p.core), 1 - p.x)
        return remote(dst, dst, self.xs.at[line], self.xr.at[line], p.beside_x())

    def d_copy(self, kind, line, src=None, core=None):
        p = self.p
        core = p.core if core is None else core
        if kind == 0:
            dst = self.slot(line, p.y, core)
        else:
            dst = self.half(self.slot(line, 1 - p.y, core), p.x if kind == 1 else 1 - p.x)
        return remote(dst if src is None else src, dst, self.ds.at[kind, line], self.dr.at[kind, line], p.sibling())

    def own_copy(self):
        p = self.p
        return pltpu.make_async_copy(self.shard, self.slot(p.line, p.y, p.core), self.own)

    def each_at(self, distance, act):
        p = self.p
        if distance == 0:
            act(p.line, 0)
            return
        pl.when(p.line - distance >= 0)(lambda: act(p.line - distance, 1))
        pl.when(p.line + distance < p.length)(lambda: act(p.line + distance, -1))

    def arrive(self, distance):
        p = self.p

        def act(line, way):
            src = None
            if way == 0:
                src = self.shard
                self.own_copy().start()
            else:
                self.up_copy(line).wait_recv()
            if way >= 0:
                pl.when(p.line < p.length - 1)(lambda: self.up_copy(line, src).start())
            if way <= 0:
                pl.when(p.line > 0)(lambda: self.down_copy(line, src).start())
            self.y_copy(line, src).start()
            self.d_copy(0, line, src).start()

        self.each_at(distance, act)

    def arrive_y(self, distance):
        def act(line, way):
            self.y_landing(line).wait_recv()
            self.x_copy(line).start()
            self.d_copy(1, line).start()

        self.each_at(distance, act)

    def arrive_x(self, distance):
        def act(line, way):
            self.x_landing(line).wait_recv()
            self.d_copy(2, line).start()

        self.each_at(distance, act)

    def stage(self, time):
        length = self.p.length
        if 0 <= time < length:
            self.arrive(time)
        if 0 <= time - 1 < length:
            self.arrive_y(time - 1)
        if 0 <= time - 2 < length:
            self.arrive_x(time - 2)

    def stages(self):
        return self.p.length + 2

    def finish(self):
        p = self.p

        def one(line):
            for kind in range(3):
                self.d_copy(kind, line, core=1 - p.core).wait_recv()
            for kind in range(3):
                self.d_copy(kind, line).wait_send()
            self.y_copy(line).wait_send()
            self.x_copy(line).wait_send()
            pl.when((p.line >= line) & (p.line < p.length - 1))(lambda: self.up_copy(line).wait_send())
            pl.when((p.line <= line) & (p.line > 0))(lambda: self.down_copy(line).wait_send())

        for line in range(p.length):
            one(line)
        self.own_copy().wait()


def gather_kernel(shards, lag, count, *refs):
    ins, outs, rest = refs[:count], refs[count : 2 * count], refs[2 * count :]
    place = Place(shards)
    place.greet()
    per = len(PlainGather.sem_shapes(1))
    gathers = [PlainGather(place, ins[k], outs[k], rest[k * per : (k + 1) * per]) for k in range(count)]
    total = max(lag[k] + g.stages() for k, g in enumerate(gathers))
    for time in range(total):
        for k, g in enumerate(gathers):
            g.stage(time - lag[k])
    for g in gathers:
        g.finish()


def gather_all(arrays, shards, lag, collective_id):
    length = shards // 4
    out = pl.pallas_call(
        functools.partial(gather_kernel, shards, lag, len(arrays)),
        out_shape=[jax.ShapeDtypeStruct((length, 2, 2) + a.shape, a.dtype) for a in arrays],
        in_specs=[ANY] * len(arrays),
        out_specs=[ANY] * len(arrays),
        scratch_shapes=PlainGather.sem_shapes(length) * len(arrays),
        compiler_params=pltpu.CompilerParams(collective_id=collective_id, has_side_effects=True),
        name="gather_weights",
    )(*arrays)
    return [o.reshape((shards,) + a.shape) for o, a in zip(out, arrays)]


class Scatter:
    def __init__(self, place, partial, out, refs):
        self.p = place
        self.g = partial
        self.out = out
        self.rows, self.cols = out.shape
        (self.s, self.d, self.xb, self.yb, self.lo, self.hi, self.fb, self.tb,
         self.load, self.ds, self.dr, self.xs, self.xr, self.ys, self.yr,
         self.us, self.ur, self.ns, self.nr, self.fs, self.fr) = refs

    @staticmethod
    def scratch(length, rows, cols, dtype):
        dma = pltpu.SemaphoreType.DMA
        full = pltpu.VMEM((length, 2, rows, cols), dtype)
        half = pltpu.VMEM((length, rows, cols // 2), dtype)
        line = pltpu.VMEM((length, rows, cols), dtype)
        one = pltpu.VMEM((rows, cols), dtype)
        return [full, full, half, half, line, line, one, one] + [dma] * 7 + [dma((length,))] * 4 + [dma] * 2

    def half(self, which):
        width = self.cols // 2
        return pl.ds(pl.multiple_of(which * width, width), width)

    def load_copy(self):
        return pltpu.make_async_copy(self.g.at[:, :, self.p.core], self.s, self.load)

    def d_copy(self):
        p = self.p
        return remote(self.g.at[:, :, 1 - p.core], self.d, self.ds, self.dr, p.sibling())

    def x_copy(self):
        p = self.p
        src = self.s.at[:, 1 - p.y, :, self.half(1 - p.x)]
        return remote(src, self.xb, self.xs, self.xr, p.beside_x())

    def y_copy(self):
        p = self.p
        src = self.s.at[:, 1 - p.y, :, self.half(p.x)]
        return remote(src, self.yb, self.ys, self.yr, p.beside_y())

    def up_copy(self, line):
        p = self.p
        return remote(self.s.at[line, p.y], self.lo.at[line], self.us.at[line], self.ur.at[line], p.above())

    def down_copy(self, line):
        p = self.p
        return remote(self.s.at[line, p.y], self.hi.at[line], self.ns.at[line], self.nr.at[line], p.below())

    def f_copy(self):
        return remote(self.tb, self.fb, self.fs, self.fr, self.p.beside_x())

    def each(self, act):
        def body(line, carry):
            act(line)
            return carry

        lax.fori_loop(0, self.p.length, body, 0)

    def start(self):
        self.load_copy().start()
        self.d_copy().start()

    def pair(self):
        p = self.p
        self.load_copy().wait()
        self.d_copy().wait()

        def other(line):
            self.s[line, 1 - p.y] = self.s[line, 1 - p.y] + self.d[line, 1 - p.y]

        self.each(other)
        self.x_copy().start()

        def own(line):
            self.s[line, p.y] = self.s[line, p.y] + self.d[line, p.y]

        self.each(own)

    def over_x(self):
        p = self.p
        self.x_copy().wait()

        def act(line):
            cols = self.half(p.x)
            self.s[line, 1 - p.y, :, cols] = self.s[line, 1 - p.y, :, cols] + self.xb[line]

        self.each(act)
        self.y_copy().start()

    def over_y(self):
        p = self.p
        self.y_copy().wait()

        def act(line):
            cols = self.half(p.x)
            self.s[line, p.y, :, cols] = self.s[line, p.y, :, cols] + self.yb[line]

        self.each(act)

    def hop(self, step):
        p = self.p
        last = p.length - 1
        up = last - step + p.line

        def upward():
            @pl.when(p.line > 0)
            def _():
                self.up_copy(up).wait_recv()
                self.s[up, p.y] = self.s[up, p.y] + self.lo[up]

            self.up_copy(up).start()

        pl.when(p.line <= step)(upward)
        down = step - last + p.line

        def downward():
            @pl.when(p.line < last)
            def _():
                self.down_copy(down).wait_recv()
                self.s[down, p.y] = self.s[down, p.y] + self.hi[down]

            self.down_copy(down).start()

        pl.when(down >= 0)(downward)

    def total(self):
        p = self.p
        mine = p.line

        @pl.when(p.line > 0)
        def _():
            self.up_copy(mine).wait_recv()
            self.s[mine, p.y] = self.s[mine, p.y] + self.lo[mine]

        @pl.when(p.line < p.length - 1)
        def _():
            self.down_copy(mine).wait_recv()
            self.s[mine, p.y] = self.s[mine, p.y] + self.hi[mine]

        self.tb[...] = self.s[mine, p.y]
        self.f_copy().start()

    def finish(self):
        p = self.p
        self.f_copy().wait()
        self.out[...] = self.tb[...].astype(jnp.float32) + self.fb[...].astype(jnp.float32)
        for line in range(p.length):
            pl.when(line > p.line)(lambda line=line: self.up_copy(line).wait_send())
            pl.when(line < p.line)(lambda line=line: self.down_copy(line).wait_send())

    def stages(self):
        acts = [self.start, self.pair, self.over_x, self.over_y]
        acts += [functools.partial(self.hop, step) for step in range(self.p.length - 1)]
        return acts + [self.total, self.finish]


def scatter_kernel(shards, lag, count, *refs):
    ins, outs, rest = refs[:count], refs[count : 2 * count], refs[2 * count :]
    place = Place(shards)
    place.greet()
    per = len(rest) // count
    lists = [
        Scatter(place, ins[k], outs[k], rest[k * per : (k + 1) * per]).stages() for k in range(count)
    ]
    total = max(lag[k] + len(s) for k, s in enumerate(lists))
    for time in range(total):
        for k, acts in enumerate(lists):
            if 0 <= time - lag[k] < len(acts):
                acts[time - lag[k]]()


def scatter_all(arrays, shards, lag, collective_id):
    length = shards // 4
    parts = [a.reshape((length, 2, 2) + a.shape[1:]) for a in arrays]
    scratch = []
    for a in arrays:
        scratch += Scatter.scratch(length, a.shape[1], a.shape[2], a.dtype)
    return pl.pallas_call(
        functools.partial(scatter_kernel, shards, lag, len(arrays)),
        out_shape=[jax.ShapeDtypeStruct(a.shape[1:], jnp.float32) for a in arrays],
        in_specs=[ANY] * len(arrays),
        out_specs=[pl.BlockSpec(memory_space=pltpu.VMEM)] * len(arrays),
        scratch_shapes=scratch,
        compiler_params=pltpu.CompilerParams(
            collective_id=collective_id, has_side_effects=True, vmem_limit_bytes=60 << 20
        ),
        name="scatter_grads",
    )(*parts)


def rms_norm(values, gain):
    return values * lax.rsqrt(jnp.mean(values * values, axis=-1, keepdims=True) + EPSILON) * gain


def center(values):
    return values - jnp.mean(values, axis=-1, keepdims=True)


def gelu_tanh(values):
    return jax.nn.gelu(values, approximate=True)


def matmul(left, right):
    return jnp.dot(left, right, preferred_element_type=jnp.float32)


def weight_grad(inputs, grads):
    return lax.dot_general(
        inputs, grads, (((0,), (0,)), ((), ())), preferred_element_type=jnp.float32
    )


def input_grad_of(grads, weight):
    return lax.dot_general(
        grads, weight, (((1,), (1,)), ((), ())), preferred_element_type=jnp.float32
    )


def block_rows(length):
    return min(length, max(512, length // 8))


def score_block(query_block, keys_part, start, scale):
    scores = (
        jnp.einsum("qhd,khd->hqk", query_block, keys_part, preferred_element_type=jnp.float32)
        * scale
    )
    query_pos = start + jnp.arange(query_block.shape[0], dtype=jnp.int32)
    key_pos = jnp.arange(keys_part.shape[0], dtype=jnp.int32)
    allowed = query_pos[:, None] >= key_pos[None, :]
    return jnp.where(allowed[None], scores, MASKED)


def attend(queries, keys_all, values_all, scale):
    length, head_count, width = queries.shape
    block = block_rows(length)
    count = length // block
    results = []
    log_totals = []
    for index in range(count):
        start = index * block
        finish = start + block
        scores = score_block(queries[start:finish], keys_all[:finish], start, scale)
        peak = jnp.max(scores, axis=-1, keepdims=True)
        weights = jnp.exp(scores - peak)
        total = jnp.sum(weights, axis=-1, keepdims=True)
        weights = weights / total
        result = jnp.einsum(
            "hqk,khd->qhd",
            weights.astype(jnp.bfloat16),
            values_all[:finish],
            preferred_element_type=jnp.float32,
        )
        results.append(result.astype(jnp.bfloat16))
        log_totals.append((peak + jnp.log(total))[..., 0])
    joined = jnp.concatenate(results, axis=0)
    return (joined.reshape(length, head_count * width), log_totals)


def attend_back(queries, keys_all, values_all, log_totals, grad_heads, scale):
    length, head_count, width = queries.shape
    block = block_rows(length)
    count = length // block
    key_sum = jnp.zeros((length, head_count, width), jnp.float32)
    value_sum = jnp.zeros((length, head_count, width), jnp.float32)
    query_grads = []
    for index in range(count):
        start = index * block
        finish = start + block
        query_block = queries[start:finish]
        grad_block = grad_heads[start:finish]
        keys_part = keys_all[:finish]
        scores = score_block(query_block, keys_part, start, scale)
        weights = jnp.exp(scores - log_totals[index][..., None])
        grad_weights = jnp.einsum(
            "qhd,khd->hqk", grad_block, values_all[:finish], preferred_element_type=jnp.float32
        )
        inner = jnp.sum(weights * grad_weights, axis=-1, keepdims=True)
        grad_scores = (weights * (grad_weights - inner)).astype(jnp.bfloat16)
        query_grad = (
            jnp.einsum("hqk,khd->qhd", grad_scores, keys_part, preferred_element_type=jnp.float32)
            * scale
        )
        key_part = (
            jnp.einsum("hqk,qhd->khd", grad_scores, query_block, preferred_element_type=jnp.float32)
            * scale
        )
        value_part = jnp.einsum(
            "hqk,qhd->khd",
            weights.astype(jnp.bfloat16),
            grad_block,
            preferred_element_type=jnp.float32,
        )
        key_sum = key_sum.at[:finish].add(key_part)
        value_sum = value_sum.at[:finish].add(value_part)
        query_grads.append(query_grad.astype(jnp.bfloat16))
    return (
        jnp.concatenate(query_grads, axis=0),
        key_sum.astype(jnp.bfloat16),
        value_sum.astype(jnp.bfloat16),
    )


def dot_nn(left, right):
    return jnp.dot(left, right, preferred_element_type=jnp.float32)


def dot_nt(left, right):
    return lax.dot_general(
        left, right, (((1,), (1,)), ((), ())), preferred_element_type=jnp.float32
    )


def dot_tn(left, right):
    return lax.dot_general(
        left, right, (((0,), (0,)), ((), ())), preferred_element_type=jnp.float32
    )


def lane_block(index, width):
    return pl.ds(pl.multiple_of(index * width, width), width)


def unit_scale(value):
    return lax.rsqrt(jnp.mean(value * value, axis=-1, keepdims=True) + EPSILON)


def over_rows(total, block, act):
    def body(step, carry):
        act(pl.ds(pl.multiple_of(step * block, block), block))
        return carry

    lax.fori_loop(0, total // block, body, 0)


def head_mask(shape, head):
    lanes = lax.broadcasted_iota(jnp.int32, shape, 1)
    return (lanes // HD) == head


class Swap:
    def __init__(self, place, src, dst, sems):
        self.p = place
        self.src, self.dst = src, dst
        self.send, self.recv = sems

    def moved(self):
        p = self.p
        return remote(self.src, self.dst, self.send, self.recv, p.at(x=1 - p.x, core=1 - p.core))

    def kept(self):
        return pltpu.make_async_copy(self.src, self.dst, self.send)

    def start(self):
        p = self.p
        pl.when(p.x != p.core)(lambda: self.moved().start())
        pl.when(p.x == p.core)(lambda: self.kept().start())

    def wait(self):
        p = self.p
        pl.when(p.x != p.core)(lambda: self.moved().wait())
        pl.when(p.x == p.core)(lambda: self.kept().wait())


def attend_pair(qkv, pair, put):
    total = qkv.shape[1]
    block = min(256, total)
    lanes = pl.ds(pair * 2 * HD, 2 * HD)
    scale = jnp.asarray(HD ** (-0.5), jnp.bfloat16)
    zero = jnp.zeros((), jnp.bfloat16)
    rows = lax.broadcasted_iota(jnp.int32, (block, block), 0)
    cols = lax.broadcasted_iota(jnp.int32, (block, block), 1)
    allowed = rows >= cols
    for index in range(total // block):
        start = index * block
        here = pl.ds(start, block)
        query = qkv[0, here, lanes] * scale
        results = []
        for head in range(2):
            masked = jnp.where(head_mask(query.shape, head), query, zero)
            near = dot_nt(masked, qkv[1, here, lanes])
            near = jnp.where(allowed, near, MASKED)
            peak = jnp.max(near, axis=-1, keepdims=True)
            if start:
                far = dot_nt(masked, qkv[1, pl.ds(0, start), lanes])
                peak = jnp.maximum(peak, jnp.max(far, axis=-1, keepdims=True))
            near = jnp.exp(near - peak)
            total_weight = jnp.sum(near, axis=-1, keepdims=True)
            if start:
                far = jnp.exp(far - peak)
                total_weight = total_weight + jnp.sum(far, axis=-1, keepdims=True)
            share = 1.0 / total_weight
            result = dot_nn((near * share).astype(jnp.bfloat16), qkv[2, here, lanes])
            if start:
                result += dot_nn(
                    (far * share).astype(jnp.bfloat16), qkv[2, pl.ds(0, start), lanes]
                )
            results.append(result)
        merged = jnp.where(head_mask(results[0].shape, 0), results[0], results[1])
        put(start, block, merged.astype(jnp.bfloat16))


def attend_back_pair(qkv, grads, pair, key_sum, value_sum, put):
    total = qkv.shape[1]
    block = min(256, total)
    lanes = pl.ds(pair * 2 * HD, 2 * HD)
    scale = jnp.asarray(HD ** (-0.5), jnp.bfloat16)
    zero = jnp.zeros((), jnp.bfloat16)
    rows = lax.broadcasted_iota(jnp.int32, (block, block), 0)
    cols = lax.broadcasted_iota(jnp.int32, (block, block), 1)
    allowed = rows <= cols
    key_sum[...] = jnp.zeros_like(key_sum)
    value_sum[...] = jnp.zeros_like(value_sum)
    for index in range(total // block):
        start = index * block
        here = pl.ds(start, block)
        spans = [here] + ([pl.ds(0, start)] if start else [])
        query = qkv[0, here, lanes] * scale
        grad = grads[start // grads.shape[1], pl.ds(start % grads.shape[1], block), lanes]
        query_grads = []
        for head in range(2):
            mask = head_mask(query.shape, head)
            masked = jnp.where(mask, query, zero)
            grad_masked = jnp.where(mask, grad, zero)
            scores = [dot_nt(qkv[1, span, lanes], masked) for span in spans]
            scores[0] = jnp.where(allowed, scores[0], MASKED)
            peak = functools.reduce(
                jnp.maximum, [jnp.max(s, axis=0, keepdims=True) for s in scores]
            )
            weights = [jnp.exp(s - peak) for s in scores]
            sums = sum(jnp.sum(w, axis=0, keepdims=True) for w in weights)
            share = 1.0 / sums
            weights = [w * share for w in weights]
            pulled = [dot_nt(qkv[2, span, lanes], grad_masked) for span in spans]
            inner = sum(jnp.sum(w * g, axis=0, keepdims=True) for w, g in zip(weights, pulled))
            query_grad = None
            for span, w, g in zip(spans, weights, pulled):
                value_sum[span, :] += dot_nn(w.astype(jnp.bfloat16), grad_masked)
                slope = (w * (g - inner)).astype(jnp.bfloat16)
                key_sum[span, :] += dot_nn(slope, masked)
                part = dot_tn(slope, qkv[1, span, lanes])
                query_grad = part if query_grad is None else query_grad + part
            query_grads.append(query_grad)
        merged = jnp.where(head_mask(query_grads[0].shape, 0), query_grads[0], query_grads[1])
        put(0, start, block, (merged * HD ** (-0.5)).astype(jnp.bfloat16))
    half = grads.shape[1]
    for start in range(0, total, half):
        put(1, start, half, key_sum[pl.ds(start, half), :].astype(jnp.bfloat16))
        put(2, start, half, value_sum[pl.ds(start, half), :].astype(jnp.bfloat16))


class Gather:
    def __init__(self, place, shard, out, sems, split=False):
        self.p = place
        self.shard = shard
        self.out = out
        self.split = split
        self.width = shard.shape[1] // 3
        (self.up, self.down, self.line_in, self.ys, self.yr, self.xs, self.xr, self.ds, self.dr, self.own) = sems
        self.time = 0

    @staticmethod
    def sem_shapes(length):
        dma = pltpu.SemaphoreType.DMA
        return [dma((length,))] * 5 + [dma((2, length))] * 2 + [dma((4, length))] * 2 + [dma]

    def thirds(self, ref, which, count=1):
        return ref.at[:, pl.ds(pl.multiple_of(which * self.width, self.width), count * self.width)]

    def slot(self, line, y, core=None):
        return self.out.at[line, y, self.p.core if core is None else core]

    def on_line(self, ref):
        return self.thirds(ref, self.p.x, 2) if self.split else ref

    def up_copy(self, line, src=None):
        p = self.p
        dst = self.slot(line, p.y)
        src = self.on_line(dst if src is None else src)
        return remote(src, self.on_line(dst), self.up.at[line], self.line_in.at[line], p.above())

    def down_copy(self, line, src=None):
        p = self.p
        dst = self.slot(line, p.y)
        src = self.on_line(dst if src is None else src)
        return remote(src, self.on_line(dst), self.down.at[line], self.line_in.at[line], p.below())

    def y_copy(self, line, src=None):
        p = self.p
        dst = self.slot(line, p.y)
        src = self.thirds(dst if src is None else src, p.x, 2)
        return remote(src, self.thirds(dst, p.x, 2), self.ys.at[line], self.yr.at[line], p.beside_y())

    def y_landing(self, line):
        p = self.p
        dst = self.thirds(self.slot(line, 1 - p.y), p.x, 2)
        return remote(dst, dst, self.ys.at[line], self.yr.at[line], p.beside_y())

    def x_copy(self, line, own):
        p = self.p
        dst = self.thirds(self.slot(line, p.y if own else 1 - p.y), 2 * p.x)
        return remote(dst, dst, self.xs.at[int(own), line], self.xr.at[int(own), line], p.beside_x())

    def x_landing(self, line, own):
        p = self.p
        dst = self.thirds(self.slot(line, p.y if own else 1 - p.y), 2 * (1 - p.x))
        return remote(dst, dst, self.xs.at[int(own), line], self.xr.at[int(own), line], p.beside_x())

    def d_copy(self, kind, line, whole=False, src=None, core=None):
        p = self.p
        dst = self.slot(line, p.y if kind in (0, 3) else 1 - p.y, core)
        src = dst if src is None else src
        if kind == 0 and not whole:
            src, dst = self.on_line(src), self.on_line(dst)
        if kind == 1:
            src, dst = self.thirds(src, p.x, 2), self.thirds(dst, p.x, 2)
        if kind >= 2:
            src, dst = self.thirds(src, 2 * (1 - p.x)), self.thirds(dst, 2 * (1 - p.x))
        return remote(src, dst, self.ds.at[kind, line], self.dr.at[kind, line], p.sibling())

    def own_copy(self):
        p = self.p
        return pltpu.make_async_copy(self.shard, self.slot(p.line, p.y), self.own)

    def each_at(self, distance, act):
        p = self.p
        if distance == 0:
            act(p.line, 0)
            return
        pl.when(p.line - distance >= 0)(lambda: act(p.line - distance, 1))
        pl.when(p.line + distance < p.length)(lambda: act(p.line + distance, -1))

    def arrive(self, distance):
        p = self.p

        def act(line, way):
            src = None
            if way == 0:
                src = self.shard
                self.own_copy().start()
            else:
                self.up_copy(line).wait_recv()
            if way >= 0:
                pl.when(p.line < p.length - 1)(lambda: self.up_copy(line, src).start())
            if way <= 0:
                pl.when(p.line > 0)(lambda: self.down_copy(line, src).start())
            self.y_copy(line, src).start()
            if way and self.split:
                self.x_copy(line, True).start()
            self.d_copy(0, line, way == 0, src).start()

        self.each_at(distance, act)

    def arrive_y(self, distance):
        def act(line, way):
            self.y_landing(line).wait_recv()
            self.x_copy(line, False).start()
            self.d_copy(1, line).start()
            if way and self.split:
                self.x_landing(line, True).wait_recv()
                self.d_copy(3, line).start()

        self.each_at(distance, act)

    def arrive_x(self, distance):
        def act(line, way):
            self.x_landing(line, False).wait_recv()
            self.d_copy(2, line).start()

        self.each_at(distance, act)

    def stage(self):
        time, length = self.time, self.p.length
        self.time += 1
        if time < length:
            self.arrive(time)
        if 0 <= time - 1 < length:
            self.arrive_y(time - 1)
        if 0 <= time - 2 < length:
            self.arrive_x(time - 2)

    def under_way(self):
        return self.time < self.p.length + 2

    def take(self):
        p = self.p
        self.own_copy().wait()
        for line in range(p.length):
            for kind in range(3):
                if kind or not self.split:
                    self.d_copy(kind, line, core=1 - p.core).wait_recv()
            if self.split:
                pl.when(p.line == line)(lambda line=line: self.d_copy(0, line, True, core=1 - p.core).wait_recv())

                @pl.when(p.line != line)
                def _(line=line):
                    self.d_copy(0, line, core=1 - p.core).wait_recv()
                    self.d_copy(3, line, core=1 - p.core).wait_recv()

    def close(self):
        p = self.p
        for line in range(p.length):
            for kind in range(3):
                if kind or not self.split:
                    self.d_copy(kind, line).wait_send()
            if self.split:
                pl.when(p.line == line)(lambda line=line: self.d_copy(0, line, True).wait_send())

                @pl.when(p.line != line)
                def _(line=line):
                    self.d_copy(0, line).wait_send()
                    self.d_copy(3, line).wait_send()
                    self.x_copy(line, True).wait_send()

            self.y_copy(line).wait_send()
            self.x_copy(line, False).wait_send()
            pl.when((p.line >= line) & (p.line < p.length - 1))(lambda line=line: self.up_copy(line).wait_send())
            pl.when((p.line <= line) & (p.line > 0))(lambda line=line: self.down_copy(line).wait_send())


class Supply:
    def __init__(self, gathers, starts):
        self.entries = list(zip(starts, gathers))
        self.time = 0

    def tick(self):
        for start, gather in self.entries:
            if start <= self.time and gather.under_way():
                gather.stage()
        self.time += 1

    def need(self, gather):
        while gather.under_way():
            self.tick()
        gather.take()


class Chunk:
    def __init__(self, place, index, refs, store):
        self.p = place
        self.store = store
        (grads, self_d, xy, lo, hi, tb, fb, ds, dr, xs, xr, ys, yr, us, ur, ns, nr, fs, fr) = refs
        self.mine, self.other = grads.at[index, 0], grads.at[index, 1]
        self.d, self.xy = self_d.at[index], xy.at[index]
        third = xy.shape[-1] // 3
        self.xb, self.yb = self.xy.at[:, :, pl.ds(0, third)], self.xy.at[:, :, pl.ds(third, 2 * third)]
        self.lo, self.hi = lo.at[index], hi.at[index]
        self.tb, self.fb = tb.at[index], fb.at[index]
        self.sems = [s.at[index] for s in (ds, dr, xs, xr, ys, yr)]
        self.us, self.ur, self.ns, self.nr = us.at[index], ur.at[index], ns.at[index], nr.at[index]
        self.fs, self.fr = fs.at[index], fr.at[index]

    @staticmethod
    def scratch(count, length, rows, cols):
        low = jnp.bfloat16
        dma = pltpu.SemaphoreType.DMA
        return [
            pltpu.VMEM((count, 2, length, 2, rows, cols), low),
            pltpu.VMEM((count, length, 2, rows, cols), low),
            pltpu.VMEM((count, length, rows, cols), low),
            pltpu.VMEM((count, length - 1, rows, cols), low),
            pltpu.VMEM((count, length - 1, rows, cols), low),
            pltpu.VMEM((count, rows, cols), low),
            pltpu.VMEM((count, rows, cols), low),
        ] + [dma((count,))] * 6 + [dma((count, length))] * 4 + [dma((count,))] * 2

    def third(self, which, count=1):
        width = self.tb.shape[1] // 3
        return pl.ds(pl.multiple_of(which * width, width), count * width)

    def d_copy(self):
        return remote(self.other, self.d, self.sems[0], self.sems[1], self.p.sibling())

    def x_copy(self):
        p = self.p
        src = self.mine.at[:, 1 - p.y, :, self.third(2 * (1 - p.x))]
        return remote(src, self.xb, self.sems[2], self.sems[3], p.beside_x())

    def y_copy(self):
        p = self.p
        src = self.mine.at[:, 1 - p.y, :, self.third(p.x, 2)]
        return remote(src, self.yb, self.sems[4], self.sems[5], p.beside_y())

    def up_copy(self, line):
        p = self.p
        return remote(self.mine.at[line, p.y], self.lo.at[line - 1], self.us.at[line], self.ur.at[line], p.above())

    def down_copy(self, line):
        p = self.p
        return remote(self.mine.at[line, p.y], self.hi.at[line], self.ns.at[line], self.nr.at[line], p.below())

    def f_copy(self):
        return remote(self.tb, self.fb, self.fs, self.fr, self.p.beside_x())

    def each(self, act):
        def body(line, carry):
            act(line)
            return carry

        lax.fori_loop(0, self.p.length, body, 0)

    def start(self):
        self.d_copy().start()

    def pair(self):
        p = self.p
        self.d_copy().wait()

        def other(line):
            self.mine[line, 1 - p.y] = self.mine[line, 1 - p.y] + self.d[line, 1 - p.y]

        self.each(other)
        self.x_copy().start()

        def own(line):
            self.mine[line, p.y] = self.mine[line, p.y] + self.d[line, p.y]

        self.each(own)

    def over_x(self):
        p = self.p
        self.x_copy().wait()

        def act(line):
            cols = self.third(2 * p.x)
            self.mine[line, 1 - p.y, :, cols] = self.mine[line, 1 - p.y, :, cols] + self.xb[line]

        self.each(act)
        self.y_copy().start()

    def over_y(self):
        p = self.p
        self.y_copy().wait()

        def act(line):
            cols = self.third(p.x, 2)
            self.mine[line, p.y, :, cols] = self.mine[line, p.y, :, cols] + self.yb[line]

        self.each(act)
        self.hop(0)

    def take_low(self, line):
        self.up_copy(line).wait_recv()
        self.mine[line, self.p.y] = self.mine[line, self.p.y] + self.lo[line - 1]

    def take_high(self, line):
        self.down_copy(line).wait_recv()
        self.mine[line, self.p.y] = self.mine[line, self.p.y] + self.hi[line]

    def hop(self, step):
        p = self.p
        last = p.length - 1
        up = last - step + p.line

        def upward():
            pl.when(p.line > 0)(lambda: self.take_low(up))
            self.up_copy(up).start()

        pl.when(p.line <= step)(upward)
        down = step - last + p.line

        def downward():
            pl.when(p.line < last)(lambda: self.take_high(down))
            self.down_copy(down).start()

        pl.when(down >= 0)(downward)

    def total(self):
        p = self.p
        mine = p.line
        pl.when(mine > 0)(lambda: self.take_low(mine))
        pl.when(mine < p.length - 1)(lambda: self.take_high(mine))
        self.tb[...] = self.mine[mine, p.y]
        self.f_copy().start()

    def finish(self):
        p = self.p
        self.f_copy().wait()
        self.store(self.tb[...].astype(jnp.float32) + self.fb[...].astype(jnp.float32))
        for line in range(p.length - 1):
            pl.when(line + 1 > p.line)(lambda line=line: self.up_copy(line + 1).wait_send())
            pl.when(line < p.line)(lambda line=line: self.down_copy(line).wait_send())

    def acts(self):
        hops = [functools.partial(self.hop, step) for step in range(1, self.p.length - 1)]
        return [self.pair, self.over_x, self.over_y] + hops + [self.total, self.finish]


class Train:
    def __init__(self):
        self.running = []

    def add(self, acts):
        self.running.append(list(acts))

    def tick(self):
        for acts in self.running:
            acts.pop(0)()
        self.running = [acts for acts in self.running if acts]

    def drain(self):
        while self.running:
            self.tick()


class SmallSum:
    def __init__(self, place, refs):
        self.p = place
        self.stages, self.got, self.lines, self.ss, self.sr, self.ls, self.lr = refs

    def copy(self, step):
        p = self.p
        goal = [p.sibling, p.beside_x, p.beside_y][step]()
        return remote(self.stages.at[step], self.got.at[step], self.ss.at[step], self.sr.at[step], goal)

    def line_copy(self, line):
        p = self.p
        return remote(
            self.stages.at[3], self.lines.at[p.line], self.ls.at[line], self.lr.at[p.line], p.at(line=line)
        )

    def line_landing(self, line):
        p = self.p
        return remote(self.stages.at[3], self.lines.at[line], self.ls.at[line], self.lr.at[line], p.at(line=line))

    def begin(self):
        self.copy(0).start()

    def step(self, index):
        p = self.p
        self.copy(index).wait()
        self.stages[index + 1] = self.stages[index] + self.got[index]
        if index < 2:
            self.copy(index + 1).start()
            return
        for line in range(p.length):
            pl.when(p.line != line)(lambda line=line: self.line_copy(line).start())
        self.lines[p.line] = self.stages[3]

    def end(self, store):
        p = self.p
        for line in range(p.length):
            pl.when(p.line != line)(lambda line=line: self.line_copy(line).wait_send())
            pl.when(p.line != line)(lambda line=line: self.line_landing(line).wait_recv())
        total = self.lines[0]
        for line in range(1, p.length):
            total = total + self.lines[line]
        store(total)

    def acts(self, store):
        return [functools.partial(self.step, k) for k in range(3)] + [lambda: self.end(store)]


def gelu_pair(hidden):
    ratio = (2.0 / 3.141592653589793) ** 0.5
    square = hidden * hidden
    curve = jnp.tanh(ratio * (hidden + 0.044715 * (square * hidden)))
    cdf = 0.5 * (1.0 + curve)
    slope = cdf + hidden * (0.5 * (1.0 - curve * curve)) * (ratio * (1.0 + (3.0 * 0.044715) * square))
    return hidden * cdf, slope


def norm_back(value, gain, grad):
    scale = unit_scale(value)
    unit = value * scale
    lifted = grad * gain
    pull = jnp.mean(lifted * unit, axis=-1, keepdims=True)
    return scale * (lifted - unit * pull), grad * unit


def column_sum(value):
    return jnp.sum(value.astype(jnp.float32), axis=0, keepdims=True)


def swap_halves(value):
    shards = lax.axis_size("fsdp")
    pairs = []
    for x in range(2):
        for index in range(shards):
            core = index % 2
            goal = (x, index) if core == x else (1 - x, index ^ 1)
            pairs.append((x * shards + index, goal[0] * shards + goal[1]))
    return lax.ppermute(value, ("seq", "fsdp"), pairs)


def pair_all_to_all(value, split_axis, concat_axis):
    shards = lax.axis_size("fsdp")
    groups = [[k, k + 1] for k in range(0, shards, 2)]
    return lax.all_to_all(
        value, "fsdp", split_axis=split_axis, concat_axis=concat_axis, axis_index_groups=groups, tiled=True
    )


def pack_rows(parts, width):
    rows = [jnp.pad(p, ((0, 0), (0, width - p.shape[1]))) for p in parts]
    packed = jnp.concatenate(rows, axis=0)
    return jnp.pad(packed, ((0, 16 - packed.shape[0]), (0, 0)))


def local_general(residual_in, cotangent, w_qkv, w_out, w_fc, w_proj, attn_bias, fc_bias, proj_bias, gains):
    shards = lax.axis_size("fsdp")
    tok_rows = residual_in.shape[1]
    model_width = w_qkv.shape[1] // 3
    hidden_width = w_fc.shape[1]
    unit = gains.shape[1]
    share = model_width // 2
    head_count = share // HD
    scale = HD ** (-0.5)
    small = pack_rows([attn_bias, gains, proj_bias[None], fc_bias[None]], 256)
    compact = swap_halves(residual_in[0]).astype(jnp.float32)
    upstream = swap_halves(cotangent[0]).astype(jnp.float32)
    qkv_w, small_all, out_w, fc_w, proj_w = gather_all(
        [w_qkv, small, w_out, w_fc, w_proj], shards, [0, 0, 2, 3, 5], 0
    )
    qkv_w = qkv_w.reshape(model_width, 3 * model_width)
    out_w = out_w.reshape(model_width, model_width)
    fc_w = fc_w.reshape(model_width, hidden_width)
    proj_w = proj_w.reshape(hidden_width, model_width)
    vectors = small_all[:, :6, :unit].transpose(1, 0, 2).reshape(6, model_width).astype(jnp.float32)
    bias_all, gain_all, proj_b = vectors[:3], vectors[3:5], vectors[5]
    fc_b = small_all[:, 6, : fc_bias.shape[0]].reshape(hidden_width).astype(jnp.float32)
    full = jnp.concatenate([compact, -jnp.sum(compact, axis=-1, keepdims=True)], axis=-1)
    normed = rms_norm(full, gain_all[0]).astype(jnp.bfloat16)
    bias_qkv = jnp.concatenate([bias_all[0], jnp.zeros_like(bias_all[0]), bias_all[1]])
    projected = (matmul(normed, qkv_w) + bias_qkv).astype(jnp.bfloat16)
    by_heads = pair_all_to_all(projected.reshape(tok_rows, 3, 2, share), 2, 0)
    length = by_heads.shape[0]
    queries = by_heads[:, 0, 0].reshape(length, head_count, HD)
    keys_all = by_heads[:, 1, 0].reshape(length, head_count, HD)
    values_all = by_heads[:, 2, 0].reshape(length, head_count, HD)
    attended, log_totals = attend(queries, keys_all, values_all, scale)
    mixed = pair_all_to_all(attended.reshape(length, 1, share), 0, 1)
    mixed = mixed.reshape(tok_rows, model_width)
    branch = matmul(mixed, out_w) + bias_all[2]
    middle = full + center(branch)
    normed_two = rms_norm(middle, gain_all[1]).astype(jnp.bfloat16)
    hidden = matmul(normed_two, fc_w) + fc_b
    activated = gelu_tanh(hidden).astype(jnp.bfloat16)
    branch_two = matmul(activated, proj_w) + proj_b
    final = middle + center(branch_two)
    residual_out = swap_halves(final[:, :-1].astype(jnp.bfloat16))[None]
    grad_final = jnp.concatenate([upstream, jnp.zeros((tok_rows, 1), jnp.float32)], axis=-1)
    grad_branch_two = center(grad_final).astype(jnp.bfloat16)
    grad_proj = weight_grad(activated, grad_branch_two)
    grad_proj_bias = jnp.sum(grad_branch_two.astype(jnp.float32), axis=0)
    grad_activated = input_grad_of(grad_branch_two, proj_w)
    gelu_pull = jax.vjp(gelu_tanh, hidden)[1]
    grad_hidden = gelu_pull(grad_activated)[0].astype(jnp.bfloat16)
    grad_fc = weight_grad(normed_two, grad_hidden)
    grad_fc_bias = jnp.sum(grad_hidden.astype(jnp.float32), axis=0)
    grad_normed_two = input_grad_of(grad_hidden, fc_w)
    second_pull = jax.vjp(rms_norm, middle, gain_all[1])[1]
    grad_middle_norm, grad_gain_two = second_pull(grad_normed_two)
    grad_middle = grad_final + grad_middle_norm
    grad_branch = center(grad_middle).astype(jnp.bfloat16)
    grad_out = weight_grad(mixed, grad_branch)
    grad_out_bias = jnp.sum(grad_branch.astype(jnp.float32), axis=0)
    grad_mixed = input_grad_of(grad_branch, out_w).astype(jnp.bfloat16)
    grad_heads = pair_all_to_all(grad_mixed.reshape(tok_rows, 2, share), 1, 0)
    grad_heads = grad_heads.reshape(length, head_count, HD)
    grad_queries, grad_keys, grad_values = attend_back(
        queries, keys_all, values_all, log_totals, grad_heads, scale
    )
    stacked = jnp.stack([grad_queries, grad_keys, grad_values], axis=1).reshape(length, 3, 1, share)
    grad_projected = pair_all_to_all(stacked, 0, 2)
    grad_projected = grad_projected.reshape(tok_rows, 3 * model_width)
    grad_qkv = weight_grad(normed, grad_projected)
    column_sums = jnp.sum(grad_projected.astype(jnp.float32), axis=0)
    grad_normed = input_grad_of(grad_projected, qkv_w)
    first_pull = jax.vjp(rms_norm, full, gain_all[0])[1]
    grad_full_norm, grad_gain_one = first_pull(grad_normed)
    grad_full = grad_middle + grad_full_norm
    input_grad = swap_halves((grad_full[:, :-1] - grad_full[:, -1:]).astype(jnp.bfloat16))[None]
    rows = jnp.stack(
        [
            column_sums[:model_width],
            column_sums[2 * model_width :],
            grad_out_bias,
            grad_gain_one,
            grad_gain_two,
            grad_proj_bias,
        ]
    )
    rows = rows.reshape(6, shards, unit).transpose(1, 0, 2)
    last = grad_fc_bias.reshape(shards, 1, fc_bias.shape[0])
    grad_small = jnp.concatenate(
        [
            jnp.pad(rows, ((0, 0), (0, 0), (0, 256 - unit))),
            jnp.pad(last, ((0, 0), (0, 9), (0, 256 - fc_bias.shape[0]))),
        ],
        axis=1,
    )

    def split(grad):
        return grad.astype(jnp.bfloat16).reshape(shards, grad.shape[0] // shards, grad.shape[1])

    total_proj, total_fc, total_out, total_qkv, total_small = scatter_all(
        [split(grad_proj), split(grad_fc), split(grad_out), split(grad_qkv), grad_small.astype(jnp.bfloat16)],
        shards,
        [0, 1, 2, 3, 3],
        1,
    )
    return (
        residual_out,
        input_grad,
        total_qkv,
        total_out,
        total_fc,
        total_proj,
        total_small[:3, :unit],
        total_small[6, : fc_bias.shape[0]],
        total_small[5, :unit],
        total_small[3:5, :unit],
    )


def layer_kernel(shards, starts, *refs):
    (resid, cot, w_qkv, w_out, w_fc, w_proj, attn_bias, fc_bias, proj_bias, gains,
     total_qkv, total_out, total_fc, total_proj, total_attn_bias, total_fc_bias, total_proj_bias, total_gains,
     resid_o, input_o, qkv_o, fc_o, proj_o,
     fc_own, proj_own, fetch, own_small, small_w, spread, vec, rs, cs, normed, heads, mixed,
     wo, tiles, work, middle, acc, gn, got, gproj, key_sum, value_sum, ro, ig, sg, *rest) = refs
    chunk_refs, rest = rest[:19], rest[19:]
    small_refs, rest = rest[:7], rest[7:]
    place = Place(shards)
    low = jnp.bfloat16
    rows, width = mixed.shape
    share = width // 2
    unit = width // shards
    parts = fc_o.shape[0]
    deep = total_proj.shape[0]
    span = 2 * HD
    pairs = share // span
    block = min(256, rows)
    per = len(Gather.sem_shapes(1))

    def columns(ref, part):
        return ref.at[:, pl.ds(part * width, width)]

    gathers = []

    def gather(src, dst, split=False):
        nonlocal rest
        item = Gather(place, src, dst, rest[:per], split)
        rest = rest[per:]
        gathers.append(item)
        return item

    qkv_in = [gather(columns(w_qkv, part), tiles.at[part]) for part in range(3)]
    small_in = gather(own_small, small_w)
    out_in = gather(w_out, wo)
    fc_in = [gather(columns(fc_own, part), fc_o.at[part]) for part in range(parts)]
    proj_in = gather(proj_own, proj_o, True)
    own_loads = [
        pltpu.make_async_copy(w_fc, fc_own, fetch.at[0]),
        pltpu.make_async_copy(w_proj, proj_own, fetch.at[1]),
    ]
    for load in own_loads:
        load.start()
    supply = Supply(gathers, starts)
    (si_s, si_r, sc_s, sc_r, ex_s, ex_r, at_s, at_r, ks, wsem, ro_s, ro_r, ig_s, ig_r,
     gm_s, gm_r, gp_s, gp_r) = rest
    swap_in = Swap(place, resid.at[0], rs, (si_s, si_r))
    swap_cot = Swap(place, cot.at[0], cs, (sc_s, sc_r))

    spread[...] = jnp.zeros_like(spread)
    spread[0, 0:3, 0:unit] = attn_bias[...].astype(jnp.float32)
    spread[0, 3:5, 0:unit] = gains[...].astype(jnp.float32)
    spread[0, 5:6, 0:unit] = proj_bias[...].reshape(1, unit).astype(jnp.float32)
    wide = fc_bias.shape[0]
    in_row = width // wide
    for part in range(parts):
        spread[1, 6 + part : 7 + part, 0:wide] = fc_bias[...].reshape(1, wide).astype(jnp.float32)
    moved = pltpu.roll(spread[0], place.index * unit, 1)
    hidden_rows = pltpu.roll(spread[1], lax.rem(place.index, in_row) * wide, 1)
    row_ids = lax.broadcasted_iota(jnp.int32, moved.shape, 0)
    moved = jnp.where(row_ids < 6, moved, jnp.where(row_ids == 6 + place.index // in_row, hidden_rows, 0.0))
    own_small[...] = moved.astype(low)

    place.greet(diagonal=True, whole_line=True)
    supply.tick()
    for load in own_loads:
        load.wait()
    swap_in.start()
    supply.need(small_in)
    swap_cot.start()
    vec[...] = jnp.sum(small_w[...].astype(jnp.float32), axis=(0, 1, 2))
    swap_in.wait()

    def whole(here):
        value = rs[here, :].astype(jnp.float32)
        return jnp.concatenate([value, -jnp.sum(value, axis=-1, keepdims=True)], axis=1)

    def normalize(here):
        full = whole(here)
        normed[here, :] = (full * unit_scale(full) * vec[3:4, :]).astype(low)

    over_rows(rows, 128, normalize)
    for item in qkv_in:
        supply.need(item)

    flat = tiles.reshape(4, width, width)
    out_flat = wo.reshape(width, width)
    keep = [pltpu.make_async_copy(tiles.at[part], qkv_o.at[part], ks.at[part]) for part in range(3)]
    for copy in keep:
        copy.start()
    my_rows = pl.ds(pl.multiple_of(place.core * rows, rows), rows)

    def exchange(part):
        src = work.at[part, :, pl.ds(0, share)]
        return remote(src, heads.at[part, my_rows], ex_s.at[part], ex_r.at[part], place.sibling())

    def project(part, group):
        result = dot_nn(normed[...], flat[part, :, lane_block(group, share)])
        if part != 1:
            bias = part // 2
            result = result + vec[bias : bias + 1, lane_block(group, share)]
        return result.astype(low)

    for part in range(3):
        work[part, :, pl.ds(0, share)] = project(part, 1 - place.core)
        exchange(part).start()
    supply.tick()
    for part in range(3):
        heads[part, my_rows, :] = project(part, place.core)
    supply.tick()
    for part in range(3):
        exchange(part).wait()

    def my_pair(pair):
        return pl.ds(pl.multiple_of(place.core * share + pair * span, span), span)

    def back(pair):
        src = got.at[1 - place.core, :, pl.ds(pair * span, span)]
        return remote(src, mixed.at[:, my_pair(pair)], at_s.at[pair], at_r.at[pair], place.sibling())

    for pair in range(pairs):
        lanes = pl.ds(pair * span, span)

        def put_result(start, size, value):
            got[start // rows, pl.ds(start % rows, size), lanes] = value

        attend_pair(heads, pair, put_result)
        back(pair).start()
        mixed[:, my_pair(pair)] = got[place.core, :, lanes]
        supply.tick()
    for copy in keep:
        copy.wait()
    for item in qkv_in:
        item.close()

    train = Train()

    def fc_load(tile):
        return pltpu.make_async_copy(fc_o.at[tile], tiles.at[tile % 2], wsem.at[tile % 2])

    def proj_load(tile):
        src = proj_o.reshape(parts, width, width).at[tile]
        return pltpu.make_async_copy(src, flat.at[2 + tile % 2], wsem.at[2 + tile % 2])

    def qkv_load(part):
        return pltpu.make_async_copy(qkv_o.at[part], tiles.at[part], wsem.at[part])

    sg[...] = jnp.zeros_like(sg)

    def put_qkv(part):
        def store(value):
            total_qkv[:, pl.ds(part * width, width)] = value
        return store

    def put_fc(tile):
        def store(value):
            total_fc[:, pl.ds(tile * width, width)] = value
        return store

    def put_proj(part):
        def store(value):
            total_proj[pl.ds(part * unit, unit), :] = value
        return store

    def put_out(value):
        total_out[...] = value

    stores = [put_fc(k) for k in range(parts)] + [put_proj(k) for k in range(parts)]
    stores += [put_out] + [put_qkv(k) for k in range(3)]
    chunks = [Chunk(place, k, chunk_refs, store) for k, store in enumerate(stores)]
    fc_chunks, proj_chunks = chunks[:parts], chunks[parts : 2 * parts]
    out_chunk, qkv_chunks = chunks[2 * parts], chunks[2 * parts + 1 :]
    grads = chunk_refs[0]

    def keep_rows(index, first, value):
        value = value.astype(low)
        for k in range(value.shape[0] // unit):
            shard = first + k
            side = lax.rem(place.core + shard % 2, 2)
            grads[index, side, shard // 4, (shard // 2) % 2] = value[k * unit : (k + 1) * unit]

    def weight_grad_chunk(index, left, right):
        for part in range(2):
            lanes = pl.ds(part * share, share)
            keep_rows(index, part * (shards // 2), dot_tn(left[:, lanes], right))
        chunks[index].start()

    act_ref, slope_ref, n2, g2 = work.at[0], work.at[1], work.at[2], work.at[3]
    supply.need(out_in)
    for pair in range(pairs):
        back(pair).wait()
    swap_cot.wait()

    def upstream(here):
        value = cs[here, :].astype(jnp.float32)
        return jnp.concatenate([value, jnp.zeros((value.shape[0], 1), jnp.float32)], axis=1)

    def enter(here):
        branch = dot_nn(mixed[here, :], out_flat[...]) + vec[2:3, :]
        value = whole(here) + branch - jnp.mean(branch, axis=-1, keepdims=True)
        middle[here, :] = value
        n2[here, :] = (value * unit_scale(value) * vec[4:5, :]).astype(low)
        grad = upstream(here)
        grad = (grad - jnp.mean(grad, axis=-1, keepdims=True)).astype(low)
        g2[here, :] = grad
        sg[5:6, :] += column_sum(grad)

    over_rows(rows, block, enter)
    supply.need(fc_in[0])
    fc_load(0).start()
    supply.need(proj_in)
    proj_load(0).start()
    proj_load(1).start()

    for tile in range(parts):
        if tile:
            supply.need(fc_in[tile])
            fc_load(tile).start()
        fc_load(tile).wait()
        proj_load(tile).wait()
        fc_tile, proj_tile = flat.at[tile % 2], flat.at[2 + tile % 2]

        def feed(here):
            hidden = dot_nn(n2[here, :], fc_tile[...]) + vec[6 + tile : 7 + tile, :]
            value, slope = gelu_pair(hidden)
            value = value.astype(low)
            act_ref[here, :] = value
            grad = (dot_nt(g2[here, :], proj_tile[...]) * slope).astype(low)
            slope_ref[here, :] = grad
            sg[6 + tile : 7 + tile, :] += column_sum(grad)
            forward = dot_nn(value, proj_tile[...])
            backward = dot_nt(grad, fc_tile[...])
            if tile == 0:
                acc[here, :] = forward
                gn[here, :] = backward
            else:
                acc[here, :] += forward
                gn[here, :] += backward

        over_rows(rows, block, feed)
        if tile + 2 < parts:
            proj_load(tile + 2).start()
        weight_grad_chunk(tile, n2, slope_ref[...])
        train.add(fc_chunks[tile].acts())
        for part in range(2):
            lanes = pl.ds(part * share, share)
            value = dot_tn(act_ref[:, lanes], g2[...])
            first = (tile * width + part * share) // deep
            for k in range(share // deep):
                for q in range(parts):
                    at = k * deep + q * unit
                    keep_rows(parts + q, first + k, value[at : at + unit])
        train.tick()

    for item in proj_chunks:
        item.start()

    def leave(here):
        branch = acc[here, :] + vec[5:6, :]
        value = middle[here, :]
        final = value + branch - jnp.mean(branch, axis=-1, keepdims=True)
        ro[here, :] = final[:, : width - 1].astype(low)
        pull, terms = norm_back(value, vec[4:5, :], gn[here, :])
        sg[4:5, :] += jnp.sum(terms, axis=0, keepdims=True)
        grad = upstream(here) + pull
        acc[here, :] = grad
        grad = (grad - jnp.mean(grad, axis=-1, keepdims=True)).astype(low)
        g2[here, :] = grad
        sg[2:3, :] += column_sum(grad)

    over_rows(rows, block // 2, leave)
    pieces = 4

    def piece(src, dst, sems, k):
        here = pl.ds(k * (rows // pieces), rows // pieces)
        return Swap(place, src.at[here], dst.at[0, here], (sems[0].at[k], sems[1].at[k]))

    swap_out = [piece(ro, resid_o, (ro_s, ro_r), k) for k in range(pieces)]
    swap_back = [piece(ig, input_o, (ig_s, ig_r), k) for k in range(pieces)]
    swap_out[0].start()
    train.add(proj_chunks[0].acts())
    train.tick()

    def mixed_grad(group):
        lanes = pl.ds(pl.multiple_of(group * share, 128), share)
        return dot_nt(g2[...], out_flat[lanes, :]).astype(low)

    n2[:, pl.ds(0, share)] = mixed_grad(1 - place.core)
    give = remote(n2.at[:, pl.ds(0, share)], got.at[place.core], gm_s, gm_r, place.sibling())
    give.start()
    got[place.core] = mixed_grad(place.core)
    weight_grad_chunk(2 * parts, mixed, g2[...])
    train.add(proj_chunks[1].acts())
    swap_out[1].start()
    for part in range(3):
        qkv_load(part).start()
    train.tick()
    give.wait()

    def send(part, pair):
        lanes = pl.multiple_of((1 - place.core) * share + pair * span, span)
        src = work.at[part, :, pl.ds(lanes, span)]
        at = pl.multiple_of((part * 2 + place.core) * share + pair * span, span)
        return remote(src, gproj.at[:, pl.ds(at, span)], gp_s.at[part, pair], gp_r.at[part, pair], place.sibling())

    waiting = proj_chunks[2:] + [out_chunk]
    for pair in range(pairs):
        for item in waiting[: -(-len(waiting) // (pairs - pair))]:
            train.add(item.acts())
            waiting.remove(item)

        def put(part, start, size, value):
            lanes = pl.ds(start // rows * share + pair * span, span)
            work[part, pl.ds(start % rows, size), lanes] = value

        attend_back_pair(heads, got, pair, key_sum, value_sum, put)
        if pair + 2 < pieces:
            swap_out[pair + 2].start()
        train.tick()
        for part in range(3):
            send(part, pair).start()
            at = pl.multiple_of((part * 2 + place.core) * share + pair * span, span)
            gproj[:, pl.ds(at, span)] = work[part, :, my_pair(pair)]
    for pair in range(pairs):
        for part in range(3):
            send(part, pair).wait()

    for part in range(3):
        lanes = pl.ds(part * width, width)
        weight_grad_chunk(2 * parts + 1 + part, normed, gproj[:, lanes])
        train.add(qkv_chunks[part].acts())
        train.tick()

    for part in range(3):
        qkv_load(part).wait()

    def last(here):
        grad = dot_nt(gproj[here, pl.ds(0, width)], flat[0])
        grad += dot_nt(gproj[here, pl.ds(width, width)], flat[1])
        grad += dot_nt(gproj[here, pl.ds(2 * width, width)], flat[2])
        sg[0:1, :] += column_sum(gproj[here, pl.ds(0, width)])
        sg[1:2, :] += column_sum(gproj[here, pl.ds(2 * width, width)])
        pull, terms = norm_back(whole(here), vec[3:4, :], grad)
        sg[3:4, :] += jnp.sum(terms, axis=0, keepdims=True)
        grad = acc[here, :] + pull
        ig[here, :] = (grad[:, : width - 1] - grad[:, width - 1 :]).astype(low)

    for k in range(pieces):
        last(pl.ds(k * (rows // pieces), rows // pieces))
        swap_back[k].start()
        if k % 2:
            train.tick()
    small = SmallSum(place, small_refs)
    small_refs[0][0] = sg[...]
    small.begin()

    def put_small(value):
        mine = pltpu.roll(value, width - place.index * unit, 1)
        total_attn_bias[...] = mine[0:3, :unit]
        total_gains[...] = mine[3:5, :unit]
        total_proj_bias[...] = mine[5:6, :unit].reshape(unit)
        hidden = pltpu.roll(value, width - lax.rem(place.index, in_row) * wide, 1)[:, :wide]
        hidden_ids = lax.broadcasted_iota(jnp.int32, hidden.shape, 0)
        hidden = jnp.where(hidden_ids == 6 + place.index // in_row, hidden, 0.0)
        total_fc_bias[...] = jnp.sum(hidden, axis=0, keepdims=True).reshape(wide)

    train.add(small.acts(put_small))
    train.drain()
    for item in gathers[3:]:
        item.close()
    for swap in swap_out + swap_back:
        swap.wait()


def finish_kernel(count, *refs):
    ins, outs, held = refs[:count], refs[count : 2 * count], refs[2 * count : 3 * count]
    sems = refs[3 * count]
    loads = [pltpu.make_async_copy(ins[k], held[k], sems.at[0, k]) for k in range(count)]
    stores = [pltpu.make_async_copy(held[k], outs[k], sems.at[1, k]) for k in range(count)]
    for load in loads:
        load.start()
    for load, store in zip(loads, stores):
        load.wait()
        store.start()
    for store in stores:
        store.wait()


def finish(arrays):
    count = len(arrays)
    return pl.pallas_call(
        functools.partial(finish_kernel, count),
        out_shape=[jax.ShapeDtypeStruct(a.shape, a.dtype) for a in arrays],
        in_specs=[ANY] * count,
        out_specs=[ANY] * count,
        scratch_shapes=[pltpu.VMEM(a.shape, a.dtype) for a in arrays]
        + [pltpu.SemaphoreType.DMA((2, count))],
        compiler_params=pltpu.CompilerParams(vmem_limit_bytes=62 << 20),
        name="finish",
    )(*arrays)


def local_tiled(residual_in, cotangent, w_qkv, w_out, w_fc, w_proj, attn_bias, fc_bias, proj_bias, gains):
    shards = lax.axis_size("fsdp")
    length = shards // 4
    rows = residual_in.shape[1]
    width = w_qkv.shape[1] // 3
    share = width // 2
    unit = width // shards
    parts = w_fc.shape[1] // width
    deep = w_proj.shape[0]
    pairs = share // (2 * HD)
    low, f32 = jnp.bfloat16, jnp.float32
    vmem = pl.BlockSpec(memory_space=pltpu.VMEM)
    dma = pltpu.SemaphoreType.DMA
    small = (16, width)
    starts = [0, 0, 0, 0, 2, 2] + [3 + part for part in range(1, parts)] + [3]
    outs = [
        jax.ShapeDtypeStruct((unit, 3 * width), f32),
        jax.ShapeDtypeStruct((unit, width), f32),
        jax.ShapeDtypeStruct((unit, parts * width), f32),
        jax.ShapeDtypeStruct((deep, width), f32),
        jax.ShapeDtypeStruct(attn_bias.shape, f32),
        jax.ShapeDtypeStruct(fc_bias.shape, f32),
        jax.ShapeDtypeStruct(proj_bias.shape, f32),
        jax.ShapeDtypeStruct(gains.shape, f32),
        jax.ShapeDtypeStruct(residual_in.shape, low),
        jax.ShapeDtypeStruct(residual_in.shape, low),
        jax.ShapeDtypeStruct((3, length, 2, 2, unit, width), low),
        jax.ShapeDtypeStruct((parts, length, 2, 2, unit, width), low),
        jax.ShapeDtypeStruct((length, 2, 2, deep, width), low),
    ]
    scratch = [
        pltpu.VMEM(w_fc.shape, low),
        pltpu.VMEM(w_proj.shape, low),
        dma((2,)),
        pltpu.VMEM(small, low),
        pltpu.VMEM((length, 2, 2) + small, low),
        pltpu.VMEM((2,) + small, f32),
        pltpu.VMEM(small, f32),
        pltpu.VMEM((rows, width - 1), low),
        pltpu.VMEM((rows, width - 1), low),
        pltpu.VMEM((rows, width), low),
        pltpu.VMEM((3, 2 * rows, share), low),
        pltpu.VMEM((rows, width), low),
        pltpu.VMEM((length, 2, 2, unit, width), low),
        pltpu.VMEM((4, length, 2, 2, unit, width), low),
        pltpu.VMEM((4, rows, width), low),
        pltpu.VMEM((rows, width), f32),
        pltpu.VMEM((rows, width), f32),
        pltpu.VMEM((rows, width), f32),
        pltpu.VMEM((2, rows, share), low),
        pltpu.VMEM((rows, 3 * width), low),
        pltpu.VMEM((2 * rows, 2 * HD), f32),
        pltpu.VMEM((2 * rows, 2 * HD), f32),
        pltpu.VMEM((rows, width - 1), low),
        pltpu.VMEM((rows, width - 1), low),
        pltpu.VMEM(small, f32),
    ]
    scratch += Chunk.scratch(2 * parts + 4, length, unit, width)
    scratch += [
        pltpu.VMEM((4,) + small, f32),
        pltpu.VMEM((3,) + small, f32),
        pltpu.VMEM((length,) + small, f32),
        dma((3,)), dma((3,)), dma((length,)), dma((length,)),
    ]
    scratch += Gather.sem_shapes(length) * len(starts)
    scratch += [dma, dma, dma, dma, dma((3,)), dma((3,)), dma((pairs,)), dma((pairs,)), dma((3,)), dma((4,))]
    scratch += [dma((4,)), dma((4,)), dma((4,)), dma((4,)), dma, dma, dma((3, pairs)), dma((3, pairs))]
    results = pl.pallas_call(
        functools.partial(layer_kernel, shards, starts),
        out_shape=outs,
        in_specs=[ANY] * 6 + [vmem] * 4,
        out_specs=[vmem] * 8 + [ANY] * 5,
        scratch_shapes=scratch,
        compiler_params=pltpu.CompilerParams(
            collective_id=0, has_side_effects=True, vmem_limit_bytes=62 << 20
        ),
        name="layer",
    )(residual_in, cotangent, w_qkv, w_out, w_fc, w_proj, attn_bias, fc_bias, proj_bias, gains)
    (total_qkv, total_out, total_fc, total_proj, total_attn_bias, total_fc_bias, total_proj_bias, total_gains,
     residual_out, input_grad) = finish(results[:10])
    return (
        residual_out, input_grad, total_qkv, total_out, total_fc, total_proj,
        total_attn_bias, total_fc_bias, total_proj_bias, total_gains,
    )


def local(residual_in, cotangent, w_qkv, w_out, w_fc, w_proj, attn_bias, fc_bias, proj_bias, gains):
    arguments = (residual_in, cotangent, w_qkv, w_out, w_fc, w_proj, attn_bias, fc_bias, proj_bias, gains)
    if w_qkv.shape[0] % 16:
        return local_general(*arguments)
    return local_tiled(*arguments)


def solution(mesh):
    in_specs = (
        P("fsdp", "seq", None),
        P("fsdp", "seq", None),
        P("fsdp", None),
        P("fsdp", None),
        P("fsdp", None),
        P("fsdp", None),
        P(None, "fsdp"),
        P("fsdp"),
        P("fsdp"),
        P(None, "fsdp"),
    )
    out_specs = (
        P("fsdp", "seq", None),
        P("fsdp", "seq", None),
        P("fsdp", None),
        P("fsdp", None),
        P("fsdp", None),
        P("fsdp", None),
        P(None, "fsdp"),
        P("fsdp"),
        P("fsdp"),
        P(None, "fsdp"),
    )
    return jax.shard_map(local, mesh=mesh, in_specs=in_specs, out_specs=out_specs, check_vma=False)
```

```python
import functools

import jax
import jax.numpy as jnp
from jax import lax
from jax.experimental import pallas as pl
from jax.experimental.pallas import tpu as pltpu
from jax.sharding import PartitionSpec as P

HD = 64
EPSILON = 1e-05
MASKED = -1e30
MESH = pl.DeviceIdType.MESH
ANY = pl.BlockSpec(memory_space=pl.ANY)


class Place:
    def __init__(self, shards):
        self.length = shards // 4
        self.x = lax.axis_index("seq")
        index = lax.axis_index("fsdp")
        self.index = index
        self.core = lax.rem(index, 2)
        self.y = lax.rem(index // 2, 2)
        self.line = index // 4

    def at(self, **moved):
        x = moved.get("x", self.x)
        line = moved.get("line", self.line)
        y = moved.get("y", self.y)
        core = moved.get("core", self.core)
        return (x, (line * 2 + y) * 2 + core)

    def beside_x(self):
        return self.at(x=1 - self.x)

    def beside_y(self):
        return self.at(y=1 - self.y)

    def sibling(self):
        return self.at(core=1 - self.core)

    def above(self):
        return self.at(line=self.line + 1)

    def below(self):
        return self.at(line=self.line - 1)

    def greet(self, diagonal=False, whole_line=False):
        barrier = pltpu.get_barrier_semaphore()

        def signal(device):
            pl.semaphore_signal(barrier, inc=1, device_id=device, device_id_type=MESH)

        signal(self.beside_x())
        signal(self.beside_y())
        signal(self.sibling())
        has_below = self.line > 0
        has_above = self.line < self.length - 1
        if whole_line:
            for line in range(self.length):
                pl.when(self.line != line)(lambda line=line: signal(self.at(line=line)))
            count = 3 + self.length - 1
        else:
            pl.when(has_below)(lambda: signal(self.below()))
            pl.when(has_above)(lambda: signal(self.above()))
            count = 3 + has_below.astype(jnp.int32) + has_above.astype(jnp.int32)
        if diagonal:
            across = self.x != self.core
            pl.when(across)(lambda: signal(self.at(x=1 - self.x, core=1 - self.core)))
            count = count + across.astype(jnp.int32)
        pl.semaphore_wait(barrier, count)


def remote(src, dst, send, recv, device):
    return pltpu.make_async_remote_copy(
        src_ref=src, dst_ref=dst, send_sem=send, recv_sem=recv, device_id=device, device_id_type=MESH
    )


class PlainGather:
    def __init__(self, place, shard, out, sems):
        self.p = place
        self.shard = shard
        self.out = out
        self.rows, self.cols = shard.shape
        (self.up, self.down, self.line_in, self.ys, self.yr, self.xs, self.xr, self.ds, self.dr, self.own) = sems

    @staticmethod
    def sem_shapes(length):
        dma = pltpu.SemaphoreType.DMA
        return [dma((length,))] * 7 + [dma((3, length))] * 2 + [dma]

    def half(self, ref, which):
        width = self.cols // 2
        return ref.at[:, pl.ds(pl.multiple_of(which * width, width), width)]

    def slot(self, line, y, core):
        return self.out.at[line, y, core]

    def up_copy(self, line, src=None):
        p = self.p
        dst = self.slot(line, p.y, p.core)
        return remote(dst if src is None else src, dst, self.up.at[line], self.line_in.at[line], p.above())

    def down_copy(self, line, src=None):
        p = self.p
        dst = self.slot(line, p.y, p.core)
        return remote(dst if src is None else src, dst, self.down.at[line], self.line_in.at[line], p.below())

    def y_copy(self, line, src=None):
        p = self.p
        dst = self.half(self.slot(line, p.y, p.core), p.x)
        src = dst if src is None else self.half(src, p.x)
        return remote(src, dst, self.ys.at[line], self.yr.at[line], p.beside_y())

    def y_landing(self, line):
        p = self.p
        dst = self.half(self.slot(line, 1 - p.y, p.core), p.x)
        return remote(dst, dst, self.ys.at[line], self.yr.at[line], p.beside_y())

    def x_copy(self, line):
        p = self.p
        dst = self.half(self.slot(line, 1 - p.y, p.core), p.x)
        return remote(dst, dst, self.xs.at[line], self.xr.at[line], p.beside_x())

    def x_landing(self, line):
        p = self.p
        dst = self.half(self.slot(line, 1 - p.y, p.core), 1 - p.x)
        return remote(dst, dst, self.xs.at[line], self.xr.at[line], p.beside_x())

    def d_copy(self, kind, line, src=None, core=None):
        p = self.p
        core = p.core if core is None else core
        if kind == 0:
            dst = self.slot(line, p.y, core)
        else:
            dst = self.half(self.slot(line, 1 - p.y, core), p.x if kind == 1 else 1 - p.x)
        return remote(dst if src is None else src, dst, self.ds.at[kind, line], self.dr.at[kind, line], p.sibling())

    def own_copy(self):
        p = self.p
        return pltpu.make_async_copy(self.shard, self.slot(p.line, p.y, p.core), self.own)

    def each_at(self, distance, act):
        p = self.p
        if distance == 0:
            act(p.line, 0)
            return
        pl.when(p.line - distance >= 0)(lambda: act(p.line - distance, 1))
        pl.when(p.line + distance < p.length)(lambda: act(p.line + distance, -1))

    def arrive(self, distance):
        p = self.p

        def act(line, way):
            src = None
            if way == 0:
                src = self.shard
                self.own_copy().start()
            else:
                self.up_copy(line).wait_recv()
            if way >= 0:
                pl.when(p.line < p.length - 1)(lambda: self.up_copy(line, src).start())
            if way <= 0:
                pl.when(p.line > 0)(lambda: self.down_copy(line, src).start())
            self.y_copy(line, src).start()
            self.d_copy(0, line, src).start()

        self.each_at(distance, act)

    def arrive_y(self, distance):
        def act(line, way):
            self.y_landing(line).wait_recv()
            self.x_copy(line).start()
            self.d_copy(1, line).start()

        self.each_at(distance, act)

    def arrive_x(self, distance):
        def act(line, way):
            self.x_landing(line).wait_recv()
            self.d_copy(2, line).start()

        self.each_at(distance, act)

    def stage(self, time):
        length = self.p.length
        if 0 <= time < length:
            self.arrive(time)
        if 0 <= time - 1 < length:
            self.arrive_y(time - 1)
        if 0 <= time - 2 < length:
            self.arrive_x(time - 2)

    def stages(self):
        return self.p.length + 2

    def finish(self):
        p = self.p

        def one(line):
            for kind in range(3):
                self.d_copy(kind, line, core=1 - p.core).wait_recv()
            for kind in range(3):
                self.d_copy(kind, line).wait_send()
            self.y_copy(line).wait_send()
            self.x_copy(line).wait_send()
            pl.when((p.line >= line) & (p.line < p.length - 1))(lambda: self.up_copy(line).wait_send())
            pl.when((p.line <= line) & (p.line > 0))(lambda: self.down_copy(line).wait_send())

        for line in range(p.length):
            one(line)
        self.own_copy().wait()


def gather_kernel(shards, lag, count, *refs):
    ins, outs, rest = refs[:count], refs[count : 2 * count], refs[2 * count :]
    place = Place(shards)
    place.greet()
    per = len(PlainGather.sem_shapes(1))
    gathers = [PlainGather(place, ins[k], outs[k], rest[k * per : (k + 1) * per]) for k in range(count)]
    total = max(lag[k] + g.stages() for k, g in enumerate(gathers))
    for time in range(total):
        for k, g in enumerate(gathers):
            g.stage(time - lag[k])
    for g in gathers:
        g.finish()


def gather_all(arrays, shards, lag, collective_id):
    length = shards // 4
    out = pl.pallas_call(
        functools.partial(gather_kernel, shards, lag, len(arrays)),
        out_shape=[jax.ShapeDtypeStruct((length, 2, 2) + a.shape, a.dtype) for a in arrays],
        in_specs=[ANY] * len(arrays),
        out_specs=[ANY] * len(arrays),
        scratch_shapes=PlainGather.sem_shapes(length) * len(arrays),
        compiler_params=pltpu.CompilerParams(collective_id=collective_id, has_side_effects=True),
        name="gather_weights",
    )(*arrays)
    return [o.reshape((shards,) + a.shape) for o, a in zip(out, arrays)]


class Scatter:
    def __init__(self, place, partial, out, refs):
        self.p = place
        self.g = partial
        self.out = out
        self.rows, self.cols = out.shape
        (self.s, self.d, self.xb, self.yb, self.lo, self.hi, self.fb, self.tb,
         self.load, self.ds, self.dr, self.xs, self.xr, self.ys, self.yr,
         self.us, self.ur, self.ns, self.nr, self.fs, self.fr) = refs

    @staticmethod
    def scratch(length, rows, cols, dtype):
        dma = pltpu.SemaphoreType.DMA
        full = pltpu.VMEM((length, 2, rows, cols), dtype)
        half = pltpu.VMEM((length, rows, cols // 2), dtype)
        line = pltpu.VMEM((length, rows, cols), dtype)
        one = pltpu.VMEM((rows, cols), dtype)
        return [full, full, half, half, line, line, one, one] + [dma] * 7 + [dma((length,))] * 4 + [dma] * 2

    def half(self, which):
        width = self.cols // 2
        return pl.ds(pl.multiple_of(which * width, width), width)

    def load_copy(self):
        return pltpu.make_async_copy(self.g.at[:, :, self.p.core], self.s, self.load)

    def d_copy(self):
        p = self.p
        return remote(self.g.at[:, :, 1 - p.core], self.d, self.ds, self.dr, p.sibling())

    def x_copy(self):
        p = self.p
        src = self.s.at[:, 1 - p.y, :, self.half(1 - p.x)]
        return remote(src, self.xb, self.xs, self.xr, p.beside_x())

    def y_copy(self):
        p = self.p
        src = self.s.at[:, 1 - p.y, :, self.half(p.x)]
        return remote(src, self.yb, self.ys, self.yr, p.beside_y())

    def up_copy(self, line):
        p = self.p
        return remote(self.s.at[line, p.y], self.lo.at[line], self.us.at[line], self.ur.at[line], p.above())

    def down_copy(self, line):
        p = self.p
        return remote(self.s.at[line, p.y], self.hi.at[line], self.ns.at[line], self.nr.at[line], p.below())

    def f_copy(self):
        return remote(self.tb, self.fb, self.fs, self.fr, self.p.beside_x())

    def each(self, act):
        def body(line, carry):
            act(line)
            return carry

        lax.fori_loop(0, self.p.length, body, 0)

    def start(self):
        self.load_copy().start()
        self.d_copy().start()

    def pair(self):
        p = self.p
        self.load_copy().wait()
        self.d_copy().wait()

        def other(line):
            self.s[line, 1 - p.y] = self.s[line, 1 - p.y] + self.d[line, 1 - p.y]

        self.each(other)
        self.x_copy().start()

        def own(line):
            self.s[line, p.y] = self.s[line, p.y] + self.d[line, p.y]

        self.each(own)

    def over_x(self):
        p = self.p
        self.x_copy().wait()

        def act(line):
            cols = self.half(p.x)
            self.s[line, 1 - p.y, :, cols] = self.s[line, 1 - p.y, :, cols] + self.xb[line]

        self.each(act)
        self.y_copy().start()

    def over_y(self):
        p = self.p
        self.y_copy().wait()

        def act(line):
            cols = self.half(p.x)
            self.s[line, p.y, :, cols] = self.s[line, p.y, :, cols] + self.yb[line]

        self.each(act)

    def hop(self, step):
        p = self.p
        last = p.length - 1
        up = last - step + p.line

        def upward():
            @pl.when(p.line > 0)
            def _():
                self.up_copy(up).wait_recv()
                self.s[up, p.y] = self.s[up, p.y] + self.lo[up]

            self.up_copy(up).start()

        pl.when(p.line <= step)(upward)
        down = step - last + p.line

        def downward():
            @pl.when(p.line < last)
            def _():
                self.down_copy(down).wait_recv()
                self.s[down, p.y] = self.s[down, p.y] + self.hi[down]

            self.down_copy(down).start()

        pl.when(down >= 0)(downward)

    def total(self):
        p = self.p
        mine = p.line

        @pl.when(p.line > 0)
        def _():
            self.up_copy(mine).wait_recv()
            self.s[mine, p.y] = self.s[mine, p.y] + self.lo[mine]

        @pl.when(p.line < p.length - 1)
        def _():
            self.down_copy(mine).wait_recv()
            self.s[mine, p.y] = self.s[mine, p.y] + self.hi[mine]

        self.tb[...] = self.s[mine, p.y]
        self.f_copy().start()

    def finish(self):
        p = self.p
        self.f_copy().wait()
        self.out[...] = self.tb[...].astype(jnp.float32) + self.fb[...].astype(jnp.float32)
        for line in range(p.length):
            pl.when(line > p.line)(lambda line=line: self.up_copy(line).wait_send())
            pl.when(line < p.line)(lambda line=line: self.down_copy(line).wait_send())

    def stages(self):
        acts = [self.start, self.pair, self.over_x, self.over_y]
        acts += [functools.partial(self.hop, step) for step in range(self.p.length - 1)]
        return acts + [self.total, self.finish]


def scatter_kernel(shards, lag, count, *refs):
    ins, outs, rest = refs[:count], refs[count : 2 * count], refs[2 * count :]
    place = Place(shards)
    place.greet()
    per = len(rest) // count
    lists = [
        Scatter(place, ins[k], outs[k], rest[k * per : (k + 1) * per]).stages() for k in range(count)
    ]
    total = max(lag[k] + len(s) for k, s in enumerate(lists))
    for time in range(total):
        for k, acts in enumerate(lists):
            if 0 <= time - lag[k] < len(acts):
                acts[time - lag[k]]()


def scatter_all(arrays, shards, lag, collective_id):
    length = shards // 4
    parts = [a.reshape((length, 2, 2) + a.shape[1:]) for a in arrays]
    scratch = []
    for a in arrays:
        scratch += Scatter.scratch(length, a.shape[1], a.shape[2], a.dtype)
    return pl.pallas_call(
        functools.partial(scatter_kernel, shards, lag, len(arrays)),
        out_shape=[jax.ShapeDtypeStruct(a.shape[1:], jnp.float32) for a in arrays],
        in_specs=[ANY] * len(arrays),
        out_specs=[pl.BlockSpec(memory_space=pltpu.VMEM)] * len(arrays),
        scratch_shapes=scratch,
        compiler_params=pltpu.CompilerParams(
            collective_id=collective_id, has_side_effects=True, vmem_limit_bytes=60 << 20
        ),
        name="scatter_grads",
    )(*parts)


def rms_norm(values, gain):
    return values * lax.rsqrt(jnp.mean(values * values, axis=-1, keepdims=True) + EPSILON) * gain


def center(values):
    return values - jnp.mean(values, axis=-1, keepdims=True)


def gelu_tanh(values):
    return jax.nn.gelu(values, approximate=True)


def matmul(left, right):
    return jnp.dot(left, right, preferred_element_type=jnp.float32)


def weight_grad(inputs, grads):
    return lax.dot_general(
        inputs, grads, (((0,), (0,)), ((), ())), preferred_element_type=jnp.float32
    )


def input_grad_of(grads, weight):
    return lax.dot_general(
        grads, weight, (((1,), (1,)), ((), ())), preferred_element_type=jnp.float32
    )


def block_rows(length):
    return min(length, max(512, length // 8))


def score_block(query_block, keys_part, start, scale):
    scores = (
        jnp.einsum("qhd,khd->hqk", query_block, keys_part, preferred_element_type=jnp.float32)
        * scale
    )
    query_pos = start + jnp.arange(query_block.shape[0], dtype=jnp.int32)
    key_pos = jnp.arange(keys_part.shape[0], dtype=jnp.int32)
    allowed = query_pos[:, None] >= key_pos[None, :]
    return jnp.where(allowed[None], scores, MASKED)


def attend(queries, keys_all, values_all, scale):
    length, head_count, width = queries.shape
    block = block_rows(length)
    count = length // block
    results = []
    log_totals = []
    for index in range(count):
        start = index * block
        finish = start + block
        scores = score_block(queries[start:finish], keys_all[:finish], start, scale)
        peak = jnp.max(scores, axis=-1, keepdims=True)
        weights = jnp.exp(scores - peak)
        total = jnp.sum(weights, axis=-1, keepdims=True)
        weights = weights / total
        result = jnp.einsum(
            "hqk,khd->qhd",
            weights.astype(jnp.bfloat16),
            values_all[:finish],
            preferred_element_type=jnp.float32,
        )
        results.append(result.astype(jnp.bfloat16))
        log_totals.append((peak + jnp.log(total))[..., 0])
    joined = jnp.concatenate(results, axis=0)
    return (joined.reshape(length, head_count * width), log_totals)


def attend_back(queries, keys_all, values_all, log_totals, grad_heads, scale):
    length, head_count, width = queries.shape
    block = block_rows(length)
    count = length // block
    key_sum = jnp.zeros((length, head_count, width), jnp.float32)
    value_sum = jnp.zeros((length, head_count, width), jnp.float32)
    query_grads = []
    for index in range(count):
        start = index * block
        finish = start + block
        query_block = queries[start:finish]
        grad_block = grad_heads[start:finish]
        keys_part = keys_all[:finish]
        scores = score_block(query_block, keys_part, start, scale)
        weights = jnp.exp(scores - log_totals[index][..., None])
        grad_weights = jnp.einsum(
            "qhd,khd->hqk", grad_block, values_all[:finish], preferred_element_type=jnp.float32
        )
        inner = jnp.sum(weights * grad_weights, axis=-1, keepdims=True)
        grad_scores = (weights * (grad_weights - inner)).astype(jnp.bfloat16)
        query_grad = (
            jnp.einsum("hqk,khd->qhd", grad_scores, keys_part, preferred_element_type=jnp.float32)
            * scale
        )
        key_part = (
            jnp.einsum("hqk,qhd->khd", grad_scores, query_block, preferred_element_type=jnp.float32)
            * scale
        )
        value_part = jnp.einsum(
            "hqk,qhd->khd",
            weights.astype(jnp.bfloat16),
            grad_block,
            preferred_element_type=jnp.float32,
        )
        key_sum = key_sum.at[:finish].add(key_part)
        value_sum = value_sum.at[:finish].add(value_part)
        query_grads.append(query_grad.astype(jnp.bfloat16))
    return (
        jnp.concatenate(query_grads, axis=0),
        key_sum.astype(jnp.bfloat16),
        value_sum.astype(jnp.bfloat16),
    )


def dot_nn(left, right):
    return jnp.dot(left, right, preferred_element_type=jnp.float32)


def dot_nt(left, right):
    return lax.dot_general(
        left, right, (((1,), (1,)), ((), ())), preferred_element_type=jnp.float32
    )


def dot_tn(left, right):
    return lax.dot_general(
        left, right, (((0,), (0,)), ((), ())), preferred_element_type=jnp.float32
    )


def lane_block(index, width):
    return pl.ds(pl.multiple_of(index * width, width), width)


def unit_scale(value):
    return lax.rsqrt(jnp.mean(value * value, axis=-1, keepdims=True) + EPSILON)


def over_rows(total, block, act):
    def body(step, carry):
        act(pl.ds(pl.multiple_of(step * block, block), block))
        return carry

    lax.fori_loop(0, total // block, body, 0)


def head_mask(shape, head):
    lanes = lax.broadcasted_iota(jnp.int32, shape, 1)
    return (lanes // HD) == head


class Swap:
    def __init__(self, place, src, dst, sems):
        self.p = place
        self.src, self.dst = src, dst
        self.send, self.recv = sems

    def moved(self):
        p = self.p
        return remote(self.src, self.dst, self.send, self.recv, p.at(x=1 - p.x, core=1 - p.core))

    def kept(self):
        return pltpu.make_async_copy(self.src, self.dst, self.send)

    def start(self):
        p = self.p
        pl.when(p.x != p.core)(lambda: self.moved().start())
        pl.when(p.x == p.core)(lambda: self.kept().start())

    def wait(self):
        p = self.p
        pl.when(p.x != p.core)(lambda: self.moved().wait())
        pl.when(p.x == p.core)(lambda: self.kept().wait())


def attend_pair(qkv, pair, put):
    total = qkv.shape[1]
    block = min(256, total)
    lanes = pl.ds(pair * 2 * HD, 2 * HD)
    scale = jnp.asarray(HD ** (-0.5), jnp.bfloat16)
    zero = jnp.zeros((), jnp.bfloat16)
    rows = lax.broadcasted_iota(jnp.int32, (block, block), 0)
    cols = lax.broadcasted_iota(jnp.int32, (block, block), 1)
    allowed = rows >= cols
    for index in range(total // block):
        start = index * block
        here = pl.ds(start, block)
        query = qkv[0, here, lanes] * scale
        results = []
        for head in range(2):
            masked = jnp.where(head_mask(query.shape, head), query, zero)
            near = dot_nt(masked, qkv[1, here, lanes])
            near = jnp.where(allowed, near, MASKED)
            peak = jnp.max(near, axis=-1, keepdims=True)
            if start:
                far = dot_nt(masked, qkv[1, pl.ds(0, start), lanes])
                peak = jnp.maximum(peak, jnp.max(far, axis=-1, keepdims=True))
            near = jnp.exp(near - peak)
            total_weight = jnp.sum(near, axis=-1, keepdims=True)
            if start:
                far = jnp.exp(far - peak)
                total_weight = total_weight + jnp.sum(far, axis=-1, keepdims=True)
            share = 1.0 / total_weight
            result = dot_nn((near * share).astype(jnp.bfloat16), qkv[2, here, lanes])
            if start:
                result += dot_nn(
                    (far * share).astype(jnp.bfloat16), qkv[2, pl.ds(0, start), lanes]
                )
            results.append(result)
        merged = jnp.where(head_mask(results[0].shape, 0), results[0], results[1])
        put(start, block, merged.astype(jnp.bfloat16))


def attend_back_pair(qkv, grads, pair, key_sum, value_sum, put):
    total = qkv.shape[1]
    block = min(256, total)
    lanes = pl.ds(pair * 2 * HD, 2 * HD)
    scale = jnp.asarray(HD ** (-0.5), jnp.bfloat16)
    zero = jnp.zeros((), jnp.bfloat16)
    rows = lax.broadcasted_iota(jnp.int32, (block, block), 0)
    cols = lax.broadcasted_iota(jnp.int32, (block, block), 1)
    allowed = rows <= cols
    key_sum[...] = jnp.zeros_like(key_sum)
    value_sum[...] = jnp.zeros_like(value_sum)
    for index in range(total // block):
        start = index * block
        here = pl.ds(start, block)
        spans = [here] + ([pl.ds(0, start)] if start else [])
        query = qkv[0, here, lanes] * scale
        grad = grads[start // grads.shape[1], pl.ds(start % grads.shape[1], block), lanes]
        query_grads = []
        for head in range(2):
            mask = head_mask(query.shape, head)
            masked = jnp.where(mask, query, zero)
            grad_masked = jnp.where(mask, grad, zero)
            scores = [dot_nt(qkv[1, span, lanes], masked) for span in spans]
            scores[0] = jnp.where(allowed, scores[0], MASKED)
            peak = functools.reduce(
                jnp.maximum, [jnp.max(s, axis=0, keepdims=True) for s in scores]
            )
            weights = [jnp.exp(s - peak) for s in scores]
            sums = sum(jnp.sum(w, axis=0, keepdims=True) for w in weights)
            share = 1.0 / sums
            weights = [w * share for w in weights]
            pulled = [dot_nt(qkv[2, span, lanes], grad_masked) for span in spans]
            inner = sum(jnp.sum(w * g, axis=0, keepdims=True) for w, g in zip(weights, pulled))
            query_grad = None
            for span, w, g in zip(spans, weights, pulled):
                value_sum[span, :] += dot_nn(w.astype(jnp.bfloat16), grad_masked)
                slope = (w * (g - inner)).astype(jnp.bfloat16)
                key_sum[span, :] += dot_nn(slope, masked)
                part = dot_tn(slope, qkv[1, span, lanes])
                query_grad = part if query_grad is None else query_grad + part
            query_grads.append(query_grad)
        merged = jnp.where(head_mask(query_grads[0].shape, 0), query_grads[0], query_grads[1])
        put(0, start, block, (merged * HD ** (-0.5)).astype(jnp.bfloat16))
    half = grads.shape[1]
    for start in range(0, total, half):
        put(1, start, half, key_sum[pl.ds(start, half), :].astype(jnp.bfloat16))
        put(2, start, half, value_sum[pl.ds(start, half), :].astype(jnp.bfloat16))


class Gather:
    def __init__(self, place, shard, out, sems, split=False):
        self.p = place
        self.shard = shard
        self.out = out
        self.split = split
        self.width = shard.shape[1] // 3
        (self.up, self.down, self.line_in, self.ys, self.yr, self.xs, self.xr, self.ds, self.dr, self.own) = sems
        self.time = 0

    @staticmethod
    def sem_shapes(length):
        dma = pltpu.SemaphoreType.DMA
        return [dma((length,))] * 5 + [dma((2, length))] * 2 + [dma((4, length))] * 2 + [dma]

    def thirds(self, ref, which, count=1):
        return ref.at[:, pl.ds(pl.multiple_of(which * self.width, self.width), count * self.width)]

    def slot(self, line, y, core=None):
        return self.out.at[line, y, self.p.core if core is None else core]

    def on_line(self, ref):
        return self.thirds(ref, self.p.x, 2) if self.split else ref

    def up_copy(self, line, src=None):
        p = self.p
        dst = self.slot(line, p.y)
        src = self.on_line(dst if src is None else src)
        return remote(src, self.on_line(dst), self.up.at[line], self.line_in.at[line], p.above())

    def down_copy(self, line, src=None):
        p = self.p
        dst = self.slot(line, p.y)
        src = self.on_line(dst if src is None else src)
        return remote(src, self.on_line(dst), self.down.at[line], self.line_in.at[line], p.below())

    def y_copy(self, line, src=None):
        p = self.p
        dst = self.slot(line, p.y)
        src = self.thirds(dst if src is None else src, p.x, 2)
        return remote(src, self.thirds(dst, p.x, 2), self.ys.at[line], self.yr.at[line], p.beside_y())

    def y_landing(self, line):
        p = self.p
        dst = self.thirds(self.slot(line, 1 - p.y), p.x, 2)
        return remote(dst, dst, self.ys.at[line], self.yr.at[line], p.beside_y())

    def x_copy(self, line, own):
        p = self.p
        dst = self.thirds(self.slot(line, p.y if own else 1 - p.y), 2 * p.x)
        return remote(dst, dst, self.xs.at[int(own), line], self.xr.at[int(own), line], p.beside_x())

    def x_landing(self, line, own):
        p = self.p
        dst = self.thirds(self.slot(line, p.y if own else 1 - p.y), 2 * (1 - p.x))
        return remote(dst, dst, self.xs.at[int(own), line], self.xr.at[int(own), line], p.beside_x())

    def d_copy(self, kind, line, whole=False, src=None, core=None):
        p = self.p
        dst = self.slot(line, p.y if kind in (0, 3) else 1 - p.y, core)
        src = dst if src is None else src
        if kind == 0 and not whole:
            src, dst = self.on_line(src), self.on_line(dst)
        if kind == 1:
            src, dst = self.thirds(src, p.x, 2), self.thirds(dst, p.x, 2)
        if kind >= 2:
            src, dst = self.thirds(src, 2 * (1 - p.x)), self.thirds(dst, 2 * (1 - p.x))
        return remote(src, dst, self.ds.at[kind, line], self.dr.at[kind, line], p.sibling())

    def own_copy(self):
        p = self.p
        return pltpu.make_async_copy(self.shard, self.slot(p.line, p.y), self.own)

    def each_at(self, distance, act):
        p = self.p
        if distance == 0:
            act(p.line, 0)
            return
        pl.when(p.line - distance >= 0)(lambda: act(p.line - distance, 1))
        pl.when(p.line + distance < p.length)(lambda: act(p.line + distance, -1))

    def arrive(self, distance):
        p = self.p

        def act(line, way):
            src = None
            if way == 0:
                src = self.shard
                self.own_copy().start()
            else:
                self.up_copy(line).wait_recv()
            if way >= 0:
                pl.when(p.line < p.length - 1)(lambda: self.up_copy(line, src).start())
            if way <= 0:
                pl.when(p.line > 0)(lambda: self.down_copy(line, src).start())
            self.y_copy(line, src).start()
            if way and self.split:
                self.x_copy(line, True).start()
            self.d_copy(0, line, way == 0, src).start()

        self.each_at(distance, act)

    def arrive_y(self, distance):
        def act(line, way):
            self.y_landing(line).wait_recv()
            self.x_copy(line, False).start()
            self.d_copy(1, line).start()
            if way and self.split:
                self.x_landing(line, True).wait_recv()
                self.d_copy(3, line).start()

        self.each_at(distance, act)

    def arrive_x(self, distance):
        def act(line, way):
            self.x_landing(line, False).wait_recv()
            self.d_copy(2, line).start()

        self.each_at(distance, act)

    def stage(self):
        time, length = self.time, self.p.length
        self.time += 1
        if time < length:
            self.arrive(time)
        if 0 <= time - 1 < length:
            self.arrive_y(time - 1)
        if 0 <= time - 2 < length:
            self.arrive_x(time - 2)

    def under_way(self):
        return self.time < self.p.length + 2

    def take(self):
        p = self.p
        self.own_copy().wait()
        for line in range(p.length):
            for kind in range(3):
                if kind or not self.split:
                    self.d_copy(kind, line, core=1 - p.core).wait_recv()
            if self.split:
                pl.when(p.line == line)(lambda line=line: self.d_copy(0, line, True, core=1 - p.core).wait_recv())

                @pl.when(p.line != line)
                def _(line=line):
                    self.d_copy(0, line, core=1 - p.core).wait_recv()
                    self.d_copy(3, line, core=1 - p.core).wait_recv()

    def close(self):
        p = self.p
        for line in range(p.length):
            for kind in range(3):
                if kind or not self.split:
                    self.d_copy(kind, line).wait_send()
            if self.split:
                pl.when(p.line == line)(lambda line=line: self.d_copy(0, line, True).wait_send())

                @pl.when(p.line != line)
                def _(line=line):
                    self.d_copy(0, line).wait_send()
                    self.d_copy(3, line).wait_send()
                    self.x_copy(line, True).wait_send()

            self.y_copy(line).wait_send()
            self.x_copy(line, False).wait_send()
            pl.when((p.line >= line) & (p.line < p.length - 1))(lambda line=line: self.up_copy(line).wait_send())
            pl.when((p.line <= line) & (p.line > 0))(lambda line=line: self.down_copy(line).wait_send())


class Supply:
    def __init__(self, gathers, starts):
        self.entries = list(zip(starts, gathers))
        self.time = 0

    def tick(self):
        for start, gather in self.entries:
            if start <= self.time and gather.under_way():
                gather.stage()
        self.time += 1

    def need(self, gather):
        while gather.under_way():
            self.tick()
        gather.take()


class Chunk:
    def __init__(self, place, index, refs, store):
        self.p = place
        self.store = store
        (grads, self_d, xy, lo, hi, tb, fb, ds, dr, xs, xr, ys, yr, us, ur, ns, nr, fs, fr) = refs
        self.mine, self.other = grads.at[index, 0], grads.at[index, 1]
        self.d, self.xy = self_d.at[index], xy.at[index]
        third = xy.shape[-1] // 3
        self.xb, self.yb = self.xy.at[:, :, pl.ds(0, third)], self.xy.at[:, :, pl.ds(third, 2 * third)]
        self.lo, self.hi = lo.at[index], hi.at[index]
        self.tb, self.fb = tb.at[index], fb.at[index]
        self.sems = [s.at[index] for s in (ds, dr, xs, xr, ys, yr)]
        self.us, self.ur, self.ns, self.nr = us.at[index], ur.at[index], ns.at[index], nr.at[index]
        self.fs, self.fr = fs.at[index], fr.at[index]

    @staticmethod
    def scratch(count, length, rows, cols):
        low = jnp.bfloat16
        dma = pltpu.SemaphoreType.DMA
        return [
            pltpu.VMEM((count, 2, length, 2, rows, cols), low),
            pltpu.VMEM((count, length, 2, rows, cols), low),
            pltpu.VMEM((count, length, rows, cols), low),
            pltpu.VMEM((count, length - 1, rows, cols), low),
            pltpu.VMEM((count, length - 1, rows, cols), low),
            pltpu.VMEM((count, rows, cols), low),
            pltpu.VMEM((count, rows, cols), low),
        ] + [dma((count,))] * 6 + [dma((count, length))] * 4 + [dma((count,))] * 2

    def third(self, which, count=1):
        width = self.tb.shape[1] // 3
        return pl.ds(pl.multiple_of(which * width, width), count * width)

    def d_copy(self):
        return remote(self.other, self.d, self.sems[0], self.sems[1], self.p.sibling())

    def x_copy(self):
        p = self.p
        src = self.mine.at[:, 1 - p.y, :, self.third(2 * (1 - p.x))]
        return remote(src, self.xb, self.sems[2], self.sems[3], p.beside_x())

    def y_copy(self):
        p = self.p
        src = self.mine.at[:, 1 - p.y, :, self.third(p.x, 2)]
        return remote(src, self.yb, self.sems[4], self.sems[5], p.beside_y())

    def up_copy(self, line):
        p = self.p
        return remote(self.mine.at[line, p.y], self.lo.at[line - 1], self.us.at[line], self.ur.at[line], p.above())

    def down_copy(self, line):
        p = self.p
        return remote(self.mine.at[line, p.y], self.hi.at[line], self.ns.at[line], self.nr.at[line], p.below())

    def f_copy(self):
        return remote(self.tb, self.fb, self.fs, self.fr, self.p.beside_x())

    def each(self, act):
        def body(line, carry):
            act(line)
            return carry

        lax.fori_loop(0, self.p.length, body, 0)

    def start(self):
        self.d_copy().start()

    def pair(self):
        p = self.p
        self.d_copy().wait()

        def other(line):
            self.mine[line, 1 - p.y] = self.mine[line, 1 - p.y] + self.d[line, 1 - p.y]

        self.each(other)
        self.x_copy().start()

        def own(line):
            self.mine[line, p.y] = self.mine[line, p.y] + self.d[line, p.y]

        self.each(own)

    def over_x(self):
        p = self.p
        self.x_copy().wait()

        def act(line):
            cols = self.third(2 * p.x)
            self.mine[line, 1 - p.y, :, cols] = self.mine[line, 1 - p.y, :, cols] + self.xb[line]

        self.each(act)
        self.y_copy().start()

    def over_y(self):
        p = self.p
        self.y_copy().wait()

        def act(line):
            cols = self.third(p.x, 2)
            self.mine[line, p.y, :, cols] = self.mine[line, p.y, :, cols] + self.yb[line]

        self.each(act)
        self.hop(0)

    def take_low(self, line):
        self.up_copy(line).wait_recv()
        self.mine[line, self.p.y] = self.mine[line, self.p.y] + self.lo[line - 1]

    def take_high(self, line):
        self.down_copy(line).wait_recv()
        self.mine[line, self.p.y] = self.mine[line, self.p.y] + self.hi[line]

    def hop(self, step):
        p = self.p
        last = p.length - 1
        up = last - step + p.line

        def upward():
            pl.when(p.line > 0)(lambda: self.take_low(up))
            self.up_copy(up).start()

        pl.when(p.line <= step)(upward)
        down = step - last + p.line

        def downward():
            pl.when(p.line < last)(lambda: self.take_high(down))
            self.down_copy(down).start()

        pl.when(down >= 0)(downward)

    def total(self):
        p = self.p
        mine = p.line
        pl.when(mine > 0)(lambda: self.take_low(mine))
        pl.when(mine < p.length - 1)(lambda: self.take_high(mine))
        self.tb[...] = self.mine[mine, p.y]
        self.f_copy().start()

    def finish(self):
        p = self.p
        self.f_copy().wait()
        self.store(self.tb[...].astype(jnp.float32) + self.fb[...].astype(jnp.float32))
        for line in range(p.length - 1):
            pl.when(line + 1 > p.line)(lambda line=line: self.up_copy(line + 1).wait_send())
            pl.when(line < p.line)(lambda line=line: self.down_copy(line).wait_send())

    def acts(self):
        hops = [functools.partial(self.hop, step) for step in range(1, self.p.length - 1)]
        return [self.pair, self.over_x, self.over_y] + hops + [self.total, self.finish]


class Train:
    def __init__(self):
        self.running = []

    def add(self, acts):
        self.running.append(list(acts))

    def tick(self):
        for acts in reversed(self.running):
            acts.pop(0)()
        self.running = [acts for acts in self.running if acts]

    def drain(self):
        while self.running:
            self.tick()


class SmallSum:
    def __init__(self, place, refs):
        self.p = place
        self.stages, self.got, self.lines, self.ss, self.sr, self.ls, self.lr = refs

    def copy(self, step):
        p = self.p
        goal = [p.sibling, p.beside_x, p.beside_y][step]()
        return remote(self.stages.at[step], self.got.at[step], self.ss.at[step], self.sr.at[step], goal)

    def line_copy(self, line):
        p = self.p
        return remote(
            self.stages.at[3], self.lines.at[p.line], self.ls.at[line], self.lr.at[p.line], p.at(line=line)
        )

    def line_landing(self, line):
        p = self.p
        return remote(self.stages.at[3], self.lines.at[line], self.ls.at[line], self.lr.at[line], p.at(line=line))

    def begin(self):
        self.copy(0).start()

    def step(self, index):
        p = self.p
        self.copy(index).wait()
        self.stages[index + 1] = self.stages[index] + self.got[index]
        if index < 2:
            self.copy(index + 1).start()
            return
        for line in range(p.length):
            pl.when(p.line != line)(lambda line=line: self.line_copy(line).start())
        self.lines[p.line] = self.stages[3]

    def end(self, store):
        p = self.p
        for line in range(p.length):
            pl.when(p.line != line)(lambda line=line: self.line_copy(line).wait_send())
            pl.when(p.line != line)(lambda line=line: self.line_landing(line).wait_recv())
        total = self.lines[0]
        for line in range(1, p.length):
            total = total + self.lines[line]
        store(total)

    def acts(self, store):
        return [functools.partial(self.step, k) for k in range(3)] + [lambda: self.end(store)]


def gelu_pair(hidden):
    ratio = (2.0 / 3.141592653589793) ** 0.5
    square = hidden * hidden
    curve = jnp.tanh(ratio * (hidden + 0.044715 * (square * hidden)))
    cdf = 0.5 * (1.0 + curve)
    slope = cdf + hidden * (0.5 * (1.0 - curve * curve)) * (ratio * (1.0 + (3.0 * 0.044715) * square))
    return hidden * cdf, slope


def norm_back(value, gain, grad):
    scale = unit_scale(value)
    unit = value * scale
    lifted = grad * gain
    pull = jnp.mean(lifted * unit, axis=-1, keepdims=True)
    return scale * (lifted - unit * pull), grad * unit


def column_sum(value):
    return jnp.sum(value.astype(jnp.float32), axis=0, keepdims=True)


def swap_halves(value):
    shards = lax.axis_size("fsdp")
    pairs = []
    for x in range(2):
        for index in range(shards):
            core = index % 2
            goal = (x, index) if core == x else (1 - x, index ^ 1)
            pairs.append((x * shards + index, goal[0] * shards + goal[1]))
    return lax.ppermute(value, ("seq", "fsdp"), pairs)


def pair_all_to_all(value, split_axis, concat_axis):
    shards = lax.axis_size("fsdp")
    groups = [[k, k + 1] for k in range(0, shards, 2)]
    return lax.all_to_all(
        value, "fsdp", split_axis=split_axis, concat_axis=concat_axis, axis_index_groups=groups, tiled=True
    )


def pack_rows(parts, width):
    rows = [jnp.pad(p, ((0, 0), (0, width - p.shape[1]))) for p in parts]
    packed = jnp.concatenate(rows, axis=0)
    return jnp.pad(packed, ((0, 16 - packed.shape[0]), (0, 0)))


def local_general(residual_in, cotangent, w_qkv, w_out, w_fc, w_proj, attn_bias, fc_bias, proj_bias, gains):
    shards = lax.axis_size("fsdp")
    tok_rows = residual_in.shape[1]
    model_width = w_qkv.shape[1] // 3
    hidden_width = w_fc.shape[1]
    unit = gains.shape[1]
    share = model_width // 2
    head_count = share // HD
    scale = HD ** (-0.5)
    small = pack_rows([attn_bias, gains, proj_bias[None], fc_bias[None]], 256)
    compact = swap_halves(residual_in[0]).astype(jnp.float32)
    upstream = swap_halves(cotangent[0]).astype(jnp.float32)
    qkv_w, small_all, out_w, fc_w, proj_w = gather_all(
        [w_qkv, small, w_out, w_fc, w_proj], shards, [0, 0, 2, 3, 5], 0
    )
    qkv_w = qkv_w.reshape(model_width, 3 * model_width)
    out_w = out_w.reshape(model_width, model_width)
    fc_w = fc_w.reshape(model_width, hidden_width)
    proj_w = proj_w.reshape(hidden_width, model_width)
    vectors = small_all[:, :6, :unit].transpose(1, 0, 2).reshape(6, model_width).astype(jnp.float32)
    bias_all, gain_all, proj_b = vectors[:3], vectors[3:5], vectors[5]
    fc_b = small_all[:, 6, : fc_bias.shape[0]].reshape(hidden_width).astype(jnp.float32)
    full = jnp.concatenate([compact, -jnp.sum(compact, axis=-1, keepdims=True)], axis=-1)
    normed = rms_norm(full, gain_all[0]).astype(jnp.bfloat16)
    bias_qkv = jnp.concatenate([bias_all[0], jnp.zeros_like(bias_all[0]), bias_all[1]])
    projected = (matmul(normed, qkv_w) + bias_qkv).astype(jnp.bfloat16)
    by_heads = pair_all_to_all(projected.reshape(tok_rows, 3, 2, share), 2, 0)
    length = by_heads.shape[0]
    queries = by_heads[:, 0, 0].reshape(length, head_count, HD)
    keys_all = by_heads[:, 1, 0].reshape(length, head_count, HD)
    values_all = by_heads[:, 2, 0].reshape(length, head_count, HD)
    attended, log_totals = attend(queries, keys_all, values_all, scale)
    mixed = pair_all_to_all(attended.reshape(length, 1, share), 0, 1)
    mixed = mixed.reshape(tok_rows, model_width)
    branch = matmul(mixed, out_w) + bias_all[2]
    middle = full + center(branch)
    normed_two = rms_norm(middle, gain_all[1]).astype(jnp.bfloat16)
    hidden = matmul(normed_two, fc_w) + fc_b
    activated = gelu_tanh(hidden).astype(jnp.bfloat16)
    branch_two = matmul(activated, proj_w) + proj_b
    final = middle + center(branch_two)
    residual_out = swap_halves(final[:, :-1].astype(jnp.bfloat16))[None]
    grad_final = jnp.concatenate([upstream, jnp.zeros((tok_rows, 1), jnp.float32)], axis=-1)
    grad_branch_two = center(grad_final).astype(jnp.bfloat16)
    grad_proj = weight_grad(activated, grad_branch_two)
    grad_proj_bias = jnp.sum(grad_branch_two.astype(jnp.float32), axis=0)
    grad_activated = input_grad_of(grad_branch_two, proj_w)
    gelu_pull = jax.vjp(gelu_tanh, hidden)[1]
    grad_hidden = gelu_pull(grad_activated)[0].astype(jnp.bfloat16)
    grad_fc = weight_grad(normed_two, grad_hidden)
    grad_fc_bias = jnp.sum(grad_hidden.astype(jnp.float32), axis=0)
    grad_normed_two = input_grad_of(grad_hidden, fc_w)
    second_pull = jax.vjp(rms_norm, middle, gain_all[1])[1]
    grad_middle_norm, grad_gain_two = second_pull(grad_normed_two)
    grad_middle = grad_final + grad_middle_norm
    grad_branch = center(grad_middle).astype(jnp.bfloat16)
    grad_out = weight_grad(mixed, grad_branch)
    grad_out_bias = jnp.sum(grad_branch.astype(jnp.float32), axis=0)
    grad_mixed = input_grad_of(grad_branch, out_w).astype(jnp.bfloat16)
    grad_heads = pair_all_to_all(grad_mixed.reshape(tok_rows, 2, share), 1, 0)
    grad_heads = grad_heads.reshape(length, head_count, HD)
    grad_queries, grad_keys, grad_values = attend_back(
        queries, keys_all, values_all, log_totals, grad_heads, scale
    )
    stacked = jnp.stack([grad_queries, grad_keys, grad_values], axis=1).reshape(length, 3, 1, share)
    grad_projected = pair_all_to_all(stacked, 0, 2)
    grad_projected = grad_projected.reshape(tok_rows, 3 * model_width)
    grad_qkv = weight_grad(normed, grad_projected)
    column_sums = jnp.sum(grad_projected.astype(jnp.float32), axis=0)
    grad_normed = input_grad_of(grad_projected, qkv_w)
    first_pull = jax.vjp(rms_norm, full, gain_all[0])[1]
    grad_full_norm, grad_gain_one = first_pull(grad_normed)
    grad_full = grad_middle + grad_full_norm
    input_grad = swap_halves((grad_full[:, :-1] - grad_full[:, -1:]).astype(jnp.bfloat16))[None]
    rows = jnp.stack(
        [
            column_sums[:model_width],
            column_sums[2 * model_width :],
            grad_out_bias,
            grad_gain_one,
            grad_gain_two,
            grad_proj_bias,
        ]
    )
    rows = rows.reshape(6, shards, unit).transpose(1, 0, 2)
    last = grad_fc_bias.reshape(shards, 1, fc_bias.shape[0])
    grad_small = jnp.concatenate(
        [
            jnp.pad(rows, ((0, 0), (0, 0), (0, 256 - unit))),
            jnp.pad(last, ((0, 0), (0, 9), (0, 256 - fc_bias.shape[0]))),
        ],
        axis=1,
    )

    def split(grad):
        return grad.astype(jnp.bfloat16).reshape(shards, grad.shape[0] // shards, grad.shape[1])

    total_proj, total_fc, total_out, total_qkv, total_small = scatter_all(
        [split(grad_proj), split(grad_fc), split(grad_out), split(grad_qkv), grad_small.astype(jnp.bfloat16)],
        shards,
        [0, 1, 2, 3, 3],
        1,
    )
    return (
        residual_out,
        input_grad,
        total_qkv,
        total_out,
        total_fc,
        total_proj,
        total_small[:3, :unit],
        total_small[6, : fc_bias.shape[0]],
        total_small[5, :unit],
        total_small[3:5, :unit],
    )


def layer_kernel(shards, starts, *refs):
    (resid, cot, w_qkv, w_out, w_fc, w_proj, attn_bias, fc_bias, proj_bias, gains,
     total_qkv, total_out, total_fc, total_proj, total_attn_bias, total_fc_bias, total_proj_bias, total_gains,
     resid_o, input_o, qkv_o, fc_o, proj_o,
     fc_own, proj_own, fetch, own_small, small_w, spread, vec, rs, cs, normed, heads, mixed,
     wo, tiles, work, middle, acc, gn, got, gproj, key_sum, value_sum, ro, ig, sg, *rest) = refs
    chunk_refs, rest = rest[:19], rest[19:]
    small_refs, rest = rest[:7], rest[7:]
    place = Place(shards)
    low = jnp.bfloat16
    rows, width = mixed.shape
    share = width // 2
    unit = width // shards
    parts = fc_o.shape[0]
    deep = total_proj.shape[0]
    span = 2 * HD
    pairs = share // span
    block = min(256, rows)
    per = len(Gather.sem_shapes(1))

    def columns(ref, part):
        return ref.at[:, pl.ds(part * width, width)]

    gathers = []

    def gather(src, dst, split=False):
        nonlocal rest
        item = Gather(place, src, dst, rest[:per], split)
        rest = rest[per:]
        gathers.append(item)
        return item

    qkv_in = [gather(columns(w_qkv, part), tiles.at[part]) for part in range(3)]
    small_in = gather(own_small, small_w)
    out_in = gather(w_out, wo)
    fc_in = [gather(columns(fc_own, part), fc_o.at[part]) for part in range(parts)]
    proj_in = gather(proj_own, proj_o, True)
    own_loads = [
        pltpu.make_async_copy(w_fc, fc_own, fetch.at[0]),
        pltpu.make_async_copy(w_proj, proj_own, fetch.at[1]),
    ]
    for load in own_loads:
        load.start()
    supply = Supply(gathers, starts)
    (si_s, si_r, sc_s, sc_r, ex_s, ex_r, at_s, at_r, ks, wsem, ro_s, ro_r, ig_s, ig_r,
     gm_s, gm_r, gp_s, gp_r) = rest
    swap_in = Swap(place, resid.at[0], rs, (si_s, si_r))
    swap_cot = Swap(place, cot.at[0], cs, (sc_s, sc_r))

    spread[...] = jnp.zeros_like(spread)
    spread[0, 0:3, 0:unit] = attn_bias[...].astype(jnp.float32)
    spread[0, 3:5, 0:unit] = gains[...].astype(jnp.float32)
    spread[0, 5:6, 0:unit] = proj_bias[...].reshape(1, unit).astype(jnp.float32)
    wide = fc_bias.shape[0]
    in_row = width // wide
    for part in range(parts):
        spread[1, 6 + part : 7 + part, 0:wide] = fc_bias[...].reshape(1, wide).astype(jnp.float32)
    moved = pltpu.roll(spread[0], place.index * unit, 1)
    hidden_rows = pltpu.roll(spread[1], lax.rem(place.index, in_row) * wide, 1)
    row_ids = lax.broadcasted_iota(jnp.int32, moved.shape, 0)
    moved = jnp.where(row_ids < 6, moved, jnp.where(row_ids == 6 + place.index // in_row, hidden_rows, 0.0))
    own_small[...] = moved.astype(low)

    place.greet(diagonal=True, whole_line=True)
    supply.tick()
    for load in own_loads:
        load.wait()
    swap_in.start()
    supply.need(small_in)
    swap_cot.start()
    vec[...] = jnp.sum(small_w[...].astype(jnp.float32), axis=(0, 1, 2))
    swap_in.wait()

    def whole(here):
        value = rs[here, :].astype(jnp.float32)
        return jnp.concatenate([value, -jnp.sum(value, axis=-1, keepdims=True)], axis=1)

    def normalize(here):
        full = whole(here)
        normed[here, :] = (full * unit_scale(full) * vec[3:4, :]).astype(low)

    over_rows(rows, 128, normalize)
    for item in qkv_in:
        supply.need(item)

    flat = tiles.reshape(4, width, width)
    out_flat = wo.reshape(width, width)
    keep = [pltpu.make_async_copy(tiles.at[part], qkv_o.at[part], ks.at[part]) for part in range(3)]
    for copy in keep:
        copy.start()
    my_rows = pl.ds(pl.multiple_of(place.core * rows, rows), rows)

    def exchange(part):
        src = work.at[part, :, pl.ds(0, share)]
        return remote(src, heads.at[part, my_rows], ex_s.at[part], ex_r.at[part], place.sibling())

    def project(part, group):
        result = dot_nn(normed[...], flat[part, :, lane_block(group, share)])
        if part != 1:
            bias = part // 2
            result = result + vec[bias : bias + 1, lane_block(group, share)]
        return result.astype(low)

    for part in range(3):
        work[part, :, pl.ds(0, share)] = project(part, 1 - place.core)
        exchange(part).start()
    supply.tick()
    for part in range(3):
        heads[part, my_rows, :] = project(part, place.core)
    supply.tick()
    for part in range(3):
        exchange(part).wait()

    def my_pair(pair):
        return pl.ds(pl.multiple_of(place.core * share + pair * span, span), span)

    def back(pair):
        src = got.at[1 - place.core, :, pl.ds(pair * span, span)]
        return remote(src, mixed.at[:, my_pair(pair)], at_s.at[pair], at_r.at[pair], place.sibling())

    for pair in range(pairs):
        lanes = pl.ds(pair * span, span)

        def put_result(start, size, value):
            got[start // rows, pl.ds(start % rows, size), lanes] = value

        attend_pair(heads, pair, put_result)
        back(pair).start()
        mixed[:, my_pair(pair)] = got[place.core, :, lanes]
        supply.tick()
    for copy in keep:
        copy.wait()
    for item in qkv_in:
        item.close()

    train = Train()

    def fc_load(tile):
        return pltpu.make_async_copy(fc_o.at[tile], tiles.at[tile % 2], wsem.at[tile % 2])

    def proj_load(tile):
        src = proj_o.reshape(parts, width, width).at[tile]
        return pltpu.make_async_copy(src, flat.at[2 + tile % 2], wsem.at[2 + tile % 2])

    def qkv_load(part):
        return pltpu.make_async_copy(qkv_o.at[part], tiles.at[part], wsem.at[part])

    sg[...] = jnp.zeros_like(sg)

    def put_qkv(part):
        def store(value):
            total_qkv[:, pl.ds(part * width, width)] = value
        return store

    def put_fc(tile):
        def store(value):
            total_fc[:, pl.ds(tile * width, width)] = value
        return store

    def put_proj(part):
        def store(value):
            total_proj[pl.ds(part * unit, unit), :] = value
        return store

    def put_out(value):
        total_out[...] = value

    stores = [put_fc(k) for k in range(parts)] + [put_proj(k) for k in range(parts)]
    stores += [put_out] + [put_qkv(k) for k in range(3)]
    chunks = [Chunk(place, k, chunk_refs, store) for k, store in enumerate(stores)]
    fc_chunks, proj_chunks = chunks[:parts], chunks[parts : 2 * parts]
    out_chunk, qkv_chunks = chunks[2 * parts], chunks[2 * parts + 1 :]
    grads = chunk_refs[0]

    def keep_rows(index, first, value):
        value = value.astype(low)
        for k in range(value.shape[0] // unit):
            shard = first + k
            side = lax.rem(place.core + shard % 2, 2)
            grads[index, side, shard // 4, (shard // 2) % 2] = value[k * unit : (k + 1) * unit]

    def weight_grad_chunk(index, left, right):
        for part in range(2):
            lanes = pl.ds(part * share, share)
            keep_rows(index, part * (shards // 2), dot_tn(left[:, lanes], right))
        chunks[index].start()

    act_ref, slope_ref, n2, g2 = work.at[0], work.at[1], work.at[2], work.at[3]
    supply.need(out_in)
    for pair in range(pairs):
        back(pair).wait()
    swap_cot.wait()

    def upstream(here):
        value = cs[here, :].astype(jnp.float32)
        return jnp.concatenate([value, jnp.zeros((value.shape[0], 1), jnp.float32)], axis=1)

    def enter(here):
        branch = dot_nn(mixed[here, :], out_flat[...]) + vec[2:3, :]
        value = whole(here) + branch - jnp.mean(branch, axis=-1, keepdims=True)
        middle[here, :] = value
        n2[here, :] = (value * unit_scale(value) * vec[4:5, :]).astype(low)
        grad = upstream(here)
        grad = (grad - jnp.mean(grad, axis=-1, keepdims=True)).astype(low)
        g2[here, :] = grad
        sg[5:6, :] += column_sum(grad)

    over_rows(rows, block, enter)
    supply.need(fc_in[0])
    fc_load(0).start()
    supply.need(proj_in)
    proj_load(0).start()
    proj_load(1).start()

    for tile in range(parts):
        if tile:
            supply.need(fc_in[tile])
            fc_load(tile).start()
        fc_load(tile).wait()
        proj_load(tile).wait()
        fc_tile, proj_tile = flat.at[tile % 2], flat.at[2 + tile % 2]

        def feed(here):
            hidden = dot_nn(n2[here, :], fc_tile[...]) + vec[6 + tile : 7 + tile, :]
            value, slope = gelu_pair(hidden)
            value = value.astype(low)
            act_ref[here, :] = value
            grad = (dot_nt(g2[here, :], proj_tile[...]) * slope).astype(low)
            slope_ref[here, :] = grad
            sg[6 + tile : 7 + tile, :] += column_sum(grad)

        def carry_on(here):
            forward = dot_nn(act_ref[here, :], proj_tile[...])
            backward = dot_nt(slope_ref[here, :], fc_tile[...])
            if tile == 0:
                acc[here, :] = forward
                gn[here, :] = backward
            else:
                acc[here, :] += forward
                gn[here, :] += backward

        over_rows(rows, block, feed)
        weight_grad_chunk(tile, n2, slope_ref[...])
        train.add(fc_chunks[tile].acts())
        over_rows(rows, block, carry_on)
        if tile + 2 < parts:
            proj_load(tile + 2).start()
        for part in range(2):
            lanes = pl.ds(part * share, share)
            value = dot_tn(act_ref[:, lanes], g2[...])
            first = (tile * width + part * share) // deep
            for k in range(share // deep):
                for q in range(parts):
                    at = k * deep + q * unit
                    keep_rows(parts + q, first + k, value[at : at + unit])
        train.tick()

    for item in proj_chunks:
        item.start()

    def leave(here):
        branch = acc[here, :] + vec[5:6, :]
        value = middle[here, :]
        final = value + branch - jnp.mean(branch, axis=-1, keepdims=True)
        ro[here, :] = final[:, : width - 1].astype(low)
        pull, terms = norm_back(value, vec[4:5, :], gn[here, :])
        sg[4:5, :] += jnp.sum(terms, axis=0, keepdims=True)
        grad = upstream(here) + pull
        acc[here, :] = grad
        grad = (grad - jnp.mean(grad, axis=-1, keepdims=True)).astype(low)
        g2[here, :] = grad
        sg[2:3, :] += column_sum(grad)

    over_rows(rows, block // 2, leave)
    pieces = 4

    def piece(src, dst, sems, k):
        here = pl.ds(k * (rows // pieces), rows // pieces)
        return Swap(place, src.at[here], dst.at[0, here], (sems[0].at[k], sems[1].at[k]))

    swap_out = [piece(ro, resid_o, (ro_s, ro_r), k) for k in range(pieces)]
    swap_back = [piece(ig, input_o, (ig_s, ig_r), k) for k in range(pieces)]
    swap_out[0].start()
    train.add(proj_chunks[0].acts())
    train.tick()

    def mixed_grad(group):
        lanes = pl.ds(pl.multiple_of(group * share, 128), share)
        return dot_nt(g2[...], out_flat[lanes, :]).astype(low)

    n2[:, pl.ds(0, share)] = mixed_grad(1 - place.core)
    give = remote(n2.at[:, pl.ds(0, share)], got.at[place.core], gm_s, gm_r, place.sibling())
    give.start()
    got[place.core] = mixed_grad(place.core)
    weight_grad_chunk(2 * parts, mixed, g2[...])
    train.add(proj_chunks[1].acts())
    swap_out[1].start()
    for part in range(3):
        qkv_load(part).start()
    train.tick()
    give.wait()

    def send(part, pair):
        lanes = pl.multiple_of((1 - place.core) * share + pair * span, span)
        src = work.at[part, :, pl.ds(lanes, span)]
        at = pl.multiple_of((part * 2 + place.core) * share + pair * span, span)
        return remote(src, gproj.at[:, pl.ds(at, span)], gp_s.at[part, pair], gp_r.at[part, pair], place.sibling())

    waiting = proj_chunks[2:] + [out_chunk]
    for pair in range(pairs):
        for item in waiting[: -(-len(waiting) // (pairs - pair))]:
            train.add(item.acts())
            waiting.remove(item)

        def put(part, start, size, value):
            lanes = pl.ds(start // rows * share + pair * span, span)
            work[part, pl.ds(start % rows, size), lanes] = value

        attend_back_pair(heads, got, pair, key_sum, value_sum, put)
        if pair + 2 < pieces:
            swap_out[pair + 2].start()
        train.tick()
        for part in range(3):
            send(part, pair).start()
            at = pl.multiple_of((part * 2 + place.core) * share + pair * span, span)
            gproj[:, pl.ds(at, span)] = work[part, :, my_pair(pair)]
    for pair in range(pairs):
        for part in range(3):
            send(part, pair).wait()

    for part in range(3):
        lanes = pl.ds(part * width, width)
        weight_grad_chunk(2 * parts + 1 + part, normed, gproj[:, lanes])
        train.add(qkv_chunks[part].acts())
        train.tick()

    for part in range(3):
        qkv_load(part).wait()

    def last(here):
        grad = dot_nt(gproj[here, pl.ds(0, width)], flat[0])
        grad += dot_nt(gproj[here, pl.ds(width, width)], flat[1])
        grad += dot_nt(gproj[here, pl.ds(2 * width, width)], flat[2])
        sg[0:1, :] += column_sum(gproj[here, pl.ds(0, width)])
        sg[1:2, :] += column_sum(gproj[here, pl.ds(2 * width, width)])
        pull, terms = norm_back(whole(here), vec[3:4, :], grad)
        sg[3:4, :] += jnp.sum(terms, axis=0, keepdims=True)
        grad = acc[here, :] + pull
        ig[here, :] = (grad[:, : width - 1] - grad[:, width - 1 :]).astype(low)

    for k in range(pieces):
        last(pl.ds(k * (rows // pieces), rows // pieces))
        swap_back[k].start()
        if k % 2:
            train.tick()
    small = SmallSum(place, small_refs)
    small_refs[0][0] = sg[...]
    small.begin()

    def put_small(value):
        mine = pltpu.roll(value, width - place.index * unit, 1)
        total_attn_bias[...] = mine[0:3, :unit]
        total_gains[...] = mine[3:5, :unit]
        total_proj_bias[...] = mine[5:6, :unit].reshape(unit)
        hidden = pltpu.roll(value, width - lax.rem(place.index, in_row) * wide, 1)[:, :wide]
        hidden_ids = lax.broadcasted_iota(jnp.int32, hidden.shape, 0)
        hidden = jnp.where(hidden_ids == 6 + place.index // in_row, hidden, 0.0)
        total_fc_bias[...] = jnp.sum(hidden, axis=0, keepdims=True).reshape(wide)

    train.add(small.acts(put_small))
    train.drain()
    for item in gathers[3:]:
        item.close()
    for swap in swap_out + swap_back:
        swap.wait()


def finish_kernel(count, *refs):
    ins, outs, held = refs[:count], refs[count : 2 * count], refs[2 * count : 3 * count]
    sems = refs[3 * count]
    loads = [pltpu.make_async_copy(ins[k], held[k], sems.at[0, k]) for k in range(count)]
    stores = [pltpu.make_async_copy(held[k], outs[k], sems.at[1, k]) for k in range(count)]
    for load in loads:
        load.start()
    for load, store in zip(loads, stores):
        load.wait()
        store.start()
    for store in stores:
        store.wait()


def finish(arrays):
    count = len(arrays)
    return pl.pallas_call(
        functools.partial(finish_kernel, count),
        out_shape=[jax.ShapeDtypeStruct(a.shape, a.dtype) for a in arrays],
        in_specs=[ANY] * count,
        out_specs=[ANY] * count,
        scratch_shapes=[pltpu.VMEM(a.shape, a.dtype) for a in arrays]
        + [pltpu.SemaphoreType.DMA((2, count))],
        compiler_params=pltpu.CompilerParams(vmem_limit_bytes=62 << 20),
        name="finish",
    )(*arrays)


def local_tiled(residual_in, cotangent, w_qkv, w_out, w_fc, w_proj, attn_bias, fc_bias, proj_bias, gains):
    shards = lax.axis_size("fsdp")
    length = shards // 4
    rows = residual_in.shape[1]
    width = w_qkv.shape[1] // 3
    share = width // 2
    unit = width // shards
    parts = w_fc.shape[1] // width
    deep = w_proj.shape[0]
    pairs = share // (2 * HD)
    low, f32 = jnp.bfloat16, jnp.float32
    vmem = pl.BlockSpec(memory_space=pltpu.VMEM)
    dma = pltpu.SemaphoreType.DMA
    small = (16, width)
    starts = [0, 0, 0, 0, 5] + [5 + part for part in range(parts)] + [5]
    outs = [
        jax.ShapeDtypeStruct((unit, 3 * width), f32),
        jax.ShapeDtypeStruct((unit, width), f32),
        jax.ShapeDtypeStruct((unit, parts * width), f32),
        jax.ShapeDtypeStruct((deep, width), f32),
        jax.ShapeDtypeStruct(attn_bias.shape, f32),
        jax.ShapeDtypeStruct(fc_bias.shape, f32),
        jax.ShapeDtypeStruct(proj_bias.shape, f32),
        jax.ShapeDtypeStruct(gains.shape, f32),
        jax.ShapeDtypeStruct(residual_in.shape, low),
        jax.ShapeDtypeStruct(residual_in.shape, low),
        jax.ShapeDtypeStruct((3, length, 2, 2, unit, width), low),
        jax.ShapeDtypeStruct((parts, length, 2, 2, unit, width), low),
        jax.ShapeDtypeStruct((length, 2, 2, deep, width), low),
    ]
    scratch = [
        pltpu.VMEM(w_fc.shape, low),
        pltpu.VMEM(w_proj.shape, low),
        dma((2,)),
        pltpu.VMEM(small, low),
        pltpu.VMEM((length, 2, 2) + small, low),
        pltpu.VMEM((2,) + small, f32),
        pltpu.VMEM(small, f32),
        pltpu.VMEM((rows, width - 1), low),
        pltpu.VMEM((rows, width - 1), low),
        pltpu.VMEM((rows, width), low),
        pltpu.VMEM((3, 2 * rows, share), low),
        pltpu.VMEM((rows, width), low),
        pltpu.VMEM((length, 2, 2, unit, width), low),
        pltpu.VMEM((4, length, 2, 2, unit, width), low),
        pltpu.VMEM((4, rows, width), low),
        pltpu.VMEM((rows, width), f32),
        pltpu.VMEM((rows, width), f32),
        pltpu.VMEM((rows, width), f32),
        pltpu.VMEM((2, rows, share), low),
        pltpu.VMEM((rows, 3 * width), low),
        pltpu.VMEM((2 * rows, 2 * HD), f32),
        pltpu.VMEM((2 * rows, 2 * HD), f32),
        pltpu.VMEM((rows, width - 1), low),
        pltpu.VMEM((rows, width - 1), low),
        pltpu.VMEM(small, f32),
    ]
    scratch += Chunk.scratch(2 * parts + 4, length, unit, width)
    scratch += [
        pltpu.VMEM((4,) + small, f32),
        pltpu.VMEM((3,) + small, f32),
        pltpu.VMEM((length,) + small, f32),
        dma((3,)), dma((3,)), dma((length,)), dma((length,)),
    ]
    scratch += Gather.sem_shapes(length) * len(starts)
    scratch += [dma, dma, dma, dma, dma((3,)), dma((3,)), dma((pairs,)), dma((pairs,)), dma((3,)), dma((4,))]
    scratch += [dma((4,)), dma((4,)), dma((4,)), dma((4,)), dma, dma, dma((3, pairs)), dma((3, pairs))]
    results = pl.pallas_call(
        functools.partial(layer_kernel, shards, starts),
        out_shape=outs,
        in_specs=[ANY] * 6 + [vmem] * 4,
        out_specs=[vmem] * 8 + [ANY] * 5,
        scratch_shapes=scratch,
        compiler_params=pltpu.CompilerParams(
            collective_id=0, has_side_effects=True, vmem_limit_bytes=62 << 20
        ),
        name="layer",
    )(residual_in, cotangent, w_qkv, w_out, w_fc, w_proj, attn_bias, fc_bias, proj_bias, gains)
    (total_qkv, total_out, total_fc, total_proj, total_attn_bias, total_fc_bias, total_proj_bias, total_gains,
     residual_out, input_grad) = finish(results[:10])
    return (
        residual_out, input_grad, total_qkv, total_out, total_fc, total_proj,
        total_attn_bias, total_fc_bias, total_proj_bias, total_gains,
    )


def local(residual_in, cotangent, w_qkv, w_out, w_fc, w_proj, attn_bias, fc_bias, proj_bias, gains):
    arguments = (residual_in, cotangent, w_qkv, w_out, w_fc, w_proj, attn_bias, fc_bias, proj_bias, gains)
    if w_qkv.shape[0] % 16:
        return local_general(*arguments)
    return local_tiled(*arguments)


def solution(mesh):
    in_specs = (
        P("fsdp", "seq", None),
        P("fsdp", "seq", None),
        P("fsdp", None),
        P("fsdp", None),
        P("fsdp", None),
        P("fsdp", None),
        P(None, "fsdp"),
        P("fsdp"),
        P("fsdp"),
        P(None, "fsdp"),
    )
    out_specs = (
        P("fsdp", "seq", None),
        P("fsdp", "seq", None),
        P("fsdp", None),
        P("fsdp", None),
        P("fsdp", None),
        P("fsdp", None),
        P(None, "fsdp"),
        P("fsdp"),
        P("fsdp"),
        P(None, "fsdp"),
    )
    return jax.shard_map(local, mesh=mesh, in_specs=in_specs, out_specs=out_specs, check_vma=False)
```

```python
import functools

import jax
import jax.numpy as jnp
from jax import lax
from jax.experimental import pallas as pl
from jax.experimental.pallas import tpu as pltpu
from jax.sharding import PartitionSpec as P

HD = 64
EPSILON = 1e-05
MASKED = -1e30
MESH = pl.DeviceIdType.MESH
ANY = pl.BlockSpec(memory_space=pl.ANY)


class Place:
    def __init__(self, shards):
        self.length = shards // 4
        self.x = lax.axis_index("seq")
        index = lax.axis_index("fsdp")
        self.index = index
        self.core = lax.rem(index, 2)
        self.y = lax.rem(index // 2, 2)
        self.line = index // 4

    def at(self, **moved):
        x = moved.get("x", self.x)
        line = moved.get("line", self.line)
        y = moved.get("y", self.y)
        core = moved.get("core", self.core)
        return (x, (line * 2 + y) * 2 + core)

    def beside_x(self):
        return self.at(x=1 - self.x)

    def beside_y(self):
        return self.at(y=1 - self.y)

    def sibling(self):
        return self.at(core=1 - self.core)

    def above(self):
        return self.at(line=self.line + 1)

    def below(self):
        return self.at(line=self.line - 1)

    def greet(self, diagonal=False, whole_line=False):
        barrier = pltpu.get_barrier_semaphore()

        def signal(device):
            pl.semaphore_signal(barrier, inc=1, device_id=device, device_id_type=MESH)

        signal(self.beside_x())
        signal(self.beside_y())
        signal(self.sibling())
        has_below = self.line > 0
        has_above = self.line < self.length - 1
        if whole_line:
            for line in range(self.length):
                pl.when(self.line != line)(lambda line=line: signal(self.at(line=line)))
            count = 3 + self.length - 1
        else:
            pl.when(has_below)(lambda: signal(self.below()))
            pl.when(has_above)(lambda: signal(self.above()))
            count = 3 + has_below.astype(jnp.int32) + has_above.astype(jnp.int32)
        if diagonal:
            across = self.x != self.core
            pl.when(across)(lambda: signal(self.at(x=1 - self.x, core=1 - self.core)))
            count = count + across.astype(jnp.int32)
        pl.semaphore_wait(barrier, count)


def remote(src, dst, send, recv, device):
    return pltpu.make_async_remote_copy(
        src_ref=src, dst_ref=dst, send_sem=send, recv_sem=recv, device_id=device, device_id_type=MESH
    )


class PlainGather:
    def __init__(self, place, shard, out, sems):
        self.p = place
        self.shard = shard
        self.out = out
        self.rows, self.cols = shard.shape
        (self.up, self.down, self.line_in, self.ys, self.yr, self.xs, self.xr, self.ds, self.dr, self.own) = sems

    @staticmethod
    def sem_shapes(length):
        dma = pltpu.SemaphoreType.DMA
        return [dma((length,))] * 7 + [dma((3, length))] * 2 + [dma]

    def half(self, ref, which):
        width = self.cols // 2
        return ref.at[:, pl.ds(pl.multiple_of(which * width, width), width)]

    def slot(self, line, y, core):
        return self.out.at[line, y, core]

    def up_copy(self, line, src=None):
        p = self.p
        dst = self.slot(line, p.y, p.core)
        return remote(dst if src is None else src, dst, self.up.at[line], self.line_in.at[line], p.above())

    def down_copy(self, line, src=None):
        p = self.p
        dst = self.slot(line, p.y, p.core)
        return remote(dst if src is None else src, dst, self.down.at[line], self.line_in.at[line], p.below())

    def y_copy(self, line, src=None):
        p = self.p
        dst = self.half(self.slot(line, p.y, p.core), p.x)
        src = dst if src is None else self.half(src, p.x)
        return remote(src, dst, self.ys.at[line], self.yr.at[line], p.beside_y())

    def y_landing(self, line):
        p = self.p
        dst = self.half(self.slot(line, 1 - p.y, p.core), p.x)
        return remote(dst, dst, self.ys.at[line], self.yr.at[line], p.beside_y())

    def x_copy(self, line):
        p = self.p
        dst = self.half(self.slot(line, 1 - p.y, p.core), p.x)
        return remote(dst, dst, self.xs.at[line], self.xr.at[line], p.beside_x())

    def x_landing(self, line):
        p = self.p
        dst = self.half(self.slot(line, 1 - p.y, p.core), 1 - p.x)
        return remote(dst, dst, self.xs.at[line], self.xr.at[line], p.beside_x())

    def d_copy(self, kind, line, src=None, core=None):
        p = self.p
        core = p.core if core is None else core
        if kind == 0:
            dst = self.slot(line, p.y, core)
        else:
            dst = self.half(self.slot(line, 1 - p.y, core), p.x if kind == 1 else 1 - p.x)
        return remote(dst if src is None else src, dst, self.ds.at[kind, line], self.dr.at[kind, line], p.sibling())

    def own_copy(self):
        p = self.p
        return pltpu.make_async_copy(self.shard, self.slot(p.line, p.y, p.core), self.own)

    def each_at(self, distance, act):
        p = self.p
        if distance == 0:
            act(p.line, 0)
            return
        pl.when(p.line - distance >= 0)(lambda: act(p.line - distance, 1))
        pl.when(p.line + distance < p.length)(lambda: act(p.line + distance, -1))

    def arrive(self, distance):
        p = self.p

        def act(line, way):
            src = None
            if way == 0:
                src = self.shard
                self.own_copy().start()
            else:
                self.up_copy(line).wait_recv()
            if way >= 0:
                pl.when(p.line < p.length - 1)(lambda: self.up_copy(line, src).start())
            if way <= 0:
                pl.when(p.line > 0)(lambda: self.down_copy(line, src).start())
            self.y_copy(line, src).start()
            self.d_copy(0, line, src).start()

        self.each_at(distance, act)

    def arrive_y(self, distance):
        def act(line, way):
            self.y_landing(line).wait_recv()
            self.x_copy(line).start()
            self.d_copy(1, line).start()

        self.each_at(distance, act)

    def arrive_x(self, distance):
        def act(line, way):
            self.x_landing(line).wait_recv()
            self.d_copy(2, line).start()

        self.each_at(distance, act)

    def stage(self, time):
        length = self.p.length
        if 0 <= time < length:
            self.arrive(time)
        if 0 <= time - 1 < length:
            self.arrive_y(time - 1)
        if 0 <= time - 2 < length:
            self.arrive_x(time - 2)

    def stages(self):
        return self.p.length + 2

    def finish(self):
        p = self.p

        def one(line):
            for kind in range(3):
                self.d_copy(kind, line, core=1 - p.core).wait_recv()
            for kind in range(3):
                self.d_copy(kind, line).wait_send()
            self.y_copy(line).wait_send()
            self.x_copy(line).wait_send()
            pl.when((p.line >= line) & (p.line < p.length - 1))(lambda: self.up_copy(line).wait_send())
            pl.when((p.line <= line) & (p.line > 0))(lambda: self.down_copy(line).wait_send())

        for line in range(p.length):
            one(line)
        self.own_copy().wait()


def gather_kernel(shards, lag, count, *refs):
    ins, outs, rest = refs[:count], refs[count : 2 * count], refs[2 * count :]
    place = Place(shards)
    place.greet()
    per = len(PlainGather.sem_shapes(1))
    gathers = [PlainGather(place, ins[k], outs[k], rest[k * per : (k + 1) * per]) for k in range(count)]
    total = max(lag[k] + g.stages() for k, g in enumerate(gathers))
    for time in range(total):
        for k, g in enumerate(gathers):
            g.stage(time - lag[k])
    for g in gathers:
        g.finish()


def gather_all(arrays, shards, lag, collective_id):
    length = shards // 4
    out = pl.pallas_call(
        functools.partial(gather_kernel, shards, lag, len(arrays)),
        out_shape=[jax.ShapeDtypeStruct((length, 2, 2) + a.shape, a.dtype) for a in arrays],
        in_specs=[ANY] * len(arrays),
        out_specs=[ANY] * len(arrays),
        scratch_shapes=PlainGather.sem_shapes(length) * len(arrays),
        compiler_params=pltpu.CompilerParams(collective_id=collective_id, has_side_effects=True),
        name="gather_weights",
    )(*arrays)
    return [o.reshape((shards,) + a.shape) for o, a in zip(out, arrays)]


class Scatter:
    def __init__(self, place, partial, out, refs):
        self.p = place
        self.g = partial
        self.out = out
        self.rows, self.cols = out.shape
        (self.s, self.d, self.xb, self.yb, self.lo, self.hi, self.fb, self.tb,
         self.load, self.ds, self.dr, self.xs, self.xr, self.ys, self.yr,
         self.us, self.ur, self.ns, self.nr, self.fs, self.fr) = refs

    @staticmethod
    def scratch(length, rows, cols, dtype):
        dma = pltpu.SemaphoreType.DMA
        full = pltpu.VMEM((length, 2, rows, cols), dtype)
        half = pltpu.VMEM((length, rows, cols // 2), dtype)
        line = pltpu.VMEM((length, rows, cols), dtype)
        one = pltpu.VMEM((rows, cols), dtype)
        return [full, full, half, half, line, line, one, one] + [dma] * 7 + [dma((length,))] * 4 + [dma] * 2

    def half(self, which):
        width = self.cols // 2
        return pl.ds(pl.multiple_of(which * width, width), width)

    def load_copy(self):
        return pltpu.make_async_copy(self.g.at[:, :, self.p.core], self.s, self.load)

    def d_copy(self):
        p = self.p
        return remote(self.g.at[:, :, 1 - p.core], self.d, self.ds, self.dr, p.sibling())

    def x_copy(self):
        p = self.p
        src = self.s.at[:, 1 - p.y, :, self.half(1 - p.x)]
        return remote(src, self.xb, self.xs, self.xr, p.beside_x())

    def y_copy(self):
        p = self.p
        src = self.s.at[:, 1 - p.y, :, self.half(p.x)]
        return remote(src, self.yb, self.ys, self.yr, p.beside_y())

    def up_copy(self, line):
        p = self.p
        return remote(self.s.at[line, p.y], self.lo.at[line], self.us.at[line], self.ur.at[line], p.above())

    def down_copy(self, line):
        p = self.p
        return remote(self.s.at[line, p.y], self.hi.at[line], self.ns.at[line], self.nr.at[line], p.below())

    def f_copy(self):
        return remote(self.tb, self.fb, self.fs, self.fr, self.p.beside_x())

    def each(self, act):
        def body(line, carry):
            act(line)
            return carry

        lax.fori_loop(0, self.p.length, body, 0)

    def start(self):
        self.load_copy().start()
        self.d_copy().start()

    def pair(self):
        p = self.p
        self.load_copy().wait()
        self.d_copy().wait()

        def other(line):
            self.s[line, 1 - p.y] = self.s[line, 1 - p.y] + self.d[line, 1 - p.y]

        self.each(other)
        self.x_copy().start()

        def own(line):
            self.s[line, p.y] = self.s[line, p.y] + self.d[line, p.y]

        self.each(own)

    def over_x(self):
        p = self.p
        self.x_copy().wait()

        def act(line):
            cols = self.half(p.x)
            self.s[line, 1 - p.y, :, cols] = self.s[line, 1 - p.y, :, cols] + self.xb[line]

        self.each(act)
        self.y_copy().start()

    def over_y(self):
        p = self.p
        self.y_copy().wait()

        def act(line):
            cols = self.half(p.x)
            self.s[line, p.y, :, cols] = self.s[line, p.y, :, cols] + self.yb[line]

        self.each(act)

    def hop(self, step):
        p = self.p
        last = p.length - 1
        up = last - step + p.line

        def upward():
            @pl.when(p.line > 0)
            def _():
                self.up_copy(up).wait_recv()
                self.s[up, p.y] = self.s[up, p.y] + self.lo[up]

            self.up_copy(up).start()

        pl.when(p.line <= step)(upward)
        down = step - last + p.line

        def downward():
            @pl.when(p.line < last)
            def _():
                self.down_copy(down).wait_recv()
                self.s[down, p.y] = self.s[down, p.y] + self.hi[down]

            self.down_copy(down).start()

        pl.when(down >= 0)(downward)

    def total(self):
        p = self.p
        mine = p.line

        @pl.when(p.line > 0)
        def _():
            self.up_copy(mine).wait_recv()
            self.s[mine, p.y] = self.s[mine, p.y] + self.lo[mine]

        @pl.when(p.line < p.length - 1)
        def _():
            self.down_copy(mine).wait_recv()
            self.s[mine, p.y] = self.s[mine, p.y] + self.hi[mine]

        self.tb[...] = self.s[mine, p.y]
        self.f_copy().start()

    def finish(self):
        p = self.p
        self.f_copy().wait()
        self.out[...] = self.tb[...].astype(jnp.float32) + self.fb[...].astype(jnp.float32)
        for line in range(p.length):
            pl.when(line > p.line)(lambda line=line: self.up_copy(line).wait_send())
            pl.when(line < p.line)(lambda line=line: self.down_copy(line).wait_send())

    def stages(self):
        acts = [self.start, self.pair, self.over_x, self.over_y]
        acts += [functools.partial(self.hop, step) for step in range(self.p.length - 1)]
        return acts + [self.total, self.finish]


def scatter_kernel(shards, lag, count, *refs):
    ins, outs, rest = refs[:count], refs[count : 2 * count], refs[2 * count :]
    place = Place(shards)
    place.greet()
    per = len(rest) // count
    lists = [
        Scatter(place, ins[k], outs[k], rest[k * per : (k + 1) * per]).stages() for k in range(count)
    ]
    total = max(lag[k] + len(s) for k, s in enumerate(lists))
    for time in range(total):
        for k, acts in enumerate(lists):
            if 0 <= time - lag[k] < len(acts):
                acts[time - lag[k]]()


def scatter_all(arrays, shards, lag, collective_id):
    length = shards // 4
    parts = [a.reshape((length, 2, 2) + a.shape[1:]) for a in arrays]
    scratch = []
    for a in arrays:
        scratch += Scatter.scratch(length, a.shape[1], a.shape[2], a.dtype)
    return pl.pallas_call(
        functools.partial(scatter_kernel, shards, lag, len(arrays)),
        out_shape=[jax.ShapeDtypeStruct(a.shape[1:], jnp.float32) for a in arrays],
        in_specs=[ANY] * len(arrays),
        out_specs=[pl.BlockSpec(memory_space=pltpu.VMEM)] * len(arrays),
        scratch_shapes=scratch,
        compiler_params=pltpu.CompilerParams(
            collective_id=collective_id, has_side_effects=True, vmem_limit_bytes=60 << 20
        ),
        name="scatter_grads",
    )(*parts)


def rms_norm(values, gain):
    return values * lax.rsqrt(jnp.mean(values * values, axis=-1, keepdims=True) + EPSILON) * gain


def center(values):
    return values - jnp.mean(values, axis=-1, keepdims=True)


def gelu_tanh(values):
    return jax.nn.gelu(values, approximate=True)


def matmul(left, right):
    return jnp.dot(left, right, preferred_element_type=jnp.float32)


def weight_grad(inputs, grads):
    return lax.dot_general(
        inputs, grads, (((0,), (0,)), ((), ())), preferred_element_type=jnp.float32
    )


def input_grad_of(grads, weight):
    return lax.dot_general(
        grads, weight, (((1,), (1,)), ((), ())), preferred_element_type=jnp.float32
    )


def block_rows(length):
    return min(length, max(512, length // 8))


def score_block(query_block, keys_part, start, scale):
    scores = (
        jnp.einsum("qhd,khd->hqk", query_block, keys_part, preferred_element_type=jnp.float32)
        * scale
    )
    query_pos = start + jnp.arange(query_block.shape[0], dtype=jnp.int32)
    key_pos = jnp.arange(keys_part.shape[0], dtype=jnp.int32)
    allowed = query_pos[:, None] >= key_pos[None, :]
    return jnp.where(allowed[None], scores, MASKED)


def attend(queries, keys_all, values_all, scale):
    length, head_count, width = queries.shape
    block = block_rows(length)
    count = length // block
    results = []
    log_totals = []
    for index in range(count):
        start = index * block
        finish = start + block
        scores = score_block(queries[start:finish], keys_all[:finish], start, scale)
        peak = jnp.max(scores, axis=-1, keepdims=True)
        weights = jnp.exp(scores - peak)
        total = jnp.sum(weights, axis=-1, keepdims=True)
        weights = weights / total
        result = jnp.einsum(
            "hqk,khd->qhd",
            weights.astype(jnp.bfloat16),
            values_all[:finish],
            preferred_element_type=jnp.float32,
        )
        results.append(result.astype(jnp.bfloat16))
        log_totals.append((peak + jnp.log(total))[..., 0])
    joined = jnp.concatenate(results, axis=0)
    return (joined.reshape(length, head_count * width), log_totals)


def attend_back(queries, keys_all, values_all, log_totals, grad_heads, scale):
    length, head_count, width = queries.shape
    block = block_rows(length)
    count = length // block
    key_sum = jnp.zeros((length, head_count, width), jnp.float32)
    value_sum = jnp.zeros((length, head_count, width), jnp.float32)
    query_grads = []
    for index in range(count):
        start = index * block
        finish = start + block
        query_block = queries[start:finish]
        grad_block = grad_heads[start:finish]
        keys_part = keys_all[:finish]
        scores = score_block(query_block, keys_part, start, scale)
        weights = jnp.exp(scores - log_totals[index][..., None])
        grad_weights = jnp.einsum(
            "qhd,khd->hqk", grad_block, values_all[:finish], preferred_element_type=jnp.float32
        )
        inner = jnp.sum(weights * grad_weights, axis=-1, keepdims=True)
        grad_scores = (weights * (grad_weights - inner)).astype(jnp.bfloat16)
        query_grad = (
            jnp.einsum("hqk,khd->qhd", grad_scores, keys_part, preferred_element_type=jnp.float32)
            * scale
        )
        key_part = (
            jnp.einsum("hqk,qhd->khd", grad_scores, query_block, preferred_element_type=jnp.float32)
            * scale
        )
        value_part = jnp.einsum(
            "hqk,qhd->khd",
            weights.astype(jnp.bfloat16),
            grad_block,
            preferred_element_type=jnp.float32,
        )
        key_sum = key_sum.at[:finish].add(key_part)
        value_sum = value_sum.at[:finish].add(value_part)
        query_grads.append(query_grad.astype(jnp.bfloat16))
    return (
        jnp.concatenate(query_grads, axis=0),
        key_sum.astype(jnp.bfloat16),
        value_sum.astype(jnp.bfloat16),
    )


def dot_nn(left, right):
    return jnp.dot(left, right, preferred_element_type=jnp.float32)


def dot_nt(left, right):
    return lax.dot_general(
        left, right, (((1,), (1,)), ((), ())), preferred_element_type=jnp.float32
    )


def dot_tn(left, right):
    return lax.dot_general(
        left, right, (((0,), (0,)), ((), ())), preferred_element_type=jnp.float32
    )


def lane_block(index, width):
    return pl.ds(pl.multiple_of(index * width, width), width)


def unit_scale(value):
    return lax.rsqrt(jnp.mean(value * value, axis=-1, keepdims=True) + EPSILON)


def over_rows(total, block, act):
    def body(step, carry):
        act(pl.ds(pl.multiple_of(step * block, block), block))
        return carry

    lax.fori_loop(0, total // block, body, 0)


def head_mask(shape, head):
    lanes = lax.broadcasted_iota(jnp.int32, shape, 1)
    return (lanes // HD) == head


class Swap:
    def __init__(self, place, src, dst, sems):
        self.p = place
        self.src, self.dst = src, dst
        self.send, self.recv = sems

    def moved(self):
        p = self.p
        return remote(self.src, self.dst, self.send, self.recv, p.at(x=1 - p.x, core=1 - p.core))

    def kept(self):
        return pltpu.make_async_copy(self.src, self.dst, self.send)

    def start(self):
        p = self.p
        pl.when(p.x != p.core)(lambda: self.moved().start())
        pl.when(p.x == p.core)(lambda: self.kept().start())

    def wait(self):
        p = self.p
        pl.when(p.x != p.core)(lambda: self.moved().wait())
        pl.when(p.x == p.core)(lambda: self.kept().wait())


def attend_pair(qkv, pair, put):
    total = qkv.shape[1]
    block = min(256, total)
    lanes = pl.ds(pair * 2 * HD, 2 * HD)
    scale = jnp.asarray(HD ** (-0.5), jnp.bfloat16)
    zero = jnp.zeros((), jnp.bfloat16)
    rows = lax.broadcasted_iota(jnp.int32, (block, block), 0)
    cols = lax.broadcasted_iota(jnp.int32, (block, block), 1)
    allowed = rows >= cols
    for index in range(total // block):
        start = index * block
        here = pl.ds(start, block)
        query = qkv[0, here, lanes] * scale
        results = []
        for head in range(2):
            masked = jnp.where(head_mask(query.shape, head), query, zero)
            near = dot_nt(masked, qkv[1, here, lanes])
            near = jnp.where(allowed, near, MASKED)
            peak = jnp.max(near, axis=-1, keepdims=True)
            if start:
                far = dot_nt(masked, qkv[1, pl.ds(0, start), lanes])
                peak = jnp.maximum(peak, jnp.max(far, axis=-1, keepdims=True))
            near = jnp.exp(near - peak)
            total_weight = jnp.sum(near, axis=-1, keepdims=True)
            if start:
                far = jnp.exp(far - peak)
                total_weight = total_weight + jnp.sum(far, axis=-1, keepdims=True)
            share = 1.0 / total_weight
            result = dot_nn((near * share).astype(jnp.bfloat16), qkv[2, here, lanes])
            if start:
                result += dot_nn(
                    (far * share).astype(jnp.bfloat16), qkv[2, pl.ds(0, start), lanes]
                )
            results.append(result)
        merged = jnp.where(head_mask(results[0].shape, 0), results[0], results[1])
        put(start, block, merged.astype(jnp.bfloat16))


def attend_back_pair(qkv, grads, pair, key_sum, value_sum, put):
    total = qkv.shape[1]
    block = min(256, total)
    lanes = pl.ds(pair * 2 * HD, 2 * HD)
    scale = jnp.asarray(HD ** (-0.5), jnp.bfloat16)
    zero = jnp.zeros((), jnp.bfloat16)
    rows = lax.broadcasted_iota(jnp.int32, (block, block), 0)
    cols = lax.broadcasted_iota(jnp.int32, (block, block), 1)
    allowed = rows <= cols
    key_sum[...] = jnp.zeros_like(key_sum)
    value_sum[...] = jnp.zeros_like(value_sum)
    for index in range(total // block):
        start = index * block
        here = pl.ds(start, block)
        spans = [here] + ([pl.ds(0, start)] if start else [])
        query = qkv[0, here, lanes] * scale
        grad = grads[start // grads.shape[1], pl.ds(start % grads.shape[1], block), lanes]
        query_grads = []
        for head in range(2):
            mask = head_mask(query.shape, head)
            masked = jnp.where(mask, query, zero)
            grad_masked = jnp.where(mask, grad, zero)
            scores = [dot_nt(qkv[1, span, lanes], masked) for span in spans]
            scores[0] = jnp.where(allowed, scores[0], MASKED)
            peak = functools.reduce(
                jnp.maximum, [jnp.max(s, axis=0, keepdims=True) for s in scores]
            )
            weights = [jnp.exp(s - peak) for s in scores]
            sums = sum(jnp.sum(w, axis=0, keepdims=True) for w in weights)
            share = 1.0 / sums
            weights = [w * share for w in weights]
            pulled = [dot_nt(qkv[2, span, lanes], grad_masked) for span in spans]
            inner = sum(jnp.sum(w * g, axis=0, keepdims=True) for w, g in zip(weights, pulled))
            query_grad = None
            for span, w, g in zip(spans, weights, pulled):
                value_sum[span, :] += dot_nn(w.astype(jnp.bfloat16), grad_masked)
                slope = (w * (g - inner)).astype(jnp.bfloat16)
                key_sum[span, :] += dot_nn(slope, masked)
                part = dot_tn(slope, qkv[1, span, lanes])
                query_grad = part if query_grad is None else query_grad + part
            query_grads.append(query_grad)
        merged = jnp.where(head_mask(query_grads[0].shape, 0), query_grads[0], query_grads[1])
        put(0, start, block, (merged * HD ** (-0.5)).astype(jnp.bfloat16))
    half = grads.shape[1]
    for start in range(0, total, half):
        put(1, start, half, key_sum[pl.ds(start, half), :].astype(jnp.bfloat16))
        put(2, start, half, value_sum[pl.ds(start, half), :].astype(jnp.bfloat16))


class Gather:
    def __init__(self, place, shard, out, sems, split=False):
        self.p = place
        self.shard = shard
        self.out = out
        self.split = split
        self.width = shard.shape[1] // 3
        (self.up, self.down, self.line_in, self.ys, self.yr, self.xs, self.xr, self.ds, self.dr, self.own) = sems
        self.time = 0

    @staticmethod
    def sem_shapes(length):
        dma = pltpu.SemaphoreType.DMA
        return [dma((length,))] * 5 + [dma((2, length))] * 2 + [dma((4, length))] * 2 + [dma]

    def thirds(self, ref, which, count=1):
        return ref.at[:, pl.ds(pl.multiple_of(which * self.width, self.width), count * self.width)]

    def slot(self, line, y, core=None):
        return self.out.at[line, y, self.p.core if core is None else core]

    def on_line(self, ref):
        return self.thirds(ref, self.p.x, 2) if self.split else ref

    def up_copy(self, line, src=None):
        p = self.p
        dst = self.slot(line, p.y)
        src = self.on_line(dst if src is None else src)
        return remote(src, self.on_line(dst), self.up.at[line], self.line_in.at[line], p.above())

    def down_copy(self, line, src=None):
        p = self.p
        dst = self.slot(line, p.y)
        src = self.on_line(dst if src is None else src)
        return remote(src, self.on_line(dst), self.down.at[line], self.line_in.at[line], p.below())

    def y_copy(self, line, src=None):
        p = self.p
        dst = self.slot(line, p.y)
        src = self.thirds(dst if src is None else src, p.x, 2)
        return remote(src, self.thirds(dst, p.x, 2), self.ys.at[line], self.yr.at[line], p.beside_y())

    def y_landing(self, line):
        p = self.p
        dst = self.thirds(self.slot(line, 1 - p.y), p.x, 2)
        return remote(dst, dst, self.ys.at[line], self.yr.at[line], p.beside_y())

    def x_copy(self, line, own):
        p = self.p
        dst = self.thirds(self.slot(line, p.y if own else 1 - p.y), 2 * p.x)
        return remote(dst, dst, self.xs.at[int(own), line], self.xr.at[int(own), line], p.beside_x())

    def x_landing(self, line, own):
        p = self.p
        dst = self.thirds(self.slot(line, p.y if own else 1 - p.y), 2 * (1 - p.x))
        return remote(dst, dst, self.xs.at[int(own), line], self.xr.at[int(own), line], p.beside_x())

    def d_copy(self, kind, line, whole=False, src=None, core=None):
        p = self.p
        dst = self.slot(line, p.y if kind in (0, 3) else 1 - p.y, core)
        src = dst if src is None else src
        if kind == 0 and not whole:
            src, dst = self.on_line(src), self.on_line(dst)
        if kind == 1:
            src, dst = self.thirds(src, p.x, 2), self.thirds(dst, p.x, 2)
        if kind >= 2:
            src, dst = self.thirds(src, 2 * (1 - p.x)), self.thirds(dst, 2 * (1 - p.x))
        return remote(src, dst, self.ds.at[kind, line], self.dr.at[kind, line], p.sibling())

    def own_copy(self):
        p = self.p
        return pltpu.make_async_copy(self.shard, self.slot(p.line, p.y), self.own)

    def each_at(self, distance, act):
        p = self.p
        if distance == 0:
            act(p.line, 0)
            return
        pl.when(p.line - distance >= 0)(lambda: act(p.line - distance, 1))
        pl.when(p.line + distance < p.length)(lambda: act(p.line + distance, -1))

    def arrive(self, distance):
        p = self.p

        def act(line, way):
            src = None
            if way == 0:
                src = self.shard
                self.own_copy().start()
            else:
                self.up_copy(line).wait_recv()
            if way >= 0:
                pl.when(p.line < p.length - 1)(lambda: self.up_copy(line, src).start())
            if way <= 0:
                pl.when(p.line > 0)(lambda: self.down_copy(line, src).start())
            self.y_copy(line, src).start()
            if way and self.split:
                self.x_copy(line, True).start()
            self.d_copy(0, line, way == 0, src).start()

        self.each_at(distance, act)

    def arrive_y(self, distance):
        def act(line, way):
            self.y_landing(line).wait_recv()
            self.x_copy(line, False).start()
            self.d_copy(1, line).start()
            if way and self.split:
                self.x_landing(line, True).wait_recv()
                self.d_copy(3, line).start()

        self.each_at(distance, act)

    def arrive_x(self, distance):
        def act(line, way):
            self.x_landing(line, False).wait_recv()
            self.d_copy(2, line).start()

        self.each_at(distance, act)

    def stage(self):
        time, length = self.time, self.p.length
        self.time += 1
        if time < length:
            self.arrive(time)
        if 0 <= time - 1 < length:
            self.arrive_y(time - 1)
        if 0 <= time - 2 < length:
            self.arrive_x(time - 2)

    def under_way(self):
        return self.time < self.p.length + 2

    def take(self):
        p = self.p
        self.own_copy().wait()
        for line in range(p.length):
            for kind in range(3):
                if kind or not self.split:
                    self.d_copy(kind, line, core=1 - p.core).wait_recv()
            if self.split:
                pl.when(p.line == line)(lambda line=line: self.d_copy(0, line, True, core=1 - p.core).wait_recv())

                @pl.when(p.line != line)
                def _(line=line):
                    self.d_copy(0, line, core=1 - p.core).wait_recv()
                    self.d_copy(3, line, core=1 - p.core).wait_recv()

    def close(self):
        p = self.p
        for line in range(p.length):
            for kind in range(3):
                if kind or not self.split:
                    self.d_copy(kind, line).wait_send()
            if self.split:
                pl.when(p.line == line)(lambda line=line: self.d_copy(0, line, True).wait_send())

                @pl.when(p.line != line)
                def _(line=line):
                    self.d_copy(0, line).wait_send()
                    self.d_copy(3, line).wait_send()
                    self.x_copy(line, True).wait_send()

            self.y_copy(line).wait_send()
            self.x_copy(line, False).wait_send()
            pl.when((p.line >= line) & (p.line < p.length - 1))(lambda line=line: self.up_copy(line).wait_send())
            pl.when((p.line <= line) & (p.line > 0))(lambda line=line: self.down_copy(line).wait_send())


class Supply:
    def __init__(self, gathers, starts):
        self.entries = list(zip(starts, gathers))
        self.time = 0

    def tick(self):
        for start, gather in self.entries:
            if start <= self.time and gather.under_way():
                gather.stage()
        self.time += 1

    def need(self, gather):
        while gather.under_way():
            self.tick()
        gather.take()


class Chunk:
    def __init__(self, place, index, refs, store):
        self.p = place
        self.store = store
        (grads, self_d, xy, lo, hi, tb, fb, ds, dr, xs, xr, ys, yr, us, ur, ns, nr, fs, fr) = refs
        self.mine, self.other = grads.at[index, 0], grads.at[index, 1]
        self.d, self.xy = self_d.at[index], xy.at[index]
        third = xy.shape[-1] // 3
        self.xb, self.yb = self.xy.at[:, :, pl.ds(0, third)], self.xy.at[:, :, pl.ds(third, 2 * third)]
        self.lo, self.hi = lo.at[index], hi.at[index]
        self.tb, self.fb = tb.at[index], fb.at[index]
        self.sems = [s.at[index] for s in (ds, dr, xs, xr, ys, yr)]
        self.us, self.ur, self.ns, self.nr = us.at[index], ur.at[index], ns.at[index], nr.at[index]
        self.fs, self.fr = fs.at[index], fr.at[index]

    @staticmethod
    def scratch(count, length, rows, cols):
        low = jnp.bfloat16
        dma = pltpu.SemaphoreType.DMA
        return [
            pltpu.VMEM((count, 2, length, 2, rows, cols), low),
            pltpu.VMEM((count, length, 2, rows, cols), low),
            pltpu.VMEM((count, length, rows, cols), low),
            pltpu.VMEM((count, length - 1, rows, cols), low),
            pltpu.VMEM((count, length - 1, rows, cols), low),
            pltpu.VMEM((count, rows, cols), low),
            pltpu.VMEM((count, rows, cols), low),
        ] + [dma((count,))] * 6 + [dma((count, length))] * 4 + [dma((count,))] * 2

    def third(self, which, count=1):
        width = self.tb.shape[1] // 3
        return pl.ds(pl.multiple_of(which * width, width), count * width)

    def d_copy(self):
        return remote(self.other, self.d, self.sems[0], self.sems[1], self.p.sibling())

    def x_copy(self):
        p = self.p
        src = self.mine.at[:, 1 - p.y, :, self.third(2 * (1 - p.x))]
        return remote(src, self.xb, self.sems[2], self.sems[3], p.beside_x())

    def y_copy(self):
        p = self.p
        src = self.mine.at[:, 1 - p.y, :, self.third(p.x, 2)]
        return remote(src, self.yb, self.sems[4], self.sems[5], p.beside_y())

    def up_copy(self, line):
        p = self.p
        return remote(self.mine.at[line, p.y], self.lo.at[line - 1], self.us.at[line], self.ur.at[line], p.above())

    def down_copy(self, line):
        p = self.p
        return remote(self.mine.at[line, p.y], self.hi.at[line], self.ns.at[line], self.nr.at[line], p.below())

    def f_copy(self):
        return remote(self.tb, self.fb, self.fs, self.fr, self.p.beside_x())

    def each(self, act):
        def body(line, carry):
            act(line)
            return carry

        lax.fori_loop(0, self.p.length, body, 0)

    def start(self):
        self.d_copy().start()

    def pair(self):
        p = self.p
        self.d_copy().wait()

        def other(line):
            self.mine[line, 1 - p.y] = self.mine[line, 1 - p.y] + self.d[line, 1 - p.y]

        self.each(other)
        self.x_copy().start()

        def own(line):
            self.mine[line, p.y] = self.mine[line, p.y] + self.d[line, p.y]

        self.each(own)

    def over_x(self):
        p = self.p
        self.x_copy().wait()

        def act(line):
            cols = self.third(2 * p.x)
            self.mine[line, 1 - p.y, :, cols] = self.mine[line, 1 - p.y, :, cols] + self.xb[line]

        self.each(act)
        self.y_copy().start()

    def over_y(self):
        p = self.p
        self.y_copy().wait()

        def act(line):
            cols = self.third(p.x, 2)
            self.mine[line, p.y, :, cols] = self.mine[line, p.y, :, cols] + self.yb[line]

        self.each(act)
        self.hop(0)

    def take_low(self, line):
        self.up_copy(line).wait_recv()
        self.mine[line, self.p.y] = self.mine[line, self.p.y] + self.lo[line - 1]

    def take_high(self, line):
        self.down_copy(line).wait_recv()
        self.mine[line, self.p.y] = self.mine[line, self.p.y] + self.hi[line]

    def hop(self, step):
        p = self.p
        last = p.length - 1
        up = last - step + p.line

        def upward():
            pl.when(p.line > 0)(lambda: self.take_low(up))
            self.up_copy(up).start()

        pl.when(p.line <= step)(upward)
        down = step - last + p.line

        def downward():
            pl.when(p.line < last)(lambda: self.take_high(down))
            self.down_copy(down).start()

        pl.when(down >= 0)(downward)

    def total(self):
        p = self.p
        mine = p.line
        pl.when(mine > 0)(lambda: self.take_low(mine))
        pl.when(mine < p.length - 1)(lambda: self.take_high(mine))
        self.tb[...] = self.mine[mine, p.y]
        self.f_copy().start()

    def finish(self):
        p = self.p
        self.f_copy().wait()
        self.store(self.tb[...].astype(jnp.float32) + self.fb[...].astype(jnp.float32))
        for line in range(p.length - 1):
            pl.when(line + 1 > p.line)(lambda line=line: self.up_copy(line + 1).wait_send())
            pl.when(line < p.line)(lambda line=line: self.down_copy(line).wait_send())

    def acts(self):
        hops = [functools.partial(self.hop, step) for step in range(1, self.p.length - 1)]
        return [self.pair, self.over_x, self.over_y] + hops + [self.total, self.finish]


class Train:
    def __init__(self):
        self.running = []

    def add(self, acts):
        self.running.append(list(acts))

    def tick(self):
        for acts in reversed(self.running):
            acts.pop(0)()
        self.running = [acts for acts in self.running if acts]

    def drain(self):
        while self.running:
            self.tick()


class SmallSum:
    def __init__(self, place, refs):
        self.p = place
        self.stages, self.got, self.lines, self.ss, self.sr, self.ls, self.lr = refs

    def copy(self, step):
        p = self.p
        goal = [p.sibling, p.beside_x, p.beside_y][step]()
        return remote(self.stages.at[step], self.got.at[step], self.ss.at[step], self.sr.at[step], goal)

    def line_copy(self, line):
        p = self.p
        return remote(
            self.stages.at[3], self.lines.at[p.line], self.ls.at[line], self.lr.at[p.line], p.at(line=line)
        )

    def line_landing(self, line):
        p = self.p
        return remote(self.stages.at[3], self.lines.at[line], self.ls.at[line], self.lr.at[line], p.at(line=line))

    def begin(self):
        self.copy(0).start()

    def step(self, index):
        p = self.p
        self.copy(index).wait()
        self.stages[index + 1] = self.stages[index] + self.got[index]
        if index < 2:
            self.copy(index + 1).start()
            return
        for line in range(p.length):
            pl.when(p.line != line)(lambda line=line: self.line_copy(line).start())
        self.lines[p.line] = self.stages[3]

    def end(self, store):
        p = self.p
        for line in range(p.length):
            pl.when(p.line != line)(lambda line=line: self.line_copy(line).wait_send())
            pl.when(p.line != line)(lambda line=line: self.line_landing(line).wait_recv())
        total = self.lines[0]
        for line in range(1, p.length):
            total = total + self.lines[line]
        store(total)

    def acts(self, store):
        return [functools.partial(self.step, k) for k in range(3)] + [lambda: self.end(store)]


def gelu_pair(hidden):
    ratio = (2.0 / 3.141592653589793) ** 0.5
    square = hidden * hidden
    curve = jnp.tanh(ratio * (hidden + 0.044715 * (square * hidden)))
    cdf = 0.5 * (1.0 + curve)
    slope = cdf + hidden * (0.5 * (1.0 - curve * curve)) * (ratio * (1.0 + (3.0 * 0.044715) * square))
    return hidden * cdf, slope


def norm_back(value, gain, grad):
    scale = unit_scale(value)
    unit = value * scale
    lifted = grad * gain
    pull = jnp.mean(lifted * unit, axis=-1, keepdims=True)
    return scale * (lifted - unit * pull), grad * unit


def column_sum(value):
    return jnp.sum(value.astype(jnp.float32), axis=0, keepdims=True)


def swap_halves(value):
    shards = lax.axis_size("fsdp")
    pairs = []
    for x in range(2):
        for index in range(shards):
            core = index % 2
            goal = (x, index) if core == x else (1 - x, index ^ 1)
            pairs.append((x * shards + index, goal[0] * shards + goal[1]))
    return lax.ppermute(value, ("seq", "fsdp"), pairs)


def pair_all_to_all(value, split_axis, concat_axis):
    shards = lax.axis_size("fsdp")
    groups = [[k, k + 1] for k in range(0, shards, 2)]
    return lax.all_to_all(
        value, "fsdp", split_axis=split_axis, concat_axis=concat_axis, axis_index_groups=groups, tiled=True
    )


def pack_rows(parts, width):
    rows = [jnp.pad(p, ((0, 0), (0, width - p.shape[1]))) for p in parts]
    packed = jnp.concatenate(rows, axis=0)
    return jnp.pad(packed, ((0, 16 - packed.shape[0]), (0, 0)))


def local_general(residual_in, cotangent, w_qkv, w_out, w_fc, w_proj, attn_bias, fc_bias, proj_bias, gains):
    shards = lax.axis_size("fsdp")
    tok_rows = residual_in.shape[1]
    model_width = w_qkv.shape[1] // 3
    hidden_width = w_fc.shape[1]
    unit = gains.shape[1]
    share = model_width // 2
    head_count = share // HD
    scale = HD ** (-0.5)
    small = pack_rows([attn_bias, gains, proj_bias[None], fc_bias[None]], 256)
    compact = swap_halves(residual_in[0]).astype(jnp.float32)
    upstream = swap_halves(cotangent[0]).astype(jnp.float32)
    qkv_w, small_all, out_w, fc_w, proj_w = gather_all(
        [w_qkv, small, w_out, w_fc, w_proj], shards, [0, 0, 2, 3, 5], 0
    )
    qkv_w = qkv_w.reshape(model_width, 3 * model_width)
    out_w = out_w.reshape(model_width, model_width)
    fc_w = fc_w.reshape(model_width, hidden_width)
    proj_w = proj_w.reshape(hidden_width, model_width)
    vectors = small_all[:, :6, :unit].transpose(1, 0, 2).reshape(6, model_width).astype(jnp.float32)
    bias_all, gain_all, proj_b = vectors[:3], vectors[3:5], vectors[5]
    fc_b = small_all[:, 6, : fc_bias.shape[0]].reshape(hidden_width).astype(jnp.float32)
    full = jnp.concatenate([compact, -jnp.sum(compact, axis=-1, keepdims=True)], axis=-1)
    normed = rms_norm(full, gain_all[0]).astype(jnp.bfloat16)
    bias_qkv = jnp.concatenate([bias_all[0], jnp.zeros_like(bias_all[0]), bias_all[1]])
    projected = (matmul(normed, qkv_w) + bias_qkv).astype(jnp.bfloat16)
    by_heads = pair_all_to_all(projected.reshape(tok_rows, 3, 2, share), 2, 0)
    length = by_heads.shape[0]
    queries = by_heads[:, 0, 0].reshape(length, head_count, HD)
    keys_all = by_heads[:, 1, 0].reshape(length, head_count, HD)
    values_all = by_heads[:, 2, 0].reshape(length, head_count, HD)
    attended, log_totals = attend(queries, keys_all, values_all, scale)
    mixed = pair_all_to_all(attended.reshape(length, 1, share), 0, 1)
    mixed = mixed.reshape(tok_rows, model_width)
    branch = matmul(mixed, out_w) + bias_all[2]
    middle = full + center(branch)
    normed_two = rms_norm(middle, gain_all[1]).astype(jnp.bfloat16)
    hidden = matmul(normed_two, fc_w) + fc_b
    activated = gelu_tanh(hidden).astype(jnp.bfloat16)
    branch_two = matmul(activated, proj_w) + proj_b
    final = middle + center(branch_two)
    residual_out = swap_halves(final[:, :-1].astype(jnp.bfloat16))[None]
    grad_final = jnp.concatenate([upstream, jnp.zeros((tok_rows, 1), jnp.float32)], axis=-1)
    grad_branch_two = center(grad_final).astype(jnp.bfloat16)
    grad_proj = weight_grad(activated, grad_branch_two)
    grad_proj_bias = jnp.sum(grad_branch_two.astype(jnp.float32), axis=0)
    grad_activated = input_grad_of(grad_branch_two, proj_w)
    gelu_pull = jax.vjp(gelu_tanh, hidden)[1]
    grad_hidden = gelu_pull(grad_activated)[0].astype(jnp.bfloat16)
    grad_fc = weight_grad(normed_two, grad_hidden)
    grad_fc_bias = jnp.sum(grad_hidden.astype(jnp.float32), axis=0)
    grad_normed_two = input_grad_of(grad_hidden, fc_w)
    second_pull = jax.vjp(rms_norm, middle, gain_all[1])[1]
    grad_middle_norm, grad_gain_two = second_pull(grad_normed_two)
    grad_middle = grad_final + grad_middle_norm
    grad_branch = center(grad_middle).astype(jnp.bfloat16)
    grad_out = weight_grad(mixed, grad_branch)
    grad_out_bias = jnp.sum(grad_branch.astype(jnp.float32), axis=0)
    grad_mixed = input_grad_of(grad_branch, out_w).astype(jnp.bfloat16)
    grad_heads = pair_all_to_all(grad_mixed.reshape(tok_rows, 2, share), 1, 0)
    grad_heads = grad_heads.reshape(length, head_count, HD)
    grad_queries, grad_keys, grad_values = attend_back(
        queries, keys_all, values_all, log_totals, grad_heads, scale
    )
    stacked = jnp.stack([grad_queries, grad_keys, grad_values], axis=1).reshape(length, 3, 1, share)
    grad_projected = pair_all_to_all(stacked, 0, 2)
    grad_projected = grad_projected.reshape(tok_rows, 3 * model_width)
    grad_qkv = weight_grad(normed, grad_projected)
    column_sums = jnp.sum(grad_projected.astype(jnp.float32), axis=0)
    grad_normed = input_grad_of(grad_projected, qkv_w)
    first_pull = jax.vjp(rms_norm, full, gain_all[0])[1]
    grad_full_norm, grad_gain_one = first_pull(grad_normed)
    grad_full = grad_middle + grad_full_norm
    input_grad = swap_halves((grad_full[:, :-1] - grad_full[:, -1:]).astype(jnp.bfloat16))[None]
    rows = jnp.stack(
        [
            column_sums[:model_width],
            column_sums[2 * model_width :],
            grad_out_bias,
            grad_gain_one,
            grad_gain_two,
            grad_proj_bias,
        ]
    )
    rows = rows.reshape(6, shards, unit).transpose(1, 0, 2)
    last = grad_fc_bias.reshape(shards, 1, fc_bias.shape[0])
    grad_small = jnp.concatenate(
        [
            jnp.pad(rows, ((0, 0), (0, 0), (0, 256 - unit))),
            jnp.pad(last, ((0, 0), (0, 9), (0, 256 - fc_bias.shape[0]))),
        ],
        axis=1,
    )

    def split(grad):
        return grad.astype(jnp.bfloat16).reshape(shards, grad.shape[0] // shards, grad.shape[1])

    total_proj, total_fc, total_out, total_qkv, total_small = scatter_all(
        [split(grad_proj), split(grad_fc), split(grad_out), split(grad_qkv), grad_small.astype(jnp.bfloat16)],
        shards,
        [0, 1, 2, 3, 3],
        1,
    )
    return (
        residual_out,
        input_grad,
        total_qkv,
        total_out,
        total_fc,
        total_proj,
        total_small[:3, :unit],
        total_small[6, : fc_bias.shape[0]],
        total_small[5, :unit],
        total_small[3:5, :unit],
    )


def layer_kernel(shards, starts, *refs):
    (resid, cot, w_qkv, w_out, w_fc, w_proj, attn_bias, fc_bias, proj_bias, gains,
     total_qkv, total_out, total_fc, total_proj, total_attn_bias, total_fc_bias, total_proj_bias, total_gains,
     resid_o, input_o, qkv_o, fc_o, proj_o,
     fc_own, proj_own, fetch, own_small, small_w, spread, vec, rs, cs, normed, heads, mixed,
     wo, tiles, work, middle, acc, gn, got, gproj, key_sum, value_sum, ro, ig, sg, *rest) = refs
    chunk_refs, rest = rest[:19], rest[19:]
    small_refs, rest = rest[:7], rest[7:]
    place = Place(shards)
    low = jnp.bfloat16
    rows, width = mixed.shape
    share = width // 2
    unit = width // shards
    parts = fc_o.shape[0]
    deep = total_proj.shape[0]
    span = 2 * HD
    pairs = share // span
    block = min(256, rows)
    per = len(Gather.sem_shapes(1))

    def columns(ref, part):
        return ref.at[:, pl.ds(part * width, width)]

    gathers = []

    def gather(src, dst, split=False):
        nonlocal rest
        item = Gather(place, src, dst, rest[:per], split)
        rest = rest[per:]
        gathers.append(item)
        return item

    qkv_in = [gather(columns(w_qkv, part), tiles.at[part]) for part in range(3)]
    small_in = gather(own_small, small_w)
    out_in = gather(w_out, wo)
    fc_in = [gather(columns(fc_own, part), fc_o.at[part]) for part in range(parts)]
    proj_in = gather(proj_own, proj_o, True)
    own_loads = [
        pltpu.make_async_copy(w_fc, fc_own, fetch.at[0]),
        pltpu.make_async_copy(w_proj, proj_own, fetch.at[1]),
    ]
    for load in own_loads:
        load.start()
    supply = Supply(gathers, starts)
    (si_s, si_r, sc_s, sc_r, ex_s, ex_r, at_s, at_r, ks, wsem, ro_s, ro_r, ig_s, ig_r,
     gm_s, gm_r, gp_s, gp_r) = rest
    swap_in = Swap(place, resid.at[0], rs, (si_s, si_r))
    swap_cot = Swap(place, cot.at[0], cs, (sc_s, sc_r))

    spread[...] = jnp.zeros_like(spread)
    spread[0, 0:3, 0:unit] = attn_bias[...].astype(jnp.float32)
    spread[0, 3:5, 0:unit] = gains[...].astype(jnp.float32)
    spread[0, 5:6, 0:unit] = proj_bias[...].reshape(1, unit).astype(jnp.float32)
    wide = fc_bias.shape[0]
    in_row = width // wide
    for part in range(parts):
        spread[1, 6 + part : 7 + part, 0:wide] = fc_bias[...].reshape(1, wide).astype(jnp.float32)
    moved = pltpu.roll(spread[0], place.index * unit, 1)
    hidden_rows = pltpu.roll(spread[1], lax.rem(place.index, in_row) * wide, 1)
    row_ids = lax.broadcasted_iota(jnp.int32, moved.shape, 0)
    moved = jnp.where(row_ids < 6, moved, jnp.where(row_ids == 6 + place.index // in_row, hidden_rows, 0.0))
    own_small[...] = moved.astype(low)

    place.greet(diagonal=True, whole_line=True)
    supply.tick()
    for load in own_loads:
        load.wait()
    swap_in.start()
    supply.need(small_in)
    swap_cot.start()
    vec[...] = jnp.sum(small_w[...].astype(jnp.float32), axis=(0, 1, 2))
    swap_in.wait()

    def whole(here):
        value = rs[here, :].astype(jnp.float32)
        return jnp.concatenate([value, -jnp.sum(value, axis=-1, keepdims=True)], axis=1)

    def normalize(here):
        full = whole(here)
        normed[here, :] = (full * unit_scale(full) * vec[3:4, :]).astype(low)

    over_rows(rows, 128, normalize)
    for item in qkv_in:
        supply.need(item)

    flat = tiles.reshape(4, width, width)
    out_flat = wo.reshape(width, width)
    keep = [pltpu.make_async_copy(tiles.at[part], qkv_o.at[part], ks.at[part]) for part in range(3)]
    for copy in keep:
        copy.start()
    my_rows = pl.ds(pl.multiple_of(place.core * rows, rows), rows)

    def exchange(part):
        src = work.at[part, :, pl.ds(0, share)]
        return remote(src, heads.at[part, my_rows], ex_s.at[part], ex_r.at[part], place.sibling())

    def project(part, group):
        result = dot_nn(normed[...], flat[part, :, lane_block(group, share)])
        if part != 1:
            bias = part // 2
            result = result + vec[bias : bias + 1, lane_block(group, share)]
        return result.astype(low)

    for part in range(3):
        work[part, :, pl.ds(0, share)] = project(part, 1 - place.core)
        exchange(part).start()
    supply.tick()
    for part in range(3):
        heads[part, my_rows, :] = project(part, place.core)
    supply.tick()
    for part in range(3):
        exchange(part).wait()

    def my_pair(pair):
        return pl.ds(pl.multiple_of(place.core * share + pair * span, span), span)

    def back(pair):
        src = got.at[1 - place.core, :, pl.ds(pair * span, span)]
        return remote(src, mixed.at[:, my_pair(pair)], at_s.at[pair], at_r.at[pair], place.sibling())

    for pair in range(pairs):
        lanes = pl.ds(pair * span, span)

        def put_result(start, size, value):
            got[start // rows, pl.ds(start % rows, size), lanes] = value

        attend_pair(heads, pair, put_result)
        back(pair).start()
        mixed[:, my_pair(pair)] = got[place.core, :, lanes]
        supply.tick()
    for copy in keep:
        copy.wait()
    for item in qkv_in:
        item.close()

    train = Train()

    def fc_load(tile):
        return pltpu.make_async_copy(fc_o.at[tile], tiles.at[tile % 2], wsem.at[tile % 2])

    def proj_load(tile):
        src = proj_o.reshape(parts, width, width).at[tile]
        return pltpu.make_async_copy(src, flat.at[2 + tile % 2], wsem.at[2 + tile % 2])

    def qkv_load(part):
        return pltpu.make_async_copy(qkv_o.at[part], tiles.at[part], wsem.at[part])

    sg[...] = jnp.zeros_like(sg)

    def put_qkv(part):
        def store(value):
            total_qkv[:, pl.ds(part * width, width)] = value
        return store

    def put_fc(tile):
        def store(value):
            total_fc[:, pl.ds(tile * width, width)] = value
        return store

    def put_proj(part):
        def store(value):
            total_proj[pl.ds(part * unit, unit), :] = value
        return store

    def put_out(value):
        total_out[...] = value

    stores = [put_fc(k) for k in range(parts)] + [put_proj(k) for k in range(parts)]
    stores += [put_out] + [put_qkv(k) for k in range(3)]
    chunks = [Chunk(place, k, chunk_refs, store) for k, store in enumerate(stores)]
    fc_chunks, proj_chunks = chunks[:parts], chunks[parts : 2 * parts]
    out_chunk, qkv_chunks = chunks[2 * parts], chunks[2 * parts + 1 :]
    grads = chunk_refs[0]

    def keep_rows(index, first, value):
        value = value.astype(low)
        for k in range(value.shape[0] // unit):
            shard = first + k
            side = lax.rem(place.core + shard % 2, 2)
            grads[index, side, shard // 4, (shard // 2) % 2] = value[k * unit : (k + 1) * unit]

    def weight_grad_chunk(index, left, right):
        for part in range(2):
            lanes = pl.ds(part * share, share)
            keep_rows(index, part * (shards // 2), dot_tn(left[:, lanes], right))
        chunks[index].start()

    act_ref, slope_ref, n2, g2 = work.at[0], work.at[1], work.at[2], work.at[3]
    supply.need(out_in)
    for pair in range(pairs):
        back(pair).wait()
    swap_cot.wait()

    def upstream(here):
        value = cs[here, :].astype(jnp.float32)
        return jnp.concatenate([value, jnp.zeros((value.shape[0], 1), jnp.float32)], axis=1)

    def enter(here):
        branch = dot_nn(mixed[here, :], out_flat[...]) + vec[2:3, :]
        value = whole(here) + branch - jnp.mean(branch, axis=-1, keepdims=True)
        middle[here, :] = value
        n2[here, :] = (value * unit_scale(value) * vec[4:5, :]).astype(low)
        grad = upstream(here)
        grad = (grad - jnp.mean(grad, axis=-1, keepdims=True)).astype(low)
        g2[here, :] = grad
        sg[5:6, :] += column_sum(grad)

    over_rows(rows, block, enter)
    supply.need(fc_in[0])
    fc_load(0).start()
    supply.need(proj_in)
    proj_load(0).start()
    proj_load(1).start()

    for tile in range(parts):
        if tile:
            supply.need(fc_in[tile])
            fc_load(tile).start()
        fc_load(tile).wait()
        proj_load(tile).wait()
        fc_tile, proj_tile = flat.at[tile % 2], flat.at[2 + tile % 2]

        def feed(here):
            hidden = dot_nn(n2[here, :], fc_tile[...]) + vec[6 + tile : 7 + tile, :]
            value, slope = gelu_pair(hidden)
            value = value.astype(low)
            act_ref[here, :] = value
            grad = (dot_nt(g2[here, :], proj_tile[...]) * slope).astype(low)
            slope_ref[here, :] = grad
            sg[6 + tile : 7 + tile, :] += column_sum(grad)

        def carry_on(here):
            forward = dot_nn(act_ref[here, :], proj_tile[...])
            backward = dot_nt(slope_ref[here, :], fc_tile[...])
            if tile == 0:
                acc[here, :] = forward
                gn[here, :] = backward
            else:
                acc[here, :] += forward
                gn[here, :] += backward

        over_rows(rows, rows, feed)
        weight_grad_chunk(tile, n2, slope_ref[...])
        train.add(fc_chunks[tile].acts())
        over_rows(rows, rows, carry_on)
        if tile + 2 < parts:
            proj_load(tile + 2).start()
        for part in range(2):
            lanes = pl.ds(part * share, share)
            value = dot_tn(act_ref[:, lanes], g2[...])
            first = (tile * width + part * share) // deep
            for k in range(share // deep):
                for q in range(parts):
                    at = k * deep + q * unit
                    keep_rows(parts + q, first + k, value[at : at + unit])
        train.tick()

    for item in proj_chunks:
        item.start()

    def leave(here):
        branch = acc[here, :] + vec[5:6, :]
        value = middle[here, :]
        final = value + branch - jnp.mean(branch, axis=-1, keepdims=True)
        ro[here, :] = final[:, : width - 1].astype(low)
        pull, terms = norm_back(value, vec[4:5, :], gn[here, :])
        sg[4:5, :] += jnp.sum(terms, axis=0, keepdims=True)
        grad = upstream(here) + pull
        acc[here, :] = grad
        grad = (grad - jnp.mean(grad, axis=-1, keepdims=True)).astype(low)
        g2[here, :] = grad
        sg[2:3, :] += column_sum(grad)

    over_rows(rows, block // 2, leave)
    pieces = 4

    def piece(src, dst, sems, k):
        here = pl.ds(k * (rows // pieces), rows // pieces)
        return Swap(place, src.at[here], dst.at[0, here], (sems[0].at[k], sems[1].at[k]))

    swap_out = [piece(ro, resid_o, (ro_s, ro_r), k) for k in range(pieces)]
    swap_back = [piece(ig, input_o, (ig_s, ig_r), k) for k in range(pieces)]
    swap_out[0].start()
    train.add(proj_chunks[0].acts())
    train.tick()

    def mixed_grad(group):
        lanes = pl.ds(pl.multiple_of(group * share, 128), share)
        return dot_nt(g2[...], out_flat[lanes, :]).astype(low)

    n2[:, pl.ds(0, share)] = mixed_grad(1 - place.core)
    give = remote(n2.at[:, pl.ds(0, share)], got.at[place.core], gm_s, gm_r, place.sibling())
    give.start()
    got[place.core] = mixed_grad(place.core)
    weight_grad_chunk(2 * parts, mixed, g2[...])
    train.add(proj_chunks[1].acts())
    swap_out[1].start()
    for part in range(3):
        qkv_load(part).start()
    train.tick()
    give.wait()

    def send(part, pair):
        lanes = pl.multiple_of((1 - place.core) * share + pair * span, span)
        src = work.at[part, :, pl.ds(lanes, span)]
        at = pl.multiple_of((part * 2 + place.core) * share + pair * span, span)
        return remote(src, gproj.at[:, pl.ds(at, span)], gp_s.at[part, pair], gp_r.at[part, pair], place.sibling())

    waiting = proj_chunks[2:] + [out_chunk]
    for pair in range(pairs):
        for item in waiting[: -(-len(waiting) // (pairs - pair))]:
            train.add(item.acts())
            waiting.remove(item)

        def put(part, start, size, value):
            lanes = pl.ds(start // rows * share + pair * span, span)
            work[part, pl.ds(start % rows, size), lanes] = value

        attend_back_pair(heads, got, pair, key_sum, value_sum, put)
        if pair + 2 < pieces:
            swap_out[pair + 2].start()
        train.tick()
        for part in range(3):
            send(part, pair).start()
            at = pl.multiple_of((part * 2 + place.core) * share + pair * span, span)
            gproj[:, pl.ds(at, span)] = work[part, :, my_pair(pair)]
    for pair in range(pairs):
        for part in range(3):
            send(part, pair).wait()

    for part in range(3):
        lanes = pl.ds(part * width, width)
        weight_grad_chunk(2 * parts + 1 + part, normed, gproj[:, lanes])
        train.add(qkv_chunks[part].acts())
        train.tick()

    for part in range(3):
        qkv_load(part).wait()

    def last(here):
        grad = dot_nt(gproj[here, pl.ds(0, width)], flat[0])
        grad += dot_nt(gproj[here, pl.ds(width, width)], flat[1])
        grad += dot_nt(gproj[here, pl.ds(2 * width, width)], flat[2])
        sg[0:1, :] += column_sum(gproj[here, pl.ds(0, width)])
        sg[1:2, :] += column_sum(gproj[here, pl.ds(2 * width, width)])
        pull, terms = norm_back(whole(here), vec[3:4, :], grad)
        sg[3:4, :] += jnp.sum(terms, axis=0, keepdims=True)
        grad = acc[here, :] + pull
        ig[here, :] = (grad[:, : width - 1] - grad[:, width - 1 :]).astype(low)

    for k in range(pieces):
        last(pl.ds(k * (rows // pieces), rows // pieces))
        swap_back[k].start()
        if k % 2:
            train.tick()
    small = SmallSum(place, small_refs)
    small_refs[0][0] = sg[...]
    small.begin()

    def put_small(value):
        mine = pltpu.roll(value, width - place.index * unit, 1)
        total_attn_bias[...] = mine[0:3, :unit]
        total_gains[...] = mine[3:5, :unit]
        total_proj_bias[...] = mine[5:6, :unit].reshape(unit)
        hidden = pltpu.roll(value, width - lax.rem(place.index, in_row) * wide, 1)[:, :wide]
        hidden_ids = lax.broadcasted_iota(jnp.int32, hidden.shape, 0)
        hidden = jnp.where(hidden_ids == 6 + place.index // in_row, hidden, 0.0)
        total_fc_bias[...] = jnp.sum(hidden, axis=0, keepdims=True).reshape(wide)

    train.add(small.acts(put_small))
    train.drain()
    for item in gathers[3:]:
        item.close()
    for swap in swap_out + swap_back:
        swap.wait()


def finish_kernel(count, *refs):
    ins, outs, held = refs[:count], refs[count : 2 * count], refs[2 * count : 3 * count]
    sems = refs[3 * count]
    loads = [pltpu.make_async_copy(ins[k], held[k], sems.at[0, k]) for k in range(count)]
    stores = [pltpu.make_async_copy(held[k], outs[k], sems.at[1, k]) for k in range(count)]
    for load in loads:
        load.start()
    for load, store in zip(loads, stores):
        load.wait()
        store.start()
    for store in stores:
        store.wait()


def finish(arrays):
    count = len(arrays)
    return pl.pallas_call(
        functools.partial(finish_kernel, count),
        out_shape=[jax.ShapeDtypeStruct(a.shape, a.dtype) for a in arrays],
        in_specs=[ANY] * count,
        out_specs=[ANY] * count,
        scratch_shapes=[pltpu.VMEM(a.shape, a.dtype) for a in arrays]
        + [pltpu.SemaphoreType.DMA((2, count))],
        compiler_params=pltpu.CompilerParams(vmem_limit_bytes=62 << 20),
        name="finish",
    )(*arrays)


def local_tiled(residual_in, cotangent, w_qkv, w_out, w_fc, w_proj, attn_bias, fc_bias, proj_bias, gains):
    shards = lax.axis_size("fsdp")
    length = shards // 4
    rows = residual_in.shape[1]
    width = w_qkv.shape[1] // 3
    share = width // 2
    unit = width // shards
    parts = w_fc.shape[1] // width
    deep = w_proj.shape[0]
    pairs = share // (2 * HD)
    low, f32 = jnp.bfloat16, jnp.float32
    vmem = pl.BlockSpec(memory_space=pltpu.VMEM)
    dma = pltpu.SemaphoreType.DMA
    small = (16, width)
    starts = [0, 0, 0, 0, 5] + [5 + part for part in range(parts)] + [5]
    outs = [
        jax.ShapeDtypeStruct((unit, 3 * width), f32),
        jax.ShapeDtypeStruct((unit, width), f32),
        jax.ShapeDtypeStruct((unit, parts * width), f32),
        jax.ShapeDtypeStruct((deep, width), f32),
        jax.ShapeDtypeStruct(attn_bias.shape, f32),
        jax.ShapeDtypeStruct(fc_bias.shape, f32),
        jax.ShapeDtypeStruct(proj_bias.shape, f32),
        jax.ShapeDtypeStruct(gains.shape, f32),
        jax.ShapeDtypeStruct(residual_in.shape, low),
        jax.ShapeDtypeStruct(residual_in.shape, low),
        jax.ShapeDtypeStruct((3, length, 2, 2, unit, width), low),
        jax.ShapeDtypeStruct((parts, length, 2, 2, unit, width), low),
        jax.ShapeDtypeStruct((length, 2, 2, deep, width), low),
    ]
    scratch = [
        pltpu.VMEM(w_fc.shape, low),
        pltpu.VMEM(w_proj.shape, low),
        dma((2,)),
        pltpu.VMEM(small, low),
        pltpu.VMEM((length, 2, 2) + small, low),
        pltpu.VMEM((2,) + small, f32),
        pltpu.VMEM(small, f32),
        pltpu.VMEM((rows, width - 1), low),
        pltpu.VMEM((rows, width - 1), low),
        pltpu.VMEM((rows, width), low),
        pltpu.VMEM((3, 2 * rows, share), low),
        pltpu.VMEM((rows, width), low),
        pltpu.VMEM((length, 2, 2, unit, width), low),
        pltpu.VMEM((4, length, 2, 2, unit, width), low),
        pltpu.VMEM((4, rows, width), low),
        pltpu.VMEM((rows, width), f32),
        pltpu.VMEM((rows, width), f32),
        pltpu.VMEM((rows, width), f32),
        pltpu.VMEM((2, rows, share), low),
        pltpu.VMEM((rows, 3 * width), low),
        pltpu.VMEM((2 * rows, 2 * HD), f32),
        pltpu.VMEM((2 * rows, 2 * HD), f32),
        pltpu.VMEM((rows, width - 1), low),
        pltpu.VMEM((rows, width - 1), low),
        pltpu.VMEM(small, f32),
    ]
    scratch += Chunk.scratch(2 * parts + 4, length, unit, width)
    scratch += [
        pltpu.VMEM((4,) + small, f32),
        pltpu.VMEM((3,) + small, f32),
        pltpu.VMEM((length,) + small, f32),
        dma((3,)), dma((3,)), dma((length,)), dma((length,)),
    ]
    scratch += Gather.sem_shapes(length) * len(starts)
    scratch += [dma, dma, dma, dma, dma((3,)), dma((3,)), dma((pairs,)), dma((pairs,)), dma((3,)), dma((4,))]
    scratch += [dma((4,)), dma((4,)), dma((4,)), dma((4,)), dma, dma, dma((3, pairs)), dma((3, pairs))]
    results = pl.pallas_call(
        functools.partial(layer_kernel, shards, starts),
        out_shape=outs,
        in_specs=[ANY] * 6 + [vmem] * 4,
        out_specs=[vmem] * 8 + [ANY] * 5,
        scratch_shapes=scratch,
        compiler_params=pltpu.CompilerParams(
            collective_id=0, has_side_effects=True, vmem_limit_bytes=63 << 20
        ),
        name="layer",
    )(residual_in, cotangent, w_qkv, w_out, w_fc, w_proj, attn_bias, fc_bias, proj_bias, gains)
    (total_qkv, total_out, total_fc, total_proj, total_attn_bias, total_fc_bias, total_proj_bias, total_gains,
     residual_out, input_grad) = finish(results[:10])
    return (
        residual_out, input_grad, total_qkv, total_out, total_fc, total_proj,
        total_attn_bias, total_fc_bias, total_proj_bias, total_gains,
    )


def local(residual_in, cotangent, w_qkv, w_out, w_fc, w_proj, attn_bias, fc_bias, proj_bias, gains):
    arguments = (residual_in, cotangent, w_qkv, w_out, w_fc, w_proj, attn_bias, fc_bias, proj_bias, gains)
    if w_qkv.shape[0] % 16:
        return local_general(*arguments)
    return local_tiled(*arguments)


def solution(mesh):
    in_specs = (
        P("fsdp", "seq", None),
        P("fsdp", "seq", None),
        P("fsdp", None),
        P("fsdp", None),
        P("fsdp", None),
        P("fsdp", None),
        P(None, "fsdp"),
        P("fsdp"),
        P("fsdp"),
        P(None, "fsdp"),
    )
    out_specs = (
        P("fsdp", "seq", None),
        P("fsdp", "seq", None),
        P("fsdp", None),
        P("fsdp", None),
        P("fsdp", None),
        P("fsdp", None),
        P(None, "fsdp"),
        P("fsdp"),
        P("fsdp"),
        P(None, "fsdp"),
    )
    return jax.shard_map(local, mesh=mesh, in_specs=in_specs, out_specs=out_specs, check_vma=False)
```
